32 devices in a mesh: dp: 8 (over z, y), tensor: 4 (over x, core).
Axes of the slice: x: 2, y: 2, z: 4, core: 2. Of those that a mesh axis runs over, the one named last changes fastest.
Arguments:
- tokens: bfloat16 [2, 8192, 768], P(None, 'dp'), may hold values from -6 to 6
- cotangent: bfloat16 [2, 8192, 768], P(None, 'dp'), may hold values from -6 to 6
- prev_logits: float32 [2, 8192, 12], P(None, 'dp'), may hold values from -3 to 3
- routes: int32 [2, 8192, 2], P(None, 'dp'), may hold values from 0 to 11, all different within a row; in each aligned block of 1024 rows (0 to 1023, 1024 to 2047, ..., all dimensions but the last counted through in order) at most 256 rows name the same one
- norm_attn: bfloat16 [768], P('dp'), may hold values from 0.099609375 to 1.8984375
- norm_moe: bfloat16 [768], P('dp'), may hold values from 0.099609375 to 1.8984375
- w_qkv: bfloat16 [3, 768, 768], P(None, 'dp', 'tensor'), may hold values from -0.21875 to 0.21875
- w_out: bfloat16 [768, 768], P('tensor', 'dp'), may hold values from -3 to 3
- w_router: bfloat16 [768, 12], P('dp'), may hold values from -0.15625 to 0.15625
- w_const: bfloat16 [768, 4], P('dp'), may hold values from -0.21875 to 0.21875
- const_vec: bfloat16 [2, 768], P(None, 'dp'), may hold values from -5 to 5
- w_in: bfloat16 [8, 2, 768, 2048], P('dp', None, None, 'tensor'), may hold values from -0.21875 to 0.21875
- w_down: bfloat16 [8, 2048, 768], P('dp', 'tensor'), may hold values from -0.125 to 0.125
Outputs:
- result: bfloat16 [2, 8192, 768], P(None, 'dp')
- grad_tokens: bfloat16 [2, 8192, 768], P(None, 'dp')
- grad_prev: float32 [2, 8192, 12], P(None, 'dp')
- grad_norm_attn: float32 [768], P('dp')
- grad_norm_moe: float32 [768], P('dp')
- grad_qkv: float32 [3, 768, 768], P(None, 'dp', 'tensor')
- grad_out: float32 [768, 768], P('tensor', 'dp')
- grad_router: float32 [768, 12], P('dp')
- grad_const: float32 [768, 4], P('dp')
- grad_vec: float32 [2, 768], P(None, 'dp')
- grad_in: float32 [8, 2, 768, 2048], P('dp', None, None, 'tensor')
- grad_down: float32 [8, 2048, 768], P('dp', 'tensor')
The draws below stay inside these ranges and needn't reach their ends.
Inputs may be any that keep to these rules, and one draw needn't show every extreme that they name: Numbers below 8 name feed-forward experts; 8 is the zero expert, 9 the copy expert, 10 and 11 the constant experts. A token's two routes differ. In each micro-batch the 1024 tokens of one index of dp name each number at most 256 times, a bound that some block reaches.
All inputs are finite; a program needn't handle non-finite values.
Results may differ from the reference program's by a relative error of at most 0.015.
Values may be sent and summed in bfloat16 or wider, within the bound.
A program may use at most 320 MiB of HBM per device.

```python
import math
import jax
import jax.numpy as jnp
import numpy as np
from jax import lax

D = 768
HEADS = 12
HD = 64
FF = 2048
LEN = 1024
BLK = 256
MICRO = 2
EXPERTS = 8
ROWS = 1024
TOKENS = 8192
CAP = 256
N_DP = 8


def spiked(entries, key, source, target, shards_of, factor):
    def block_of(dim):
        return (jnp.arange(entries.shape[dim]) // (entries.shape[dim] // shards_of)).reshape((-1,) + (1,) * (entries.ndim - 1 - dim))

    first = jax.random.permutation(key, shards_of)[block_of(target)]
    second = (block_of(target) + shards_of // 2) % shards_of
    return jnp.where((block_of(source) == first) | (block_of(source) == second), factor * entries, entries)


def shard_levels(rng, shape, cuts, least, largest):
    gain = 1.0
    for position, blocks in cuts:
        steps = jax.random.uniform(jax.random.fold_in(jax.random.fold_in(rng, 6), position), (blocks,), jnp.float32, least / len(cuts), largest / len(cuts))
        gain = gain * jnp.repeat(jnp.exp(steps), shape[position] // blocks).reshape((-1,) + (1,) * (len(shape) - 1 - position))
    return gain


def deal_out(key, own, number, rows, amount, top, most, lean):
    sequence = jax.random.permutation(key, amount)
    heavy_load, ordinary = shares(amount, rows * top, most, lean, True), shares(amount, rows * top, most, lean, False)
    places = jnp.arange(amount)

    def named(sizes, rotation):
        used = int((sizes > 0).sum())
        fixed = max(1, used // 4)
        moved = fixed + (places - fixed + rotation * (used - fixed)) % max(1, amount - fixed)
        return jnp.zeros((amount,), jnp.int32).at[sequence[jnp.where(places < fixed, places, moved)]].set(jnp.asarray(sizes, jnp.int32))

    sizes = jnp.where(number % 4 == 0, named(heavy_load, number // 4), named(ordinary, number - number // 4 - 1))
    mixed = jax.random.permutation(jax.random.fold_in(own, 3), amount)
    donor, receiver = mixed[0:amount // 2 * 2:2], mixed[1:amount // 2 * 2:2]
    slack = jnp.minimum(sizes[donor] - 1, most - sizes[receiver]) // 2
    slack = jnp.where((donor == sequence[0]) | (receiver == sequence[0]) | (sizes[receiver] == 0), 0, jnp.maximum(slack, 0))
    moved = jax.random.randint(jax.random.fold_in(own, 4), (amount // 2,), 0, 1 << 20) % (slack + 1)
    sizes = sizes.at[donor].add(-moved).at[receiver].add(moved)
    items = jnp.searchsorted(jnp.cumsum(sizes), jnp.arange(rows * top), side="right").astype(jnp.int32)
    table = items.reshape(top, rows).T
    table = table[jax.random.permutation(jax.random.fold_in(own, 1), rows)]
    rotation = jax.random.randint(jax.random.fold_in(own, 2), (rows, 1), 0, top)
    return jnp.take_along_axis(table, (jnp.arange(top)[None, :] + rotation) % top, axis=1)


def shares(number_of, total, limit, skew, full):
    loads = [(1 << 20) // math.isqrt(standing ** skew) + 1 for standing in range(1, number_of + 1)]
    largest = limit if full else min(limit, max(-(-total // number_of), total * loads[0] // sum(loads)))
    least = 1 if total - largest >= number_of - 1 else 0
    counts, spare = [largest] + [least] * (number_of - 1), total - largest - least * (number_of - 1)
    while spare > 0:
        candidates = [i for i in range(1, number_of) if counts[i] < largest] or [i for i in range(1, number_of) if counts[i] < limit]
        pool, left = sum([loads[i] for i in candidates]), spare
        for i in candidates:
            addition = min(limit - counts[i], max(1, left * loads[i] // pool), spare)
            counts[i] = counts[i] + addition
            spare = spare - addition
    return np.array(counts)


def gaussian(rng, shape, scale, limit, shards=(), kind=jnp.bfloat16):
    factor_of = shard_levels(rng, shape, shards, -0.22, 0.18) if shards else 1.0
    values = jax.random.normal(rng, shape, jnp.float32) * scale * factor_of
    return jnp.minimum(jnp.maximum(values, -limit), limit).astype(kind)


def gaussian_with(key, shape, width, limit, shards, heavy, kind=jnp.bfloat16):
    drawn = width * jax.random.normal(key, shape, jnp.float32)
    if shards:
        drawn = drawn * shard_levels(key, shape, shards, -0.22, 0.18)
    return jnp.clip(spiked(drawn, jax.random.fold_in(key, 3), *heavy), -limit, limit).astype(kind)


def setup_inputs(seed: int = 0) -> dict:
    streams_of = jax.random.split(jax.random.key(seed), 14)
    tokens = gaussian(streams_of[0], (MICRO, TOKENS, D), 1.0, 6.0, ((1, 8),))
    cotangent = gaussian_with(streams_of[1], (MICRO, TOKENS, D), 1.0, 6.0, ((1, 8),), (1, 2, 8, 2.0))
    prev_logits = gaussian(streams_of[2], (MICRO, TOKENS, EXPERTS + 4), 0.5, 3.0, ((1, 8),), jnp.float32)
    routes_keys = jax.random.split(jax.random.fold_in(streams_of[3], 1), MICRO * TOKENS // ROWS)
    routes_turns = jax.random.permutation(jax.random.fold_in(streams_of[3], 3), MICRO * TOKENS // ROWS)
    routes = jax.vmap(lambda own, number: deal_out(jax.random.fold_in(streams_of[3], 2), own, number, ROWS, EXPERTS + 4, 2, CAP, 1))(routes_keys, routes_turns).reshape((MICRO, TOKENS, 2))
    norm_attn = jnp.clip(1.0 + 0.18 * jax.random.normal(streams_of[4], (D,), jnp.float32), 0.099609375, 1.8984375).astype(jnp.bfloat16)
    norm_moe = jnp.clip(1.0 + 0.18 * jax.random.normal(streams_of[5], (D,), jnp.float32), 0.099609375, 1.8984375).astype(jnp.bfloat16)
    w_qkv = gaussian(streams_of[6], (3, D, D), D ** -0.5, 0.21875, ((1, 8), (2, 4)))
    w_out = gaussian(streams_of[7], (D, D), (max(1, D // 192)) ** -0.5, 3.0, ((0, 4), (1, 8)))
    w_router = gaussian(streams_of[8], (D, EXPERTS + 4), (2 * D) ** -0.5, 0.15625, ((0, 8),))
    w_const = gaussian(streams_of[9], (D, 4), D ** -0.5, 0.21875, ((0, 8),))
    const_vec = gaussian(streams_of[10], (2, D), 1.0, 5.0, ((1, 8),))
    w_in = gaussian(streams_of[11], (EXPERTS, 2, D, FF), D ** -0.5, 0.21875, ((0, 8), (3, 4)))
    w_down = gaussian(streams_of[12], (EXPERTS, FF, D), FF ** -0.5, 0.125, ((0, 8), (1, 4)))
    return dict(tokens=tokens, cotangent=cotangent, prev_logits=prev_logits, routes=routes, norm_attn=norm_attn, norm_moe=norm_moe, w_qkv=w_qkv, w_out=w_out, w_router=w_router, w_const=w_const, const_vec=const_vec, w_in=w_in, w_down=w_down)


EPSILON = 1e-06
HIGH = lax.Precision.HIGHEST

@jax.custom_vjp
def low(v):
    return lax.optimization_barrier(v.astype(jnp.bfloat16)).astype(jnp.float32)

@jax.custom_vjp
def low_back(v):
    return v

def low_keep(v):
    return (low(v), None)

def low_pass(kept, grad):
    return (grad,)

def back_keep(v):
    return (v, None)

def back_low(kept, grad):
    return (low(grad),)
low.defvjp(low_keep, low_pass)
low_back.defvjp(back_keep, back_low)

def normalize(values):
    return values * lax.rsqrt(lax.optimization_barrier(jnp.mean(values * values, axis=-1, keepdims=True)) + EPSILON)

def rope_tables():
    half = HD // 2
    ladder = jnp.arange(half, dtype=jnp.float32) * (2.0 / HD)
    frequency = jnp.exp(ladder * -jnp.log(jnp.float32(10000.0)))
    angle = jnp.arange(LEN, dtype=jnp.float32)[:, None] * frequency[None, :]
    return (jnp.cos(angle), jnp.sin(angle))

def rotate(field, cosine, sine):
    half = field.shape[-1] // 2
    first = field[..., :half]
    second = field[..., half:]
    return jnp.concatenate([first * cosine - second * sine, second * cosine + first * sine], axis=-1)

def block_mask():
    block_index = jnp.arange(LEN, dtype=jnp.int32) // BLK
    return block_index[None, :] <= block_index[:, None]

def attention_group(normed, qkv_weight, out_weight):
    cosine, sine = rope_tables()
    cosine = cosine[:, None, :]
    sine = sine[:, None, :]
    group = normed.shape[0]
    projected = jnp.einsum('gld,idc->iglc', normed, qkv_weight, precision=HIGH)
    projected = projected.reshape(3, group, LEN, HEADS, HD)
    query = low(rotate(low_back(projected[0]), cosine, sine))
    keys = low(rotate(low_back(projected[1]), cosine, sine))
    values = low(low_back(projected[2]))
    scores = jnp.einsum('gqhd,gkhd->ghqk', query, keys, precision=HIGH) * HD ** (-0.5)
    scores = jnp.where(block_mask(), low_back(scores), -1e+30)
    weights = low(jax.nn.softmax(scores, axis=-1))
    attended = jnp.einsum('ghqk,gkhd->gqhd', weights, values, precision=HIGH)
    attended = low(low_back(attended)).reshape(group, LEN, D)
    return low_back(jnp.einsum('gld,de->gle', attended, out_weight, precision=HIGH))

def expert_block(packed):
    rows, pair_weight, down_weight = packed
    rows = low_back(rows)
    gate = low_back(jnp.dot(rows, pair_weight[0], precision=HIGH))
    upper = low_back(jnp.dot(rows, pair_weight[1], precision=HIGH))
    hidden = low(jax.nn.silu(gate) * upper)
    return low(low_back(jnp.dot(hidden, down_weight, precision=HIGH)))

def route_tables(choose):
    flat_routes = choose.reshape(N_DP, ROWS * 2)
    expert_hits = (flat_routes[:, :, None] == jnp.arange(EXPERTS, dtype=jnp.int32)[None, None, :]).astype(jnp.int32)
    order = lax.optimization_barrier(jnp.sum(jnp.cumsum(expert_hits, axis=1) * expert_hits, axis=2)) - 1
    source = jnp.arange(N_DP, dtype=jnp.int32)[:, None]
    slot_index = jnp.where(flat_routes < EXPERTS, flat_routes * (N_DP * CAP) + source * CAP + order, EXPERTS * N_DP * CAP)
    slot_index = slot_index.reshape(TOKENS * 2).astype(jnp.int32)
    table = jnp.full((EXPERTS * N_DP * CAP + 1,), TOKENS, jnp.int32)
    table = table.at[slot_index].set(jnp.arange(TOKENS * 2, dtype=jnp.int32) // 2)[:EXPERTS * N_DP * CAP]
    return (slot_index.reshape(TOKENS, 2), table)

def layer(inputs, previous, choose, params):
    slot_index, table = route_tables(choose)
    gain_attn, gain_moe, qkv_weight, out_weight, router_weight, const_weight, const_vector, pair_weight, down_weight = params
    normed_attn = low(normalize(inputs) * gain_attn)
    seq_count = TOKENS // LEN
    group = 4 if seq_count % 4 == 0 else 1
    attend_fn = jax.checkpoint(lambda block: attention_group(block, qkv_weight, out_weight))
    mixed = lax.map(attend_fn, normed_attn.reshape(seq_count // group, group, LEN, D)).reshape(TOKENS, D)
    state = inputs + mixed
    normed = normalize(state) * gain_moe
    normed_low = low(normed)
    logits = low_back(jnp.dot(normed_low, router_weight, precision=HIGH)) + previous
    route_hot = (choose[:, :, None] == jnp.arange(EXPERTS + 4, dtype=jnp.int32)[None, None, :]).astype(jnp.float32)
    picked = lax.optimization_barrier(jnp.sum(route_hot * logits[:, None, :], axis=2))
    gates = jax.nn.softmax(picked, axis=-1)
    const_logits = low_back(jnp.dot(normed_low, const_weight, precision=HIGH))
    alpha_zero = jax.nn.softmax(const_logits[:, 0:2], axis=-1)
    alpha_one = jax.nn.softmax(const_logits[:, 2:4], axis=-1)
    const_zero = alpha_zero[:, 0:1] * normed + alpha_zero[:, 1:2] * const_vector[0]
    const_one = alpha_one[:, 0:1] * normed + alpha_one[:, 1:2] * const_vector[1]
    padded = jnp.concatenate([normed_low, jnp.zeros((1, D), jnp.float32)], axis=0)
    rows = padded[table].reshape(EXPERTS, N_DP * CAP, D)
    answers = lax.map(jax.checkpoint(expert_block), (rows, pair_weight, down_weight))
    answers = jnp.concatenate([answers.reshape(EXPERTS * N_DP * CAP, D), jnp.zeros((1, D), jnp.float32)], axis=0)
    routed = answers[slot_index]
    kind = choose[:, :, None]
    branch = (kind < EXPERTS).astype(jnp.float32) * routed
    branch = branch + (kind == EXPERTS + 1).astype(jnp.float32) * normed[:, None, :]
    branch = branch + (kind == EXPERTS + 2).astype(jnp.float32) * const_zero[:, None, :]
    branch = branch + (kind == EXPERTS + 3).astype(jnp.float32) * const_one[:, None, :]
    return state + lax.optimization_barrier(jnp.sum(gates[:, :, None] * branch, axis=1))

def make_section(choose):

    def section(inputs, previous, params):
        return layer(inputs, previous, choose, params)
    return jax.checkpoint(section)

def reference(tokens, cotangent, prev_logits, routes, norm_attn, norm_moe, w_qkv, w_out, w_router, w_const, const_vec, w_in, w_down):
    params = tuple((weight.astype(jnp.float32) for weight in (norm_attn, norm_moe, w_qkv, w_out, w_router, w_const, const_vec, w_in, w_down)))

    def forward(inputs, previous, weights):
        outputs = []
        for index in range(MICRO):
            outputs.append(make_section(routes[index])(inputs[index], previous[index], weights))
        return jnp.stack(outputs)
    result, pullback = jax.vjp(forward, tokens.astype(jnp.float32), prev_logits, params)
    grad_inputs, grad_previous, grad_params = pullback(cotangent.astype(jnp.float32))
    return (result.astype(jnp.bfloat16), grad_inputs.astype(jnp.bfloat16), grad_previous, grad_params[0], grad_params[1], grad_params[2], grad_params[3], grad_params[4], grad_params[5], grad_params[6], grad_params[7], grad_params[8])
```

```python
import functools

import jax
import jax.numpy as jnp
import numpy as np
from jax import lax
from jax.experimental import pallas as pl
from jax.experimental.pallas import tpu as pltpu
from jax.sharding import PartitionSpec as P

HD = 64
LEN = 1024
BLK = 256
EPSILON = 1e-06
LANES = 128
F32 = jnp.float32
BF16 = jnp.bfloat16
MESH = pl.DeviceIdType.MESH
VMEM_LIMIT = 56 * 1024 * 1024


def mm(a, b):
    return lax.dot_general(a, b, (((1,), (0,)), ((), ())), preferred_element_type=F32)


def mm_nt(a, b):
    return lax.dot_general(a, b, (((1,), (1,)), ((), ())), preferred_element_type=F32)


def mm_tn(a, b):
    return lax.dot_general(a, b, (((0,), (0,)), ((), ())), preferred_element_type=F32)


def vspec():
    return pl.BlockSpec(memory_space=pltpu.VMEM)


def aspec():
    return pl.BlockSpec(memory_space=pl.ANY)


def struct(shape, dtype):
    return jax.ShapeDtypeStruct(shape, dtype)


def compute_call(kernel, outs, *args, flops=1e9, scratch=()):
    nbytes = sum(int(np.prod(a.shape)) * a.dtype.itemsize for a in args) + sum(
        int(np.prod(o.shape)) * o.dtype.itemsize for o in outs
    )
    return pl.pallas_call(
        kernel,
        out_shape=outs,
        in_specs=[vspec()] * len(args),
        out_specs=[vspec()] * len(outs),
        scratch_shapes=list(scratch),
        compiler_params=pltpu.CompilerParams(vmem_limit_bytes=VMEM_LIMIT),
        cost_estimate=pl.CostEstimate(
            flops=int(flops), bytes_accessed=nbytes, transcendentals=0
        ),
    )(*args)


def greet(peers):
    barrier = pltpu.get_barrier_semaphore()
    for peer in peers:
        pl.semaphore_signal(barrier, inc=1, device_id=peer, device_id_type=MESH)
    pl.semaphore_wait(barrier, len(peers))


def remote(src, dst, send, recv, peer):
    return pltpu.make_async_remote_copy(
        src_ref=src,
        dst_ref=dst,
        send_sem=send,
        recv_sem=recv,
        device_id=peer,
        device_id_type=MESH,
    )


def comm_call(kernel, outs, sems, cid, *args):
    return pl.pallas_call(
        kernel,
        out_shape=outs,
        in_specs=[aspec()] * len(args),
        out_specs=[aspec()] * len(outs),
        scratch_shapes=[pltpu.SemaphoreType.DMA(s) for s in sems],
        compiler_params=pltpu.CompilerParams(collective_id=cid, has_side_effects=True),
    )(*args)


def core_share(cid, *arrays):
    count = len(arrays)

    def kernel(*refs):
        ins, outs, (send, recv, local) = refs[:count], refs[count : 2 * count], refs[2 * count :]
        d, t = lax.axis_index("dp"), lax.axis_index("tensor")
        c = lax.rem(t, 2)
        peer = (d, t + 1 - 2 * c)
        greet([peer])
        copies = []
        for i in range(count):
            copies.append(remote(ins[i], outs[i].at[c], send.at[i], recv.at[i], peer))
            copies.append(pltpu.make_async_copy(ins[i], outs[i].at[c], local.at[i]))
        for copy in copies:
            copy.start()
        for copy in copies:
            copy.wait()

    outs = [struct((2,) + a.shape, a.dtype) for a in arrays]
    return comm_call(kernel, outs, [(count,)] * 3, cid, *arrays)


def plane_peers(n, d, t):
    return [(lax.rem(d + j, n), t) for j in range(1, n)]


def all_peers(n, d, t):
    other = lax.rem(t + 2, 4)
    return plane_peers(n, d, t) + [(lax.rem(d + j, n), other) for j in range(n)]


def gather_weights(cid, n, packed):
    def kernel(in_ref, out_ref, send, recv, local):
        d, t = lax.axis_index("dp"), lax.axis_index("tensor")
        m = lax.div(t, 2)
        peers = all_peers(n, d, t)
        greet(peers)
        mine = pltpu.make_async_copy(in_ref, out_ref.at[m, d], local.at[0])
        mine.start()
        copies = []
        for i, peer in enumerate(peers):
            copies.append(remote(in_ref, out_ref.at[m, d], send.at[i], recv.at[i], peer))
        for copy in copies:
            copy.start()
        for copy in copies:
            copy.wait()
        mine.wait()

    outs = [struct((2, n) + packed.shape, packed.dtype)]
    return comm_call(kernel, outs, [(2 * n,), (2 * n,), (1,)], cid, packed)[0]


def spread_gradients(cid, n, *arrays):
    count = len(arrays)

    def kernel(*refs):
        ins, outs, (send, recv, local) = refs[:count], refs[count : 2 * count], refs[2 * count :]
        d, t = lax.axis_index("dp"), lax.axis_index("tensor")
        m = lax.div(t, 2)
        peers = all_peers(n, d, t)
        greet(peers)
        copies = []
        for k in range(count):
            copies.append(
                pltpu.make_async_copy(ins[k].at[m, d], outs[k].at[m, d], local.at[k])
            )
            for i, (pd, pt) in enumerate(peers):
                pm = lax.div(pt, 2)
                copies.append(
                    remote(
                        ins[k].at[pm, pd],
                        outs[k].at[m, d],
                        send.at[k, i],
                        recv.at[k, i],
                        (pd, pt),
                    )
                )
        for copy in copies:
            copy.start()
        for copy in copies:
            copy.wait()

    outs = [struct(a.shape, a.dtype) for a in arrays]
    return comm_call(kernel, outs, [(count, 2 * n), (count, 2 * n), (count,)], cid, *arrays)


def dispatch(cid, n, *arrays):
    count = len(arrays)

    def kernel(*refs):
        ins, outs, (send, recv, local) = refs[:count], refs[count : 2 * count], refs[2 * count :]
        d, t = lax.axis_index("dp"), lax.axis_index("tensor")
        peers = plane_peers(n, d, t)
        greet(peers)
        copies = []
        for k in range(count):
            copies.append(pltpu.make_async_copy(ins[k].at[d], outs[k].at[d], local.at[k]))
            for i, (pd, pt) in enumerate(peers):
                copies.append(
                    remote(ins[k].at[pd], outs[k].at[d], send.at[k, i], recv.at[k, i], (pd, pt))
                )
        for copy in copies:
            copy.start()
        for copy in copies:
            copy.wait()

    outs = [struct(a.shape, a.dtype) for a in arrays]
    return comm_call(kernel, outs, [(count, n), (count, n), (count,)], cid, *arrays)


def give_back(cid, n, *arrays):
    count = len(arrays)

    def kernel(*refs):
        ins, outs = refs[:count], refs[count : 2 * count]
        send, recv, local, csend, crecv = refs[2 * count :]
        d, t = lax.axis_index("dp"), lax.axis_index("tensor")
        c = lax.rem(t, 2)
        partner = (d, t + 1 - 2 * c)
        peers = plane_peers(n, d, t)
        greet(peers + [partner])
        arrivals = []
        own = []
        passed = []
        for k in range(count):
            own.append(pltpu.make_async_copy(ins[k].at[d], outs[k].at[c, d], local.at[k]))
            passed.append(
                remote(ins[k].at[d], outs[k].at[c, d], csend.at[k, 0], crecv.at[k, 0], partner)
            )
            for i, (pd, pt) in enumerate(peers):
                arrivals.append(
                    remote(
                        ins[k].at[pd], outs[k].at[c, d], send.at[k, i], recv.at[k, i], (pd, pt)
                    )
                )
        for copy in own + passed + arrivals:
            copy.start()
        for k in range(count):
            for i in range(n - 1):
                arrivals[k * (n - 1) + i].wait_recv()
                source = lax.rem(d + n - 1 - i, n)
                block = outs[k].at[c, source]
                copy = remote(block, block, csend.at[k, i + 1], crecv.at[k, i + 1], partner)
                copy.start()
                passed.append(copy)
        for copy in arrivals:
            copy.wait_send()
        for copy in own + passed:
            copy.wait()

    outs = [struct((2,) + a.shape, a.dtype) for a in arrays]
    return comm_call(
        kernel, outs, [(count, n), (count, n), (count,), (count, n), (count, n)], cid, *arrays
    )


def share_output(cid, full):
    rows = full.shape[0]
    half = rows // 2

    def kernel(in_ref, out_ref, send, recv, local):
        d, t = lax.axis_index("dp"), lax.axis_index("tensor")
        m, c = lax.div(t, 2), lax.rem(t, 2)
        across = (d, lax.rem(t + 2, 4))
        partner = (d, t + 1 - 2 * c)
        greet([across, partner])
        mine = pltpu.make_async_copy(in_ref, out_ref.at[m], local.at[0])
        mine.start()
        first = remote(
            in_ref.at[pl.ds(c * half, half)],
            out_ref.at[m, pl.ds(c * half, half)],
            send.at[0],
            recv.at[0],
            across,
        )
        first.start()
        first.wait_recv()
        block = out_ref.at[1 - m, pl.ds(c * half, half)]
        second = remote(block, block, send.at[1], recv.at[1], partner)
        second.start()
        first.wait_send()
        second.wait()
        mine.wait()

    outs = [struct((2,) + full.shape, full.dtype)]
    return comm_call(kernel, outs, [(2,), (2,), (1,)], cid, full)[0]


def route_kernel(experts, half, padded, columns_ref, rows_ref, dy_ref, pos_ref, post_ref, slot_ref):
    rows = columns_ref.shape[0]
    lanes = post_ref.shape[0]
    first, second = rows_ref[0:1, :], rows_ref[1:2, :]
    ids = lax.broadcasted_iota(jnp.int32, (lanes, rows), 0)
    hit = ((ids == first) | (ids == second)) & (ids < experts)
    before = (
        lax.broadcasted_iota(jnp.int32, (rows, rows), 0)
        < lax.broadcasted_iota(jnp.int32, (rows, rows), 1)
    )
    count = mm(hit.astype(F32).astype(BF16), before.astype(F32).astype(BF16))
    place = jnp.where(hit, count, -1.0)
    post_ref[...] = place
    pos_ref[...] = jnp.transpose(place)
    base = lax.rem(lax.axis_index("tensor"), 2) * half
    build_slots(experts, half, padded, base, post_ref, dy_ref, slot_ref)


def slot_hot(half, padded, base, places):
    rows = places.shape[1]
    slot = lax.broadcasted_iota(jnp.int32, (padded, rows), 0)
    wanted = jnp.where(slot < half, slot + base, -2).astype(F32)
    return (wanted == places).astype(F32).astype(BF16)


def build_slots(experts, half, padded, base, post_ref, source_ref, slot_ref):
    def step(e, carry):
        hot = slot_hot(half, padded, base, post_ref[pl.ds(e, 1), :])
        slot_ref[e] = mm(hot, source_ref[...]).astype(BF16)
        return carry

    lax.fori_loop(0, experts, step, 0)


def rope_constants():
    half = HD // 2
    frequency = 10000.0 ** (-2.0 * np.arange(half) / HD)
    angle = np.arange(LEN)[:, None] * frequency[None, :]
    cosine, sine = np.cos(angle), np.sin(angle)
    cosine = np.concatenate([cosine, cosine, cosine, cosine], axis=1)
    sine = np.concatenate([-sine, sine, -sine, sine], axis=1)
    return cosine.astype(np.float32), sine.astype(np.float32)


def turn(field, cosine, sine):
    lane = lax.broadcasted_iota(jnp.int32, field.shape, 1)
    other = jnp.where(
        lax.rem(lane, HD) < HD // 2,
        pltpu.roll(field, LANES - HD // 2, 1),
        pltpu.roll(field, HD // 2, 1),
    )
    return field * cosine + other * sine


def attention_kernel(
    x_ref, gain_ref, w_ref, cos_ref, sin_ref, a_ref, q_ref, k_ref, v_ref, o_ref, lse_ref
):
    width = q_ref.shape[1]
    pairs = width // LANES
    blocks = LEN // BLK
    for i in range(blocks):
        rows = pl.ds(i * BLK, BLK)
        x = x_ref[rows, :].astype(F32)
        r = lax.rsqrt(jnp.mean(x * x, axis=-1, keepdims=True) + EPSILON)
        a = (x * r * gain_ref[...]).astype(BF16)
        a_ref[rows, :] = a
        cosine, sine = cos_ref[rows, :], sin_ref[rows, :]
        for p in range(pairs):
            lanes = pl.ds(p * LANES, LANES)
            q = turn(mm(a, w_ref[:, p * LANES : (p + 1) * LANES]), cosine, sine).astype(BF16)
            q_ref[rows, lanes] = q * BF16(HD**-0.5)
            start = width + p * LANES
            k_ref[rows, lanes] = turn(mm(a, w_ref[:, start : start + LANES]), cosine, sine).astype(
                BF16
            )
            start = 2 * width + p * LANES
            v_ref[rows, lanes] = mm(a, w_ref[:, start : start + LANES]).astype(BF16)
    head = lax.broadcasted_iota(jnp.int32, (BLK, LANES), 1) < HD
    for p in range(pairs):
        lanes = pl.ds(p * LANES, LANES)
        for i in range(blocks):
            rows = pl.ds(i * BLK, BLK)
            seen = pl.ds(0, (i + 1) * BLK)
            q, k, v = q_ref[rows, lanes], k_ref[seen, lanes], v_ref[seen, lanes]
            halves = []
            for side in range(2):
                mask = head if side == 0 else jnp.logical_not(head)
                s = mm_nt(jnp.where(mask, q, jnp.zeros_like(q)), k)
                high = jnp.max(s, axis=-1, keepdims=True)
                e = jnp.exp(s - high)
                total = jnp.sum(e, axis=-1, keepdims=True)
                halves.append(mm((e / total).astype(BF16), v))
                log_total = jnp.broadcast_to(high + jnp.log(total), (BLK, LANES))
                lse_ref[2 * p + side : 2 * p + side + 1, rows] = jnp.transpose(log_total)[0:1, :]
            o_ref[rows, lanes] = jnp.where(head, halves[0], halves[1]).astype(BF16)


def pick(hot, values):
    return jnp.sum(jnp.where(hot, values, 0.0), axis=-1, keepdims=True)


def lane_ids(rows):
    return lax.broadcasted_iota(jnp.int32, (rows, LANES), 1)


def column(value, lane, rows):
    return jnp.where(lane_ids(rows) == lane, value, 0.0)


def soft_pair(first, second):
    high = jnp.maximum(first, second)
    e0, e1 = jnp.exp(first - high), jnp.exp(second - high)
    return e0 / (e0 + e1), e1 / (e0 + e1)


def middle_kernel(
    experts,
    half,
    padded,
    x_ref,
    o_ref,
    wo_ref,
    small_ref,
    gain_ref,
    prev_ref,
    routes_ref,
    post_ref,
    h_ref,
    ub_ref,
    stat_ref,
    slot_ref,
    gate_ref,
    pieces_ref,
):
    rows_all = x_ref.shape[0]
    for i in range(rows_all // BLK):
        rows = pl.ds(i * BLK, BLK)
        z = mm_nt(o_ref[0, rows, :], wo_ref[0]) + mm_nt(o_ref[1, rows, :], wo_ref[1])
        h = x_ref[rows, :].astype(F32) + z
        r = lax.rsqrt(jnp.mean(h * h, axis=-1, keepdims=True) + EPSILON)
        ub = (h * r * gain_ref[...]).astype(BF16)
        h_ref[rows, :] = h
        ub_ref[rows, :] = ub
        scores = mm(ub, small_ref[...])
        logits = scores + prev_ref[rows, :]
        ids = lane_ids(BLK)
        hot0 = ids == routes_ref[rows, 0:1]
        hot1 = ids == routes_ref[rows, 1:2]
        g0, g1 = soft_pair(pick(hot0, logits), pick(hot1, logits))
        base = experts + 4
        c = [pick(ids == base + j, scores) for j in range(4)]
        a00, a01 = soft_pair(c[0], c[1])
        a10, a11 = soft_pair(c[2], c[3])
        stats = [g0, g1, a00, a01, a10, a11, r]
        table = column(stats[0], 0, BLK)
        for j in range(1, len(stats)):
            table = table + column(stats[j], j, BLK)
        stat_ref[rows, :] = table
        gates = jnp.where(hot0, g0, 0.0) + jnp.where(hot1, g1, 0.0)
        gates = jnp.transpose(gates)
        for piece in range(3):
            part = gates.astype(BF16)
            pieces_ref[piece, :, rows] = part
            gates = gates - part.astype(F32)
    base = lax.rem(lax.axis_index("tensor"), 2) * half

    def step(e, carry):
        hot = slot_hot(half, padded, base, post_ref[pl.ds(e, 1), :])
        slot_ref[e] = mm(hot, ub_ref[...]).astype(BF16)
        total = jnp.zeros((8, padded), F32)
        for piece in range(3):
            group = pl.ds(pl.multiple_of(lax.div(e, 16) * 16, 16), 16)
            chosen = lax.broadcasted_iota(jnp.int32, (16, rows_all), 0) == lax.rem(e, 16)
            line = jnp.where(chosen, pieces_ref[piece, group, :].astype(F32), 0.0)
            line = jnp.broadcast_to(jnp.sum(line, axis=0, keepdims=True), (8, rows_all))
            total = total + mm_nt(line.astype(BF16), hot)
        gate_ref[e] = total
        return carry

    lax.fori_loop(0, experts, step, 0)


def expert_kernel(
    sources,
    padded,
    x_ref,
    dy_ref,
    gate_ref,
    *refs,
):
    weights, outs = refs[:8], refs[8:19]
    in_refs, down_refs = weights[0:4], weights[4:8]
    gy_ref, dx_ref, dg_ref = outs[0:3]
    gin_refs, gdown_refs = outs[3:7], outs[7:11]
    xt_ref, scaled_ref, scale_ref, y_acc, dx_acc, win_ref, wdown_ref = refs[19:]
    step = pl.program_id(0)
    last = pl.num_programs(0) - 1

    @pl.when(step == 0)
    def _():
        xt_ref[...] = jnp.transpose(x_ref[...])
        for s in range(sources):
            rows = pl.ds(s * padded, padded)
            line = jnp.broadcast_to(gate_ref[s, 0:1, :], (LANES, padded))
            scale = jnp.transpose(line)
            scale_ref[rows, :] = scale
            scaled_ref[rows, :] = (dy_ref[rows, :].astype(F32) * scale[:, 0:1]).astype(BF16)
        y_acc[...] = jnp.zeros_like(y_acc)
        dx_acc[...] = jnp.zeros_like(dx_acc)

    per = pl.num_programs(0) // 4
    for i in range(4):

        @pl.when(lax.div(step, per) == i)
        def _():
            win_ref[...] = in_refs[i][0]
            wdown_ref[...] = down_refs[i][0]

    x = x_ref[...]
    gate = mm(x, win_ref[0])
    up = mm(x, win_ref[1])
    sigma = 1.0 / (1.0 + jnp.exp(-gate))
    active = gate * sigma
    hidden = (active * up).astype(BF16)
    y_acc[...] += mm(hidden, wdown_ref[...])
    scaled = scaled_ref[...]
    grad_hidden = mm_nt(scaled, wdown_ref[...])
    grad_gate = (grad_hidden * up * (sigma * (1.0 + gate * (1.0 - sigma)))).astype(BF16)
    grad_up = (grad_hidden * active).astype(BF16)
    dx_acc[...] += mm_nt(grad_gate, win_ref[0]) + mm_nt(grad_up, win_ref[1])
    xt = xt_ref[...]
    part_gate = mm(xt, grad_gate).astype(BF16)
    part_up = mm(xt, grad_up).astype(BF16)
    part_down = mm_tn(hidden, scaled).astype(BF16)
    for i in range(4):

        @pl.when(lax.div(step, per) == i)
        def _():
            gin_refs[i][0, 0] = part_gate
            gin_refs[i][0, 1] = part_up
            gdown_refs[i][0] = part_down

    @pl.when(step == last)
    def _():
        for s in range(sources):
            rows = pl.ds(s * padded, padded)
            y = y_acc[rows, :]
            gy_ref[s] = (y * scale_ref[rows, 0:1]).astype(BF16)
            dot = jnp.sum(y * dy_ref[rows, :].astype(F32), axis=-1, keepdims=True)
            dg_ref[s] = jnp.transpose(jnp.broadcast_to(dot, (padded, LANES)))[0:8, :]
            dx_ref[s] = dx_acc[rows, :].astype(BF16)


def back_kernel(
    experts,
    half,
    padded,
    h_ref,
    ub_ref,
    stat_ref,
    routes_ref,
    pos_ref,
    dy_ref,
    gy_ref,
    dx_ref,
    dg_ref,
    small_ref,
    gain_ref,
    vec_ref,
    o_ref,
    wo_ref,
    result_ref,
    prev_ref,
    dh_ref,
    do_ref,
    grad_wo_ref,
    grad_small_ref,
    mixed_ref,
    low_ref,
    dzb_ref,
    row_ref,
):
    rows_all = h_ref.shape[0]
    width = h_ref.shape[1]
    row_ref[...] = jnp.zeros_like(row_ref)
    columns = experts + 4
    for i in range(rows_all // BLK):
        rows = pl.ds(i * BLK, BLK)
        ids = lane_ids(BLK)
        stats = stat_ref[rows, :]
        g0, g1, a00, a01, a10, a11, r = [stats[:, j : j + 1] for j in range(7)]
        e0, e1 = routes_ref[rows, 0:1], routes_ref[rows, 1:2]
        hot0, hot1 = ids == e0, ids == e1
        places = pos_ref[rows, :]
        sums = jnp.zeros((BLK, width), F32)
        grads = jnp.zeros((BLK, width), F32)
        gate_grads = jnp.zeros((BLK, LANES), F32)

        def step(e, carry):
            sums, grads, gate_grads = carry
            place = pick(ids == e, places)
            for side in range(2):
                slot = lax.broadcasted_iota(jnp.int32, (BLK, padded), 1)
                wanted = jnp.where(slot < half, slot + side * half, -2).astype(F32)
                hot = wanted == place
                low = hot.astype(F32).astype(BF16)
                sums = sums + mm(low, gy_ref[side, e])
                grads = grads + mm(low, dx_ref[side, e])
                value = jnp.sum(
                    jnp.where(hot, dg_ref[side, e, 0:1, :], 0.0), axis=-1, keepdims=True
                )
                gate_grads = gate_grads + jnp.where(ids == e, value, 0.0)
            return sums, grads, gate_grads

        sums, grads, gate_grads = lax.fori_loop(
            0, experts, step, (sums, grads, gate_grads)
        )
        h = h_ref[rows, :]
        n = h * r
        u = n * gain_ref[...]
        dy = dy_ref[rows, :].astype(F32)
        vec0, vec1 = vec_ref[0:1, :], vec_ref[1:2, :]

        def named(number):
            return jnp.where(e0 == number, g0, 0.0) + jnp.where(e1 == number, g1, 0.0)

        copied, first, second = named(experts + 1), named(experts + 2), named(experts + 3)
        on_u = copied + first * a00 + second * a10
        result = h + (sums + on_u * u + (first * a01) * vec0 + (second * a11) * vec1)
        result_ref[rows, :] = result.astype(BF16)
        s_u = jnp.sum(dy * u, axis=-1, keepdims=True)
        s_0 = jnp.sum(dy * vec0, axis=-1, keepdims=True)
        s_1 = jnp.sum(dy * vec1, axis=-1, keepdims=True)
        table = (
            gate_grads
            + jnp.where(ids == experts + 1, s_u, 0.0)
            + jnp.where(ids == experts + 2, a00 * s_u + a01 * s_0, 0.0)
            + jnp.where(ids == experts + 3, a10 * s_u + a11 * s_1, 0.0)
        )
        dg0, dg1 = pick(hot0, table), pick(hot1, table)
        mean = g0 * dg0 + g1 * dg1
        dl = jnp.where(hot0, g0 * (dg0 - mean), 0.0) + jnp.where(hot1, g1 * (dg1 - mean), 0.0)
        prev_ref[rows, :] = dl
        d00, d01 = first * s_u, first * s_0
        d10, d11 = second * s_u, second * s_1
        m0 = a00 * d00 + a01 * d01
        m1 = a10 * d10 + a11 * d11
        mixing = (
            jnp.where(ids == columns, a00 * (d00 - m0), 0.0)
            + jnp.where(ids == columns + 1, a01 * (d01 - m0), 0.0)
            + jnp.where(ids == columns + 2, a10 * (d10 - m1), 0.0)
            + jnp.where(ids == columns + 3, a11 * (d11 - m1), 0.0)
        )
        low = (dl + mixing).astype(BF16)
        low_ref[rows, :] = low
        du = grads + mm_nt(low, small_ref[...]) + on_u * dy
        row_ref[0:1, :] += jnp.sum(du * n, axis=0, keepdims=True)
        row_ref[1:2, :] += jnp.sum((first * a01) * dy, axis=0, keepdims=True)
        row_ref[2:3, :] += jnp.sum((second * a11) * dy, axis=0, keepdims=True)
        dn = du * gain_ref[...]
        dh = dy + r * (dn - n * jnp.mean(dn * n, axis=-1, keepdims=True))
        dh_ref[rows, :] = dh
        dzb = dh.astype(BF16)
        dzb_ref[rows, :] = dzb
        do_ref[rows, :] = mm(dzb, wo_ref[...]).astype(BF16)
    grad_wo_ref[...] = mm_tn(dzb_ref[...], o_ref[...]).astype(BF16)
    lines = jnp.concatenate([row_ref[...], jnp.zeros((LANES - 8, width), F32)], axis=0)
    grad_small_ref[...] = mm_tn(ub_ref[...], low_ref[...])
    mixed_ref[...] = jnp.transpose(lines)


def attention_back_kernel(
    q_ref,
    k_ref,
    v_ref,
    do_ref,
    lse_ref,
    a_ref,
    w_ref,
    cos_ref,
    sin_ref,
    da_ref,
    grad_w_ref,
    dp_ref,
    dk_acc,
    dv_acc,
):
    width = q_ref.shape[1]
    pairs = width // LANES
    blocks = LEN // BLK
    head = lax.broadcasted_iota(jnp.int32, (BLK, LANES), 1) < HD
    for p in range(pairs):
        lanes = pl.ds(p * LANES, LANES)
        dk_acc[...] = jnp.zeros_like(dk_acc)
        dv_acc[...] = jnp.zeros_like(dv_acc)
        for i in range(blocks):
            rows = pl.ds(i * BLK, BLK)
            seen = pl.ds(0, (i + 1) * BLK)
            q, do = q_ref[rows, lanes], do_ref[rows, lanes]
            k, v = k_ref[seen, lanes], v_ref[seen, lanes]
            zero = jnp.zeros_like(q)
            parts = []
            dk = dk_acc[seen, :]
            dv = dv_acc[seen, :]
            for side in range(2):
                mask = head if side == 0 else jnp.logical_not(head)
                qm, dom = jnp.where(mask, q, zero), jnp.where(mask, do, zero)
                log_total = lse_ref[2 * p + side : 2 * p + side + 1, rows]
                prob = jnp.exp(mm_nt(k, qm) - log_total)
                grad_prob = mm_nt(v, dom)
                total = jnp.sum(prob * grad_prob, axis=0, keepdims=True)
                grad_score = (prob * (grad_prob - total)).astype(BF16)
                dv = dv + mm(prob.astype(BF16), dom)
                dk = dk + mm(grad_score, qm)
                parts.append(mm_tn(grad_score, k))
            dk_acc[seen, :] = dk
            dv_acc[seen, :] = dv
            dq = jnp.where(head, parts[0], parts[1]) * (HD**-0.5)
            dp_ref[rows, lanes] = turn(dq, cos_ref[rows, :], -sin_ref[rows, :]).astype(BF16)
        dp_ref[:, pl.ds(width + p * LANES, LANES)] = turn(
            dk_acc[...], cos_ref[...], -sin_ref[...]
        ).astype(BF16)
        dp_ref[:, pl.ds(2 * width + p * LANES, LANES)] = dv_acc[...].astype(BF16)
    for i in range(blocks):
        rows = pl.ds(i * BLK, BLK)
        da_ref[rows, :] = mm_nt(dp_ref[rows, :], w_ref[...]).astype(BF16)
    for j in range(3 * pairs):
        lanes = pl.ds(j * LANES, LANES)
        grad_w_ref[:, lanes] = mm_tn(a_ref[...], dp_ref[:, lanes]).astype(BF16)


def finish_kernel(x_ref, dh_ref, da_ref, gain_ref, grad_ref, row_ref):
    rows_all, width = x_ref.shape
    total = jnp.zeros((1, width), F32)
    for i in range(rows_all // BLK):
        rows = pl.ds(i * BLK, BLK)
        x = x_ref[rows, :].astype(F32)
        r = lax.rsqrt(jnp.mean(x * x, axis=-1, keepdims=True) + EPSILON)
        n = x * r
        da = da_ref[0, rows, :].astype(F32) + da_ref[1, rows, :].astype(F32)
        total = total + jnp.sum(da * n, axis=0, keepdims=True)
        dn = da * gain_ref[...]
        grad = dh_ref[rows, :] + r * (dn - n * jnp.mean(dn * n, axis=-1, keepdims=True))
        grad_ref[rows, :] = grad.astype(BF16)
    row_ref[...] = jnp.broadcast_to(total, row_ref.shape)


def across_chips(value):
    return lax.ppermute(value, "tensor", [(0, 2), (2, 0), (1, 3), (3, 1)])


def across_cores(value):
    return lax.ppermute(value, "tensor", [(0, 1), (1, 0), (2, 3), (3, 2)])


def body(
    tokens,
    cotangent,
    prev_logits,
    routes,
    norm_attn,
    norm_moe,
    w_qkv,
    w_out,
    w_router,
    w_const,
    const_vec,
    w_in,
    w_down,
):
    rows, width = tokens.shape[1:]
    n = lax.axis_size("dp")
    experts = n
    columns = prev_logits.shape[2]
    capacity = 4 * max(1, 3 * rows // (4 * (experts + 4)))
    half = capacity // 2
    padded = -(-half // 16) * 16
    share = w_qkv.shape[2]
    local = 2 * share
    part = w_qkv.shape[1]
    t = lax.axis_index("tensor")
    m, c = t // 2, t % 2

    def mine(value):
        return lax.dynamic_index_in_dim(value, m, 0, keepdims=False)

    x, dy, choose = mine(tokens), mine(cotangent), mine(routes)
    prev = jnp.pad(mine(prev_logits), ((0, 0), (0, LANES - columns)))
    cosine, sine = (jnp.asarray(v) for v in rope_constants())

    small = jnp.concatenate(
        [
            w_router,
            w_const,
            norm_attn[:, None],
            norm_moe[:, None],
            const_vec.T,
            jnp.zeros((part, LANES - columns - 8), BF16),
        ],
        axis=1,
    )
    packed = jnp.concatenate([w_qkv[0], w_qkv[1], w_qkv[2], w_out.T, small], axis=1)
    spread = gather_weights(0, n, packed).reshape(2, n * part, packed.shape[1])
    w_heads = jnp.concatenate(
        [spread[j, :, i * share : (i + 1) * share] for i in range(3) for j in range(2)], axis=1
    )
    wo_own = jnp.concatenate(
        [spread[j, :, 3 * share : 4 * share] for j in range(2)], axis=1
    )
    table = spread[0, :, 4 * share :]
    extra = table[:, columns + 4 : columns + 8].astype(F32).T
    gain_attn, gain_moe, vectors = extra[0:1], extra[1:2], extra[2:4]
    keep = jnp.arange(LANES) < columns + 4
    small_all = jnp.where(keep[None, :], table, jnp.zeros_like(table))
    wo_all = core_share(1, wo_own)[0]

    in_x, down_x = across_chips(w_in), across_chips(w_down)
    in_c, down_c = across_cores(w_in), across_cores(w_down)
    in_d, down_d = across_cores(in_x), across_cores(down_x)

    pos, post, dy_slots = compute_call(
        functools.partial(route_kernel, experts, half, padded),
        [
            struct((rows, LANES), F32),
            struct((LANES, rows), F32),
            struct((experts, padded, width), BF16),
        ],
        choose,
        choose.T,
        dy,
        flops=2 * experts * padded * rows * width,
    )
    dy_arrived = lax.all_to_all(dy_slots, "dp", split_axis=0, concat_axis=0, tiled=True)

    a, q, k, v, o, lse = compute_call(
        attention_kernel,
        [
            struct((rows, width), BF16),
            struct((rows, local), BF16),
            struct((rows, local), BF16),
            struct((rows, local), BF16),
            struct((rows, local), BF16),
            struct((8, rows), F32),
        ],
        x,
        gain_attn,
        w_heads,
        cosine,
        sine,
        flops=2 * rows * width * 3 * local + 8 * rows * rows * local,
    )
    o_all = core_share(2, o)[0]
    h, ub, stats, slots, gate_slots = compute_call(
        functools.partial(middle_kernel, experts, half, padded),
        [
            struct((rows, width), F32),
            struct((rows, width), BF16),
            struct((rows, LANES), F32),
            struct((experts, padded, width), BF16),
            struct((experts, 8, padded), F32),
        ],
        x,
        o_all,
        wo_all,
        small_all,
        gain_moe,
        prev,
        choose,
        post,
        flops=4 * rows * width * width + 2 * experts * padded * rows * width,
        scratch=[pltpu.VMEM((3, LANES, rows), BF16)],
    )
    arrived, gate_arrived = dispatch(3, n, slots, gate_slots)

    hidden_width = w_in.shape[3]
    slots_all = experts * padded
    chunk = min(256 if slots_all <= 1024 else 128, hidden_width)
    per = hidden_width // chunk

    def in_map(i):
        return lambda f: (0, 0, 0, jnp.clip(f - per * i, 0, per - 1))

    def down_map(i):
        return lambda f: (0, jnp.clip(f - per * i, 0, per - 1), 0)

    in_blocks = [pl.BlockSpec((1, 2, width, chunk), in_map(i)) for i in range(4)]
    down_blocks = [pl.BlockSpec((1, chunk, width), down_map(i)) for i in range(4)]
    expert_outs = (
        [
            struct((n, padded, width), BF16),
            struct((n, padded, width), BF16),
            struct((n, 8, padded), F32),
        ]
        + [struct(w_in.shape, BF16)] * 4
        + [struct(w_down.shape, BF16)] * 4
    )

    def whole(shape):
        return pl.BlockSpec(
            shape, lambda f: (0,) * len(shape), pipeline_mode=pl.Buffered(1)
        )

    parts = pl.pallas_call(
        functools.partial(expert_kernel, n, padded),
        grid=(4 * per,),
        out_shape=expert_outs,
        in_specs=[
            whole((slots_all, width)),
            whole((slots_all, width)),
            whole((n, 8, padded)),
        ]
        + in_blocks
        + down_blocks,
        out_specs=[
            whole((n, padded, width)),
            whole((n, padded, width)),
            whole((n, 8, padded)),
        ]
        + in_blocks
        + down_blocks,
        scratch_shapes=[
            pltpu.VMEM((width, slots_all), BF16),
            pltpu.VMEM((slots_all, width), BF16),
            pltpu.VMEM((slots_all, LANES), F32),
            pltpu.VMEM((slots_all, width), F32),
            pltpu.VMEM((slots_all, width), F32),
            pltpu.VMEM((2, width, chunk), BF16),
            pltpu.VMEM((chunk, width), BF16),
        ],
        compiler_params=pltpu.CompilerParams(vmem_limit_bytes=VMEM_LIMIT),
        cost_estimate=pl.CostEstimate(
            flops=18 * slots_all * width * 4 * hidden_width,
            bytes_accessed=30_000_000,
            transcendentals=0,
        ),
    )(
        arrived.reshape(slots_all, width),
        dy_arrived.reshape(slots_all, width),
        gate_arrived,
        w_in,
        in_c,
        in_x,
        in_d,
        w_down,
        down_c,
        down_x,
        down_d,
    )
    gy, dx, dg = parts[0:3]
    gin, gdown = parts[3:7], parts[7:11]
    gy_all, dx_all, dg_all = give_back(4, n, gy, dx, dg)

    def total_in(own, core, chip, diagonal):
        own = own.astype(F32) + across_cores(core).astype(F32)
        chip = (chip.astype(F32) + across_cores(diagonal).astype(F32)).astype(BF16)
        return own + across_chips(chip).astype(F32)

    grad_in = total_in(*gin)
    grad_down = total_in(*gdown)

    result, dl, dh, do, grad_wo, grad_small, grad_lines = compute_call(
        functools.partial(back_kernel, experts, half, padded),
        [
            struct((rows, width), BF16),
            struct((rows, LANES), F32),
            struct((rows, width), F32),
            struct((rows, local), BF16),
            struct((width, local), BF16),
            struct((width, LANES), F32),
            struct((width, LANES), F32),
        ],
        h,
        ub,
        stats,
        choose,
        pos,
        dy,
        gy_all,
        dx_all,
        dg_all,
        small_all,
        gain_moe,
        vectors,
        o,
        wo_own,
        flops=8 * experts * padded * rows * width,
        scratch=[
            pltpu.VMEM((rows, LANES), BF16),
            pltpu.VMEM((rows, width), BF16),
            pltpu.VMEM((8, width), F32),
        ],
    )
    results = share_output(5, result)
    da, grad_heads = compute_call(
        attention_back_kernel,
        [struct((rows, width), BF16), struct((width, 3 * local), BF16)],
        q,
        k,
        v,
        do,
        lse,
        a,
        w_heads,
        cosine,
        sine,
        flops=4 * rows * width * 3 * local + 20 * rows * rows * local,
        scratch=[
            pltpu.VMEM((rows, 3 * local), BF16),
            pltpu.VMEM((rows, LANES), F32),
            pltpu.VMEM((rows, LANES), F32),
        ],
    )
    da_all = core_share(6, da)[0]
    grad_x, grad_line = compute_call(
        finish_kernel,
        [struct((rows, width), BF16), struct((8, width), F32)],
        x,
        dh,
        da_all,
        gain_attn,
    )
    input_grads = share_output(7, grad_x)

    grads = jnp.stack(
        [
            jnp.concatenate(
                [
                    grad_heads[:, (2 * i + j) * share : (2 * i + j + 1) * share]
                    for i in range(3)
                ]
                + [grad_wo[:, j * share : (j + 1) * share]],
                axis=1,
            )
            for j in range(2)
        ]
    ).reshape(2, n, part, 4 * share)
    lines = grad_small + jnp.pad(
        jnp.concatenate([grad_line[0:1].T, grad_lines[:, 0:3]], axis=1),
        ((0, 0), (columns + 4, LANES - columns - 8)),
    )
    lines = jnp.broadcast_to(lines.reshape(1, n, part, LANES), (2, n, part, LANES))
    grads_in, lines_in = spread_gradients(8, n, grads, lines)
    grads = jnp.sum(grads_in.astype(F32), axis=(0, 1))
    lines = jnp.sum(lines_in, axis=(0, 1))
    dl = dl[:, :columns]
    dl_x = across_chips(dl)
    logit_grads = jnp.where(m == 0, jnp.stack([dl, dl_x]), jnp.stack([dl_x, dl]))
    return (
        results,
        input_grads,
        logit_grads,
        lines[:, columns + 4],
        lines[:, columns + 5],
        jnp.stack([grads[:, i * share : (i + 1) * share] for i in range(3)]),
        grads[:, 3 * share :].T,
        lines[:, :columns],
        lines[:, columns : columns + 4],
        lines[:, columns + 6 : columns + 8].T,
        grad_in,
        grad_down,
    )


def solution(mesh):
    in_specs = (
        P(None, "dp", None),
        P(None, "dp", None),
        P(None, "dp", None),
        P(None, "dp", None),
        P("dp"),
        P("dp"),
        P(None, "dp", "tensor"),
        P("tensor", "dp"),
        P("dp", None),
        P("dp", None),
        P(None, "dp"),
        P("dp", None, None, "tensor"),
        P("dp", "tensor", None),
    )
    out_specs = (
        P(None, "dp", None),
        P(None, "dp", None),
        P(None, "dp", None),
        P("dp"),
        P("dp"),
        P(None, "dp", "tensor"),
        P("tensor", "dp"),
        P("dp", None),
        P("dp", None),
        P(None, "dp"),
        P("dp", None, None, "tensor"),
        P("dp", "tensor", None),
    )
    return jax.shard_map(body, mesh=mesh, in_specs=in_specs, out_specs=out_specs, check_vma=False)
```

```python
import functools

import jax
import jax.numpy as jnp
import numpy as np
from jax import lax
from jax.experimental import pallas as pl
from jax.experimental.pallas import tpu as pltpu
from jax.sharding import PartitionSpec as P

HD = 64
LEN = 1024
BLK = 256
EPSILON = 1e-06
LANES = 128
F32 = jnp.float32
BF16 = jnp.bfloat16
MESH = pl.DeviceIdType.MESH
VMEM_LIMIT = 56 * 1024 * 1024


def mm(a, b):
    return lax.dot_general(a, b, (((1,), (0,)), ((), ())), preferred_element_type=F32)


def mm_nt(a, b):
    return lax.dot_general(a, b, (((1,), (1,)), ((), ())), preferred_element_type=F32)


def mm_tn(a, b):
    return lax.dot_general(a, b, (((0,), (0,)), ((), ())), preferred_element_type=F32)


def vspec():
    return pl.BlockSpec(memory_space=pltpu.VMEM)


def aspec():
    return pl.BlockSpec(memory_space=pl.ANY)


def struct(shape, dtype):
    return jax.ShapeDtypeStruct(shape, dtype)


def compute_call(kernel, outs, *args, flops=1e9, scratch=()):
    nbytes = sum(int(np.prod(a.shape)) * a.dtype.itemsize for a in args) + sum(
        int(np.prod(o.shape)) * o.dtype.itemsize for o in outs
    )
    return pl.pallas_call(
        kernel,
        out_shape=outs,
        in_specs=[vspec()] * len(args),
        out_specs=[vspec()] * len(outs),
        scratch_shapes=list(scratch),
        compiler_params=pltpu.CompilerParams(vmem_limit_bytes=VMEM_LIMIT),
        cost_estimate=pl.CostEstimate(
            flops=int(flops), bytes_accessed=nbytes, transcendentals=0
        ),
    )(*args)


def greet(peers):
    barrier = pltpu.get_barrier_semaphore()
    for peer in peers:
        pl.semaphore_signal(barrier, inc=1, device_id=peer, device_id_type=MESH)
    pl.semaphore_wait(barrier, len(peers))


def remote(src, dst, send, recv, peer):
    return pltpu.make_async_remote_copy(
        src_ref=src,
        dst_ref=dst,
        send_sem=send,
        recv_sem=recv,
        device_id=peer,
        device_id_type=MESH,
    )


def comm_call(kernel, outs, sems, cid, *args):
    return pl.pallas_call(
        kernel,
        out_shape=outs,
        in_specs=[aspec()] * len(args),
        out_specs=[aspec()] * len(outs),
        scratch_shapes=[pltpu.SemaphoreType.DMA(s) for s in sems],
        compiler_params=pltpu.CompilerParams(collective_id=cid, has_side_effects=True),
    )(*args)


def core_share(cid, *arrays):
    count = len(arrays)

    def kernel(*refs):
        ins, outs, (send, recv, local) = refs[:count], refs[count : 2 * count], refs[2 * count :]
        d, t = lax.axis_index("dp"), lax.axis_index("tensor")
        c = lax.rem(t, 2)
        peer = (d, t + 1 - 2 * c)
        greet([peer])
        copies = []
        for i in range(count):
            copies.append(remote(ins[i], outs[i].at[c], send.at[i], recv.at[i], peer))
            copies.append(pltpu.make_async_copy(ins[i], outs[i].at[c], local.at[i]))
        for copy in copies:
            copy.start()
        for copy in copies:
            copy.wait()

    outs = [struct((2,) + a.shape, a.dtype) for a in arrays]
    return comm_call(kernel, outs, [(count,)] * 3, cid, *arrays)


def plane_peers(n, d, t):
    return [(lax.rem(d + j, n), t) for j in range(1, n)]


def all_peers(n, d, t):
    other = lax.rem(t + 2, 4)
    return plane_peers(n, d, t) + [(lax.rem(d + j, n), other) for j in range(n)]


def spread_gradients(cid, n, *arrays):
    count = len(arrays)

    def kernel(*refs):
        ins, outs, (send, recv, local) = refs[:count], refs[count : 2 * count], refs[2 * count :]
        d, t = lax.axis_index("dp"), lax.axis_index("tensor")
        m = lax.div(t, 2)
        peers = all_peers(n, d, t)
        greet(peers)
        copies = []
        for k in range(count):
            copies.append(
                pltpu.make_async_copy(ins[k].at[m, d], outs[k].at[m, d], local.at[k])
            )
            for i, (pd, pt) in enumerate(peers):
                pm = lax.div(pt, 2)
                copies.append(
                    remote(
                        ins[k].at[pm, pd],
                        outs[k].at[m, d],
                        send.at[k, i],
                        recv.at[k, i],
                        (pd, pt),
                    )
                )
        for copy in copies:
            copy.start()
        for copy in copies:
            copy.wait()

    outs = [struct(a.shape, a.dtype) for a in arrays]
    return comm_call(kernel, outs, [(count, 2 * n), (count, 2 * n), (count,)], cid, *arrays)


def give_back(cid, n, *arrays):
    count = len(arrays)

    def kernel(*refs):
        ins, outs = refs[:count], refs[count : 2 * count]
        send, recv, local, csend, crecv = refs[2 * count :]
        d, t = lax.axis_index("dp"), lax.axis_index("tensor")
        c = lax.rem(t, 2)
        partner = (d, t + 1 - 2 * c)
        peers = plane_peers(n, d, t)
        greet(peers + [partner])
        arrivals = []
        own = []
        passed = []
        for k in range(count):
            own.append(pltpu.make_async_copy(ins[k].at[d], outs[k].at[c, d], local.at[k]))
            passed.append(
                remote(ins[k].at[d], outs[k].at[c, d], csend.at[k, 0], crecv.at[k, 0], partner)
            )
            for i, (pd, pt) in enumerate(peers):
                arrivals.append(
                    remote(
                        ins[k].at[pd], outs[k].at[c, d], send.at[k, i], recv.at[k, i], (pd, pt)
                    )
                )
        for copy in own + passed + arrivals:
            copy.start()
        for k in range(count):
            for i in range(n - 1):
                arrivals[k * (n - 1) + i].wait_recv()
                source = lax.rem(d + n - 1 - i, n)
                block = outs[k].at[c, source]
                copy = remote(block, block, csend.at[k, i + 1], crecv.at[k, i + 1], partner)
                copy.start()
                passed.append(copy)
        for copy in arrivals:
            copy.wait_send()
        for copy in own + passed:
            copy.wait()

    outs = [struct((2,) + a.shape, a.dtype) for a in arrays]
    return comm_call(
        kernel, outs, [(count, n), (count, n), (count,), (count, n), (count, n)], cid, *arrays
    )


def share_output(cid, full):
    rows = full.shape[0]
    half = rows // 2

    def kernel(in_ref, out_ref, send, recv, local):
        d, t = lax.axis_index("dp"), lax.axis_index("tensor")
        m, c = lax.div(t, 2), lax.rem(t, 2)
        across = (d, lax.rem(t + 2, 4))
        partner = (d, t + 1 - 2 * c)
        greet([across, partner])
        mine = pltpu.make_async_copy(in_ref, out_ref.at[m], local.at[0])
        mine.start()
        first = remote(
            in_ref.at[pl.ds(c * half, half)],
            out_ref.at[m, pl.ds(c * half, half)],
            send.at[0],
            recv.at[0],
            across,
        )
        first.start()
        first.wait_recv()
        block = out_ref.at[1 - m, pl.ds(c * half, half)]
        second = remote(block, block, send.at[1], recv.at[1], partner)
        second.start()
        first.wait_send()
        second.wait()
        mine.wait()

    outs = [struct((2,) + full.shape, full.dtype)]
    return comm_call(kernel, outs, [(2,), (2,), (1,)], cid, full)[0]


def slot_hot(half, padded, base, places):
    rows = places.shape[1]
    slot = lax.broadcasted_iota(jnp.int32, (padded, rows), 0)
    wanted = jnp.where(slot < half, slot + base, -2).astype(F32)
    return (wanted == places).astype(F32).astype(BF16)


def rope_constants():
    half = HD // 2
    frequency = 10000.0 ** (-2.0 * np.arange(half) / HD)
    angle = np.arange(LEN)[:, None] * frequency[None, :]
    cosine, sine = np.cos(angle), np.sin(angle)
    cosine = np.concatenate([cosine, cosine, cosine, cosine], axis=1)
    sine = np.concatenate([-sine, sine, -sine, sine], axis=1)
    return cosine.astype(np.float32), sine.astype(np.float32)


def turn(field, cosine, sine):
    lane = lax.broadcasted_iota(jnp.int32, field.shape, 1)
    other = jnp.where(
        lax.rem(lane, HD) < HD // 2,
        pltpu.roll(field, LANES - HD // 2, 1),
        pltpu.roll(field, HD // 2, 1),
    )
    return field * cosine + other * sine


def pick(hot, values):
    return jnp.sum(jnp.where(hot, values, 0.0), axis=-1, keepdims=True)


def lane_ids(rows):
    return lax.broadcasted_iota(jnp.int32, (rows, LANES), 1)


def soft_pair(first, second):
    high = jnp.maximum(first, second)
    e0, e1 = jnp.exp(first - high), jnp.exp(second - high)
    return e0 / (e0 + e1), e1 / (e0 + e1)


def half_mask(rows):
    return lax.broadcasted_iota(jnp.int32, (rows, LANES), 1) < HD


def swap_halves(value):
    return pltpu.roll(value, HD, 1)


def front_kernel(
    n,
    half,
    padded,
    gathered,
    tokens_ref,
    cotangent_ref,
    prev_all_ref,
    routes_all_ref,
    packed_ref,
    cos_ref,
    sin_ref,
    win_ref,
    wdown_ref,
    a_ref,
    q_ref,
    k_ref,
    v_ref,
    o_ref,
    lse_ref,
    h_ref,
    ub_ref,
    stat_ref,
    pos_ref,
    wo_ref,
    small_ref,
    extra_ref,
    spread_ref,
    arrived_ref,
    gate_arrived_ref,
    dy_arrived_ref,
    in_c_ref,
    in_x_ref,
    in_d_ref,
    down_c_ref,
    down_x_ref,
    down_d_ref,
    x_ref,
    dy_ref,
    prev_ref,
    routes_ref,
    place_ref,
    gates_ref,
    slot_ref,
    gate_ref,
    dy_slot_ref,
    load,
    pack_send,
    pack_recv,
    dy_send,
    dy_recv,
    slot_send,
    slot_recv,
    gate_send,
    gate_recv,
    stay,
    core_send,
    core_recv,
    w_send,
    w_recv,
):
    rows_all, width = x_ref.shape
    blocks = rows_all // BLK
    pairs = q_ref.shape[0]
    local = pairs * LANES
    columns = prev_ref.shape[1]
    d, t = lax.axis_index("dp"), lax.axis_index("tensor")
    m, c = lax.div(t, 2), lax.rem(t, 2)
    partner = (d, t + 1 - 2 * c)
    across = (d, lax.rem(t + 2, 4))
    loads = [
        pltpu.make_async_copy(src.at[m], dst, load.at[i])
        for i, (src, dst) in enumerate(
            [
                (routes_all_ref, routes_ref),
                (cotangent_ref, dy_ref),
                (tokens_ref, x_ref),
                (prev_all_ref, prev_ref),
            ]
        )
    ]
    for copy in loads:
        copy.start()
    peers = all_peers(n, d, t)
    greet(peers + [partner])
    pack_copies = []
    if gathered:
        spread_ref[...] = packed_ref[...]
    else:
        part = packed_ref.shape[0]
        place = pl.ds(pl.multiple_of(d * part, part), part)
        spread_ref[m, place, :] = packed_ref[...]
        for i, peer in enumerate(peers):
            pack_copies.append(
                remote(
                    packed_ref,
                    spread_ref.at[m, place, :],
                    pack_send.at[i],
                    pack_recv.at[i],
                    peer,
                )
            )
        for copy in pack_copies:
            copy.start()

    loads[0].wait()
    line = lax.broadcasted_iota(jnp.int32, (rows_all, LANES), 1)
    named = jnp.where(
        line == 0,
        routes_ref[:, 0:1].astype(F32),
        jnp.where(line == 1, routes_ref[:, 1:2].astype(F32), 0.0),
    )
    named = jnp.transpose(named)
    ids = lax.broadcasted_iota(jnp.int32, (LANES, rows_all), 0).astype(F32)
    hit = ((ids == named[0:1, :]) | (ids == named[1:2, :])) & (ids < float(n))
    before = lax.broadcasted_iota(jnp.int32, (rows_all, rows_all), 0) < lax.broadcasted_iota(
        jnp.int32, (rows_all, rows_all), 1
    )
    count = mm(hit.astype(F32).astype(BF16), before.astype(F32).astype(BF16))
    places = jnp.where(hit, count, -1.0)
    place_ref[...] = places
    pos_ref[...] = jnp.transpose(places)
    base = c * half

    def dy_copy(j):
        e = lax.rem(d + j, n)
        return remote(
            dy_slot_ref.at[e], dy_arrived_ref.at[d], dy_send.at[j], dy_recv.at[j], (e, t)
        )

    def slot_copy(j):
        e = lax.rem(d + j, n)
        return remote(
            slot_ref.at[e], arrived_ref.at[d], slot_send.at[j], slot_recv.at[j], (e, t)
        )

    def gate_copy(j):
        e = lax.rem(d + j, n)
        return remote(
            gate_ref.at[e], gate_arrived_ref.at[d], gate_send.at[j], gate_recv.at[j], (e, t)
        )

    stays = [
        pltpu.make_async_copy(src.at[d], dst.at[d], stay.at[i])
        for i, (src, dst) in enumerate(
            [
                (dy_slot_ref, dy_arrived_ref),
                (slot_ref, arrived_ref),
                (gate_ref, gate_arrived_ref),
            ]
        )
    ]
    loads[1].wait()

    def dy_step(i, carry):
        j = lax.rem(i + 1, n)
        e = lax.rem(d + j, n)
        hot = slot_hot(half, padded, base, place_ref[pl.ds(e, 1), :])
        dy_slot_ref[e] = mm(hot, dy_ref[...]).astype(BF16)

        @pl.when(i < n - 1)
        def _():
            dy_copy(j).start()

        return carry

    lax.fori_loop(0, n, dy_step, 0)
    stays[0].start()

    for copy in pack_copies:
        copy.wait_recv()
    weight_copies = [
        remote(win_ref, in_x_ref, w_send.at[0], w_recv.at[0], across),
        remote(wdown_ref, down_x_ref, w_send.at[1], w_recv.at[1], across),
        remote(win_ref, in_c_ref, w_send.at[2], w_recv.at[2], partner),
        remote(wdown_ref, down_c_ref, w_send.at[3], w_recv.at[3], partner),
        remote(in_x_ref, in_d_ref, w_send.at[4], w_recv.at[4], partner),
        remote(down_x_ref, down_d_ref, w_send.at[5], w_recv.at[5], partner),
    ]
    for copy in weight_copies[0:4]:
        copy.start()

    table = spread_ref[0, :, 6 * LANES : 7 * LANES]
    extra_ref[...] = jnp.transpose(table.astype(F32))
    keep = lax.broadcasted_iota(jnp.int32, (width, LANES), 1) < columns + 4
    small_ref[...] = jnp.where(keep, table, jnp.zeros_like(table))
    mask = half_mask(width)
    own = pl.multiple_of(c * local, LANES)
    wo_ref[:, pl.ds(own, LANES)] = spread_ref[0, :, 3 * LANES : 4 * LANES]
    wo_ref[:, pl.ds(own + LANES, LANES)] = spread_ref[1, :, 3 * LANES : 4 * LANES]
    wo_ref[:, pl.ds(own + 2 * LANES, LANES)] = jnp.where(
        mask,
        swap_halves(spread_ref[0, :, 5 * LANES : 6 * LANES].astype(F32)),
        spread_ref[1, :, 5 * LANES : 6 * LANES].astype(F32),
    ).astype(BF16)
    own_lanes = pl.ds(own, local)
    wo_copy = remote(
        wo_ref.at[:, own_lanes],
        wo_ref.at[:, own_lanes],
        core_send.at[pairs],
        core_recv.at[pairs],
        partner,
    )
    wo_copy.start()

    loads[2].wait()
    gain = extra_ref[columns + 4 : columns + 5, :]
    head = half_mask(BLK)

    def project(i, carry):
        rows = pl.ds(pl.multiple_of(i * BLK, BLK), BLK)
        x = x_ref[rows, :].astype(F32)
        r = lax.rsqrt(jnp.mean(x * x, axis=-1, keepdims=True) + EPSILON)
        a = (x * r * gain).astype(BF16)
        a_ref[rows, :] = a
        cosine, sine = cos_ref[rows, :], sin_ref[rows, :]

        def put(pair, q, k, v):
            q_ref[pair, rows, :] = turn(q, cosine, sine).astype(BF16) * BF16(HD**-0.5)
            k_ref[pair, rows, :] = turn(k, cosine, sine).astype(BF16)
            v_ref[pair, rows, :] = v.astype(BF16)

        odd = []
        for s in range(2):
            both = mm(a, spread_ref[s, :, 0 : 3 * LANES])
            put(s, *(both[:, j * LANES : (j + 1) * LANES] for j in range(3)))
            both = mm(a, spread_ref[s, :, 4 * LANES : 6 * LANES])
            odd.append((both[:, :LANES], both[:, LANES:]))
        put(
            2,
            jnp.where(head, odd[0][0], swap_halves(odd[1][0])),
            jnp.where(head, swap_halves(odd[0][0]), odd[1][0]),
            jnp.where(head, odd[0][1], swap_halves(odd[1][1])),
        )
        return carry

    lax.fori_loop(0, blocks, project, 0)

    def o_copy(p):
        lanes = pl.ds(pl.multiple_of(own + p * LANES, LANES), LANES)
        return remote(
            o_ref.at[:, lanes], o_ref.at[:, lanes], core_send.at[p], core_recv.at[p], partner
        )

    def attend(p, carry):
        lanes = pl.ds(pl.multiple_of(own + p * LANES, LANES), LANES)
        for i in range(blocks):
            rows = pl.ds(i * BLK, BLK)
            seen = pl.ds(0, (i + 1) * BLK)
            q, k, v = q_ref[p, rows, :], k_ref[p, seen, :], v_ref[p, seen, :]
            halves = []
            for side in range(2):
                chosen = head if side == 0 else jnp.logical_not(head)
                s = mm_nt(jnp.where(chosen, q, jnp.zeros_like(q)), k)
                high = jnp.max(s, axis=-1, keepdims=True)
                e = jnp.exp(s - high)
                total = jnp.sum(e, axis=-1, keepdims=True)
                halves.append(mm((e / total).astype(BF16), v))
                log_total = jnp.broadcast_to(high + jnp.log(total), (BLK, LANES))
                lse_ref[2 * p + side, :, rows] = jnp.transpose(log_total)[0:8, :]
            o_ref[rows, lanes] = jnp.where(head, halves[0], halves[1]).astype(BF16)
        o_copy(p).start()
        return carry

    lax.fori_loop(0, pairs, attend, 0)
    loads[3].wait()
    wo_copy.wait()
    for p in range(pairs):
        o_copy(p).wait()

    gain_moe = extra_ref[columns + 5 : columns + 6, :]

    def middle(i, carry):
        rows = pl.ds(pl.multiple_of(i * BLK, BLK), BLK)
        z = mm_nt(o_ref[rows, :], wo_ref[...])
        h = x_ref[rows, :].astype(F32) + z
        r = lax.rsqrt(jnp.mean(h * h, axis=-1, keepdims=True) + EPSILON)
        ub = (h * r * gain_moe).astype(BF16)
        h_ref[rows, :] = h
        ub_ref[rows, :] = ub
        scores = mm(ub, small_ref[...])
        lane = lane_ids(BLK)
        e0, e1 = routes_ref[rows, 0:1], routes_ref[rows, 1:2]
        hot0, hot1 = lane == e0, lane == e1
        prev = prev_ref[rows, :]
        few = lax.broadcasted_iota(jnp.int32, (BLK, columns), 1)
        g0, g1 = soft_pair(
            pick(hot0, scores) + pick(few == e0, prev), pick(hot1, scores) + pick(few == e1, prev)
        )
        mix = [pick(lane == columns + j, scores) for j in range(4)]
        a00, a01 = soft_pair(mix[0], mix[1])
        a10, a11 = soft_pair(mix[2], mix[3])
        table = jnp.zeros((BLK, LANES), F32)
        for j, value in enumerate([g0, g1, a00, a01, a10, a11, r]):
            table = jnp.where(lane == j, value, table)
        stat_ref[rows, :] = table
        gates = jnp.where(hot0, g0, 0.0) + jnp.where(hot1, g1, 0.0)
        gates_ref[:, rows] = jnp.transpose(gates)
        return carry

    lax.fori_loop(0, blocks, middle, 0)
    piece = lax.broadcasted_iota(jnp.int32, (8, rows_all), 0)

    def slot_step(i, carry):
        j = lax.rem(i + 1, n)
        e = lax.rem(d + j, n)
        hot = slot_hot(half, padded, base, place_ref[pl.ds(e, 1), :])
        slot_ref[e] = mm(hot, ub_ref[...]).astype(BF16)
        gate = gates_ref[pl.ds(e, 1), :]
        high = gate.astype(BF16).astype(F32)
        mid = (gate - high).astype(BF16).astype(F32)
        low = gate - high - mid
        lines = jnp.where(piece == 0, high, jnp.where(piece == 1, mid, low))
        lines = jnp.where(piece < 3, lines, 0.0).astype(BF16)
        gate = jnp.sum(mm_nt(lines, hot), axis=0, keepdims=True)
        gate_ref[e] = jnp.broadcast_to(gate, (8, padded))

        @pl.when(i < n - 1)
        def _():
            slot_copy(j).start()
            gate_copy(j).start()

        return carry

    lax.fori_loop(0, n, slot_step, 0)
    stays[1].start()
    stays[2].start()
    weight_copies[0].wait_recv()
    weight_copies[1].wait_recv()
    weight_copies[4].start()
    weight_copies[5].start()

    def finish(j, carry):
        for copy in (dy_copy(j), slot_copy(j), gate_copy(j)):
            copy.wait()
        return carry

    lax.fori_loop(1, n, finish, 0)
    for copy in stays:
        copy.wait()
    for copy in pack_copies + weight_copies[0:2]:
        copy.wait_send()
    for copy in weight_copies[2:6]:
        copy.wait()


def expert_kernel(
    sources,
    padded,
    x_ref,
    dy_ref,
    gate_ref,
    *refs,
):
    weights, outs = refs[:8], refs[8:19]
    in_refs, down_refs = weights[0:4], weights[4:8]
    gy_ref, dx_ref, dg_ref = outs[0:3]
    gin_refs, gdown_refs = outs[3:7], outs[7:11]
    xt_ref, scaled_ref, scale_ref, y_acc, dx_acc, win_ref, wdown_ref = refs[19:]
    step = pl.program_id(0)
    last = pl.num_programs(0) - 1

    @pl.when(step == 0)
    def _():
        xt_ref[...] = jnp.transpose(x_ref[...])
        for s in range(sources):
            rows = pl.ds(s * padded, padded)
            line = jnp.broadcast_to(gate_ref[s, 0:1, :], (LANES, padded))
            scale = jnp.transpose(line)
            scale_ref[rows, :] = scale
            scaled_ref[rows, :] = (dy_ref[rows, :].astype(F32) * scale[:, 0:1]).astype(BF16)
        y_acc[...] = jnp.zeros_like(y_acc)
        dx_acc[...] = jnp.zeros_like(dx_acc)

    per = pl.num_programs(0) // 4
    for i in range(4):

        @pl.when(lax.div(step, per) == i)
        def _():
            win_ref[...] = in_refs[i][0]
            wdown_ref[...] = down_refs[i][0]

    x = x_ref[...]
    gate = mm(x, win_ref[0])
    up = mm(x, win_ref[1])
    sigma = 1.0 / (1.0 + jnp.exp(-gate))
    active = gate * sigma
    hidden = (active * up).astype(BF16)
    y_acc[...] += mm(hidden, wdown_ref[...])
    scaled = scaled_ref[...]
    grad_hidden = mm_nt(scaled, wdown_ref[...])
    grad_gate = (grad_hidden * up * (sigma * (1.0 + gate * (1.0 - sigma)))).astype(BF16)
    grad_up = (grad_hidden * active).astype(BF16)
    dx_acc[...] += mm_nt(grad_gate, win_ref[0]) + mm_nt(grad_up, win_ref[1])
    xt = xt_ref[...]
    part_gate = mm(xt, grad_gate).astype(BF16)
    part_up = mm(xt, grad_up).astype(BF16)
    part_down = mm_tn(hidden, scaled).astype(BF16)
    for i in range(4):

        @pl.when(lax.div(step, per) == i)
        def _():
            gin_refs[i][0, 0] = part_gate
            gin_refs[i][0, 1] = part_up
            gdown_refs[i][0] = part_down

    @pl.when(step == last)
    def _():
        for s in range(sources):
            rows = pl.ds(s * padded, padded)
            y = y_acc[rows, :]
            gy_ref[s] = (y * scale_ref[rows, 0:1]).astype(BF16)
            dot = jnp.sum(y * dy_ref[rows, :].astype(F32), axis=-1, keepdims=True)
            dg_ref[s] = jnp.transpose(jnp.broadcast_to(dot, (padded, LANES)))[0:8, :]
            dx_ref[s] = dx_acc[rows, :].astype(BF16)


def back_kernel(
    experts,
    half,
    padded,
    h_ref,
    ub_ref,
    stat_ref,
    routes_ref,
    pos_ref,
    dy_ref,
    gy_ref,
    dx_ref,
    dg_ref,
    small_ref,
    gain_ref,
    vec_ref,
    o_ref,
    wo_ref,
    result_ref,
    prev_ref,
    dh_ref,
    do_ref,
    grad_wo_ref,
    grad_small_ref,
    mixed_ref,
    low_ref,
    dzb_ref,
    row_ref,
):
    rows_all = h_ref.shape[0]
    width = h_ref.shape[1]
    row_ref[...] = jnp.zeros_like(row_ref)
    columns = experts + 4
    for i in range(rows_all // BLK):
        rows = pl.ds(i * BLK, BLK)
        ids = lane_ids(BLK)
        stats = stat_ref[rows, :]
        g0, g1, a00, a01, a10, a11, r = [stats[:, j : j + 1] for j in range(7)]
        e0, e1 = routes_ref[rows, 0:1], routes_ref[rows, 1:2]
        hot0, hot1 = ids == e0, ids == e1
        places = pos_ref[rows, :]
        sums = jnp.zeros((BLK, width), F32)
        grads = jnp.zeros((BLK, width), F32)
        gate_grads = jnp.zeros((BLK, LANES), F32)

        def step(e, carry):
            sums, grads, gate_grads = carry
            place = pick(ids == e, places)
            for side in range(2):
                slot = lax.broadcasted_iota(jnp.int32, (BLK, padded), 1)
                wanted = jnp.where(slot < half, slot + side * half, -2).astype(F32)
                hot = wanted == place
                low = hot.astype(F32).astype(BF16)
                sums = sums + mm(low, gy_ref[side, e])
                grads = grads + mm(low, dx_ref[side, e])
                value = jnp.sum(
                    jnp.where(hot, dg_ref[side, e, 0:1, :], 0.0), axis=-1, keepdims=True
                )
                gate_grads = gate_grads + jnp.where(ids == e, value, 0.0)
            return sums, grads, gate_grads

        sums, grads, gate_grads = lax.fori_loop(
            0, experts, step, (sums, grads, gate_grads)
        )
        h = h_ref[rows, :]
        n = h * r
        u = n * gain_ref[...]
        dy = dy_ref[rows, :].astype(F32)
        vec0, vec1 = vec_ref[0:1, :], vec_ref[1:2, :]

        def named(number):
            return jnp.where(e0 == number, g0, 0.0) + jnp.where(e1 == number, g1, 0.0)

        copied, first, second = named(experts + 1), named(experts + 2), named(experts + 3)
        on_u = copied + first * a00 + second * a10
        result = h + (sums + on_u * u + (first * a01) * vec0 + (second * a11) * vec1)
        result_ref[rows, :] = result.astype(BF16)
        s_u = jnp.sum(dy * u, axis=-1, keepdims=True)
        s_0 = jnp.sum(dy * vec0, axis=-1, keepdims=True)
        s_1 = jnp.sum(dy * vec1, axis=-1, keepdims=True)
        table = (
            gate_grads
            + jnp.where(ids == experts + 1, s_u, 0.0)
            + jnp.where(ids == experts + 2, a00 * s_u + a01 * s_0, 0.0)
            + jnp.where(ids == experts + 3, a10 * s_u + a11 * s_1, 0.0)
        )
        dg0, dg1 = pick(hot0, table), pick(hot1, table)
        mean = g0 * dg0 + g1 * dg1
        dl = jnp.where(hot0, g0 * (dg0 - mean), 0.0) + jnp.where(hot1, g1 * (dg1 - mean), 0.0)
        prev_ref[rows, :] = dl
        d00, d01 = first * s_u, first * s_0
        d10, d11 = second * s_u, second * s_1
        m0 = a00 * d00 + a01 * d01
        m1 = a10 * d10 + a11 * d11
        mixing = (
            jnp.where(ids == columns, a00 * (d00 - m0), 0.0)
            + jnp.where(ids == columns + 1, a01 * (d01 - m0), 0.0)
            + jnp.where(ids == columns + 2, a10 * (d10 - m1), 0.0)
            + jnp.where(ids == columns + 3, a11 * (d11 - m1), 0.0)
        )
        low = (dl + mixing).astype(BF16)
        low_ref[rows, :] = low
        du = grads + mm_nt(low, small_ref[...]) + on_u * dy
        row_ref[0:1, :] += jnp.sum(du * n, axis=0, keepdims=True)
        row_ref[1:2, :] += jnp.sum((first * a01) * dy, axis=0, keepdims=True)
        row_ref[2:3, :] += jnp.sum((second * a11) * dy, axis=0, keepdims=True)
        dn = du * gain_ref[...]
        dh = dy + r * (dn - n * jnp.mean(dn * n, axis=-1, keepdims=True))
        dh_ref[rows, :] = dh
        dzb = dh.astype(BF16)
        dzb_ref[rows, :] = dzb
        do_ref[rows, :] = mm(dzb, wo_ref[...]).astype(BF16)
    grad_wo_ref[...] = mm_tn(dzb_ref[...], o_ref[...]).astype(BF16)
    lines = jnp.concatenate([row_ref[...], jnp.zeros((LANES - 8, width), F32)], axis=0)
    grad_small_ref[...] = mm_tn(ub_ref[...], low_ref[...])
    mixed_ref[...] = jnp.transpose(lines)


def attention_back_kernel(
    q_ref,
    k_ref,
    v_ref,
    do_ref,
    lse_ref,
    a_ref,
    w_ref,
    cos_ref,
    sin_ref,
    da_ref,
    grad_w_ref,
    dp_ref,
    dk_acc,
    dv_acc,
):
    pairs = q_ref.shape[0]
    width = pairs * LANES
    blocks = LEN // BLK
    head = lax.broadcasted_iota(jnp.int32, (BLK, LANES), 1) < HD
    for p in range(pairs):
        lanes = pl.ds(p * LANES, LANES)
        dk_acc[...] = jnp.zeros_like(dk_acc)
        dv_acc[...] = jnp.zeros_like(dv_acc)
        for i in range(blocks):
            rows = pl.ds(i * BLK, BLK)
            seen = pl.ds(0, (i + 1) * BLK)
            q, do = q_ref[p, rows, :], do_ref[rows, lanes]
            k, v = k_ref[p, seen, :], v_ref[p, seen, :]
            zero = jnp.zeros_like(q)
            parts = []
            dk = dk_acc[seen, :]
            dv = dv_acc[seen, :]
            for side in range(2):
                mask = head if side == 0 else jnp.logical_not(head)
                qm, dom = jnp.where(mask, q, zero), jnp.where(mask, do, zero)
                log_total = lse_ref[2 * p + side, 0:1, rows]
                prob = jnp.exp(mm_nt(k, qm) - log_total)
                grad_prob = mm_nt(v, dom)
                total = jnp.sum(prob * grad_prob, axis=0, keepdims=True)
                grad_score = (prob * (grad_prob - total)).astype(BF16)
                dv = dv + mm(prob.astype(BF16), dom)
                dk = dk + mm(grad_score, qm)
                parts.append(mm_tn(grad_score, k))
            dk_acc[seen, :] = dk
            dv_acc[seen, :] = dv
            dq = jnp.where(head, parts[0], parts[1]) * (HD**-0.5)
            dp_ref[rows, lanes] = turn(dq, cos_ref[rows, :], -sin_ref[rows, :]).astype(BF16)
        dp_ref[:, pl.ds(width + p * LANES, LANES)] = turn(
            dk_acc[...], cos_ref[...], -sin_ref[...]
        ).astype(BF16)
        dp_ref[:, pl.ds(2 * width + p * LANES, LANES)] = dv_acc[...].astype(BF16)
    for i in range(blocks):
        rows = pl.ds(i * BLK, BLK)
        da_ref[rows, :] = mm_nt(dp_ref[rows, :], w_ref[...]).astype(BF16)
    for j in range(3 * pairs):
        lanes = pl.ds(j * LANES, LANES)
        grad_w_ref[:, lanes] = mm_tn(a_ref[...], dp_ref[:, lanes]).astype(BF16)


def finish_kernel(x_ref, dh_ref, da_ref, gain_ref, grad_ref, row_ref):
    rows_all, width = x_ref.shape
    total = jnp.zeros((1, width), F32)
    for i in range(rows_all // BLK):
        rows = pl.ds(i * BLK, BLK)
        x = x_ref[rows, :].astype(F32)
        r = lax.rsqrt(jnp.mean(x * x, axis=-1, keepdims=True) + EPSILON)
        n = x * r
        da = da_ref[0, rows, :].astype(F32) + da_ref[1, rows, :].astype(F32)
        total = total + jnp.sum(da * n, axis=0, keepdims=True)
        dn = da * gain_ref[...]
        grad = dh_ref[rows, :] + r * (dn - n * jnp.mean(dn * n, axis=-1, keepdims=True))
        grad_ref[rows, :] = grad.astype(BF16)
    row_ref[...] = jnp.broadcast_to(total, row_ref.shape)


def across_chips(value):
    return lax.ppermute(value, "tensor", [(0, 2), (2, 0), (1, 3), (3, 1)])


def across_cores(value):
    return lax.ppermute(value, "tensor", [(0, 1), (1, 0), (2, 3), (3, 2)])


def body(
    tokens,
    cotangent,
    prev_logits,
    routes,
    norm_attn,
    norm_moe,
    w_qkv,
    w_out,
    w_router,
    w_const,
    const_vec,
    w_in,
    w_down,
):
    rows, width = tokens.shape[1:]
    n = lax.axis_size("dp")
    experts = n
    columns = prev_logits.shape[2]
    capacity = 4 * max(1, 3 * rows // (4 * (experts + 4)))
    half = capacity // 2
    padded = -(-half // 16) * 16
    share = w_qkv.shape[2]
    local = 2 * share
    part = w_qkv.shape[1]
    t = lax.axis_index("tensor")
    m, c = t // 2, t % 2

    def mine(value):
        return lax.dynamic_index_in_dim(value, m, 0, keepdims=False)

    x, dy, choose = mine(tokens), mine(cotangent), mine(routes)
    cosine, sine = (jnp.asarray(v) for v in rope_constants())
    pairs = local // LANES

    wo_rows = w_out.T
    packed = jnp.concatenate(
        [w_qkv[i, :, :LANES] for i in range(3)]
        + [wo_rows[:, :LANES]]
        + [w_qkv[i, :, LANES:] for i in range(3)]
        + [
            wo_rows[:, LANES:],
            w_router,
            w_const,
            norm_attn[:, None],
            norm_moe[:, None],
            const_vec.T,
            jnp.zeros((part, LANES - columns - 8), BF16),
        ],
        axis=1,
    )
    gathered = part % 16 != 0
    if gathered:
        packed = lax.all_gather(packed, "dp", axis=0, tiled=True)
        other = across_chips(packed)
        packed = jnp.where(m == 0, jnp.stack([packed, other]), jnp.stack([other, packed]))
    spread_width = packed.shape[-1]
    front_outs = [
        struct((rows, width), BF16),
        struct((pairs, rows, LANES), BF16),
        struct((pairs, rows, LANES), BF16),
        struct((pairs, rows, LANES), BF16),
        struct((rows, width), BF16),
        struct((8, 8, rows), F32),
        struct((rows, width), F32),
        struct((rows, width), BF16),
        struct((rows, LANES), F32),
        struct((rows, LANES), F32),
        struct((width, width), BF16),
        struct((width, LANES), BF16),
        struct((LANES, width), F32),
        struct((2, width, spread_width), BF16),
    ]
    landing = [
        struct((n, padded, width), BF16),
        struct((n, 8, padded), F32),
        struct((n, padded, width), BF16),
    ] + [struct(w_in.shape, BF16)] * 3 + [struct(w_down.shape, BF16)] * 3
    dma = pltpu.SemaphoreType.DMA
    (
        a,
        q,
        k,
        v,
        o_all,
        lse,
        h,
        ub,
        stats,
        pos,
        wo_all,
        small_all,
        extra,
        spread,
        arrived,
        gate_arrived,
        dy_arrived,
        in_c,
        in_x,
        in_d,
        down_c,
        down_x,
        down_d,
    ) = pl.pallas_call(
        functools.partial(front_kernel, n, half, padded, gathered),
        out_shape=front_outs + landing,
        in_specs=[aspec()] * 4 + [vspec()] * 3 + [aspec()] * 2,
        out_specs=[vspec()] * len(front_outs) + [aspec()] * len(landing),
        scratch_shapes=[
            pltpu.VMEM((rows, width), BF16),
            pltpu.VMEM((rows, width), BF16),
            pltpu.VMEM((rows, columns), F32),
            pltpu.VMEM((rows, 2), jnp.int32),
            pltpu.VMEM((LANES, rows), F32),
            pltpu.VMEM((LANES, rows), F32),
            pltpu.VMEM((n, padded, width), BF16),
            pltpu.VMEM((n, 8, padded), F32),
            pltpu.VMEM((n, padded, width), BF16),
            dma((4,)),
            dma((2 * n,)),
            dma((2 * n,)),
            dma((n,)),
            dma((n,)),
            dma((n,)),
            dma((n,)),
            dma((n,)),
            dma((n,)),
            dma((3,)),
            dma((pairs + 1,)),
            dma((pairs + 1,)),
            dma((6,)),
            dma((6,)),
        ],
        compiler_params=pltpu.CompilerParams(
            collective_id=0, has_side_effects=True, vmem_limit_bytes=VMEM_LIMIT
        ),
    )(tokens, cotangent, prev_logits, routes, packed, cosine, sine, w_in, w_down)
    gain_attn = extra[columns + 4 : columns + 5]
    gain_moe = extra[columns + 5 : columns + 6]
    vectors = extra[columns + 6 : columns + 8]
    o = lax.dynamic_slice_in_dim(o_all, c * local, local, axis=1)
    wo_own = lax.dynamic_slice_in_dim(wo_all, c * local, local, axis=1)

    def group(j, g):
        return spread[j, :, g * LANES : (g + 1) * LANES]

    w_heads = jnp.concatenate(
        [
            group(0, 0),
            group(1, 0),
            group(0, 4)[:, :HD],
            group(1, 4)[:, :HD],
            group(0, 1),
            group(1, 1),
            group(0, 4)[:, HD:],
            group(1, 4)[:, HD:],
            group(0, 2),
            group(1, 2),
            group(0, 5)[:, :HD],
            group(1, 5)[:, :HD],
        ],
        axis=1,
    )

    hidden_width = w_in.shape[3]
    slots_all = experts * padded
    chunk = min(256 if slots_all <= 1024 else 128, hidden_width)
    per = hidden_width // chunk

    def in_map(i):
        return lambda f: (0, 0, 0, jnp.clip(f - per * i, 0, per - 1))

    def down_map(i):
        return lambda f: (0, jnp.clip(f - per * i, 0, per - 1), 0)

    in_blocks = [pl.BlockSpec((1, 2, width, chunk), in_map(i)) for i in range(4)]
    down_blocks = [pl.BlockSpec((1, chunk, width), down_map(i)) for i in range(4)]
    expert_outs = (
        [
            struct((n, padded, width), BF16),
            struct((n, padded, width), BF16),
            struct((n, 8, padded), F32),
        ]
        + [struct(w_in.shape, BF16)] * 4
        + [struct(w_down.shape, BF16)] * 4
    )

    def whole(shape):
        return pl.BlockSpec(
            shape, lambda f: (0,) * len(shape), pipeline_mode=pl.Buffered(1)
        )

    parts = pl.pallas_call(
        functools.partial(expert_kernel, n, padded),
        grid=(4 * per,),
        out_shape=expert_outs,
        in_specs=[
            whole((slots_all, width)),
            whole((slots_all, width)),
            whole((n, 8, padded)),
        ]
        + in_blocks
        + down_blocks,
        out_specs=[
            whole((n, padded, width)),
            whole((n, padded, width)),
            whole((n, 8, padded)),
        ]
        + in_blocks
        + down_blocks,
        scratch_shapes=[
            pltpu.VMEM((width, slots_all), BF16),
            pltpu.VMEM((slots_all, width), BF16),
            pltpu.VMEM((slots_all, LANES), F32),
            pltpu.VMEM((slots_all, width), F32),
            pltpu.VMEM((slots_all, width), F32),
            pltpu.VMEM((2, width, chunk), BF16),
            pltpu.VMEM((chunk, width), BF16),
        ],
        compiler_params=pltpu.CompilerParams(vmem_limit_bytes=VMEM_LIMIT),
        cost_estimate=pl.CostEstimate(
            flops=18 * slots_all * width * 4 * hidden_width,
            bytes_accessed=30_000_000,
            transcendentals=0,
        ),
    )(
        arrived.reshape(slots_all, width),
        dy_arrived.reshape(slots_all, width),
        gate_arrived,
        w_in,
        in_c,
        in_x,
        in_d,
        w_down,
        down_c,
        down_x,
        down_d,
    )
    gy, dx, dg = parts[0:3]
    gin, gdown = parts[3:7], parts[7:11]
    gy_all, dx_all, dg_all = give_back(4, n, gy, dx, dg)

    def total_in(own, core, chip, diagonal):
        own = own.astype(F32) + across_cores(core).astype(F32)
        chip = (chip.astype(F32) + across_cores(diagonal).astype(F32)).astype(BF16)
        return own + across_chips(chip).astype(F32)

    grad_in = total_in(*gin)
    grad_down = total_in(*gdown)

    result, dl, dh, do, grad_wo, grad_small, grad_lines = compute_call(
        functools.partial(back_kernel, experts, half, padded),
        [
            struct((rows, width), BF16),
            struct((rows, LANES), F32),
            struct((rows, width), F32),
            struct((rows, local), BF16),
            struct((width, local), BF16),
            struct((width, LANES), F32),
            struct((width, LANES), F32),
        ],
        h,
        ub,
        stats,
        choose,
        pos,
        dy,
        gy_all,
        dx_all,
        dg_all,
        small_all,
        gain_moe,
        vectors,
        o,
        wo_own,
        flops=8 * experts * padded * rows * width,
        scratch=[
            pltpu.VMEM((rows, LANES), BF16),
            pltpu.VMEM((rows, width), BF16),
            pltpu.VMEM((8, width), F32),
        ],
    )
    results = share_output(5, result)
    da, grad_heads = compute_call(
        attention_back_kernel,
        [struct((rows, width), BF16), struct((width, 3 * local), BF16)],
        q,
        k,
        v,
        do,
        lse,
        a,
        w_heads,
        cosine,
        sine,
        flops=4 * rows * width * 3 * local + 20 * rows * rows * local,
        scratch=[
            pltpu.VMEM((rows, 3 * local), BF16),
            pltpu.VMEM((rows, LANES), F32),
            pltpu.VMEM((rows, LANES), F32),
        ],
    )
    da_all = core_share(6, da)[0]
    grad_x, grad_line = compute_call(
        finish_kernel,
        [struct((rows, width), BF16), struct((8, width), F32)],
        x,
        dh,
        da_all,
        gain_attn,
    )
    input_grads = share_output(7, grad_x)

    grads = jnp.stack(
        [
            jnp.concatenate(
                [
                    piece[:, i * local + start : i * local + start + size]
                    for piece, i in [(grad_heads, 0), (grad_heads, 1), (grad_heads, 2), (grad_wo, 0)]
                    for start, size in [(j * LANES, LANES), (2 * LANES + j * HD, HD)]
                ],
                axis=1,
            )
            for j in range(2)
        ]
    ).reshape(2, n, part, 4 * share)
    lines = grad_small + jnp.pad(
        jnp.concatenate([grad_line[0:1].T, grad_lines[:, 0:3]], axis=1),
        ((0, 0), (columns + 4, LANES - columns - 8)),
    )
    lines = jnp.broadcast_to(lines.reshape(1, n, part, LANES), (2, n, part, LANES))
    grads_in, lines_in = spread_gradients(8, n, grads, lines)
    grads = jnp.sum(grads_in.astype(F32), axis=(0, 1))
    lines = jnp.sum(lines_in, axis=(0, 1))
    dl = dl[:, :columns]
    dl_x = across_chips(dl)
    logit_grads = jnp.where(m == 0, jnp.stack([dl, dl_x]), jnp.stack([dl_x, dl]))
    return (
        results,
        input_grads,
        logit_grads,
        lines[:, columns + 4],
        lines[:, columns + 5],
        jnp.stack([grads[:, i * share : (i + 1) * share] for i in range(3)]),
        grads[:, 3 * share :].T,
        lines[:, :columns],
        lines[:, columns : columns + 4],
        lines[:, columns + 6 : columns + 8].T,
        grad_in,
        grad_down,
    )


def solution(mesh):
    in_specs = (
        P(None, "dp", None),
        P(None, "dp", None),
        P(None, "dp", None),
        P(None, "dp", None),
        P("dp"),
        P("dp"),
        P(None, "dp", "tensor"),
        P("tensor", "dp"),
        P("dp", None),
        P("dp", None),
        P(None, "dp"),
        P("dp", None, None, "tensor"),
        P("dp", "tensor", None),
    )
    out_specs = (
        P(None, "dp", None),
        P(None, "dp", None),
        P(None, "dp", None),
        P("dp"),
        P("dp"),
        P(None, "dp", "tensor"),
        P("tensor", "dp"),
        P("dp", None),
        P("dp", None),
        P(None, "dp"),
        P("dp", None, None, "tensor"),
        P("dp", "tensor", None),
    )
    return jax.shard_map(body, mesh=mesh, in_specs=in_specs, out_specs=out_specs, check_vma=False)
```

```python
import functools

import jax
import jax.numpy as jnp
import numpy as np
from jax import lax
from jax.experimental import pallas as pl
from jax.experimental.pallas import tpu as pltpu
from jax.sharding import PartitionSpec as P

HD = 64
LEN = 1024
BLK = 256
EPSILON = 1e-06
LANES = 128
F32 = jnp.float32
BF16 = jnp.bfloat16
MESH = pl.DeviceIdType.MESH
VMEM_LIMIT = 60 * 1024 * 1024


def mm(a, b):
    return lax.dot_general(a, b, (((1,), (0,)), ((), ())), preferred_element_type=F32)


def mm_nt(a, b):
    return lax.dot_general(a, b, (((1,), (1,)), ((), ())), preferred_element_type=F32)


def mm_tn(a, b):
    return lax.dot_general(a, b, (((0,), (0,)), ((), ())), preferred_element_type=F32)


def vspec():
    return pl.BlockSpec(memory_space=pltpu.VMEM)


def aspec():
    return pl.BlockSpec(memory_space=pl.ANY)


def struct(shape, dtype):
    return jax.ShapeDtypeStruct(shape, dtype)


def greet(peers):
    barrier = pltpu.get_barrier_semaphore()
    for peer in peers:
        pl.semaphore_signal(barrier, inc=1, device_id=peer, device_id_type=MESH)
    pl.semaphore_wait(barrier, len(peers))


def remote(src, dst, send, recv, peer):
    return pltpu.make_async_remote_copy(
        src_ref=src,
        dst_ref=dst,
        send_sem=send,
        recv_sem=recv,
        device_id=peer,
        device_id_type=MESH,
    )


def plane_peers(n, d, t):
    return [(lax.rem(d + j, n), t) for j in range(1, n)]


def all_peers(n, d, t):
    other = lax.rem(t + 2, 4)
    return plane_peers(n, d, t) + [(lax.rem(d + j, n), other) for j in range(n)]


def slot_hot(half, padded, base, places):
    rows = places.shape[1]
    slot = lax.broadcasted_iota(jnp.int32, (padded, rows), 0)
    wanted = jnp.where(slot < half, slot + base, -2).astype(F32)
    return (wanted == places).astype(F32).astype(BF16)


def rope_constants():
    half = HD // 2
    frequency = 10000.0 ** (-2.0 * np.arange(half) / HD)
    angle = np.arange(LEN)[:, None] * frequency[None, :]
    cosine, sine = np.cos(angle), np.sin(angle)
    cosine = np.concatenate([cosine, cosine, cosine, cosine], axis=1)
    sine = np.concatenate([-sine, sine, -sine, sine], axis=1)
    return cosine.astype(np.float32), sine.astype(np.float32)


def turn(field, cosine, sine):
    lane = lax.broadcasted_iota(jnp.int32, field.shape, 1)
    other = jnp.where(
        lax.rem(lane, HD) < HD // 2,
        pltpu.roll(field, LANES - HD // 2, 1),
        pltpu.roll(field, HD // 2, 1),
    )
    return field * cosine + other * sine


def pick(hot, values):
    return jnp.sum(jnp.where(hot, values, 0.0), axis=-1, keepdims=True)


def lane_ids(rows):
    return lax.broadcasted_iota(jnp.int32, (rows, LANES), 1)


def soft_pair(first, second):
    high = jnp.maximum(first, second)
    e0, e1 = jnp.exp(first - high), jnp.exp(second - high)
    return e0 / (e0 + e1), e1 / (e0 + e1)


def half_mask(rows):
    return lax.broadcasted_iota(jnp.int32, (rows, LANES), 1) < HD


def swap_halves(value):
    return pltpu.roll(value, HD, 1)


def front_kernel(
    n,
    half,
    padded,
    gathered,
    tokens_ref,
    cotangent_ref,
    prev_all_ref,
    routes_all_ref,
    packed_ref,
    cos_ref,
    sin_ref,
    win_ref,
    wdown_ref,
    a_ref,
    q_ref,
    k_ref,
    v_ref,
    o_ref,
    lse_ref,
    h_ref,
    ub_ref,
    stat_ref,
    pos_ref,
    wo_ref,
    small_ref,
    extra_ref,
    spread_ref,
    arrived_ref,
    gate_arrived_ref,
    dy_arrived_ref,
    in_c_ref,
    in_x_ref,
    in_d_ref,
    down_c_ref,
    down_x_ref,
    down_d_ref,
    x_ref,
    dy_ref,
    prev_ref,
    routes_ref,
    place_ref,
    gates_ref,
    slot_ref,
    gate_ref,
    dy_slot_ref,
    load,
    pack_send,
    pack_recv,
    dy_send,
    dy_recv,
    slot_send,
    slot_recv,
    gate_send,
    gate_recv,
    stay,
    core_send,
    core_recv,
    w_send,
    w_recv,
):
    rows_all, width = x_ref.shape
    blocks = rows_all // BLK
    pairs = q_ref.shape[0]
    local = pairs * LANES
    columns = prev_ref.shape[1]
    d, t = lax.axis_index("dp"), lax.axis_index("tensor")
    m, c = lax.div(t, 2), lax.rem(t, 2)
    partner = (d, t + 1 - 2 * c)
    across = (d, lax.rem(t + 2, 4))
    loads = [
        pltpu.make_async_copy(src.at[m], dst, load.at[i])
        for i, (src, dst) in enumerate(
            [
                (routes_all_ref, routes_ref),
                (cotangent_ref, dy_ref),
                (tokens_ref, x_ref),
                (prev_all_ref, prev_ref),
            ]
        )
    ]
    for copy in loads:
        copy.start()
    peers = all_peers(n, d, t)
    greet(peers + [partner])
    pack_copies = []
    if gathered:
        spread_ref[...] = packed_ref[...]
    else:
        part = packed_ref.shape[0]
        place = pl.ds(pl.multiple_of(d * part, part), part)
        spread_ref[m, place, :] = packed_ref[...]
        for i, peer in enumerate(peers):
            pack_copies.append(
                remote(
                    packed_ref,
                    spread_ref.at[m, place, :],
                    pack_send.at[i],
                    pack_recv.at[i],
                    peer,
                )
            )
        for copy in pack_copies:
            copy.start()

    loads[0].wait()
    line = lax.broadcasted_iota(jnp.int32, (rows_all, LANES), 1)
    named = jnp.where(
        line == 0,
        routes_ref[:, 0:1].astype(F32),
        jnp.where(line == 1, routes_ref[:, 1:2].astype(F32), 0.0),
    )
    named = jnp.transpose(named)
    ids = lax.broadcasted_iota(jnp.int32, (LANES, rows_all), 0).astype(F32)
    hit = ((ids == named[0:1, :]) | (ids == named[1:2, :])) & (ids < float(n))
    before = lax.broadcasted_iota(jnp.int32, (rows_all, rows_all), 0) < lax.broadcasted_iota(
        jnp.int32, (rows_all, rows_all), 1
    )
    count = mm(hit.astype(F32).astype(BF16), before.astype(F32).astype(BF16))
    places = jnp.where(hit, count, -1.0)
    place_ref[...] = places
    pos_ref[...] = jnp.transpose(places)
    base = c * half

    def dy_copy(j):
        e = lax.rem(d + j, n)
        return remote(
            dy_slot_ref.at[e], dy_arrived_ref.at[d], dy_send.at[j], dy_recv.at[j], (e, t)
        )

    def slot_copy(j):
        e = lax.rem(d + j, n)
        return remote(
            slot_ref.at[e], arrived_ref.at[d], slot_send.at[j], slot_recv.at[j], (e, t)
        )

    def gate_copy(j):
        e = lax.rem(d + j, n)
        return remote(
            gate_ref.at[e], gate_arrived_ref.at[d], gate_send.at[j], gate_recv.at[j], (e, t)
        )

    stays = [
        pltpu.make_async_copy(src.at[d], dst.at[d], stay.at[i])
        for i, (src, dst) in enumerate(
            [
                (dy_slot_ref, dy_arrived_ref),
                (slot_ref, arrived_ref),
                (gate_ref, gate_arrived_ref),
            ]
        )
    ]
    loads[1].wait()

    def dy_step(i, carry):
        j = lax.rem(i + 1, n)
        e = lax.rem(d + j, n)
        hot = slot_hot(half, padded, base, place_ref[pl.ds(e, 1), :])
        dy_slot_ref[e] = mm(hot, dy_ref[...]).astype(BF16)

        @pl.when(i < n - 1)
        def _():
            dy_copy(j).start()

        return carry

    lax.fori_loop(0, n, dy_step, 0)
    stays[0].start()

    for copy in pack_copies:
        copy.wait_recv()
    weight_copies = [
        remote(win_ref, in_x_ref, w_send.at[0], w_recv.at[0], across),
        remote(wdown_ref, down_x_ref, w_send.at[1], w_recv.at[1], across),
        remote(win_ref, in_c_ref, w_send.at[2], w_recv.at[2], partner),
        remote(wdown_ref, down_c_ref, w_send.at[3], w_recv.at[3], partner),
        remote(in_x_ref, in_d_ref, w_send.at[4], w_recv.at[4], partner),
        remote(down_x_ref, down_d_ref, w_send.at[5], w_recv.at[5], partner),
    ]
    for copy in weight_copies[0:4]:
        copy.start()

    table = spread_ref[0, :, 6 * LANES : 7 * LANES]
    extra_ref[...] = jnp.transpose(table.astype(F32))
    keep = lax.broadcasted_iota(jnp.int32, (width, LANES), 1) < columns + 4
    small_ref[...] = jnp.where(keep, table, jnp.zeros_like(table))
    mask = half_mask(width)
    own = pl.multiple_of(c * local, LANES)
    wo_ref[:, pl.ds(own, LANES)] = spread_ref[0, :, 3 * LANES : 4 * LANES]
    wo_ref[:, pl.ds(own + LANES, LANES)] = spread_ref[1, :, 3 * LANES : 4 * LANES]
    wo_ref[:, pl.ds(own + 2 * LANES, LANES)] = jnp.where(
        mask,
        swap_halves(spread_ref[0, :, 5 * LANES : 6 * LANES].astype(F32)),
        spread_ref[1, :, 5 * LANES : 6 * LANES].astype(F32),
    ).astype(BF16)
    own_lanes = pl.ds(own, local)
    wo_copy = remote(
        wo_ref.at[:, own_lanes],
        wo_ref.at[:, own_lanes],
        core_send.at[pairs],
        core_recv.at[pairs],
        partner,
    )
    wo_copy.start()

    loads[2].wait()
    gain = extra_ref[columns + 4 : columns + 5, :]
    head = half_mask(BLK)

    def project(i, carry):
        rows = pl.ds(pl.multiple_of(i * BLK, BLK), BLK)
        x = x_ref[rows, :].astype(F32)
        r = lax.rsqrt(jnp.mean(x * x, axis=-1, keepdims=True) + EPSILON)
        a = (x * r * gain).astype(BF16)
        a_ref[rows, :] = a
        cosine, sine = cos_ref[rows, :], sin_ref[rows, :]

        def put(pair, q, k, v):
            q_ref[pair, rows, :] = turn(q, cosine, sine).astype(BF16) * BF16(HD**-0.5)
            k_ref[pair, rows, :] = turn(k, cosine, sine).astype(BF16)
            v_ref[pair, rows, :] = v.astype(BF16)

        odd = []
        for s in range(2):
            both = mm(a, spread_ref[s, :, 0 : 3 * LANES])
            put(s, *(both[:, j * LANES : (j + 1) * LANES] for j in range(3)))
            both = mm(a, spread_ref[s, :, 4 * LANES : 6 * LANES])
            odd.append((both[:, :LANES], both[:, LANES:]))
        put(
            2,
            jnp.where(head, odd[0][0], swap_halves(odd[1][0])),
            jnp.where(head, swap_halves(odd[0][0]), odd[1][0]),
            jnp.where(head, odd[0][1], swap_halves(odd[1][1])),
        )
        return carry

    lax.fori_loop(0, blocks, project, 0)

    def o_copy(p):
        lanes = pl.ds(pl.multiple_of(own + p * LANES, LANES), LANES)
        return remote(
            o_ref.at[:, lanes], o_ref.at[:, lanes], core_send.at[p], core_recv.at[p], partner
        )

    def attend(p, carry):
        lanes = pl.ds(pl.multiple_of(own + p * LANES, LANES), LANES)
        for i in range(blocks):
            rows = pl.ds(i * BLK, BLK)
            seen = pl.ds(0, (i + 1) * BLK)
            q, k, v = q_ref[p, rows, :], k_ref[p, seen, :], v_ref[p, seen, :]
            halves = []
            for side in range(2):
                chosen = head if side == 0 else jnp.logical_not(head)
                s = mm_nt(jnp.where(chosen, q, jnp.zeros_like(q)), k)
                high = jnp.max(s, axis=-1, keepdims=True)
                e = jnp.exp(s - high)
                total = jnp.sum(e, axis=-1, keepdims=True)
                halves.append(mm((e / total).astype(BF16), v))
                log_total = jnp.broadcast_to(high + jnp.log(total), (BLK, LANES))
                lse_ref[2 * p + side, :, rows] = jnp.transpose(log_total)[0:8, :]
            o_ref[rows, lanes] = jnp.where(head, halves[0], halves[1]).astype(BF16)
        o_copy(p).start()
        return carry

    lax.fori_loop(0, pairs, attend, 0)
    loads[3].wait()
    wo_copy.wait()
    for p in range(pairs):
        o_copy(p).wait()

    gain_moe = extra_ref[columns + 5 : columns + 6, :]

    def middle(i, carry):
        rows = pl.ds(pl.multiple_of(i * BLK, BLK), BLK)
        z = mm_nt(o_ref[rows, :], wo_ref[...])
        h = x_ref[rows, :].astype(F32) + z
        r = lax.rsqrt(jnp.mean(h * h, axis=-1, keepdims=True) + EPSILON)
        ub = (h * r * gain_moe).astype(BF16)
        h_ref[rows, :] = h
        ub_ref[rows, :] = ub
        scores = mm(ub, small_ref[...])
        lane = lane_ids(BLK)
        e0, e1 = routes_ref[rows, 0:1], routes_ref[rows, 1:2]
        hot0, hot1 = lane == e0, lane == e1
        prev = prev_ref[rows, :]
        few = lax.broadcasted_iota(jnp.int32, (BLK, columns), 1)
        g0, g1 = soft_pair(
            pick(hot0, scores) + pick(few == e0, prev), pick(hot1, scores) + pick(few == e1, prev)
        )
        mix = [pick(lane == columns + j, scores) for j in range(4)]
        a00, a01 = soft_pair(mix[0], mix[1])
        a10, a11 = soft_pair(mix[2], mix[3])
        table = jnp.zeros((BLK, LANES), F32)
        for j, value in enumerate([g0, g1, a00, a01, a10, a11, r]):
            table = jnp.where(lane == j, value, table)
        stat_ref[rows, :] = table
        gates = jnp.where(hot0, g0, 0.0) + jnp.where(hot1, g1, 0.0)
        gates_ref[:, rows] = jnp.transpose(gates)
        return carry

    lax.fori_loop(0, blocks, middle, 0)
    piece = lax.broadcasted_iota(jnp.int32, (8, rows_all), 0)

    def slot_step(i, carry):
        j = lax.rem(i + 1, n)
        e = lax.rem(d + j, n)
        hot = slot_hot(half, padded, base, place_ref[pl.ds(e, 1), :])
        slot_ref[e] = mm(hot, ub_ref[...]).astype(BF16)
        gate = gates_ref[pl.ds(e, 1), :]
        high = gate.astype(BF16).astype(F32)
        mid = (gate - high).astype(BF16).astype(F32)
        low = gate - high - mid
        lines = jnp.where(piece == 0, high, jnp.where(piece == 1, mid, low))
        lines = jnp.where(piece < 3, lines, 0.0).astype(BF16)
        gate = jnp.sum(mm_nt(lines, hot), axis=0, keepdims=True)
        gate_ref[e] = jnp.broadcast_to(gate, (8, padded))

        @pl.when(i < n - 1)
        def _():
            slot_copy(j).start()
            gate_copy(j).start()

        return carry

    lax.fori_loop(0, n, slot_step, 0)
    stays[1].start()
    stays[2].start()
    weight_copies[0].wait_recv()
    weight_copies[1].wait_recv()
    weight_copies[4].start()
    weight_copies[5].start()

    def finish(j, carry):
        for copy in (dy_copy(j), slot_copy(j), gate_copy(j)):
            copy.wait()
        return carry

    lax.fori_loop(1, n, finish, 0)
    for copy in stays:
        copy.wait()
    for copy in pack_copies + weight_copies[0:2]:
        copy.wait_send()
    for copy in weight_copies[2:6]:
        copy.wait()


def expert_kernel(
    sources,
    padded,
    x_ref,
    dy_ref,
    gate_ref,
    *refs,
):
    weights, outs = refs[:8], refs[8:19]
    in_refs, down_refs = weights[0:4], weights[4:8]
    gy_ref, dx_ref, dg_ref = outs[0:3]
    gin_refs, gdown_refs = outs[3:7], outs[7:11]
    xt_ref, scaled_ref, scale_ref, y_acc, dx_acc, win_ref, wdown_ref = refs[19:]
    step = pl.program_id(0)
    last = pl.num_programs(0) - 1

    @pl.when(step == 0)
    def _():
        xt_ref[...] = jnp.transpose(x_ref[...])
        for s in range(sources):
            rows = pl.ds(s * padded, padded)
            line = jnp.broadcast_to(gate_ref[s, 0:1, :], (LANES, padded))
            scale = jnp.transpose(line)
            scale_ref[rows, :] = scale
            scaled_ref[rows, :] = (dy_ref[rows, :].astype(F32) * scale[:, 0:1]).astype(BF16)
        y_acc[...] = jnp.zeros_like(y_acc)
        dx_acc[...] = jnp.zeros_like(dx_acc)

    per = pl.num_programs(0) // 4
    for i in range(4):

        @pl.when(lax.div(step, per) == i)
        def _():
            win_ref[...] = in_refs[i][0]
            wdown_ref[...] = down_refs[i][0]

    x = x_ref[...]
    gate = mm(x, win_ref[0])
    up = mm(x, win_ref[1])
    sigma = 1.0 / (1.0 + jnp.exp(-gate))
    active = gate * sigma
    hidden = (active * up).astype(BF16)
    y_acc[...] += mm(hidden, wdown_ref[...])
    scaled = scaled_ref[...]
    grad_hidden = mm_nt(scaled, wdown_ref[...])
    grad_gate = (grad_hidden * up * (sigma * (1.0 + gate * (1.0 - sigma)))).astype(BF16)
    grad_up = (grad_hidden * active).astype(BF16)
    dx_acc[...] += mm_nt(grad_gate, win_ref[0]) + mm_nt(grad_up, win_ref[1])
    xt = xt_ref[...]
    part_gate = mm(xt, grad_gate).astype(BF16)
    part_up = mm(xt, grad_up).astype(BF16)
    part_down = mm_tn(hidden, scaled).astype(BF16)
    for i in range(4):

        @pl.when(lax.div(step, per) == i)
        def _():
            gin_refs[i][0, 0] = part_gate
            gin_refs[i][0, 1] = part_up
            gdown_refs[i][0] = part_down

    @pl.when(step == last)
    def _():
        for s in range(sources):
            rows = pl.ds(s * padded, padded)
            y = y_acc[rows, :]
            gy_ref[s] = (y * scale_ref[rows, 0:1]).astype(BF16)
            dot = jnp.sum(y * dy_ref[rows, :].astype(F32), axis=-1, keepdims=True)
            dg_ref[s] = jnp.transpose(jnp.broadcast_to(dot, (padded, LANES)))[0:8, :]
            dx_ref[s] = dx_acc[rows, :].astype(BF16)


def rear_kernel(
    n,
    half,
    padded,
    gathered,
    part,
    gy_src_ref,
    dx_src_ref,
    dg_src_ref,
    tokens_ref,
    cotangent_ref,
    routes_all_ref,
    o_all_ref,
    h_ref,
    ub_ref,
    stat_ref,
    pos_ref,
    small_ref,
    extra_ref,
    wo_ref,
    q_ref,
    k_ref,
    v_ref,
    a_ref,
    lse_ref,
    spread_ref,
    cos_ref,
    sin_ref,
    result_ref,
    grad_x_ref,
    logit_ref,
    grads_ref,
    lines_ref,
    x_ref,
    dy_ref,
    routes_ref,
    o_ref,
    dx_ref,
    gy_ref,
    dg_ref,
    dh_ref,
    dzb_ref,
    do_ref,
    low_ref,
    row_ref,
    dp_ref,
    dk_acc,
    dv_acc,
    wo_odd_ref,
    pack_ref,
    line_ref,
    pack_in_ref,
    line_in_ref,
    cross_ref,
    cross_in_ref,
    cross_line_ref,
    da_out_ref,
    da_in_ref,
    da_own_ref,
    norm_ref,
    norm_in_ref,
    half_ref,
    load,
    dx_send,
    dx_recv,
    gy_send,
    gy_recv,
    dg_send,
    dg_recv,
    stay,
    pass_send,
    pass_recv,
    grad_send,
    grad_recv,
    pair_send,
    pair_recv,
    out_send,
    out_recv,
):
    rows_all, width = dy_ref.shape
    blocks = rows_all // BLK
    pairs = q_ref.shape[0]
    local = pairs * LANES
    columns = n + 4
    slots = n * padded
    d, t = lax.axis_index("dp"), lax.axis_index("tensor")
    m, c = lax.div(t, 2), lax.rem(t, 2)
    partner = (d, t + 1 - 2 * c)
    across = (d, lax.rem(t + 2, 4))
    rows_half = rows_all // 2
    own = pl.multiple_of(c * local, LANES)
    own_lanes = pl.ds(own, local)
    place = pl.ds(pl.multiple_of(c * rows_half, BLK), rows_half)
    loads = [
        pltpu.make_async_copy(src, dst, load.at[i])
        for i, (src, dst) in enumerate(
            [
                (routes_all_ref.at[m], routes_ref),
                (cotangent_ref.at[m], dy_ref),
                (tokens_ref.at[m, place], x_ref),
                (o_all_ref.at[:, own_lanes], o_ref),
            ]
        )
    ]
    for copy in loads:
        copy.start()
    greet(plane_peers(n, d, t) + [partner, across])

    kinds = [
        (dx_src_ref, dx_ref, dx_send, dx_recv),
        (dg_src_ref, dg_ref, dg_send, dg_recv),
        (gy_src_ref, gy_ref, gy_send, gy_recv),
    ]

    def give(kind, j):
        src, dst, send, recv = kinds[kind]
        s = lax.rem(d + j, n)
        return remote(src.at[s], dst.at[c, d], send.at[j], recv.at[j], (s, t))

    def hand(kind, j):
        dst = kinds[kind][1]
        s = lax.rem(d + n - j, n)
        block = dst.at[c, s]
        return remote(block, block, pass_send.at[kind, j], pass_recv.at[kind, j], partner)

    def keep(kind):
        src, dst = kinds[kind][0:2]
        return pltpu.make_async_copy(src.at[d], dst.at[c, d], stay.at[kind])

    def begin(*chosen):
        for kind in chosen:
            keep(kind).start()

        def step(j, carry):
            for kind in chosen:
                give(kind, j).start()
            return carry

        lax.fori_loop(1, n, step, 0)

    def collect(*chosen):
        for kind in chosen:
            keep(kind).wait()
            hand(kind, 0).start()

        def step(j, carry):
            for kind in chosen:
                give(kind, j).wait_recv()
                hand(kind, j).start()
            return carry

        lax.fori_loop(1, n, step, 0)

    def settle(*chosen):
        def step(j, carry):
            for kind in chosen:
                hand(kind, j).wait_recv()
            return carry

        lax.fori_loop(0, n, step, 0)

    begin(0, 1)
    row_ref[...] = jnp.zeros_like(row_ref)
    for copy in loads:
        copy.wait()
    collect(0, 1)
    begin(2)
    settle(0, 1)

    gain_moe = extra_ref[columns + 5 : columns + 6, :]
    vec0 = extra_ref[columns + 6 : columns + 7, :]
    vec1 = extra_ref[columns + 7 : columns + 8, :]
    group = max(1, min(n, (1024 if slots <= 1024 else 512) // padded))
    span = group * padded

    def combine(wheres, ref, lines=None):
        total = jnp.zeros((BLK, width), F32)
        entries = [jnp.zeros((BLK, 1), F32) for _ in wheres]
        slot = lax.broadcasted_iota(jnp.int32, (BLK, span), 1)
        for side in range(2):
            for first in range(0, n, group):
                start = side * slots + first * padded
                hots = [slot == where - start for where in wheres]
                hot = jnp.where(hots[0] | hots[1], 1.0, 0.0).astype(BF16)
                block = ref[side, first : first + group].reshape(span, width)
                total = total + mm(hot, block)
                if lines is not None:
                    line = jnp.concatenate(
                        [lines[side, first + e, 0:1, :] for e in range(group)], axis=1
                    )
                    entries = [
                        entry + jnp.sum(jnp.where(one, line, 0.0), axis=-1, keepdims=True)
                        for entry, one in zip(entries, hots)
                    ]
        return total, entries

    def facts(rows):
        lane = lane_ids(BLK)
        stats = stat_ref[rows, :]
        values = [stats[:, j : j + 1] for j in range(7)]
        e0, e1 = routes_ref[rows, 0:1], routes_ref[rows, 1:2]
        wheres = []
        places = pos_ref[rows, :]
        for e in (e0, e1):
            place = pick(lane == e, places).astype(jnp.int32)
            side = (place >= half).astype(jnp.int32)
            where = side * (slots - half) + e * padded + place
            wheres.append(jnp.where(e < n, where, -1))
        g0, g1 = values[0:2]

        def named(number):
            return jnp.where(e0 == number, g0, 0.0) + jnp.where(e1 == number, g1, 0.0)

        copied, first, second = named(n + 1), named(n + 2), named(n + 3)
        on_u = copied + first * values[2] + second * values[4]
        return values, e0, e1, wheres, first, second, on_u

    def back(i, carry):
        rows = pl.ds(pl.multiple_of(i * BLK, BLK), BLK)
        values, e0, e1, wheres, first, second, on_u = facts(rows)
        g0, g1, a00, a01, a10, a11, r = values
        lane = lane_ids(BLK)
        grads, (f0, f1) = combine(wheres, dx_ref, dg_ref)
        h = h_ref[rows, :]
        normed = h * r
        u = normed * gain_moe
        dy = dy_ref[rows, :].astype(F32)
        s_u = jnp.sum(dy * u, axis=-1, keepdims=True)
        s_0 = jnp.sum(dy * vec0, axis=-1, keepdims=True)
        s_1 = jnp.sum(dy * vec1, axis=-1, keepdims=True)

        def other(e):
            value = jnp.where(e == n + 1, s_u, 0.0)
            value = jnp.where(e == n + 2, a00 * s_u + a01 * s_0, value)
            return jnp.where(e == n + 3, a10 * s_u + a11 * s_1, value)

        dg0, dg1 = f0 + other(e0), f1 + other(e1)
        mean = g0 * dg0 + g1 * dg1
        dl = jnp.where(lane == e0, g0 * (dg0 - mean), 0.0) + jnp.where(
            lane == e1, g1 * (dg1 - mean), 0.0
        )
        turned = jnp.transpose(dl)
        logit_ref[m, :, rows] = turned[0 : logit_ref.shape[1], :]
        d00, d01 = first * s_u, first * s_0
        d10, d11 = second * s_u, second * s_1
        m0 = a00 * d00 + a01 * d01
        m1 = a10 * d10 + a11 * d11
        low = dl
        for j, value in enumerate(
            [a00 * (d00 - m0), a01 * (d01 - m0), a10 * (d10 - m1), a11 * (d11 - m1)]
        ):
            low = jnp.where(lane == columns + j, value, low)
        low = low.astype(BF16)
        low_ref[rows, :] = low
        du = grads + mm_nt(low, small_ref[...]) + on_u * dy
        row_ref[0:1, :] += jnp.sum(du * normed, axis=0, keepdims=True)
        row_ref[1:2, :] += jnp.sum((first * a01) * dy, axis=0, keepdims=True)
        row_ref[2:3, :] += jnp.sum((second * a11) * dy, axis=0, keepdims=True)
        dn = du * gain_moe
        dh = dy + r * (dn - normed * jnp.mean(dn * normed, axis=-1, keepdims=True))

        @pl.when(lax.div(i, blocks // 2) == c)
        def _():
            near = pl.multiple_of(i * BLK - c * rows_half, BLK)
            dh_ref[pl.ds(near, BLK), :] = dh

        dzb = dh.astype(BF16)
        dzb_ref[rows, :] = dzb
        do_ref[rows, :] = mm(dzb, wo_ref[:, own_lanes]).astype(BF16)
        return carry

    lax.fori_loop(0, blocks, back, 0)
    logit_copy = remote(
        logit_ref.at[m], logit_ref.at[m], pair_send.at[0], pair_recv.at[0], across
    )
    logit_copy.start()
    collect(2)

    grad_wo = mm_tn(dzb_ref[...], o_ref[...])
    pack_ref[0, :, 3 * LANES : 4 * LANES] = grad_wo[:, 0:LANES].astype(BF16)
    pack_ref[1, :, 3 * LANES : 4 * LANES] = grad_wo[:, LANES : 2 * LANES].astype(BF16)
    wo_odd_ref[...] = grad_wo[:, 2 * LANES : 3 * LANES]
    line_ref[...] = mm_tn(ub_ref[...], low_ref[...])

    def spread_rows(s, d_to):
        place = pl.ds(pl.multiple_of(d_to * part, part), part)
        return place

    def grad_copy(s, stage, j):
        e = lax.rem(d + j, n)
        lanes = pl.ds(0, 4 * LANES) if stage == 0 else pl.ds(4 * LANES, 2 * LANES)
        return remote(
            pack_ref.at[s, spread_rows(s, e), lanes],
            pack_in_ref.at[s, d, :, lanes],
            grad_send.at[stage, s, j],
            grad_recv.at[stage, s, j],
            (e, t),
        )

    def line_copy(j):
        e = lax.rem(d + j, n)
        return remote(
            line_ref.at[spread_rows(0, e), :],
            line_in_ref.at[d],
            grad_send.at[2, 0, j],
            grad_recv.at[2, 0, j],
            (e, t),
        )

    head = half_mask(BLK)

    def attend_back(p):
        dk_acc[...] = jnp.zeros_like(dk_acc)
        dv_acc[...] = jnp.zeros_like(dv_acc)
        dq = []
        for i in range(blocks):
            rows = pl.ds(i * BLK, BLK)
            seen = pl.ds(0, (i + 1) * BLK)
            lanes = pl.ds(pl.multiple_of(p * LANES, LANES), LANES)
            q, do = q_ref[p, rows, :], do_ref[rows, lanes]
            k, v = k_ref[p, seen, :], v_ref[p, seen, :]
            zero = jnp.zeros_like(q)
            parts = []
            dk, dv = dk_acc[seen, :], dv_acc[seen, :]
            for side in range(2):
                chosen = head if side == 0 else jnp.logical_not(head)
                qm, dom = jnp.where(chosen, q, zero), jnp.where(chosen, do, zero)
                prob = jnp.exp(mm_nt(k, qm) - lse_ref[2 * p + side, 0:1, rows])
                grad_prob = mm_nt(v, dom)
                total = jnp.sum(prob * grad_prob, axis=0, keepdims=True)
                grad_score = (prob * (grad_prob - total)).astype(BF16)
                dv = dv + mm(prob.astype(BF16), dom)
                dk = dk + mm(grad_score, qm)
                parts.append(mm_tn(grad_score, k))
            dk_acc[seen, :] = dk
            dv_acc[seen, :] = dv
            value = jnp.where(head, parts[0], parts[1]) * (HD**-0.5)
            dq.append(turn(value, cos_ref[rows, :], -sin_ref[rows, :]))
        return (
            jnp.concatenate(dq, axis=0),
            turn(dk_acc[...], cos_ref[...], -sin_ref[...]),
            dv_acc[...],
        )

    def shard_step(i, carry):
        s = lax.rem(m + 1 + i, 2)
        for j, value in enumerate(attend_back(s)):
            dp_ref[s, :, j * LANES : (j + 1) * LANES] = value.astype(BF16)
        for j in range(3):
            lanes = pl.ds(j * LANES, LANES)
            pack_ref[s, :, lanes] = mm_tn(a_ref[...], dp_ref[s, :, lanes]).astype(BF16)
        if not gathered:

            def send(j, carry):
                grad_copy(s, 0, j).start()
                return carry

            lax.fori_loop(1, n, send, 0)
        return carry

    lax.fori_loop(0, 2, shard_step, 0)
    dq, dk, dv = attend_back(2)
    wide = half_mask(rows_all)
    odd = [
        (jnp.where(wide, dq, swap_halves(dk)), jnp.where(wide, dv, 0.0)),
        (jnp.where(wide, swap_halves(dq), dk), jnp.where(wide, swap_halves(dv), 0.0)),
    ]
    tall = half_mask(width)
    for s in range(2):
        for j in range(2):
            dp_ref[s, :, (3 + j) * LANES : (4 + j) * LANES] = odd[s][j].astype(BF16)
    for s in range(2):
        pack_ref[s, :, 4 * LANES : 5 * LANES] = mm_tn(
            a_ref[...], dp_ref[s, :, 3 * LANES : 4 * LANES]
        ).astype(BF16)
        last = mm_tn(a_ref[...], dp_ref[s, :, 4 * LANES : 5 * LANES])
        side = wo_odd_ref[...]
        side = swap_halves(side) if s == 0 else side
        pack_ref[s, :, 5 * LANES : 6 * LANES] = jnp.where(tall, last, side).astype(BF16)
    if not gathered:
        for s in range(2):

            def send(j, carry, s=s):
                grad_copy(s, 1, j).start()
                return carry

            lax.fori_loop(1, n, send, 0)

    def da_rows(start):
        rows = pl.ds(pl.multiple_of(start, BLK), BLK)
        total = jnp.zeros((BLK, width), F32)
        for s in range(2):
            total = total + mm_nt(dp_ref[s, rows, 0 : 3 * LANES], spread_ref[s, :, 0 : 3 * LANES])
            total = total + mm_nt(
                dp_ref[s, rows, 3 * LANES : 5 * LANES], spread_ref[s, :, 4 * LANES : 6 * LANES]
            )
        return total

    def da_other(i, carry):
        rows = pl.ds(pl.multiple_of(i * BLK, BLK), BLK)
        da_out_ref[rows, :] = da_rows((1 - c) * rows_half + i * BLK).astype(BF16)
        return carry

    lax.fori_loop(0, rows_half // BLK, da_other, 0)
    da_copy = remote(da_out_ref, da_in_ref, pair_send.at[1], pair_recv.at[1], partner)
    da_copy.start()

    def da_own(i, carry):
        rows = pl.ds(pl.multiple_of(i * BLK, BLK), BLK)
        da_own_ref[rows, :] = da_rows(c * rows_half + i * BLK)
        return carry

    lax.fori_loop(0, rows_half // BLK, da_own, 0)
    da_copy.wait()
    gain_attn = extra_ref[columns + 4 : columns + 5, :]
    norm_ref[...] = jnp.zeros_like(norm_ref)

    def finish(i, carry):
        rows = pl.ds(pl.multiple_of(i * BLK, BLK), BLK)
        x = x_ref[rows, :].astype(F32)
        r = lax.rsqrt(jnp.mean(x * x, axis=-1, keepdims=True) + EPSILON)
        normed = x * r
        da = da_own_ref[rows, :] + da_in_ref[rows, :].astype(F32)
        norm_ref[0:1, :] += jnp.sum(da * normed, axis=0, keepdims=True)
        dn = da * gain_attn
        grad = dh_ref[rows, :] + r * (dn - normed * jnp.mean(dn * normed, axis=-1, keepdims=True))
        half_ref[0, rows, :] = grad.astype(BF16)
        return carry

    lax.fori_loop(0, rows_half // BLK, finish, 0)
    norm_copy = remote(norm_ref, norm_in_ref, pair_send.at[2], pair_recv.at[2], partner)
    norm_copy.start()

    def publish(kind, out_ref):
        block = out_ref.at[m, place]
        copies = [
            remote(half_ref.at[kind], block, out_send.at[kind, 0], out_recv.at[kind, 0], across),
            remote(half_ref.at[kind], block, out_send.at[kind, 1], out_recv.at[kind, 1], partner),
            pltpu.make_async_copy(half_ref.at[kind], block, stay.at[3 + kind]),
        ]
        for copy in copies:
            copy.start()
        block = out_ref.at[1 - m, place]
        relay = remote(block, block, out_send.at[kind, 2], out_recv.at[kind, 2], partner)
        return copies, relay

    grad_x_copies, grad_x_relay = publish(0, grad_x_ref)

    settle(2)

    def results(i, carry):
        rows = pl.ds(pl.multiple_of(i * BLK, BLK), BLK)
        far = pl.ds(pl.multiple_of(c * rows_half + i * BLK, BLK), BLK)
        values, e0, e1, wheres, first, second, on_u = facts(far)
        sums, _ = combine(wheres, gy_ref)
        h = h_ref[far, :]
        u = h * values[6] * gain_moe
        result = h + (sums + on_u * u + (first * values[3]) * vec0 + (second * values[5]) * vec1)
        half_ref[1, rows, :] = result.astype(BF16)
        return carry

    lax.fori_loop(0, rows_half // BLK, results, 0)
    result_copies, result_relay = publish(1, result_ref)

    norm_copy.wait()
    row_ref[3:4, :] = norm_ref[0:1, :] + norm_in_ref[0:1, :]
    turned = jnp.concatenate([row_ref[...], jnp.zeros((LANES - 8, width), F32)], axis=0)
    turned = jnp.transpose(turned)
    lane = lax.broadcasted_iota(jnp.int32, (width, LANES), 1)
    lines = line_ref[...]
    for j, source in enumerate([3, 0, 1, 2]):
        lines = jnp.where(lane == columns + 4 + j, turned[:, source : source + 1], lines)
    line_ref[...] = lines
    if gathered:
        stores = [
            pltpu.make_async_copy(pack_ref, grads_ref, load.at[0]),
            pltpu.make_async_copy(line_ref, lines_ref, load.at[1]),
        ]
        for copy in stores:
            copy.start()
        for copy in stores:
            copy.wait()
    else:

        def send(j, carry):
            line_copy(j).start()
            return carry

        lax.fori_loop(1, n, send, 0)
        mine = pl.ds(pl.multiple_of(d * part, part), part)
        for s in range(2):
            pack_in_ref[s, d] = pack_ref[s, mine, :]
        line_in_ref[d] = line_ref[mine, :]

        def arrive(j, carry):
            for s in range(2):
                for stage in range(2):
                    grad_copy(s, stage, j).wait_recv()
            return carry

        lax.fori_loop(1, n, arrive, 0)

        def total(s):
            value = pack_in_ref[s, 0].astype(F32)
            for e in range(1, n):
                value = value + pack_in_ref[s, e].astype(F32)
            return value

        cross_ref[...] = total(1 - m).astype(BF16)
        cross_copy = remote(cross_ref, cross_in_ref, pair_send.at[3], pair_recv.at[3], across)
        cross_copy.start()
        grads_ref[...] = total(m)

        def arrive_lines(j, carry):
            line_copy(j).wait()
            return carry

        lax.fori_loop(1, n, arrive_lines, 0)
        value = line_in_ref[0]
        for e in range(1, n):
            value = value + line_in_ref[e]
        cross_line_ref[0] = value
        cross_line_copy = remote(
            cross_line_ref.at[0], cross_line_ref.at[1], pair_send.at[4], pair_recv.at[4], across
        )
        cross_line_copy.start()
        cross_copy.wait()
        grads_ref[...] += cross_in_ref[...].astype(F32)
        cross_line_copy.wait()
        lines_ref[...] = cross_line_ref[0] + cross_line_ref[1]

        def sent(j, carry):
            for s in range(2):
                for stage in range(2):
                    grad_copy(s, stage, j).wait_send()
            return carry

        lax.fori_loop(1, n, sent, 0)

    for copies, relay in ((grad_x_copies, grad_x_relay), (result_copies, result_relay)):
        copies[0].wait_recv()
        relay.start()
    for copies, relay in ((grad_x_copies, grad_x_relay), (result_copies, result_relay)):
        copies[0].wait_send()
        copies[1].wait()
        copies[2].wait()
        relay.wait()
    logit_copy.wait()

    def clear(j, carry):
        for kind in range(3):
            give(kind, j).wait_send()
        return carry

    lax.fori_loop(1, n, clear, 0)

    def passed(j, carry):
        for kind in range(3):
            hand(kind, j).wait_send()
        return carry

    lax.fori_loop(0, n, passed, 0)


def across_chips(value):
    return lax.ppermute(value, "tensor", [(0, 2), (2, 0), (1, 3), (3, 1)])


def across_cores(value):
    return lax.ppermute(value, "tensor", [(0, 1), (1, 0), (2, 3), (3, 2)])


def body(
    tokens,
    cotangent,
    prev_logits,
    routes,
    norm_attn,
    norm_moe,
    w_qkv,
    w_out,
    w_router,
    w_const,
    const_vec,
    w_in,
    w_down,
):
    rows, width = tokens.shape[1:]
    n = lax.axis_size("dp")
    experts = n
    columns = prev_logits.shape[2]
    capacity = 4 * max(1, 3 * rows // (4 * (experts + 4)))
    half = capacity // 2
    padded = -(-half // 16) * 16
    share = w_qkv.shape[2]
    local = 2 * share
    part = w_qkv.shape[1]
    t = lax.axis_index("tensor")
    m, c = t // 2, t % 2

    def mine(value):
        return lax.dynamic_index_in_dim(value, m, 0, keepdims=False)

    x, dy, choose = mine(tokens), mine(cotangent), mine(routes)
    cosine, sine = (jnp.asarray(v) for v in rope_constants())
    pairs = local // LANES

    wo_rows = w_out.T
    packed = jnp.concatenate(
        [w_qkv[i, :, :LANES] for i in range(3)]
        + [wo_rows[:, :LANES]]
        + [w_qkv[i, :, LANES:] for i in range(3)]
        + [
            wo_rows[:, LANES:],
            w_router,
            w_const,
            norm_attn[:, None],
            norm_moe[:, None],
            const_vec.T,
            jnp.zeros((part, LANES - columns - 8), BF16),
        ],
        axis=1,
    )
    gathered = part % 16 != 0
    if gathered:
        packed = lax.all_gather(packed, "dp", axis=0, tiled=True)
        other = across_chips(packed)
        packed = jnp.where(m == 0, jnp.stack([packed, other]), jnp.stack([other, packed]))
    spread_width = packed.shape[-1]
    front_outs = [
        struct((rows, width), BF16),
        struct((pairs, rows, LANES), BF16),
        struct((pairs, rows, LANES), BF16),
        struct((pairs, rows, LANES), BF16),
        struct((rows, width), BF16),
        struct((8, 8, rows), F32),
        struct((rows, width), F32),
        struct((rows, width), BF16),
        struct((rows, LANES), F32),
        struct((rows, LANES), F32),
        struct((width, width), BF16),
        struct((width, LANES), BF16),
        struct((LANES, width), F32),
        struct((2, width, spread_width), BF16),
    ]
    landing = [
        struct((n, padded, width), BF16),
        struct((n, 8, padded), F32),
        struct((n, padded, width), BF16),
    ] + [struct(w_in.shape, BF16)] * 3 + [struct(w_down.shape, BF16)] * 3
    dma = pltpu.SemaphoreType.DMA
    (
        a,
        q,
        k,
        v,
        o_all,
        lse,
        h,
        ub,
        stats,
        pos,
        wo_all,
        small_all,
        extra,
        spread,
        arrived,
        gate_arrived,
        dy_arrived,
        in_c,
        in_x,
        in_d,
        down_c,
        down_x,
        down_d,
    ) = pl.pallas_call(
        functools.partial(front_kernel, n, half, padded, gathered),
        out_shape=front_outs + landing,
        in_specs=[aspec()] * 4 + [vspec()] * 3 + [aspec()] * 2,
        out_specs=[vspec()] * len(front_outs) + [aspec()] * len(landing),
        scratch_shapes=[
            pltpu.VMEM((rows, width), BF16),
            pltpu.VMEM((rows, width), BF16),
            pltpu.VMEM((rows, columns), F32),
            pltpu.VMEM((rows, 2), jnp.int32),
            pltpu.VMEM((LANES, rows), F32),
            pltpu.VMEM((LANES, rows), F32),
            pltpu.VMEM((n, padded, width), BF16),
            pltpu.VMEM((n, 8, padded), F32),
            pltpu.VMEM((n, padded, width), BF16),
            dma((4,)),
            dma((2 * n,)),
            dma((2 * n,)),
            dma((n,)),
            dma((n,)),
            dma((n,)),
            dma((n,)),
            dma((n,)),
            dma((n,)),
            dma((3,)),
            dma((pairs + 1,)),
            dma((pairs + 1,)),
            dma((6,)),
            dma((6,)),
        ],
        compiler_params=pltpu.CompilerParams(
            collective_id=0, has_side_effects=True, vmem_limit_bytes=VMEM_LIMIT
        ),
    )(tokens, cotangent, prev_logits, routes, packed, cosine, sine, w_in, w_down)

    hidden_width = w_in.shape[3]
    slots_all = experts * padded
    chunk = min(256 if slots_all <= 1024 else 128, hidden_width)
    per = hidden_width // chunk

    def in_map(i):
        return lambda f: (0, 0, 0, jnp.clip(f - per * i, 0, per - 1))

    def down_map(i):
        return lambda f: (0, jnp.clip(f - per * i, 0, per - 1), 0)

    in_blocks = [pl.BlockSpec((1, 2, width, chunk), in_map(i)) for i in range(4)]
    down_blocks = [pl.BlockSpec((1, chunk, width), down_map(i)) for i in range(4)]
    expert_outs = (
        [
            struct((n, padded, width), BF16),
            struct((n, padded, width), BF16),
            struct((n, 8, padded), F32),
        ]
        + [struct(w_in.shape, BF16)] * 4
        + [struct(w_down.shape, BF16)] * 4
    )

    def whole(shape):
        return pl.BlockSpec(
            shape, lambda f: (0,) * len(shape), pipeline_mode=pl.Buffered(1)
        )

    parts = pl.pallas_call(
        functools.partial(expert_kernel, n, padded),
        grid=(4 * per,),
        out_shape=expert_outs,
        in_specs=[
            whole((slots_all, width)),
            whole((slots_all, width)),
            whole((n, 8, padded)),
        ]
        + in_blocks
        + down_blocks,
        out_specs=[
            whole((n, padded, width)),
            whole((n, padded, width)),
            whole((n, 8, padded)),
        ]
        + in_blocks
        + down_blocks,
        scratch_shapes=[
            pltpu.VMEM((width, slots_all), BF16),
            pltpu.VMEM((slots_all, width), BF16),
            pltpu.VMEM((slots_all, LANES), F32),
            pltpu.VMEM((slots_all, width), F32),
            pltpu.VMEM((slots_all, width), F32),
            pltpu.VMEM((2, width, chunk), BF16),
            pltpu.VMEM((chunk, width), BF16),
        ],
        compiler_params=pltpu.CompilerParams(vmem_limit_bytes=VMEM_LIMIT),
        cost_estimate=pl.CostEstimate(
            flops=18 * slots_all * width * 4 * hidden_width,
            bytes_accessed=30_000_000,
            transcendentals=0,
        ),
    )(
        arrived.reshape(slots_all, width),
        dy_arrived.reshape(slots_all, width),
        gate_arrived,
        w_in,
        in_c,
        in_x,
        in_d,
        w_down,
        down_c,
        down_x,
        down_d,
    )
    gy, dx, dg = parts[0:3]
    gin, gdown = parts[3:7], parts[7:11]
    def chip_part(core, chip, diagonal):
        mine = across_cores(core)
        chip = (chip.astype(F32) + across_cores(diagonal).astype(F32)).astype(BF16)
        return mine, chip

    mine_in, chip_in = chip_part(gin[1], gin[2], gin[3])
    mine_down, chip_down = chip_part(gdown[1], gdown[2], gdown[3])
    chip_in, chip_down, dx = lax.optimization_barrier((chip_in, chip_down, dx))
    grad_in = gin[0].astype(F32) + mine_in.astype(F32) + across_chips(chip_in).astype(F32)
    grad_down = gdown[0].astype(F32) + mine_down.astype(F32) + across_chips(chip_down).astype(F32)

    groups = 6 * LANES
    logit_rows = -(-columns // 8) * 8
    rear_outs = [
        struct((2, logit_rows, rows), F32),
        struct((2, width, groups), BF16) if gathered else struct((part, groups), F32),
        struct((width if gathered else part, LANES), F32),
    ]
    half_rows = rows // 2
    spread_n = 1 if gathered else n
    results, input_grads, logits, grads, lines = pl.pallas_call(
        functools.partial(rear_kernel, n, half, padded, gathered, part),
        out_shape=[struct((2, rows, width), BF16)] * 2 + rear_outs,
        in_specs=[aspec()] * 7 + [vspec()] * 15,
        out_specs=[aspec()] * 2 + [vspec()] + [aspec() if gathered else vspec()] * 2,
        scratch_shapes=[
            pltpu.VMEM((half_rows, width), BF16),
            pltpu.VMEM((rows, width), BF16),
            pltpu.VMEM((rows, 2), jnp.int32),
            pltpu.VMEM((rows, local), BF16),
            pltpu.VMEM((2, n, padded, width), BF16),
            pltpu.VMEM((2, n, padded, width), BF16),
            pltpu.VMEM((2, n, 8, padded), F32),
            pltpu.VMEM((half_rows, width), F32),
            pltpu.VMEM((rows, width), BF16),
            pltpu.VMEM((rows, local), BF16),
            pltpu.VMEM((rows, LANES), BF16),
            pltpu.VMEM((8, width), F32),
            pltpu.VMEM((2, rows, 5 * LANES), BF16),
            pltpu.VMEM((rows, LANES), F32),
            pltpu.VMEM((rows, LANES), F32),
            pltpu.VMEM((width, LANES), F32),
            pltpu.VMEM((2, width, groups), BF16),
            pltpu.VMEM((width, LANES), F32),
            pltpu.VMEM((2, spread_n, part, groups), BF16),
            pltpu.VMEM((spread_n, part, LANES), F32),
            pltpu.VMEM((part, groups), BF16),
            pltpu.VMEM((part, groups), BF16),
            pltpu.VMEM((2, part, LANES), F32),
            pltpu.VMEM((half_rows, width), BF16),
            pltpu.VMEM((half_rows, width), BF16),
            pltpu.VMEM((half_rows, width), F32),
            pltpu.VMEM((8, width), F32),
            pltpu.VMEM((8, width), F32),
            pltpu.VMEM((2, half_rows, width), BF16),
            dma((4,)),
            dma((n,)),
            dma((n,)),
            dma((n,)),
            dma((n,)),
            dma((n,)),
            dma((n,)),
            dma((5,)),
            dma((3, n)),
            dma((3, n)),
            dma((3, 2, n)),
            dma((3, 2, n)),
            dma((5,)),
            dma((5,)),
            dma((2, 3)),
            dma((2, 3)),
        ],
        compiler_params=pltpu.CompilerParams(
            collective_id=1, has_side_effects=True, vmem_limit_bytes=VMEM_LIMIT
        ),
    )(
        gy,
        dx,
        dg,
        tokens,
        cotangent,
        routes,
        o_all,
        h,
        ub,
        stats,
        pos,
        small_all,
        extra,
        wo_all,
        q,
        k,
        v,
        a,
        lse,
        spread,
        cosine,
        sine,
    )
    if gathered:
        grads = lax.psum_scatter(grads.astype(F32), "dp", scatter_dimension=1, tiled=True)
        lines = lax.psum_scatter(lines, "dp", scatter_dimension=0, tiled=True)
        other = lax.dynamic_index_in_dim(grads, 1 - m, 0, keepdims=False)
        grads = lax.dynamic_index_in_dim(grads, m, 0, keepdims=False) + across_chips(other)
        lines = lines + across_chips(lines)

    def heads(j):
        start = (4 + (j % 4) // 2) * LANES + (j % 2) * HD
        return jnp.concatenate(
            [grads[:, j * LANES : (j + 1) * LANES], grads[:, start : start + HD]], axis=1
        )

    return (
        results,
        input_grads,
        jnp.swapaxes(logits[:, :columns], 1, 2),
        lines[:, columns + 4],
        lines[:, columns + 5],
        jnp.stack([heads(i) for i in range(3)]),
        heads(3).T,
        lines[:, :columns],
        lines[:, columns : columns + 4],
        lines[:, columns + 6 : columns + 8].T,
        grad_in,
        grad_down,
    )


def solution(mesh):
    in_specs = (
        P(None, "dp", None),
        P(None, "dp", None),
        P(None, "dp", None),
        P(None, "dp", None),
        P("dp"),
        P("dp"),
        P(None, "dp", "tensor"),
        P("tensor", "dp"),
        P("dp", None),
        P("dp", None),
        P(None, "dp"),
        P("dp", None, None, "tensor"),
        P("dp", "tensor", None),
    )
    out_specs = (
        P(None, "dp", None),
        P(None, "dp", None),
        P(None, "dp", None),
        P("dp"),
        P("dp"),
        P(None, "dp", "tensor"),
        P("tensor", "dp"),
        P("dp", None),
        P("dp", None),
        P(None, "dp"),
        P("dp", None, None, "tensor"),
        P("dp", "tensor", None),
    )
    return jax.shard_map(body, mesh=mesh, in_specs=in_specs, out_specs=out_specs, check_vma=False)
```

```python
import functools

import jax
import jax.numpy as jnp
import numpy as np
from jax import lax
from jax.experimental import pallas as pl
from jax.experimental.pallas import tpu as pltpu
from jax.sharding import PartitionSpec as P

HD = 64
LEN = 1024
BLK = 256
EPSILON = 1e-06
LANES = 128
F32 = jnp.float32
BF16 = jnp.bfloat16
MESH = pl.DeviceIdType.MESH
VMEM_LIMIT = 60 * 1024 * 1024


def mm(a, b):
    return lax.dot_general(a, b, (((1,), (0,)), ((), ())), preferred_element_type=F32)


def mm_nt(a, b):
    return lax.dot_general(a, b, (((1,), (1,)), ((), ())), preferred_element_type=F32)


def mm_tn(a, b):
    return lax.dot_general(a, b, (((0,), (0,)), ((), ())), preferred_element_type=F32)


def vspec():
    return pl.BlockSpec(memory_space=pltpu.VMEM)


def aspec():
    return pl.BlockSpec(memory_space=pl.ANY)


def struct(shape, dtype):
    return jax.ShapeDtypeStruct(shape, dtype)


def greet(peers):
    barrier = pltpu.get_barrier_semaphore()
    for peer in peers:
        pl.semaphore_signal(barrier, inc=1, device_id=peer, device_id_type=MESH)
    pl.semaphore_wait(barrier, len(peers))


def remote(src, dst, send, recv, peer):
    return pltpu.make_async_remote_copy(
        src_ref=src,
        dst_ref=dst,
        send_sem=send,
        recv_sem=recv,
        device_id=peer,
        device_id_type=MESH,
    )


def plane_peers(n, d, t):
    return [(lax.rem(d + j, n), t) for j in range(1, n)]


def slot_hot(half, padded, base, places):
    rows = places.shape[1]
    slot = lax.broadcasted_iota(jnp.int32, (padded, rows), 0)
    wanted = jnp.where(slot < half, slot + base, -2).astype(F32)
    return (wanted == places).astype(F32).astype(BF16)


def rope_constants():
    half = HD // 2
    frequency = 10000.0 ** (-2.0 * np.arange(half) / HD)
    angle = np.arange(LEN)[:, None] * frequency[None, :]
    cosine, sine = np.cos(angle), np.sin(angle)
    cosine = np.concatenate([cosine, cosine, cosine, cosine], axis=1)
    sine = np.concatenate([-sine, sine, -sine, sine], axis=1)
    return cosine.astype(np.float32), sine.astype(np.float32)


def turn(field, cosine, sine):
    lane = lax.broadcasted_iota(jnp.int32, field.shape, 1)
    other = jnp.where(
        lax.rem(lane, HD) < HD // 2,
        pltpu.roll(field, LANES - HD // 2, 1),
        pltpu.roll(field, HD // 2, 1),
    )
    return field * cosine + other * sine


def pick(hot, values):
    return jnp.sum(jnp.where(hot, values, 0.0), axis=-1, keepdims=True)


def lane_ids(rows):
    return lax.broadcasted_iota(jnp.int32, (rows, LANES), 1)


def soft_pair(first, second):
    high = jnp.maximum(first, second)
    e0, e1 = jnp.exp(first - high), jnp.exp(second - high)
    return e0 / (e0 + e1), e1 / (e0 + e1)


def half_mask(rows):
    return lax.broadcasted_iota(jnp.int32, (rows, LANES), 1) < HD


def swap_halves(value):
    return pltpu.roll(value, HD, 1)


def front_kernel(
    n,
    half,
    padded,
    gathered,
    tokens_ref,
    cotangent_ref,
    prev_all_ref,
    routes_all_ref,
    packed_ref,
    cos_ref,
    sin_ref,
    win_ref,
    wdown_ref,
    a_ref,
    q_ref,
    k_ref,
    v_ref,
    o_ref,
    lse_ref,
    h_ref,
    ub_ref,
    stat_ref,
    pos_ref,
    wo_ref,
    small_ref,
    extra_ref,
    spread_ref,
    arrived_ref,
    gate_arrived_ref,
    dy_arrived_ref,
    in_c_ref,
    in_x_ref,
    in_d_ref,
    down_c_ref,
    down_x_ref,
    down_d_ref,
    x_ref,
    dy_ref,
    prev_ref,
    routes_ref,
    place_ref,
    gates_ref,
    slot_ref,
    gate_ref,
    dy_slot_ref,
    load,
    pack_send,
    pack_recv,
    dy_send,
    dy_recv,
    slot_send,
    slot_recv,
    gate_send,
    gate_recv,
    stay,
    core_send,
    core_recv,
    w_send,
    w_recv,
):
    rows_all, width = x_ref.shape
    blocks = rows_all // BLK
    pairs = q_ref.shape[0]
    local = pairs * LANES
    columns = prev_ref.shape[1]
    d, t = lax.axis_index("dp"), lax.axis_index("tensor")
    m, c = lax.div(t, 2), lax.rem(t, 2)
    partner = (d, t + 1 - 2 * c)
    across = (d, lax.rem(t + 2, 4))
    loads = [
        pltpu.make_async_copy(src.at[m], dst, load.at[i])
        for i, (src, dst) in enumerate(
            [
                (routes_all_ref, routes_ref),
                (cotangent_ref, dy_ref),
                (tokens_ref, x_ref),
                (prev_all_ref, prev_ref),
            ]
        )
    ]
    for copy in loads:
        copy.start()
    greet(plane_peers(n, d, t) + [partner, across])
    part = packed_ref.shape[0]
    beside = (d + 1 - 2 * lax.rem(d, 2), t)
    lanes_a = pl.ds(0, 4 * LANES)
    lanes_b = pl.ds(4 * LANES, packed_ref.shape[-1] - 4 * LANES)

    def behind(j):
        return lax.rem(d + n - 2 * j, n)

    def shard(chip, owner, lanes):
        return spread_ref.at[chip, pl.ds(pl.multiple_of(owner * part, part), part), lanes]

    def pass_on(chip, owner, lanes, row, j, peer):
        block = shard(chip, owner, lanes)
        return remote(block, block, pack_send.at[row, j], pack_recv.at[row, j], peer)

    def ahead(j):
        return (lax.rem(d + 2 * j, n), t)

    ring = n // 2
    if gathered:
        spread_ref[...] = packed_ref[...]
    else:
        spread_ref[m, pl.ds(pl.multiple_of(d * part, part), part), :] = packed_ref[...]
        a_x = pass_on(m, d, lanes_a, 4, 0, across)
        sends = [a_x]
        for j in range(1, ring):
            sends.append(pass_on(m, d, lanes_a, 0, j, ahead(j)))
            sends.append(pass_on(m, d, lanes_b, 4, j, ahead(j)))
        sends.append(pass_on(m, d, lanes_a, 2, 0, beside))
        sends.append(pass_on(m, d, lanes_b, 5, 0, beside))
        sends.append(pass_on(m, d, lanes_b, 6, 0, across))
        for copy in sends:
            copy.start()

    def relay_gather():
        if gathered:
            return
        a_x.wait_recv()
        more = [pass_on(1 - m, d, lanes_a, 1, j, ahead(j)) for j in range(1, ring)]
        more.append(pass_on(1 - m, d, lanes_a, 3, 0, beside))
        for copy in more:
            copy.start()
        sends.extend(more)
        for j in range(1, ring):
            pass_on(m, d, lanes_b, 4, j, ahead(j)).wait_recv()
            more = [
                pass_on(m, behind(j), lanes_b, 5, j, beside),
                pass_on(m, behind(j), lanes_b, 6, j, across),
            ]
            pass_on(m, d, lanes_a, 0, j, ahead(j)).wait_recv()
            more.append(pass_on(m, behind(j), lanes_a, 2, j, beside))
            for copy in more:
                copy.start()
            sends.extend(more)
        for j in range(1, ring):
            pass_on(1 - m, d, lanes_a, 1, j, ahead(j)).wait_recv()
            copy = pass_on(1 - m, behind(j), lanes_a, 3, j, beside)
            copy.start()
            sends.append(copy)
        for j in range(ring):
            pass_on(m, d, lanes_b, 5, j, beside).wait_recv()
            owner = lax.rem(beside[0] + n - 2 * j, n)
            copy = pass_on(m, owner, lanes_b, 7, j, across)
            copy.start()
            sends.append(copy)
        for j in range(ring):
            pass_on(m, d, lanes_a, 2, j, beside).wait_recv()
            pass_on(m, d, lanes_a, 3, j, beside).wait_recv()
            pass_on(m, d, lanes_b, 6, j, across).wait_recv()
            pass_on(m, d, lanes_b, 7, j, across).wait_recv()

    loads[0].wait()
    line = lax.broadcasted_iota(jnp.int32, (rows_all, LANES), 1)
    named = jnp.where(
        line == 0,
        routes_ref[:, 0:1].astype(F32),
        jnp.where(line == 1, routes_ref[:, 1:2].astype(F32), 0.0),
    )
    named = jnp.transpose(named)
    ids = lax.broadcasted_iota(jnp.int32, (LANES, rows_all), 0).astype(F32)
    hit = ((ids == named[0:1, :]) | (ids == named[1:2, :])) & (ids < float(n))
    before = lax.broadcasted_iota(jnp.int32, (rows_all, rows_all), 0) < lax.broadcasted_iota(
        jnp.int32, (rows_all, rows_all), 1
    )
    count = mm(hit.astype(F32).astype(BF16), before.astype(F32).astype(BF16))
    places = jnp.where(hit, count, -1.0)
    place_ref[...] = places
    pos_ref[...] = jnp.transpose(places)
    base = c * half

    def dy_copy(j):
        e = lax.rem(d + j, n)
        return remote(
            dy_slot_ref.at[e], dy_arrived_ref.at[d], dy_send.at[j], dy_recv.at[j], (e, t)
        )

    def slot_copy(j):
        e = lax.rem(d + j, n)
        return remote(
            slot_ref.at[e], arrived_ref.at[d], slot_send.at[j], slot_recv.at[j], (e, t)
        )

    def gate_copy(j):
        e = lax.rem(d + j, n)
        return remote(
            gate_ref.at[e], gate_arrived_ref.at[d], gate_send.at[j], gate_recv.at[j], (e, t)
        )

    stays = [
        pltpu.make_async_copy(src.at[d], dst.at[d], stay.at[i])
        for i, (src, dst) in enumerate(
            [
                (dy_slot_ref, dy_arrived_ref),
                (slot_ref, arrived_ref),
                (gate_ref, gate_arrived_ref),
            ]
        )
    ]
    loads[1].wait()

    def dy_step(i, carry):
        j = lax.rem(i + 1, n)
        e = lax.rem(d + j, n)
        hot = slot_hot(half, padded, base, place_ref[pl.ds(e, 1), :])
        dy_slot_ref[e] = mm(hot, dy_ref[...]).astype(BF16)
        return carry

    lax.fori_loop(0, n, dy_step, 0)
    relay_gather()
    stays[0].start()

    def dy_start(j, carry):
        dy_copy(j).start()
        return carry

    lax.fori_loop(1, n, dy_start, 0)
    weight_copies = [
        remote(win_ref, in_x_ref, w_send.at[0], w_recv.at[0], across),
        remote(wdown_ref, down_x_ref, w_send.at[1], w_recv.at[1], across),
        remote(win_ref, in_c_ref, w_send.at[2], w_recv.at[2], partner),
        remote(wdown_ref, down_c_ref, w_send.at[3], w_recv.at[3], partner),
        remote(in_x_ref, in_d_ref, w_send.at[4], w_recv.at[4], partner),
        remote(down_x_ref, down_d_ref, w_send.at[5], w_recv.at[5], partner),
    ]
    for copy in weight_copies[0:4]:
        copy.start()

    table = spread_ref[0, :, 6 * LANES : 7 * LANES]
    extra_ref[...] = jnp.transpose(table.astype(F32))
    keep = lax.broadcasted_iota(jnp.int32, (width, LANES), 1) < columns + 4
    small_ref[...] = jnp.where(keep, table, jnp.zeros_like(table))
    mask = half_mask(width)
    own = pl.multiple_of(c * local, LANES)
    wo_ref[:, pl.ds(own, LANES)] = spread_ref[0, :, 3 * LANES : 4 * LANES]
    wo_ref[:, pl.ds(own + LANES, LANES)] = spread_ref[1, :, 3 * LANES : 4 * LANES]
    wo_ref[:, pl.ds(own + 2 * LANES, LANES)] = jnp.where(
        mask,
        swap_halves(spread_ref[0, :, 5 * LANES : 6 * LANES].astype(F32)),
        spread_ref[1, :, 5 * LANES : 6 * LANES].astype(F32),
    ).astype(BF16)
    own_lanes = pl.ds(own, local)
    wo_copy = remote(
        wo_ref.at[:, own_lanes],
        wo_ref.at[:, own_lanes],
        core_send.at[pairs],
        core_recv.at[pairs],
        partner,
    )
    wo_copy.start()

    loads[2].wait()
    gain = extra_ref[columns + 4 : columns + 5, :]
    head = half_mask(BLK)

    def project(i, carry):
        rows = pl.ds(pl.multiple_of(i * BLK, BLK), BLK)
        x = x_ref[rows, :].astype(F32)
        r = lax.rsqrt(jnp.mean(x * x, axis=-1, keepdims=True) + EPSILON)
        a = (x * r * gain).astype(BF16)
        a_ref[rows, :] = a
        cosine, sine = cos_ref[rows, :], sin_ref[rows, :]

        def put(pair, q, k, v):
            q_ref[pair, rows, :] = turn(q, cosine, sine).astype(BF16) * BF16(HD**-0.5)
            k_ref[pair, rows, :] = turn(k, cosine, sine).astype(BF16)
            v_ref[pair, rows, :] = v.astype(BF16)

        odd = []
        for s in range(2):
            both = mm(a, spread_ref[s, :, 0 : 3 * LANES])
            put(s, *(both[:, j * LANES : (j + 1) * LANES] for j in range(3)))
            both = mm(a, spread_ref[s, :, 4 * LANES : 6 * LANES])
            odd.append((both[:, :LANES], both[:, LANES:]))
        put(
            2,
            jnp.where(head, odd[0][0], swap_halves(odd[1][0])),
            jnp.where(head, swap_halves(odd[0][0]), odd[1][0]),
            jnp.where(head, odd[0][1], swap_halves(odd[1][1])),
        )
        return carry

    lax.fori_loop(0, blocks, project, 0)

    def o_copy(p):
        lanes = pl.ds(pl.multiple_of(own + p * LANES, LANES), LANES)
        return remote(
            o_ref.at[:, lanes], o_ref.at[:, lanes], core_send.at[p], core_recv.at[p], partner
        )

    def attend(p, carry):
        lanes = pl.ds(pl.multiple_of(own + p * LANES, LANES), LANES)
        for i in range(blocks):
            rows = pl.ds(i * BLK, BLK)
            seen = pl.ds(0, (i + 1) * BLK)
            q, k, v = q_ref[p, rows, :], k_ref[p, seen, :], v_ref[p, seen, :]
            halves = []
            for side in range(2):
                chosen = head if side == 0 else jnp.logical_not(head)
                s = mm_nt(jnp.where(chosen, q, jnp.zeros_like(q)), k)
                high = jnp.max(s, axis=-1, keepdims=True)
                e = jnp.exp(s - high)
                total = jnp.sum(e, axis=-1, keepdims=True)
                halves.append(mm((e / total).astype(BF16), v))
                log_total = jnp.broadcast_to(high + jnp.log(total), (BLK, LANES))
                lse_ref[2 * p + side, :, rows] = jnp.transpose(log_total)[0:8, :]
            o_ref[rows, lanes] = jnp.where(head, halves[0], halves[1]).astype(BF16)
        o_copy(p).start()
        return carry

    lax.fori_loop(0, pairs, attend, 0)
    loads[3].wait()
    wo_copy.wait()
    for p in range(pairs):
        o_copy(p).wait()

    gain_moe = extra_ref[columns + 5 : columns + 6, :]

    def middle(i, carry):
        rows = pl.ds(pl.multiple_of(i * BLK, BLK), BLK)
        z = mm_nt(o_ref[rows, :], wo_ref[...])
        h = x_ref[rows, :].astype(F32) + z
        r = lax.rsqrt(jnp.mean(h * h, axis=-1, keepdims=True) + EPSILON)
        ub = (h * r * gain_moe).astype(BF16)
        h_ref[rows, :] = h
        ub_ref[rows, :] = ub
        scores = mm(ub, small_ref[...])
        lane = lane_ids(BLK)
        e0, e1 = routes_ref[rows, 0:1], routes_ref[rows, 1:2]
        hot0, hot1 = lane == e0, lane == e1
        prev = prev_ref[rows, :]
        few = lax.broadcasted_iota(jnp.int32, (BLK, columns), 1)
        g0, g1 = soft_pair(
            pick(hot0, scores) + pick(few == e0, prev), pick(hot1, scores) + pick(few == e1, prev)
        )
        mix = [pick(lane == columns + j, scores) for j in range(4)]
        a00, a01 = soft_pair(mix[0], mix[1])
        a10, a11 = soft_pair(mix[2], mix[3])
        table = jnp.zeros((BLK, LANES), F32)
        for j, value in enumerate([g0, g1, a00, a01, a10, a11, r]):
            table = jnp.where(lane == j, value, table)
        stat_ref[rows, :] = table
        gates = jnp.where(hot0, g0, 0.0) + jnp.where(hot1, g1, 0.0)
        gates_ref[:, rows] = jnp.transpose(gates)
        return carry

    lax.fori_loop(0, blocks, middle, 0)
    piece = lax.broadcasted_iota(jnp.int32, (8, rows_all), 0)

    def slot_step(i, carry):
        j = lax.rem(i + 1, n)
        e = lax.rem(d + j, n)
        hot = slot_hot(half, padded, base, place_ref[pl.ds(e, 1), :])
        slot_ref[e] = mm(hot, ub_ref[...]).astype(BF16)
        gate = gates_ref[pl.ds(e, 1), :]
        high = gate.astype(BF16).astype(F32)
        mid = (gate - high).astype(BF16).astype(F32)
        low = gate - high - mid
        lines = jnp.where(piece == 0, high, jnp.where(piece == 1, mid, low))
        lines = jnp.where(piece < 3, lines, 0.0).astype(BF16)
        gate = jnp.sum(mm_nt(lines, hot), axis=0, keepdims=True)
        gate_ref[e] = jnp.broadcast_to(gate, (8, padded))

        @pl.when(i < n - 1)
        def _():
            slot_copy(j).start()
            gate_copy(j).start()

        return carry

    lax.fori_loop(0, n, slot_step, 0)
    stays[1].start()
    stays[2].start()
    weight_copies[0].wait_recv()
    weight_copies[1].wait_recv()
    weight_copies[4].start()
    weight_copies[5].start()

    def finish(j, carry):
        for copy in (dy_copy(j), slot_copy(j), gate_copy(j)):
            copy.wait()
        return carry

    lax.fori_loop(1, n, finish, 0)
    for copy in stays:
        copy.wait()
    for copy in ([] if gathered else sends) + weight_copies[0:2]:
        copy.wait_send()
    for copy in weight_copies[2:6]:
        copy.wait()


def expert_kernel(
    sources,
    padded,
    x_ref,
    dy_ref,
    gate_ref,
    *refs,
):
    weights, outs = refs[:8], refs[8:19]
    in_refs, down_refs = weights[0:4], weights[4:8]
    gy_ref, dx_ref, dg_ref = outs[0:3]
    gin_refs, gdown_refs = outs[3:7], outs[7:11]
    xt_ref, scaled_ref, scale_ref, y_acc, dx_acc, win_ref, wdown_ref = refs[19:]
    step = pl.program_id(0)
    last = pl.num_programs(0) - 1

    @pl.when(step == 0)
    def _():
        xt_ref[...] = jnp.transpose(x_ref[...])
        for s in range(sources):
            rows = pl.ds(s * padded, padded)
            line = jnp.broadcast_to(gate_ref[s, 0:1, :], (LANES, padded))
            scale = jnp.transpose(line)
            scale_ref[rows, :] = scale
            scaled_ref[rows, :] = (dy_ref[rows, :].astype(F32) * scale[:, 0:1]).astype(BF16)
        y_acc[...] = jnp.zeros_like(y_acc)
        dx_acc[...] = jnp.zeros_like(dx_acc)

    per = pl.num_programs(0) // 4
    for i in range(4):

        @pl.when(lax.div(step, per) == i)
        def _():
            win_ref[...] = in_refs[i][0]
            wdown_ref[...] = down_refs[i][0]

    x = x_ref[...]
    gate = mm(x, win_ref[0])
    up = mm(x, win_ref[1])
    sigma = 1.0 / (1.0 + jnp.exp(-gate))
    active = gate * sigma
    hidden = (active * up).astype(BF16)
    y_acc[...] += mm(hidden, wdown_ref[...])
    scaled = scaled_ref[...]
    grad_hidden = mm_nt(scaled, wdown_ref[...])
    grad_gate = (grad_hidden * up * (sigma * (1.0 + gate * (1.0 - sigma)))).astype(BF16)
    grad_up = (grad_hidden * active).astype(BF16)
    dx_acc[...] += mm_nt(grad_gate, win_ref[0]) + mm_nt(grad_up, win_ref[1])
    xt = xt_ref[...]
    part_gate = mm(xt, grad_gate).astype(BF16)
    part_up = mm(xt, grad_up).astype(BF16)
    part_down = mm_tn(hidden, scaled).astype(BF16)
    for i in range(4):

        @pl.when(lax.div(step, per) == i)
        def _():
            gin_refs[i][0, 0] = part_gate
            gin_refs[i][0, 1] = part_up
            gdown_refs[i][0] = part_down

    @pl.when(step == last)
    def _():
        for s in range(sources):
            rows = pl.ds(s * padded, padded)
            y = y_acc[rows, :]
            gy_ref[s] = (y * scale_ref[rows, 0:1]).astype(BF16)
            dot = jnp.sum(y * dy_ref[rows, :].astype(F32), axis=-1, keepdims=True)
            dg_ref[s] = jnp.transpose(jnp.broadcast_to(dot, (padded, LANES)))[0:8, :]
            dx_ref[s] = dx_acc[rows, :].astype(BF16)


def rear_kernel(
    n,
    half,
    padded,
    gathered,
    part,
    gy_src_ref,
    dx_src_ref,
    dg_src_ref,
    tokens_ref,
    cotangent_ref,
    routes_all_ref,
    o_all_ref,
    h_ref,
    ub_ref,
    stat_ref,
    pos_ref,
    small_ref,
    extra_ref,
    wo_ref,
    q_ref,
    k_ref,
    v_ref,
    a_ref,
    lse_ref,
    spread_ref,
    cos_ref,
    sin_ref,
    result_ref,
    grad_x_ref,
    logit_ref,
    grads_ref,
    lines_ref,
    x_ref,
    dy_ref,
    routes_ref,
    o_ref,
    dx_ref,
    gy_ref,
    dg_ref,
    dh_ref,
    dzb_ref,
    do_ref,
    low_ref,
    row_ref,
    dp_ref,
    dk_acc,
    dv_acc,
    wo_odd_ref,
    pack_ref,
    line_ref,
    y_in_ref,
    z_in_ref,
    line_in_ref,
    cross_ref,
    cross_in_ref,
    cross_line_ref,
    da_out_ref,
    da_in_ref,
    da_own_ref,
    norm_ref,
    norm_in_ref,
    half_ref,
    load,
    dx_send,
    dx_recv,
    gy_send,
    gy_recv,
    dg_send,
    dg_recv,
    stay,
    pass_send,
    pass_recv,
    grad_send,
    grad_recv,
    line_send,
    line_recv,
    pair_send,
    pair_recv,
    out_send,
    out_recv,
):
    rows_all, width = dy_ref.shape
    blocks = rows_all // BLK
    pairs = q_ref.shape[0]
    local = pairs * LANES
    columns = n + 4
    slots = n * padded
    d, t = lax.axis_index("dp"), lax.axis_index("tensor")
    m, c = lax.div(t, 2), lax.rem(t, 2)
    partner = (d, t + 1 - 2 * c)
    across = (d, lax.rem(t + 2, 4))
    rows_half = rows_all // 2
    own = pl.multiple_of(c * local, LANES)
    own_lanes = pl.ds(own, local)
    place = pl.ds(pl.multiple_of(c * rows_half, BLK), rows_half)
    loads = [
        pltpu.make_async_copy(src, dst, load.at[i])
        for i, (src, dst) in enumerate(
            [
                (routes_all_ref.at[m], routes_ref),
                (cotangent_ref.at[m], dy_ref),
                (tokens_ref.at[m, place], x_ref),
                (o_all_ref.at[:, own_lanes], o_ref),
            ]
        )
    ]
    for copy in loads:
        copy.start()
    greet(plane_peers(n, d, t) + [partner, across])

    kinds = [
        (dx_src_ref, dx_ref, dx_send, dx_recv),
        (dg_src_ref, dg_ref, dg_send, dg_recv),
        (gy_src_ref, gy_ref, gy_send, gy_recv),
    ]

    def give(kind, j):
        src, dst, send, recv = kinds[kind]
        s = lax.rem(d + j, n)
        return remote(src.at[s], dst.at[c, d], send.at[j], recv.at[j], (s, t))

    def hand(kind, j):
        dst = kinds[kind][1]
        s = lax.rem(d + n - j, n)
        block = dst.at[c, s]
        return remote(block, block, pass_send.at[kind, j], pass_recv.at[kind, j], partner)

    def keep(kind):
        src, dst = kinds[kind][0:2]
        return pltpu.make_async_copy(src.at[d], dst.at[c, d], stay.at[kind])

    def begin(*chosen):
        for kind in chosen:
            keep(kind).start()

        def step(j, carry):
            for kind in chosen:
                give(kind, j).start()
            return carry

        lax.fori_loop(1, n, step, 0)

    def collect(*chosen):
        for kind in chosen:
            keep(kind).wait()
            hand(kind, 0).start()

        def step(j, carry):
            for kind in chosen:
                give(kind, j).wait_recv()
                hand(kind, j).start()
            return carry

        lax.fori_loop(1, n, step, 0)

    def settle(*chosen):
        def step(j, carry):
            for kind in chosen:
                hand(kind, j).wait_recv()
            return carry

        lax.fori_loop(0, n, step, 0)

    begin(0, 1)
    row_ref[...] = jnp.zeros_like(row_ref)
    for copy in loads:
        copy.wait()
    collect(0, 1)
    begin(2)
    settle(0, 1)

    gain_moe = extra_ref[columns + 5 : columns + 6, :]
    vec0 = extra_ref[columns + 6 : columns + 7, :]
    vec1 = extra_ref[columns + 7 : columns + 8, :]
    group = max(1, min(n, (1024 if slots <= 1024 else 512) // padded))
    span = group * padded

    def combine(wheres, ref, lines=None):
        total = jnp.zeros((BLK, width), F32)
        entries = [jnp.zeros((BLK, 1), F32) for _ in wheres]
        slot = lax.broadcasted_iota(jnp.int32, (BLK, span), 1)
        for side in range(2):
            for first in range(0, n, group):
                start = side * slots + first * padded
                hots = [slot == where - start for where in wheres]
                hot = jnp.where(hots[0] | hots[1], 1.0, 0.0).astype(BF16)
                block = ref[side, first : first + group].reshape(span, width)
                total = total + mm(hot, block)
                if lines is not None:
                    line = jnp.concatenate(
                        [lines[side, first + e, 0:1, :] for e in range(group)], axis=1
                    )
                    entries = [
                        entry + jnp.sum(jnp.where(one, line, 0.0), axis=-1, keepdims=True)
                        for entry, one in zip(entries, hots)
                    ]
        return total, entries

    def facts(rows):
        lane = lane_ids(BLK)
        stats = stat_ref[rows, :]
        values = [stats[:, j : j + 1] for j in range(7)]
        e0, e1 = routes_ref[rows, 0:1], routes_ref[rows, 1:2]
        wheres = []
        places = pos_ref[rows, :]
        for e in (e0, e1):
            place = pick(lane == e, places).astype(jnp.int32)
            side = (place >= half).astype(jnp.int32)
            where = side * (slots - half) + e * padded + place
            wheres.append(jnp.where(e < n, where, -1))
        g0, g1 = values[0:2]

        def named(number):
            return jnp.where(e0 == number, g0, 0.0) + jnp.where(e1 == number, g1, 0.0)

        copied, first, second = named(n + 1), named(n + 2), named(n + 3)
        on_u = copied + first * values[2] + second * values[4]
        return values, e0, e1, wheres, first, second, on_u

    def back(i, carry):
        rows = pl.ds(pl.multiple_of(i * BLK, BLK), BLK)
        values, e0, e1, wheres, first, second, on_u = facts(rows)
        g0, g1, a00, a01, a10, a11, r = values
        lane = lane_ids(BLK)
        grads, (f0, f1) = combine(wheres, dx_ref, dg_ref)
        h = h_ref[rows, :]
        normed = h * r
        u = normed * gain_moe
        dy = dy_ref[rows, :].astype(F32)
        s_u = jnp.sum(dy * u, axis=-1, keepdims=True)
        s_0 = jnp.sum(dy * vec0, axis=-1, keepdims=True)
        s_1 = jnp.sum(dy * vec1, axis=-1, keepdims=True)

        def other(e):
            value = jnp.where(e == n + 1, s_u, 0.0)
            value = jnp.where(e == n + 2, a00 * s_u + a01 * s_0, value)
            return jnp.where(e == n + 3, a10 * s_u + a11 * s_1, value)

        dg0, dg1 = f0 + other(e0), f1 + other(e1)
        mean = g0 * dg0 + g1 * dg1
        dl = jnp.where(lane == e0, g0 * (dg0 - mean), 0.0) + jnp.where(
            lane == e1, g1 * (dg1 - mean), 0.0
        )
        turned = jnp.transpose(dl)
        logit_ref[m, :, rows] = turned[0 : logit_ref.shape[1], :]
        d00, d01 = first * s_u, first * s_0
        d10, d11 = second * s_u, second * s_1
        m0 = a00 * d00 + a01 * d01
        m1 = a10 * d10 + a11 * d11
        low = dl
        for j, value in enumerate(
            [a00 * (d00 - m0), a01 * (d01 - m0), a10 * (d10 - m1), a11 * (d11 - m1)]
        ):
            low = jnp.where(lane == columns + j, value, low)
        low = low.astype(BF16)
        low_ref[rows, :] = low
        du = grads + mm_nt(low, small_ref[...]) + on_u * dy
        row_ref[0:1, :] += jnp.sum(du * normed, axis=0, keepdims=True)
        row_ref[1:2, :] += jnp.sum((first * a01) * dy, axis=0, keepdims=True)
        row_ref[2:3, :] += jnp.sum((second * a11) * dy, axis=0, keepdims=True)
        dn = du * gain_moe
        dh = dy + r * (dn - normed * jnp.mean(dn * normed, axis=-1, keepdims=True))

        @pl.when(lax.div(i, blocks // 2) == c)
        def _():
            near = pl.multiple_of(i * BLK - c * rows_half, BLK)
            dh_ref[pl.ds(near, BLK), :] = dh

        dzb = dh.astype(BF16)
        dzb_ref[rows, :] = dzb
        do_ref[rows, :] = mm(dzb, wo_ref[:, own_lanes]).astype(BF16)
        return carry

    lax.fori_loop(0, blocks, back, 0)
    logit_copy = remote(
        logit_ref.at[m], logit_ref.at[m], pair_send.at[0], pair_recv.at[0], across
    )
    logit_copy.start()
    collect(2)

    grad_wo = mm_tn(dzb_ref[...], o_ref[...])
    pack_ref[0, :, 3 * LANES : 4 * LANES] = grad_wo[:, 0:LANES].astype(BF16)
    pack_ref[1, :, 3 * LANES : 4 * LANES] = grad_wo[:, LANES : 2 * LANES].astype(BF16)
    wo_odd_ref[...] = grad_wo[:, 2 * LANES : 3 * LANES]
    line_ref[...] = mm_tn(ub_ref[...], low_ref[...])

    def slab(owner):
        return pl.ds(pl.multiple_of(owner * part, part), part)

    ring = n // 2
    y_own = lax.rem(d, 2)
    beside = (d + 1 - 2 * y_own, t)
    z_own = lax.div(d, 2)
    wide_lanes = (pl.ds(0, 4 * LANES), pl.ds(4 * LANES, 2 * LANES))

    def y_copy(s, stage, z):
        lanes = wide_lanes[stage]
        return remote(
            pack_ref.at[s, slab(2 * z + 1 - y_own), lanes],
            y_in_ref.at[s, z, :, lanes],
            grad_send.at[stage, s, z],
            grad_recv.at[stage, s, z],
            beside,
        )

    def z_copy(s, stage, j):
        lanes = wide_lanes[stage]
        z = lax.rem(z_own + j, ring)
        return remote(
            pack_ref.at[s, slab(2 * z + y_own), lanes],
            z_in_ref.at[s, j, :, lanes],
            grad_send.at[2 + stage, s, j],
            grad_recv.at[2 + stage, s, j],
            (2 * z + y_own, t),
        )

    def y_start(s, stage):
        for z in range(ring):
            y_copy(s, stage, z).start()

    def z_start(s, stage):
        lanes = wide_lanes[stage]
        for z in range(ring):
            y_copy(s, stage, z).wait()
            rows = slab(2 * z + y_own)
            value = pack_ref[s, rows, lanes].astype(F32) + y_in_ref[s, z, :, lanes].astype(F32)
            pack_ref[s, rows, lanes] = value.astype(BF16)
        for j in range(1, ring):
            z_copy(s, stage, j).start()

    def line_copy(j):
        e = lax.rem(d + j, n)
        return remote(
            line_ref.at[slab(e), :],
            line_in_ref.at[d],
            line_send.at[j],
            line_recv.at[j],
            (e, t),
        )

    head = half_mask(BLK)

    def attend_back(p):
        dk_acc[...] = jnp.zeros_like(dk_acc)
        dv_acc[...] = jnp.zeros_like(dv_acc)
        dq = []
        for i in range(blocks):
            rows = pl.ds(i * BLK, BLK)
            seen = pl.ds(0, (i + 1) * BLK)
            lanes = pl.ds(pl.multiple_of(p * LANES, LANES), LANES)
            q, do = q_ref[p, rows, :], do_ref[rows, lanes]
            k, v = k_ref[p, seen, :], v_ref[p, seen, :]
            zero = jnp.zeros_like(q)
            parts = []
            dk, dv = dk_acc[seen, :], dv_acc[seen, :]
            for side in range(2):
                chosen = head if side == 0 else jnp.logical_not(head)
                qm, dom = jnp.where(chosen, q, zero), jnp.where(chosen, do, zero)
                prob = jnp.exp(mm_nt(k, qm) - lse_ref[2 * p + side, 0:1, rows])
                grad_prob = mm_nt(v, dom)
                total = jnp.sum(prob * grad_prob, axis=0, keepdims=True)
                grad_score = (prob * (grad_prob - total)).astype(BF16)
                dv = dv + mm(prob.astype(BF16), dom)
                dk = dk + mm(grad_score, qm)
                parts.append(mm_tn(grad_score, k))
            dk_acc[seen, :] = dk
            dv_acc[seen, :] = dv
            value = jnp.where(head, parts[0], parts[1]) * (HD**-0.5)
            dq.append(turn(value, cos_ref[rows, :], -sin_ref[rows, :]))
        return (
            jnp.concatenate(dq, axis=0),
            turn(dk_acc[...], cos_ref[...], -sin_ref[...]),
            dv_acc[...],
        )

    def shard_step(i, carry):
        s = lax.rem(m + 1 + i, 2)
        for j, value in enumerate(attend_back(s)):
            dp_ref[s, :, j * LANES : (j + 1) * LANES] = value.astype(BF16)
        for j in range(3):
            lanes = pl.ds(j * LANES, LANES)
            pack_ref[s, :, lanes] = mm_tn(a_ref[...], dp_ref[s, :, lanes]).astype(BF16)
        if not gathered:
            y_start(s, 0)

            @pl.when(i == 1)
            def _():
                z_start(lax.rem(m + 1, 2), 0)

        return carry

    lax.fori_loop(0, 2, shard_step, 0)
    dq, dk, dv = attend_back(2)
    wide = half_mask(rows_all)
    odd = [
        (jnp.where(wide, dq, swap_halves(dk)), jnp.where(wide, dv, 0.0)),
        (jnp.where(wide, swap_halves(dq), dk), jnp.where(wide, swap_halves(dv), 0.0)),
    ]
    tall = half_mask(width)
    for s in range(2):
        for j in range(2):
            dp_ref[s, :, (3 + j) * LANES : (4 + j) * LANES] = odd[s][j].astype(BF16)
    for s in range(2):
        pack_ref[s, :, 4 * LANES : 5 * LANES] = mm_tn(
            a_ref[...], dp_ref[s, :, 3 * LANES : 4 * LANES]
        ).astype(BF16)
        last = mm_tn(a_ref[...], dp_ref[s, :, 4 * LANES : 5 * LANES])
        side = wo_odd_ref[...]
        side = swap_halves(side) if s == 0 else side
        pack_ref[s, :, 5 * LANES : 6 * LANES] = jnp.where(tall, last, side).astype(BF16)
    if not gathered:
        y_start(0, 1)
        y_start(1, 1)
        z_start(m, 0)

    def da_rows(start):
        rows = pl.ds(pl.multiple_of(start, BLK), BLK)
        total = jnp.zeros((BLK, width), F32)
        for s in range(2):
            total = total + mm_nt(dp_ref[s, rows, 0 : 3 * LANES], spread_ref[s, :, 0 : 3 * LANES])
            total = total + mm_nt(
                dp_ref[s, rows, 3 * LANES : 5 * LANES], spread_ref[s, :, 4 * LANES : 6 * LANES]
            )
        return total

    def da_other(i, carry):
        rows = pl.ds(pl.multiple_of(i * BLK, BLK), BLK)
        da_out_ref[rows, :] = da_rows((1 - c) * rows_half + i * BLK).astype(BF16)
        return carry

    lax.fori_loop(0, rows_half // BLK, da_other, 0)
    da_copy = remote(da_out_ref, da_in_ref, pair_send.at[1], pair_recv.at[1], partner)
    da_copy.start()

    def da_own(i, carry):
        rows = pl.ds(pl.multiple_of(i * BLK, BLK), BLK)
        da_own_ref[rows, :] = da_rows(c * rows_half + i * BLK)
        return carry

    lax.fori_loop(0, rows_half // BLK, da_own, 0)
    if not gathered:
        z_start(0, 1)
        z_start(1, 1)
    da_copy.wait()
    gain_attn = extra_ref[columns + 4 : columns + 5, :]
    norm_ref[...] = jnp.zeros_like(norm_ref)

    def finish(i, carry):
        rows = pl.ds(pl.multiple_of(i * BLK, BLK), BLK)
        x = x_ref[rows, :].astype(F32)
        r = lax.rsqrt(jnp.mean(x * x, axis=-1, keepdims=True) + EPSILON)
        normed = x * r
        da = da_own_ref[rows, :] + da_in_ref[rows, :].astype(F32)
        norm_ref[0:1, :] += jnp.sum(da * normed, axis=0, keepdims=True)
        dn = da * gain_attn
        grad = dh_ref[rows, :] + r * (dn - normed * jnp.mean(dn * normed, axis=-1, keepdims=True))
        half_ref[0, rows, :] = grad.astype(BF16)
        return carry

    lax.fori_loop(0, rows_half // BLK, finish, 0)
    norm_copy = remote(norm_ref, norm_in_ref, pair_send.at[2], pair_recv.at[2], partner)
    norm_copy.start()

    def publish(kind, out_ref):
        block = out_ref.at[m, place]
        copies = [
            remote(half_ref.at[kind], block, out_send.at[kind, 0], out_recv.at[kind, 0], across),
            remote(half_ref.at[kind], block, out_send.at[kind, 1], out_recv.at[kind, 1], partner),
            pltpu.make_async_copy(half_ref.at[kind], block, stay.at[3 + kind]),
        ]
        for copy in copies:
            copy.start()
        block = out_ref.at[1 - m, place]
        relay = remote(block, block, out_send.at[kind, 2], out_recv.at[kind, 2], partner)
        return copies, relay

    grad_x_copies, grad_x_relay = publish(0, grad_x_ref)

    settle(2)

    def results(i, carry):
        rows = pl.ds(pl.multiple_of(i * BLK, BLK), BLK)
        far = pl.ds(pl.multiple_of(c * rows_half + i * BLK, BLK), BLK)
        values, e0, e1, wheres, first, second, on_u = facts(far)
        sums, _ = combine(wheres, gy_ref)
        h = h_ref[far, :]
        u = h * values[6] * gain_moe
        result = h + (sums + on_u * u + (first * values[3]) * vec0 + (second * values[5]) * vec1)
        half_ref[1, rows, :] = result.astype(BF16)
        return carry

    lax.fori_loop(0, rows_half // BLK, results, 0)
    result_copies, result_relay = publish(1, result_ref)

    norm_copy.wait()
    row_ref[3:4, :] = norm_ref[0:1, :] + norm_in_ref[0:1, :]
    turned = jnp.concatenate([row_ref[...], jnp.zeros((LANES - 8, width), F32)], axis=0)
    turned = jnp.transpose(turned)
    lane = lax.broadcasted_iota(jnp.int32, (width, LANES), 1)
    lines = line_ref[...]
    for j, source in enumerate([3, 0, 1, 2]):
        lines = jnp.where(lane == columns + 4 + j, turned[:, source : source + 1], lines)
    line_ref[...] = lines
    if gathered:
        stores = [
            pltpu.make_async_copy(pack_ref, grads_ref, load.at[0]),
            pltpu.make_async_copy(line_ref, lines_ref, load.at[1]),
        ]
        for copy in stores:
            copy.start()
        for copy in stores:
            copy.wait()
    else:

        def send(j, carry):
            line_copy(j).start()
            return carry

        lax.fori_loop(1, n, send, 0)
        line_in_ref[d] = line_ref[slab(d), :]
        for s in range(2):
            for stage in range(2):
                for j in range(1, ring):
                    z_copy(s, stage, j).wait()

        def total(s):
            value = pack_ref[s, slab(d), :].astype(F32)
            for j in range(1, ring):
                value = value + z_in_ref[s, j].astype(F32)
            return value

        cross_ref[...] = total(1 - m).astype(BF16)
        cross_copy = remote(cross_ref, cross_in_ref, pair_send.at[3], pair_recv.at[3], across)
        cross_copy.start()
        grads_ref[...] = total(m)

        def arrive_lines(j, carry):
            line_copy(j).wait()
            return carry

        lax.fori_loop(1, n, arrive_lines, 0)
        value = line_in_ref[0]
        for e in range(1, n):
            value = value + line_in_ref[e]
        cross_line_ref[0] = value
        cross_line_copy = remote(
            cross_line_ref.at[0], cross_line_ref.at[1], pair_send.at[4], pair_recv.at[4], across
        )
        cross_line_copy.start()
        cross_copy.wait()
        grads_ref[...] += cross_in_ref[...].astype(F32)
        cross_line_copy.wait()
        lines_ref[...] = cross_line_ref[0] + cross_line_ref[1]

    for copies, relay in ((grad_x_copies, grad_x_relay), (result_copies, result_relay)):
        copies[0].wait_recv()
        relay.start()
    for copies, relay in ((grad_x_copies, grad_x_relay), (result_copies, result_relay)):
        copies[0].wait_send()
        copies[1].wait()
        copies[2].wait()
        relay.wait()
    logit_copy.wait()

    def clear(j, carry):
        for kind in range(3):
            give(kind, j).wait_send()
        return carry

    lax.fori_loop(1, n, clear, 0)

    def passed(j, carry):
        for kind in range(3):
            hand(kind, j).wait_send()
        return carry

    lax.fori_loop(0, n, passed, 0)


def across_chips(value):
    return lax.ppermute(value, "tensor", [(0, 2), (2, 0), (1, 3), (3, 1)])


def across_cores(value):
    return lax.ppermute(value, "tensor", [(0, 1), (1, 0), (2, 3), (3, 2)])


def body(
    tokens,
    cotangent,
    prev_logits,
    routes,
    norm_attn,
    norm_moe,
    w_qkv,
    w_out,
    w_router,
    w_const,
    const_vec,
    w_in,
    w_down,
):
    rows, width = tokens.shape[1:]
    n = lax.axis_size("dp")
    experts = n
    columns = prev_logits.shape[2]
    capacity = 4 * max(1, 3 * rows // (4 * (experts + 4)))
    half = capacity // 2
    padded = -(-half // 16) * 16
    share = w_qkv.shape[2]
    local = 2 * share
    part = w_qkv.shape[1]
    t = lax.axis_index("tensor")
    m, c = t // 2, t % 2

    def mine(value):
        return lax.dynamic_index_in_dim(value, m, 0, keepdims=False)

    x, dy, choose = mine(tokens), mine(cotangent), mine(routes)
    cosine, sine = (jnp.asarray(v) for v in rope_constants())
    pairs = local // LANES

    wo_rows = w_out.T
    packed = jnp.concatenate(
        [w_qkv[i, :, :LANES] for i in range(3)]
        + [wo_rows[:, :LANES]]
        + [w_qkv[i, :, LANES:] for i in range(3)]
        + [
            wo_rows[:, LANES:],
            w_router,
            w_const,
            norm_attn[:, None],
            norm_moe[:, None],
            const_vec.T,
            jnp.zeros((part, LANES - columns - 8), BF16),
        ],
        axis=1,
    )
    gathered = part % 16 != 0
    if gathered:
        packed = lax.all_gather(packed, "dp", axis=0, tiled=True)
        other = across_chips(packed)
        packed = jnp.where(m == 0, jnp.stack([packed, other]), jnp.stack([other, packed]))
    spread_width = packed.shape[-1]
    front_outs = [
        struct((rows, width), BF16),
        struct((pairs, rows, LANES), BF16),
        struct((pairs, rows, LANES), BF16),
        struct((pairs, rows, LANES), BF16),
        struct((rows, width), BF16),
        struct((8, 8, rows), F32),
        struct((rows, width), F32),
        struct((rows, width), BF16),
        struct((rows, LANES), F32),
        struct((rows, LANES), F32),
        struct((width, width), BF16),
        struct((width, LANES), BF16),
        struct((LANES, width), F32),
        struct((2, width, spread_width), BF16),
    ]
    landing = [
        struct((n, padded, width), BF16),
        struct((n, 8, padded), F32),
        struct((n, padded, width), BF16),
    ] + [struct(w_in.shape, BF16)] * 3 + [struct(w_down.shape, BF16)] * 3
    dma = pltpu.SemaphoreType.DMA
    (
        a,
        q,
        k,
        v,
        o_all,
        lse,
        h,
        ub,
        stats,
        pos,
        wo_all,
        small_all,
        extra,
        spread,
        arrived,
        gate_arrived,
        dy_arrived,
        in_c,
        in_x,
        in_d,
        down_c,
        down_x,
        down_d,
    ) = pl.pallas_call(
        functools.partial(front_kernel, n, half, padded, gathered),
        out_shape=front_outs + landing,
        in_specs=[aspec()] * 4 + [vspec()] * 3 + [aspec()] * 2,
        out_specs=[vspec()] * len(front_outs) + [aspec()] * len(landing),
        scratch_shapes=[
            pltpu.VMEM((rows, width), BF16),
            pltpu.VMEM((rows, width), BF16),
            pltpu.VMEM((rows, columns), F32),
            pltpu.VMEM((rows, 2), jnp.int32),
            pltpu.VMEM((LANES, rows), F32),
            pltpu.VMEM((LANES, rows), F32),
            pltpu.VMEM((n, padded, width), BF16),
            pltpu.VMEM((n, 8, padded), F32),
            pltpu.VMEM((n, padded, width), BF16),
            dma((4,)),
            dma((8, n // 2)),
            dma((8, n // 2)),
            dma((n,)),
            dma((n,)),
            dma((n,)),
            dma((n,)),
            dma((n,)),
            dma((n,)),
            dma((3,)),
            dma((pairs + 1,)),
            dma((pairs + 1,)),
            dma((6,)),
            dma((6,)),
        ],
        compiler_params=pltpu.CompilerParams(
            collective_id=0, has_side_effects=True, vmem_limit_bytes=VMEM_LIMIT
        ),
        cost_estimate=pl.CostEstimate(
            flops=60_000_000_000, bytes_accessed=60_000_000, transcendentals=0
        ),
    )(tokens, cotangent, prev_logits, routes, packed, cosine, sine, w_in, w_down)

    hidden_width = w_in.shape[3]
    slots_all = experts * padded
    chunk = min(256 if slots_all <= 1024 else 128, hidden_width)
    per = hidden_width // chunk

    def in_map(i):
        return lambda f: (0, 0, 0, jnp.clip(f - per * i, 0, per - 1))

    def down_map(i):
        return lambda f: (0, jnp.clip(f - per * i, 0, per - 1), 0)

    in_blocks = [pl.BlockSpec((1, 2, width, chunk), in_map(i)) for i in range(4)]
    down_blocks = [pl.BlockSpec((1, chunk, width), down_map(i)) for i in range(4)]
    expert_outs = (
        [
            struct((n, padded, width), BF16),
            struct((n, padded, width), BF16),
            struct((n, 8, padded), F32),
        ]
        + [struct(w_in.shape, BF16)] * 4
        + [struct(w_down.shape, BF16)] * 4
    )

    def whole(shape):
        return pl.BlockSpec(
            shape, lambda f: (0,) * len(shape), pipeline_mode=pl.Buffered(1)
        )

    parts = pl.pallas_call(
        functools.partial(expert_kernel, n, padded),
        grid=(4 * per,),
        out_shape=expert_outs,
        in_specs=[
            whole((slots_all, width)),
            whole((slots_all, width)),
            whole((n, 8, padded)),
        ]
        + in_blocks
        + down_blocks,
        out_specs=[
            whole((n, padded, width)),
            whole((n, padded, width)),
            whole((n, 8, padded)),
        ]
        + in_blocks
        + down_blocks,
        scratch_shapes=[
            pltpu.VMEM((width, slots_all), BF16),
            pltpu.VMEM((slots_all, width), BF16),
            pltpu.VMEM((slots_all, LANES), F32),
            pltpu.VMEM((slots_all, width), F32),
            pltpu.VMEM((slots_all, width), F32),
            pltpu.VMEM((2, width, chunk), BF16),
            pltpu.VMEM((chunk, width), BF16),
        ],
        compiler_params=pltpu.CompilerParams(vmem_limit_bytes=VMEM_LIMIT),
        cost_estimate=pl.CostEstimate(
            flops=18 * slots_all * width * 4 * hidden_width,
            bytes_accessed=30_000_000,
            transcendentals=0,
        ),
    )(
        arrived.reshape(slots_all, width),
        dy_arrived.reshape(slots_all, width),
        gate_arrived,
        w_in,
        in_c,
        in_x,
        in_d,
        w_down,
        down_c,
        down_x,
        down_d,
    )
    gy, dx, dg = parts[0:3]
    gin, gdown = parts[3:7], parts[7:11]
    def chip_part(core, chip, diagonal):
        mine = across_cores(core)
        chip = (chip.astype(F32) + across_cores(diagonal).astype(F32)).astype(BF16)
        return mine, chip

    mine_in, chip_in = chip_part(gin[1], gin[2], gin[3])
    mine_down, chip_down = chip_part(gdown[1], gdown[2], gdown[3])
    chip_in, chip_down, dx = lax.optimization_barrier((chip_in, chip_down, dx))
    grad_in = gin[0].astype(F32) + mine_in.astype(F32) + across_chips(chip_in).astype(F32)
    grad_down = gdown[0].astype(F32) + mine_down.astype(F32) + across_chips(chip_down).astype(F32)

    groups = 6 * LANES
    logit_rows = -(-columns // 8) * 8
    rear_outs = [
        struct((2, logit_rows, rows), F32),
        struct((2, width, groups), BF16) if gathered else struct((part, groups), F32),
        struct((width if gathered else part, LANES), F32),
    ]
    half_rows = rows // 2
    spread_n = 1 if gathered else n // 2
    line_n = 1 if gathered else n
    results, input_grads, logits, grads, lines = pl.pallas_call(
        functools.partial(rear_kernel, n, half, padded, gathered, part),
        out_shape=[struct((2, rows, width), BF16)] * 2 + rear_outs,
        in_specs=[aspec()] * 7 + [vspec()] * 15,
        out_specs=[aspec()] * 2 + [vspec()] + [aspec() if gathered else vspec()] * 2,
        scratch_shapes=[
            pltpu.VMEM((half_rows, width), BF16),
            pltpu.VMEM((rows, width), BF16),
            pltpu.VMEM((rows, 2), jnp.int32),
            pltpu.VMEM((rows, local), BF16),
            pltpu.VMEM((2, n, padded, width), BF16),
            pltpu.VMEM((2, n, padded, width), BF16),
            pltpu.VMEM((2, n, 8, padded), F32),
            pltpu.VMEM((half_rows, width), F32),
            pltpu.VMEM((rows, width), BF16),
            pltpu.VMEM((rows, local), BF16),
            pltpu.VMEM((rows, LANES), BF16),
            pltpu.VMEM((8, width), F32),
            pltpu.VMEM((2, rows, 5 * LANES), BF16),
            pltpu.VMEM((rows, LANES), F32),
            pltpu.VMEM((rows, LANES), F32),
            pltpu.VMEM((width, LANES), F32),
            pltpu.VMEM((2, width, groups), BF16),
            pltpu.VMEM((width, LANES), F32),
            pltpu.VMEM((2, spread_n, part, groups), BF16),
            pltpu.VMEM((2, spread_n, part, groups), BF16),
            pltpu.VMEM((line_n, part, LANES), F32),
            pltpu.VMEM((part, groups), BF16),
            pltpu.VMEM((part, groups), BF16),
            pltpu.VMEM((2, part, LANES), F32),
            pltpu.VMEM((half_rows, width), BF16),
            pltpu.VMEM((half_rows, width), BF16),
            pltpu.VMEM((half_rows, width), F32),
            pltpu.VMEM((8, width), F32),
            pltpu.VMEM((8, width), F32),
            pltpu.VMEM((2, half_rows, width), BF16),
            dma((4,)),
            dma((n,)),
            dma((n,)),
            dma((n,)),
            dma((n,)),
            dma((n,)),
            dma((n,)),
            dma((5,)),
            dma((3, n)),
            dma((3, n)),
            dma((4, 2, n // 2)),
            dma((4, 2, n // 2)),
            dma((n,)),
            dma((n,)),
            dma((5,)),
            dma((5,)),
            dma((2, 3)),
            dma((2, 3)),
        ],
        compiler_params=pltpu.CompilerParams(
            collective_id=1, has_side_effects=True, vmem_limit_bytes=VMEM_LIMIT
        ),
        cost_estimate=pl.CostEstimate(
            flops=100_000_000_000, bytes_accessed=60_000_000, transcendentals=0
        ),
    )(
        gy,
        dx,
        dg,
        tokens,
        cotangent,
        routes,
        o_all,
        h,
        ub,
        stats,
        pos,
        small_all,
        extra,
        wo_all,
        q,
        k,
        v,
        a,
        lse,
        spread,
        cosine,
        sine,
    )
    if gathered:
        grads = lax.psum_scatter(grads.astype(F32), "dp", scatter_dimension=1, tiled=True)
        lines = lax.psum_scatter(lines, "dp", scatter_dimension=0, tiled=True)
        other = lax.dynamic_index_in_dim(grads, 1 - m, 0, keepdims=False)
        grads = lax.dynamic_index_in_dim(grads, m, 0, keepdims=False) + across_chips(other)
        lines = lines + across_chips(lines)

    def heads(j):
        start = (4 + (j % 4) // 2) * LANES + (j % 2) * HD
        return jnp.concatenate(
            [grads[:, j * LANES : (j + 1) * LANES], grads[:, start : start + HD]], axis=1
        )

    return (
        results,
        input_grads,
        jnp.swapaxes(logits[:, :columns], 1, 2),
        lines[:, columns + 4],
        lines[:, columns + 5],
        jnp.stack([heads(i) for i in range(3)]),
        heads(3).T,
        lines[:, :columns],
        lines[:, columns : columns + 4],
        lines[:, columns + 6 : columns + 8].T,
        grad_in,
        grad_down,
    )


def solution(mesh):
    in_specs = (
        P(None, "dp", None),
        P(None, "dp", None),
        P(None, "dp", None),
        P(None, "dp", None),
        P("dp"),
        P("dp"),
        P(None, "dp", "tensor"),
        P("tensor", "dp"),
        P("dp", None),
        P("dp", None),
        P(None, "dp"),
        P("dp", None, None, "tensor"),
        P("dp", "tensor", None),
    )
    out_specs = (
        P(None, "dp", None),
        P(None, "dp", None),
        P(None, "dp", None),
        P("dp"),
        P("dp"),
        P(None, "dp", "tensor"),
        P("tensor", "dp"),
        P("dp", None),
        P("dp", None),
        P(None, "dp"),
        P("dp", None, None, "tensor"),
        P("dp", "tensor", None),
    )
    return jax.shard_map(body, mesh=mesh, in_specs=in_specs, out_specs=out_specs, check_vma=False)
```

```python
import functools

import jax
import jax.numpy as jnp
import numpy as np
from jax import lax
from jax.experimental import pallas as pl
from jax.experimental.pallas import tpu as pltpu
from jax.sharding import PartitionSpec as P

HD = 64
LEN = 1024
BLK = 256
EPSILON = 1e-06
LANES = 128
F32 = jnp.float32
BF16 = jnp.bfloat16
MESH = pl.DeviceIdType.MESH
VMEM_LIMIT = 60 * 1024 * 1024


def mm(a, b):
    return lax.dot_general(a, b, (((1,), (0,)), ((), ())), preferred_element_type=F32)


def mm_nt(a, b):
    return lax.dot_general(a, b, (((1,), (1,)), ((), ())), preferred_element_type=F32)


def mm_tn(a, b):
    return lax.dot_general(a, b, (((0,), (0,)), ((), ())), preferred_element_type=F32)


def vspec():
    return pl.BlockSpec(memory_space=pltpu.VMEM)


def aspec():
    return pl.BlockSpec(memory_space=pl.ANY)


def struct(shape, dtype):
    return jax.ShapeDtypeStruct(shape, dtype)


def greet(peers):
    barrier = pltpu.get_barrier_semaphore()
    for peer in peers:
        pl.semaphore_signal(barrier, inc=1, device_id=peer, device_id_type=MESH)
    pl.semaphore_wait(barrier, len(peers))


def remote(src, dst, send, recv, peer):
    return pltpu.make_async_remote_copy(
        src_ref=src,
        dst_ref=dst,
        send_sem=send,
        recv_sem=recv,
        device_id=peer,
        device_id_type=MESH,
    )


def plane_peers(n, d, t):
    return [(lax.rem(d + j, n), t) for j in range(1, n)]


def slot_hot(half, padded, base, places):
    rows = places.shape[1]
    slot = lax.broadcasted_iota(jnp.int32, (padded, rows), 0)
    wanted = jnp.where(slot < half, slot + base, -2).astype(F32)
    return (wanted == places).astype(F32).astype(BF16)


def rope_constants():
    half = HD // 2
    frequency = 10000.0 ** (-2.0 * np.arange(half) / HD)
    angle = np.arange(LEN)[:, None] * frequency[None, :]
    cosine, sine = np.cos(angle), np.sin(angle)
    cosine = np.concatenate([cosine, cosine, cosine, cosine], axis=1)
    sine = np.concatenate([-sine, sine, -sine, sine], axis=1)
    return cosine.astype(np.float32), sine.astype(np.float32)


def turn(field, cosine, sine):
    lane = lax.broadcasted_iota(jnp.int32, field.shape, 1)
    other = jnp.where(
        lax.rem(lane, HD) < HD // 2,
        pltpu.roll(field, LANES - HD // 2, 1),
        pltpu.roll(field, HD // 2, 1),
    )
    return field * cosine + other * sine


def pick(hot, values):
    return jnp.sum(jnp.where(hot, values, 0.0), axis=-1, keepdims=True)


def lane_ids(rows):
    return lax.broadcasted_iota(jnp.int32, (rows, LANES), 1)


def soft_pair(first, second):
    high = jnp.maximum(first, second)
    e0, e1 = jnp.exp(first - high), jnp.exp(second - high)
    return e0 / (e0 + e1), e1 / (e0 + e1)


def half_mask(rows):
    return lax.broadcasted_iota(jnp.int32, (rows, LANES), 1) < HD


def swap_halves(value):
    return pltpu.roll(value, HD, 1)


def front_kernel(
    n,
    half,
    padded,
    gathered,
    tokens_ref,
    cotangent_ref,
    prev_all_ref,
    routes_all_ref,
    packed_ref,
    cos_ref,
    sin_ref,
    win_ref,
    wdown_ref,
    a_ref,
    q_ref,
    k_ref,
    v_ref,
    o_ref,
    lse_ref,
    h_ref,
    ub_ref,
    stat_ref,
    pos_ref,
    wo_ref,
    small_ref,
    extra_ref,
    spread_ref,
    slot_ref,
    gate_ref,
    dy_arrived_ref,
    in_c_ref,
    in_x_ref,
    in_d_ref,
    down_c_ref,
    down_x_ref,
    down_d_ref,
    x_ref,
    dy_ref,
    prev_ref,
    routes_ref,
    place_ref,
    gates_ref,
    dy_slot_ref,
    load,
    pack_send,
    pack_recv,
    dy_send,
    dy_recv,
    stay,
    core_send,
    core_recv,
    w_send,
    w_recv,
):
    rows_all, width = x_ref.shape
    blocks = rows_all // BLK
    pairs = q_ref.shape[0]
    local = pairs * LANES
    columns = prev_ref.shape[1]
    d, t = lax.axis_index("dp"), lax.axis_index("tensor")
    m, c = lax.div(t, 2), lax.rem(t, 2)
    partner = (d, t + 1 - 2 * c)
    across = (d, lax.rem(t + 2, 4))
    loads = [
        pltpu.make_async_copy(src.at[m], dst, load.at[i])
        for i, (src, dst) in enumerate(
            [
                (routes_all_ref, routes_ref),
                (cotangent_ref, dy_ref),
                (tokens_ref, x_ref),
                (prev_all_ref, prev_ref),
            ]
        )
    ]
    for copy in loads:
        copy.start()
    greet(plane_peers(n, d, t) + [partner, across])
    part = packed_ref.shape[0]
    beside = (d + 1 - 2 * lax.rem(d, 2), t)
    lanes_a = pl.ds(0, 4 * LANES)
    lanes_b = pl.ds(4 * LANES, packed_ref.shape[-1] - 4 * LANES)

    def behind(j):
        return lax.rem(d + n - 2 * j, n)

    def shard(chip, owner, lanes):
        return spread_ref.at[chip, pl.ds(pl.multiple_of(owner * part, part), part), lanes]

    def pass_on(chip, owner, lanes, row, j, peer):
        block = shard(chip, owner, lanes)
        return remote(block, block, pack_send.at[row, j], pack_recv.at[row, j], peer)

    def ahead(j):
        return (lax.rem(d + 2 * j, n), t)

    ring = n // 2
    if gathered:
        spread_ref[...] = packed_ref[...]
    else:
        spread_ref[m, pl.ds(pl.multiple_of(d * part, part), part), :] = packed_ref[...]
        a_x = pass_on(m, d, lanes_a, 4, 0, across)
        sends = [a_x]
        for j in range(1, ring):
            sends.append(pass_on(m, d, lanes_a, 0, j, ahead(j)))
            sends.append(pass_on(m, d, lanes_b, 4, j, ahead(j)))
        sends.append(pass_on(m, d, lanes_a, 2, 0, beside))
        sends.append(pass_on(m, d, lanes_b, 5, 0, beside))
        sends.append(pass_on(m, d, lanes_b, 6, 0, across))
        for copy in sends:
            copy.start()

    def relay_gather():
        if gathered:
            return
        a_x.wait_recv()
        more = [pass_on(1 - m, d, lanes_a, 1, j, ahead(j)) for j in range(1, ring)]
        more.append(pass_on(1 - m, d, lanes_a, 3, 0, beside))
        for copy in more:
            copy.start()
        sends.extend(more)
        for j in range(1, ring):
            pass_on(m, d, lanes_b, 4, j, ahead(j)).wait_recv()
            more = [
                pass_on(m, behind(j), lanes_b, 5, j, beside),
                pass_on(m, behind(j), lanes_b, 6, j, across),
            ]
            pass_on(m, d, lanes_a, 0, j, ahead(j)).wait_recv()
            more.append(pass_on(m, behind(j), lanes_a, 2, j, beside))
            for copy in more:
                copy.start()
            sends.extend(more)
        for j in range(1, ring):
            pass_on(1 - m, d, lanes_a, 1, j, ahead(j)).wait_recv()
            copy = pass_on(1 - m, behind(j), lanes_a, 3, j, beside)
            copy.start()
            sends.append(copy)
        for j in range(ring):
            pass_on(m, d, lanes_b, 5, j, beside).wait_recv()
            owner = lax.rem(beside[0] + n - 2 * j, n)
            copy = pass_on(m, owner, lanes_b, 7, j, across)
            copy.start()
            sends.append(copy)
        for j in range(ring):
            pass_on(m, d, lanes_a, 2, j, beside).wait_recv()
            pass_on(m, d, lanes_a, 3, j, beside).wait_recv()
            pass_on(m, d, lanes_b, 6, j, across).wait_recv()
            pass_on(m, d, lanes_b, 7, j, across).wait_recv()

    loads[0].wait()
    line = lax.broadcasted_iota(jnp.int32, (rows_all, LANES), 1)
    named = jnp.where(
        line == 0,
        routes_ref[:, 0:1].astype(F32),
        jnp.where(line == 1, routes_ref[:, 1:2].astype(F32), 0.0),
    )
    named = jnp.transpose(named)
    ids = lax.broadcasted_iota(jnp.int32, (LANES, rows_all), 0).astype(F32)
    hit = ((ids == named[0:1, :]) | (ids == named[1:2, :])) & (ids < float(n))
    before = lax.broadcasted_iota(jnp.int32, (rows_all, rows_all), 0) < lax.broadcasted_iota(
        jnp.int32, (rows_all, rows_all), 1
    )
    count = mm(hit.astype(F32).astype(BF16), before.astype(F32).astype(BF16))
    places = jnp.where(hit, count, -1.0)
    place_ref[...] = places
    pos_ref[...] = jnp.transpose(places)
    base = c * half

    def dy_copy(j):
        e = lax.rem(d + j, n)
        return remote(
            dy_slot_ref.at[e], dy_arrived_ref.at[d], dy_send.at[j], dy_recv.at[j], (e, t)
        )

    stays = [pltpu.make_async_copy(dy_slot_ref.at[d], dy_arrived_ref.at[d], stay.at[0])]
    loads[1].wait()

    def dy_step(i, carry):
        j = lax.rem(i + 1, n)
        e = lax.rem(d + j, n)
        hot = slot_hot(half, padded, base, place_ref[pl.ds(e, 1), :])
        dy_slot_ref[e] = mm(hot, dy_ref[...]).astype(BF16)
        return carry

    lax.fori_loop(0, n, dy_step, 0)
    relay_gather()
    stays[0].start()

    def dy_start(j, carry):
        dy_copy(j).start()
        return carry

    lax.fori_loop(1, n, dy_start, 0)
    weight_copies = [
        remote(win_ref, in_x_ref, w_send.at[0], w_recv.at[0], across),
        remote(wdown_ref, down_x_ref, w_send.at[1], w_recv.at[1], across),
        remote(win_ref, in_c_ref, w_send.at[2], w_recv.at[2], partner),
        remote(wdown_ref, down_c_ref, w_send.at[3], w_recv.at[3], partner),
        remote(in_x_ref, in_d_ref, w_send.at[4], w_recv.at[4], partner),
        remote(down_x_ref, down_d_ref, w_send.at[5], w_recv.at[5], partner),
    ]
    for copy in weight_copies[0:4]:
        copy.start()

    table = spread_ref[0, :, 6 * LANES : 7 * LANES]
    extra_ref[...] = jnp.transpose(table.astype(F32))
    keep = lax.broadcasted_iota(jnp.int32, (width, LANES), 1) < columns + 4
    small_ref[...] = jnp.where(keep, table, jnp.zeros_like(table))
    mask = half_mask(width)
    own = pl.multiple_of(c * local, LANES)
    wo_ref[:, pl.ds(own, LANES)] = spread_ref[0, :, 3 * LANES : 4 * LANES]
    wo_ref[:, pl.ds(own + LANES, LANES)] = spread_ref[1, :, 3 * LANES : 4 * LANES]
    wo_ref[:, pl.ds(own + 2 * LANES, LANES)] = jnp.where(
        mask,
        swap_halves(spread_ref[0, :, 5 * LANES : 6 * LANES].astype(F32)),
        spread_ref[1, :, 5 * LANES : 6 * LANES].astype(F32),
    ).astype(BF16)
    own_lanes = pl.ds(own, local)
    wo_copy = remote(
        wo_ref.at[:, own_lanes],
        wo_ref.at[:, own_lanes],
        core_send.at[pairs],
        core_recv.at[pairs],
        partner,
    )
    wo_copy.start()

    loads[2].wait()
    gain = extra_ref[columns + 4 : columns + 5, :]
    head = half_mask(BLK)

    def project(i, carry):
        rows = pl.ds(pl.multiple_of(i * BLK, BLK), BLK)
        x = x_ref[rows, :].astype(F32)
        r = lax.rsqrt(jnp.mean(x * x, axis=-1, keepdims=True) + EPSILON)
        a = (x * r * gain).astype(BF16)
        a_ref[rows, :] = a
        cosine, sine = cos_ref[rows, :], sin_ref[rows, :]

        def put(pair, q, k, v):
            q_ref[pair, rows, :] = turn(q, cosine, sine).astype(BF16) * BF16(HD**-0.5)
            k_ref[pair, rows, :] = turn(k, cosine, sine).astype(BF16)
            v_ref[pair, rows, :] = v.astype(BF16)

        odd = []
        for s in range(2):
            both = mm(a, spread_ref[s, :, 0 : 3 * LANES])
            put(s, *(both[:, j * LANES : (j + 1) * LANES] for j in range(3)))
            both = mm(a, spread_ref[s, :, 4 * LANES : 6 * LANES])
            odd.append((both[:, :LANES], both[:, LANES:]))
        put(
            2,
            jnp.where(head, odd[0][0], swap_halves(odd[1][0])),
            jnp.where(head, swap_halves(odd[0][0]), odd[1][0]),
            jnp.where(head, odd[0][1], swap_halves(odd[1][1])),
        )
        return carry

    lax.fori_loop(0, blocks, project, 0)

    def o_copy(p):
        lanes = pl.ds(pl.multiple_of(own + p * LANES, LANES), LANES)
        return remote(
            o_ref.at[:, lanes], o_ref.at[:, lanes], core_send.at[p], core_recv.at[p], partner
        )

    def attend(p, carry):
        lanes = pl.ds(pl.multiple_of(own + p * LANES, LANES), LANES)
        for i in range(blocks):
            rows = pl.ds(i * BLK, BLK)
            seen = pl.ds(0, (i + 1) * BLK)
            q, k, v = q_ref[p, rows, :], k_ref[p, seen, :], v_ref[p, seen, :]
            halves = []
            for side in range(2):
                chosen = head if side == 0 else jnp.logical_not(head)
                s = mm_nt(jnp.where(chosen, q, jnp.zeros_like(q)), k)
                high = jnp.max(s, axis=-1, keepdims=True)
                e = jnp.exp(s - high)
                total = jnp.sum(e, axis=-1, keepdims=True)
                halves.append(mm((e / total).astype(BF16), v))
                log_total = jnp.broadcast_to(high + jnp.log(total), (BLK, LANES))
                lse_ref[2 * p + side, :, rows] = jnp.transpose(log_total)[0:8, :]
            o_ref[rows, lanes] = jnp.where(head, halves[0], halves[1]).astype(BF16)
        o_copy(p).start()
        return carry

    lax.fori_loop(0, pairs, attend, 0)
    loads[3].wait()
    wo_copy.wait()
    for p in range(pairs):
        o_copy(p).wait()

    gain_moe = extra_ref[columns + 5 : columns + 6, :]

    def middle(i, carry):
        rows = pl.ds(pl.multiple_of(i * BLK, BLK), BLK)
        z = mm_nt(o_ref[rows, :], wo_ref[...])
        h = x_ref[rows, :].astype(F32) + z
        r = lax.rsqrt(jnp.mean(h * h, axis=-1, keepdims=True) + EPSILON)
        ub = (h * r * gain_moe).astype(BF16)
        h_ref[rows, :] = h
        ub_ref[rows, :] = ub
        scores = mm(ub, small_ref[...])
        lane = lane_ids(BLK)
        e0, e1 = routes_ref[rows, 0:1], routes_ref[rows, 1:2]
        hot0, hot1 = lane == e0, lane == e1
        prev = prev_ref[rows, :]
        few = lax.broadcasted_iota(jnp.int32, (BLK, columns), 1)
        g0, g1 = soft_pair(
            pick(hot0, scores) + pick(few == e0, prev), pick(hot1, scores) + pick(few == e1, prev)
        )
        mix = [pick(lane == columns + j, scores) for j in range(4)]
        a00, a01 = soft_pair(mix[0], mix[1])
        a10, a11 = soft_pair(mix[2], mix[3])
        table = jnp.zeros((BLK, LANES), F32)
        for j, value in enumerate([g0, g1, a00, a01, a10, a11, r]):
            table = jnp.where(lane == j, value, table)
        stat_ref[rows, :] = table
        gates = jnp.where(hot0, g0, 0.0) + jnp.where(hot1, g1, 0.0)
        gates_ref[:, rows] = jnp.transpose(gates)
        return carry

    lax.fori_loop(0, blocks, middle, 0)
    piece = lax.broadcasted_iota(jnp.int32, (8, rows_all), 0)

    def slot_step(i, carry):
        j = lax.rem(i + 1, n)
        e = lax.rem(d + j, n)
        hot = slot_hot(half, padded, base, place_ref[pl.ds(e, 1), :])
        slot_ref[e] = mm(hot, ub_ref[...]).astype(BF16)
        gate = gates_ref[pl.ds(e, 1), :]
        high = gate.astype(BF16).astype(F32)
        mid = (gate - high).astype(BF16).astype(F32)
        low = gate - high - mid
        lines = jnp.where(piece == 0, high, jnp.where(piece == 1, mid, low))
        lines = jnp.where(piece < 3, lines, 0.0).astype(BF16)
        gate = jnp.sum(mm_nt(lines, hot), axis=0, keepdims=True)
        gate_ref[e] = jnp.broadcast_to(gate, (8, padded))
        return carry

    lax.fori_loop(0, n, slot_step, 0)
    weight_copies[0].wait_recv()
    weight_copies[1].wait_recv()
    weight_copies[4].start()
    weight_copies[5].start()

    def finish(j, carry):
        dy_copy(j).wait()
        return carry

    lax.fori_loop(1, n, finish, 0)
    for copy in stays:
        copy.wait()
    for copy in ([] if gathered else sends) + weight_copies[0:2]:
        copy.wait_send()
    for copy in weight_copies[2:6]:
        copy.wait()


def flip(value, index, size):
    bit = 1
    while bit < size:
        chosen = lax.rem(lax.div(index, bit), 2)
        value = value + chosen * (bit - 2 * bit * lax.rem(lax.div(value, bit), 2))
        bit *= 2
    return value


def expert_exchange_kernel(
    n,
    padded,
    slot_src_ref,
    gate_src_ref,
    dy_src_ref,
    in_own_ref,
    in_core_ref,
    in_chip_ref,
    in_diag_ref,
    down_own_ref,
    down_core_ref,
    down_chip_ref,
    down_diag_ref,
    gy_ref,
    own_in_ref,
    own_down_ref,
    chip_in_ref,
    chip_down_ref,
    dx_all_ref,
    dg_all_ref,
    x_ref,
    xt_ref,
    dy_ref,
    scaled_ref,
    scale_ref,
    gate_ref,
    win_ref,
    wdown_ref,
    hidden_ref,
    dgate_ref,
    dup_ref,
    y_ref,
    dx_ref,
    dg_ref,
    land_in_ref,
    land_down_ref,
    load,
    slot_send,
    slot_recv,
    gate_send,
    gate_recv,
    dx_send,
    dx_recv,
    dg_send,
    dg_recv,
    pass_send,
    pass_recv,
    sum_send,
    sum_recv,
):
    width = x_ref.shape[1]
    share = win_ref.shape[3]
    chunks = 4
    group = n // chunks
    span = group * padded
    block = 256
    d, t = lax.axis_index("dp"), lax.axis_index("tensor")
    c = lax.rem(t, 2)
    partner = (d, t + 1 - 2 * c)
    greet(plane_peers(n, d, t) + [partner])

    def rows_of(i):
        return pl.ds(pl.multiple_of(i * padded, padded), padded)

    def slot_copy(i):
        e = flip(d, i, n)
        return remote(
            slot_src_ref.at[e], x_ref.at[rows_of(i)], slot_send.at[i], slot_recv.at[i], (e, t)
        )

    def gate_copy(i):
        e = flip(d, i, n)
        return remote(
            gate_src_ref.at[e], gate_ref.at[i], gate_send.at[i], gate_recv.at[i], (e, t)
        )

    def dx_copy(i):
        e = flip(d, i, n)
        return remote(
            dx_ref.at[rows_of(i)], dx_all_ref.at[c, d], dx_send.at[i], dx_recv.at[i], (e, t)
        )

    def dg_copy(i):
        e = flip(d, i, n)
        return remote(dg_ref.at[i], dg_all_ref.at[c, d], dg_send.at[i], dg_recv.at[i], (e, t))

    def hand(kind, i):
        ref = (dx_all_ref, dg_all_ref)[kind]
        block_ref = ref.at[c, flip(d, i, n)]
        return remote(
            block_ref, block_ref, pass_send.at[kind, i], pass_recv.at[kind, i], partner
        )

    def send_chunk(k, carry):
        for q in range(group):
            i = (chunks - 1 - k) * group + q

            @pl.when(i > 0)
            def _():
                slot_copy(i).start()
                gate_copy(i).start()

        return carry

    lax.fori_loop(0, chunks, send_chunk, 0)
    stays = [
        pltpu.make_async_copy(slot_src_ref.at[d], x_ref.at[rows_of(0)], load.at[0]),
        pltpu.make_async_copy(gate_src_ref.at[d], gate_ref.at[0], load.at[1]),
    ]
    loads = []
    for s, (win, down) in enumerate(
        [
            (in_own_ref, down_own_ref),
            (in_core_ref, down_core_ref),
            (in_chip_ref, down_chip_ref),
            (in_diag_ref, down_diag_ref),
        ]
    ):
        loads.append(pltpu.make_async_copy(win.at[0], win_ref.at[s], load.at[2 + s]))
        loads.append(
            pltpu.make_async_copy(
                down.at[0], wdown_ref.at[pl.ds(s * share, share)], load.at[6 + s]
            )
        )

    def dy_load(i):
        return pltpu.make_async_copy(
            dy_src_ref.at[flip(d, i, n)], dy_ref.at[rows_of(i)], load.at[10 + i]
        )

    for copy in stays + loads:
        copy.start()
    for i in range(n):
        dy_load(i).start()
    for copy in stays + loads:
        copy.wait()

    def chunk(k, carry):
        rows = pl.ds(pl.multiple_of(k * span, span), span)
        for q in range(group):
            i = k * group + q

            @pl.when(i > 0)
            def _():
                slot_copy(i).wait_recv()
                gate_copy(i).wait_recv()

            dy_load(i).wait()
            near = rows_of(i)
            line = jnp.broadcast_to(gate_ref[i, 0:1, :], (LANES, padded))
            scale = jnp.transpose(line)
            scale_ref[near, :] = scale
            scaled_ref[near, :] = (dy_ref[near, :].astype(F32) * scale[:, 0:1]).astype(BF16)
        x = x_ref[rows, :]
        xt_ref[:, rows] = jnp.transpose(x)
        scaled = scaled_ref[rows, :]
        for s in range(4):

            def unit(b, carry, s=s):
                lanes = pl.ds(pl.multiple_of(b * block, block), block)
                far = pl.ds(pl.multiple_of(s * share + b * block, block), block)
                gate = mm(x, win_ref[s, 0, :, lanes])
                up = mm(x, win_ref[s, 1, :, lanes])
                grad = mm_nt(scaled, wdown_ref[far, :])
                sigma = 1.0 / (1.0 + jnp.exp(-gate))
                active = gate * sigma
                hidden_ref[rows, far] = (active * up).astype(BF16)
                dgate_ref[rows, far] = (
                    grad * up * (sigma * (1.0 + gate * (1.0 - sigma)))
                ).astype(BF16)
                dup_ref[rows, far] = (grad * active).astype(BF16)
                return carry

            lax.fori_loop(0, share // block, unit, 0)
        for j in range(width // block):
            lanes = pl.ds(j * block, block)
            total = jnp.zeros((span, block), F32)
            for s in range(4):
                far = pl.ds(s * share, share)
                total = total + mm_nt(dgate_ref[rows, far], win_ref[s, 0, lanes, :])
                total = total + mm_nt(dup_ref[rows, far], win_ref[s, 1, lanes, :])
            dx_ref[rows, lanes] = total.astype(BF16)
        for q in range(group):
            i = k * group + q

            @pl.when(i > 0)
            def _():
                dx_copy(i).start()

        for j in range(width // block):
            lanes = pl.ds(j * block, block)
            y_ref[:, lanes] = mm(hidden_ref[rows, :], wdown_ref[:, lanes])
        for q in range(group):
            i = k * group + q
            near = rows_of(i)
            y = y_ref[pl.ds(q * padded, padded), :]
            gy_ref[flip(d, i, n)] = (y * scale_ref[near, 0:1]).astype(BF16)
            dot = jnp.sum(y * dy_ref[near, :].astype(F32), axis=-1, keepdims=True)
            dg_ref[i] = jnp.transpose(jnp.broadcast_to(dot, (padded, LANES)))[0:8, :]

            @pl.when(i > 0)
            def _():
                dg_copy(i).start()

        return carry

    lax.fori_loop(0, chunks, chunk, 0)
    keeps = [
        pltpu.make_async_copy(dx_ref.at[rows_of(0)], dx_all_ref.at[c, d], load.at[0]),
        pltpu.make_async_copy(dg_ref.at[0], dg_all_ref.at[c, d], load.at[1]),
    ]
    for copy in keeps:
        copy.start()

    def forward(first, last):
        def step(i, carry):
            dx_copy(i).wait_recv()
            dg_copy(i).wait_recv()
            hand(0, i).start()
            hand(1, i).start()
            return carry

        lax.fori_loop(first, last, step, 0)

    def grad_in(s, kind, b):
        far = pl.ds(pl.multiple_of(s * share + b * block, block), block)
        return mm(xt_ref[...], (dgate_ref, dup_ref)[kind][:, far])

    def grad_down(s, b):
        far = pl.ds(pl.multiple_of(s * share + b * block, block), block)
        return mm_tn(hidden_ref[:, far], scaled_ref[...])

    def sums(s, put_in, put_down):
        def unit(b, carry):
            lanes = pl.ds(pl.multiple_of(b * block, block), block)
            for kind in range(2):
                put_in(kind, lanes, grad_in(s, kind, b))
            put_down(lanes, grad_down(s, b))
            return carry

        lax.fori_loop(0, share // block, unit, 0)

    def sum_copies(j):
        return [
            remote(win_ref.at[j], land_in_ref.at[j], sum_send.at[j], sum_recv.at[j], partner),
            remote(
                wdown_ref.at[pl.ds(j * share, share)],
                land_down_ref.at[j],
                sum_send.at[2 + j],
                sum_recv.at[2 + j],
                partner,
            ),
        ]

    for j, s in enumerate((3, 1)):

        def put_in(kind, lanes, value, j=j):
            win_ref[j, kind, :, lanes] = value.astype(BF16)

        def put_down(rows, value, j=j):
            near = pl.multiple_of(rows.start + j * share, block)
            wdown_ref[pl.ds(near, block), :] = value.astype(BF16)

        sums(s, put_in, put_down)
        for copy in sum_copies(j):
            copy.start()
        if j == 0:
            for copy in keeps:
                copy.wait()
            hand(0, 0).start()
            hand(1, 0).start()
            forward(1, group)

    forward(group, 2 * group)
    for copy in sum_copies(0):
        copy.wait_recv()

    def chip_in(kind, lanes, value):
        chip_in_ref[0, kind, :, lanes] = (
            value + land_in_ref[0, kind, :, lanes].astype(F32)
        ).astype(BF16)

    def chip_down(lanes, value):
        chip_down_ref[0, lanes, :] = (value + land_down_ref[0, lanes, :].astype(F32)).astype(BF16)

    sums(2, chip_in, chip_down)
    for copy in sum_copies(1):
        copy.wait_recv()

    def own_in(kind, lanes, value):
        own_in_ref[0, kind, :, lanes] = value + land_in_ref[1, kind, :, lanes].astype(F32)

    def own_down(lanes, value):
        own_down_ref[0, lanes, :] = value + land_down_ref[1, lanes, :].astype(F32)

    sums(0, own_in, own_down)
    forward(2 * group, n)

    def clear(i, carry):
        for copy in (slot_copy(i), gate_copy(i), dx_copy(i), dg_copy(i)):
            copy.wait_send()
        return carry

    lax.fori_loop(1, n, clear, 0)

    def passed(i, carry):
        hand(0, i).wait()
        hand(1, i).wait()
        return carry

    lax.fori_loop(0, n, passed, 0)
    for j in range(2):
        for copy in sum_copies(j):
            copy.wait_send()


def expert_kernel(
    sources,
    padded,
    x_ref,
    dy_ref,
    gate_ref,
    *refs,
):
    weights, outs = refs[:8], refs[8:19]
    in_refs, down_refs = weights[0:4], weights[4:8]
    gy_ref, dx_ref, dg_ref = outs[0:3]
    gin_refs, gdown_refs = outs[3:7], outs[7:11]
    xt_ref, scaled_ref, scale_ref, y_acc, dx_acc, win_ref, wdown_ref = refs[19:]
    step = pl.program_id(0)
    last = pl.num_programs(0) - 1

    @pl.when(step == 0)
    def _():
        xt_ref[...] = jnp.transpose(x_ref[...])
        for s in range(sources):
            rows = pl.ds(s * padded, padded)
            line = jnp.broadcast_to(gate_ref[s, 0:1, :], (LANES, padded))
            scale = jnp.transpose(line)
            scale_ref[rows, :] = scale
            scaled_ref[rows, :] = (dy_ref[rows, :].astype(F32) * scale[:, 0:1]).astype(BF16)
        y_acc[...] = jnp.zeros_like(y_acc)
        dx_acc[...] = jnp.zeros_like(dx_acc)

    per = pl.num_programs(0) // 4
    for i in range(4):

        @pl.when(lax.div(step, per) == i)
        def _():
            win_ref[...] = in_refs[i][0]
            wdown_ref[...] = down_refs[i][0]

    x = x_ref[...]
    gate = mm(x, win_ref[0])
    up = mm(x, win_ref[1])
    sigma = 1.0 / (1.0 + jnp.exp(-gate))
    active = gate * sigma
    hidden = (active * up).astype(BF16)
    y_acc[...] += mm(hidden, wdown_ref[...])
    scaled = scaled_ref[...]
    grad_hidden = mm_nt(scaled, wdown_ref[...])
    grad_gate = (grad_hidden * up * (sigma * (1.0 + gate * (1.0 - sigma)))).astype(BF16)
    grad_up = (grad_hidden * active).astype(BF16)
    dx_acc[...] += mm_nt(grad_gate, win_ref[0]) + mm_nt(grad_up, win_ref[1])
    xt = xt_ref[...]
    part_gate = mm(xt, grad_gate).astype(BF16)
    part_up = mm(xt, grad_up).astype(BF16)
    part_down = mm_tn(hidden, scaled).astype(BF16)
    for i in range(4):

        @pl.when(lax.div(step, per) == i)
        def _():
            gin_refs[i][0, 0] = part_gate
            gin_refs[i][0, 1] = part_up
            gdown_refs[i][0] = part_down

    @pl.when(step == last)
    def _():
        for s in range(sources):
            rows = pl.ds(s * padded, padded)
            y = y_acc[rows, :]
            gy_ref[s] = (y * scale_ref[rows, 0:1]).astype(BF16)
            dot = jnp.sum(y * dy_ref[rows, :].astype(F32), axis=-1, keepdims=True)
            dg_ref[s] = jnp.transpose(jnp.broadcast_to(dot, (padded, LANES)))[0:8, :]
            dx_ref[s] = dx_acc[rows, :].astype(BF16)


def rear_kernel(
    n,
    half,
    padded,
    gathered,
    part,
    *refs,
):
    count = 0 if gathered else 2
    sums, refs = refs[: 2 * count], refs[2 * count :]
    totals, rest = refs[27 : 27 + count], refs[27 + count :]
    rear_body(n, half, padded, gathered, part, sums, totals, *refs[:27], *rest)


def rear_body(
    n,
    half,
    padded,
    gathered,
    part,
    sum_refs,
    total_refs,
    gy_src_ref,
    dx_ref,
    dg_ref,
    tokens_ref,
    cotangent_ref,
    routes_all_ref,
    o_all_ref,
    h_ref,
    ub_ref,
    stat_ref,
    pos_ref,
    small_ref,
    extra_ref,
    wo_ref,
    q_ref,
    k_ref,
    v_ref,
    a_ref,
    lse_ref,
    spread_ref,
    cos_ref,
    sin_ref,
    result_ref,
    grad_x_ref,
    logit_ref,
    grads_ref,
    lines_ref,
    x_ref,
    dy_ref,
    routes_ref,
    o_ref,
    gy_ref,
    dh_ref,
    dzb_ref,
    do_ref,
    low_ref,
    row_ref,
    dp_ref,
    dk_acc,
    dv_acc,
    wo_odd_ref,
    pack_ref,
    line_ref,
    y_in_ref,
    z_in_ref,
    line_in_ref,
    cross_ref,
    cross_in_ref,
    cross_line_ref,
    da_out_ref,
    da_in_ref,
    da_own_ref,
    norm_ref,
    norm_in_ref,
    half_ref,
    *more,
):
    if gathered:
        stages, lands = (), ()
    else:
        stages, lands, more = more[0:2], more[2:4], more[4:]
    rear_steps(
        n,
        half,
        padded,
        gathered,
        part,
        (sum_refs, total_refs, stages, lands),
        gy_src_ref,
        dx_ref,
        dg_ref,
        tokens_ref,
        cotangent_ref,
        routes_all_ref,
        o_all_ref,
        h_ref,
        ub_ref,
        stat_ref,
        pos_ref,
        small_ref,
        extra_ref,
        wo_ref,
        q_ref,
        k_ref,
        v_ref,
        a_ref,
        lse_ref,
        spread_ref,
        cos_ref,
        sin_ref,
        result_ref,
        grad_x_ref,
        logit_ref,
        grads_ref,
        lines_ref,
        x_ref,
        dy_ref,
        routes_ref,
        o_ref,
        gy_ref,
        dh_ref,
        dzb_ref,
        do_ref,
        low_ref,
        row_ref,
        dp_ref,
        dk_acc,
        dv_acc,
        wo_odd_ref,
        pack_ref,
        line_ref,
        y_in_ref,
        z_in_ref,
        line_in_ref,
        cross_ref,
        cross_in_ref,
        cross_line_ref,
        da_out_ref,
        da_in_ref,
        da_own_ref,
        norm_ref,
        norm_in_ref,
        half_ref,
        *more,
    )


def rear_steps(
    n,
    half,
    padded,
    gathered,
    part,
    sums,
    gy_src_ref,
    dx_ref,
    dg_ref,
    tokens_ref,
    cotangent_ref,
    routes_all_ref,
    o_all_ref,
    h_ref,
    ub_ref,
    stat_ref,
    pos_ref,
    small_ref,
    extra_ref,
    wo_ref,
    q_ref,
    k_ref,
    v_ref,
    a_ref,
    lse_ref,
    spread_ref,
    cos_ref,
    sin_ref,
    result_ref,
    grad_x_ref,
    logit_ref,
    grads_ref,
    lines_ref,
    x_ref,
    dy_ref,
    routes_ref,
    o_ref,
    gy_ref,
    dh_ref,
    dzb_ref,
    do_ref,
    low_ref,
    row_ref,
    dp_ref,
    dk_acc,
    dv_acc,
    wo_odd_ref,
    pack_ref,
    line_ref,
    y_in_ref,
    z_in_ref,
    line_in_ref,
    cross_ref,
    cross_in_ref,
    cross_line_ref,
    da_out_ref,
    da_in_ref,
    da_own_ref,
    norm_ref,
    norm_in_ref,
    half_ref,
    load,
    gy_send,
    gy_recv,
    stay,
    pass_send,
    pass_recv,
    grad_send,
    grad_recv,
    line_send,
    line_recv,
    pair_send,
    pair_recv,
    out_send,
    out_recv,
    sum_send,
    sum_recv,
):
    rows_all, width = dy_ref.shape
    blocks = rows_all // BLK
    pairs = q_ref.shape[0]
    local = pairs * LANES
    columns = n + 4
    slots = n * padded
    d, t = lax.axis_index("dp"), lax.axis_index("tensor")
    m, c = lax.div(t, 2), lax.rem(t, 2)
    partner = (d, t + 1 - 2 * c)
    across = (d, lax.rem(t + 2, 4))
    rows_half = rows_all // 2
    own = pl.multiple_of(c * local, LANES)
    own_lanes = pl.ds(own, local)
    place = pl.ds(pl.multiple_of(c * rows_half, BLK), rows_half)
    loads = [
        pltpu.make_async_copy(src, dst, load.at[i])
        for i, (src, dst) in enumerate(
            [
                (routes_all_ref.at[m], routes_ref),
                (cotangent_ref.at[m], dy_ref),
                (tokens_ref.at[m, place], x_ref),
                (o_all_ref.at[:, own_lanes], o_ref),
            ]
        )
    ]
    for copy in loads:
        copy.start()
    greet(plane_peers(n, d, t) + [partner, across])

    sum_refs, total_refs, stages, lands = sums
    sum_copies = [
        remote(src, land, sum_send.at[i], sum_recv.at[i], across)
        for i, (src, land) in enumerate(zip(sum_refs[2:4], lands))
    ]
    for copy in sum_copies:
        copy.start()

    def give(j):
        s = lax.rem(d + j, n)
        return remote(gy_src_ref.at[s], gy_ref.at[c, d], gy_send.at[j], gy_recv.at[j], (s, t))

    def hand(j):
        block = gy_ref.at[c, lax.rem(d + n - j, n)]
        return remote(block, block, pass_send.at[j], pass_recv.at[j], partner)

    keep = pltpu.make_async_copy(gy_src_ref.at[d], gy_ref.at[c, d], stay.at[0])
    keep.start()

    def give_start(j, carry):
        give(j).start()
        return carry

    lax.fori_loop(1, n, give_start, 0)

    def collect():
        keep.wait()
        hand(0).start()

        def step(j, carry):
            give(j).wait_recv()
            hand(j).start()
            return carry

        lax.fori_loop(1, n, step, 0)

    def settle():
        def step(j, carry):
            hand(j).wait_recv()
            return carry

        lax.fori_loop(0, n, step, 0)

    row_ref[...] = jnp.zeros_like(row_ref)
    for copy in loads:
        copy.wait()

    gain_moe = extra_ref[columns + 5 : columns + 6, :]
    vec0 = extra_ref[columns + 6 : columns + 7, :]
    vec1 = extra_ref[columns + 7 : columns + 8, :]
    group = max(1, min(n, (1024 if slots <= 1024 else 512) // padded))
    span = group * padded

    def combine(wheres, ref, lines=None):
        total = jnp.zeros((BLK, width), F32)
        entries = [jnp.zeros((BLK, 1), F32) for _ in wheres]
        slot = lax.broadcasted_iota(jnp.int32, (BLK, span), 1)
        for side in range(2):
            for first in range(0, n, group):
                start = side * slots + first * padded
                hots = [slot == where - start for where in wheres]
                hot = jnp.where(hots[0] | hots[1], 1.0, 0.0).astype(BF16)
                block = ref[side, first : first + group].reshape(span, width)
                total = total + mm(hot, block)
                if lines is not None:
                    line = jnp.concatenate(
                        [lines[side, first + e, 0:1, :] for e in range(group)], axis=1
                    )
                    entries = [
                        entry + jnp.sum(jnp.where(one, line, 0.0), axis=-1, keepdims=True)
                        for entry, one in zip(entries, hots)
                    ]
        return total, entries

    def facts(rows):
        lane = lane_ids(BLK)
        stats = stat_ref[rows, :]
        values = [stats[:, j : j + 1] for j in range(7)]
        e0, e1 = routes_ref[rows, 0:1], routes_ref[rows, 1:2]
        wheres = []
        places = pos_ref[rows, :]
        for e in (e0, e1):
            place = pick(lane == e, places).astype(jnp.int32)
            side = (place >= half).astype(jnp.int32)
            where = side * (slots - half) + e * padded + place
            wheres.append(jnp.where(e < n, where, -1))
        g0, g1 = values[0:2]

        def named(number):
            return jnp.where(e0 == number, g0, 0.0) + jnp.where(e1 == number, g1, 0.0)

        copied, first, second = named(n + 1), named(n + 2), named(n + 3)
        on_u = copied + first * values[2] + second * values[4]
        return values, e0, e1, wheres, first, second, on_u

    def back(i, carry):
        rows = pl.ds(pl.multiple_of(i * BLK, BLK), BLK)
        values, e0, e1, wheres, first, second, on_u = facts(rows)
        g0, g1, a00, a01, a10, a11, r = values
        lane = lane_ids(BLK)
        grads, (f0, f1) = combine(wheres, dx_ref, dg_ref)
        h = h_ref[rows, :]
        normed = h * r
        u = normed * gain_moe
        dy = dy_ref[rows, :].astype(F32)
        s_u = jnp.sum(dy * u, axis=-1, keepdims=True)
        s_0 = jnp.sum(dy * vec0, axis=-1, keepdims=True)
        s_1 = jnp.sum(dy * vec1, axis=-1, keepdims=True)

        def other(e):
            value = jnp.where(e == n + 1, s_u, 0.0)
            value = jnp.where(e == n + 2, a00 * s_u + a01 * s_0, value)
            return jnp.where(e == n + 3, a10 * s_u + a11 * s_1, value)

        dg0, dg1 = f0 + other(e0), f1 + other(e1)
        mean = g0 * dg0 + g1 * dg1
        dl = jnp.where(lane == e0, g0 * (dg0 - mean), 0.0) + jnp.where(
            lane == e1, g1 * (dg1 - mean), 0.0
        )
        turned = jnp.transpose(dl)
        logit_ref[m, :, rows] = turned[0 : logit_ref.shape[1], :]
        d00, d01 = first * s_u, first * s_0
        d10, d11 = second * s_u, second * s_1
        m0 = a00 * d00 + a01 * d01
        m1 = a10 * d10 + a11 * d11
        low = dl
        for j, value in enumerate(
            [a00 * (d00 - m0), a01 * (d01 - m0), a10 * (d10 - m1), a11 * (d11 - m1)]
        ):
            low = jnp.where(lane == columns + j, value, low)
        low = low.astype(BF16)
        low_ref[rows, :] = low
        du = grads + mm_nt(low, small_ref[...]) + on_u * dy
        row_ref[0:1, :] += jnp.sum(du * normed, axis=0, keepdims=True)
        row_ref[1:2, :] += jnp.sum((first * a01) * dy, axis=0, keepdims=True)
        row_ref[2:3, :] += jnp.sum((second * a11) * dy, axis=0, keepdims=True)
        dn = du * gain_moe
        dh = dy + r * (dn - normed * jnp.mean(dn * normed, axis=-1, keepdims=True))

        @pl.when(lax.div(i, blocks // 2) == c)
        def _():
            near = pl.multiple_of(i * BLK - c * rows_half, BLK)
            dh_ref[pl.ds(near, BLK), :] = dh

        dzb = dh.astype(BF16)
        dzb_ref[rows, :] = dzb
        do_ref[rows, :] = mm(dzb, wo_ref[:, own_lanes]).astype(BF16)
        return carry

    lax.fori_loop(0, blocks, back, 0)
    logit_copy = remote(
        logit_ref.at[m], logit_ref.at[m], pair_send.at[0], pair_recv.at[0], across
    )
    logit_copy.start()

    grad_wo = mm_tn(dzb_ref[...], o_ref[...])
    pack_ref[0, :, 3 * LANES : 4 * LANES] = grad_wo[:, 0:LANES].astype(BF16)
    pack_ref[1, :, 3 * LANES : 4 * LANES] = grad_wo[:, LANES : 2 * LANES].astype(BF16)
    wo_odd_ref[...] = grad_wo[:, 2 * LANES : 3 * LANES]
    line_ref[...] = mm_tn(ub_ref[...], low_ref[...])

    def slab(owner):
        return pl.ds(pl.multiple_of(owner * part, part), part)

    ring = n // 2
    y_own = lax.rem(d, 2)
    beside = (d + 1 - 2 * y_own, t)
    z_own = lax.div(d, 2)
    wide_lanes = (pl.ds(0, 4 * LANES), pl.ds(4 * LANES, 2 * LANES))

    def y_copy(s, stage, z):
        lanes = wide_lanes[stage]
        return remote(
            pack_ref.at[s, slab(2 * z + 1 - y_own), lanes],
            y_in_ref.at[s, z, :, lanes],
            grad_send.at[stage, s, z],
            grad_recv.at[stage, s, z],
            beside,
        )

    def z_copy(s, stage, j):
        lanes = wide_lanes[stage]
        z = lax.rem(z_own + j, ring)
        return remote(
            pack_ref.at[s, slab(2 * z + y_own), lanes],
            z_in_ref.at[s, j, :, lanes],
            grad_send.at[2 + stage, s, j],
            grad_recv.at[2 + stage, s, j],
            (2 * z + y_own, t),
        )

    def y_start(s, stage):
        for z in range(ring):
            y_copy(s, stage, z).start()

    def z_start(s, stage):
        lanes = wide_lanes[stage]
        for z in range(ring):
            y_copy(s, stage, z).wait()
            rows = slab(2 * z + y_own)
            value = pack_ref[s, rows, lanes].astype(F32) + y_in_ref[s, z, :, lanes].astype(F32)
            pack_ref[s, rows, lanes] = value.astype(BF16)
        for j in range(1, ring):
            z_copy(s, stage, j).start()

    def line_copy(j):
        e = lax.rem(d + j, n)
        return remote(
            line_ref.at[slab(e), :],
            line_in_ref.at[d],
            line_send.at[j],
            line_recv.at[j],
            (e, t),
        )

    head = half_mask(BLK)

    def attend_back(p):
        dk_acc[...] = jnp.zeros_like(dk_acc)
        dv_acc[...] = jnp.zeros_like(dv_acc)
        dq = []
        for i in range(blocks):
            rows = pl.ds(i * BLK, BLK)
            seen = pl.ds(0, (i + 1) * BLK)
            lanes = pl.ds(pl.multiple_of(p * LANES, LANES), LANES)
            q, do = q_ref[p, rows, :], do_ref[rows, lanes]
            k, v = k_ref[p, seen, :], v_ref[p, seen, :]
            zero = jnp.zeros_like(q)
            parts = []
            dk, dv = dk_acc[seen, :], dv_acc[seen, :]
            for side in range(2):
                chosen = head if side == 0 else jnp.logical_not(head)
                qm, dom = jnp.where(chosen, q, zero), jnp.where(chosen, do, zero)
                prob = jnp.exp(mm_nt(k, qm) - lse_ref[2 * p + side, 0:1, rows])
                grad_prob = mm_nt(v, dom)
                total = jnp.sum(prob * grad_prob, axis=0, keepdims=True)
                grad_score = (prob * (grad_prob - total)).astype(BF16)
                dv = dv + mm(prob.astype(BF16), dom)
                dk = dk + mm(grad_score, qm)
                parts.append(mm_tn(grad_score, k))
            dk_acc[seen, :] = dk
            dv_acc[seen, :] = dv
            value = jnp.where(head, parts[0], parts[1]) * (HD**-0.5)
            dq.append(turn(value, cos_ref[rows, :], -sin_ref[rows, :]))
        return (
            jnp.concatenate(dq, axis=0),
            turn(dk_acc[...], cos_ref[...], -sin_ref[...]),
            dv_acc[...],
        )

    def shard_step(i, carry):
        s = lax.rem(m + 1 + i, 2)
        for j, value in enumerate(attend_back(s)):
            dp_ref[s, :, j * LANES : (j + 1) * LANES] = value.astype(BF16)
        for j in range(3):
            lanes = pl.ds(j * LANES, LANES)
            pack_ref[s, :, lanes] = mm_tn(a_ref[...], dp_ref[s, :, lanes]).astype(BF16)
        if not gathered:
            y_start(s, 0)

            @pl.when(i == 1)
            def _():
                z_start(lax.rem(m + 1, 2), 0)

        return carry

    lax.fori_loop(0, 2, shard_step, 0)
    dq, dk, dv = attend_back(2)
    wide = half_mask(rows_all)
    odd = [
        (jnp.where(wide, dq, swap_halves(dk)), jnp.where(wide, dv, 0.0)),
        (jnp.where(wide, swap_halves(dq), dk), jnp.where(wide, swap_halves(dv), 0.0)),
    ]
    tall = half_mask(width)
    for s in range(2):
        for j in range(2):
            dp_ref[s, :, (3 + j) * LANES : (4 + j) * LANES] = odd[s][j].astype(BF16)
    for s in range(2):
        pack_ref[s, :, 4 * LANES : 5 * LANES] = mm_tn(
            a_ref[...], dp_ref[s, :, 3 * LANES : 4 * LANES]
        ).astype(BF16)
        last = mm_tn(a_ref[...], dp_ref[s, :, 4 * LANES : 5 * LANES])
        side = wo_odd_ref[...]
        side = swap_halves(side) if s == 0 else side
        pack_ref[s, :, 5 * LANES : 6 * LANES] = jnp.where(tall, last, side).astype(BF16)
    if not gathered:
        y_start(0, 1)
        y_start(1, 1)
        z_start(m, 0)

    collect()

    def da_rows(start):
        rows = pl.ds(pl.multiple_of(start, BLK), BLK)
        total = jnp.zeros((BLK, width), F32)
        for s in range(2):
            total = total + mm_nt(dp_ref[s, rows, 0 : 3 * LANES], spread_ref[s, :, 0 : 3 * LANES])
            total = total + mm_nt(
                dp_ref[s, rows, 3 * LANES : 5 * LANES], spread_ref[s, :, 4 * LANES : 6 * LANES]
            )
        return total

    def da_other(i, carry):
        rows = pl.ds(pl.multiple_of(i * BLK, BLK), BLK)
        da_out_ref[rows, :] = da_rows((1 - c) * rows_half + i * BLK).astype(BF16)
        return carry

    lax.fori_loop(0, rows_half // BLK, da_other, 0)
    da_copy = remote(da_out_ref, da_in_ref, pair_send.at[1], pair_recv.at[1], partner)
    da_copy.start()

    def da_own(i, carry):
        rows = pl.ds(pl.multiple_of(i * BLK, BLK), BLK)
        da_own_ref[rows, :] = da_rows(c * rows_half + i * BLK)
        return carry

    lax.fori_loop(0, rows_half // BLK, da_own, 0)
    if not gathered:
        z_start(0, 1)
        z_start(1, 1)
    da_copy.wait()
    gain_attn = extra_ref[columns + 4 : columns + 5, :]
    norm_ref[...] = jnp.zeros_like(norm_ref)

    def finish(i, carry):
        rows = pl.ds(pl.multiple_of(i * BLK, BLK), BLK)
        x = x_ref[rows, :].astype(F32)
        r = lax.rsqrt(jnp.mean(x * x, axis=-1, keepdims=True) + EPSILON)
        normed = x * r
        da = da_own_ref[rows, :] + da_in_ref[rows, :].astype(F32)
        norm_ref[0:1, :] += jnp.sum(da * normed, axis=0, keepdims=True)
        dn = da * gain_attn
        grad = dh_ref[rows, :] + r * (dn - normed * jnp.mean(dn * normed, axis=-1, keepdims=True))
        half_ref[0, rows, :] = grad.astype(BF16)
        return carry

    lax.fori_loop(0, rows_half // BLK, finish, 0)
    norm_copy = remote(norm_ref, norm_in_ref, pair_send.at[2], pair_recv.at[2], partner)
    norm_copy.start()

    def publish(kind, out_ref):
        block = out_ref.at[m, place]
        copies = [
            remote(half_ref.at[kind], block, out_send.at[kind, 0], out_recv.at[kind, 0], across),
            remote(half_ref.at[kind], block, out_send.at[kind, 1], out_recv.at[kind, 1], partner),
            pltpu.make_async_copy(half_ref.at[kind], block, stay.at[1 + kind]),
        ]
        for copy in copies:
            copy.start()
        block = out_ref.at[1 - m, place]
        relay = remote(block, block, out_send.at[kind, 2], out_recv.at[kind, 2], partner)
        return copies, relay

    grad_x_copies, grad_x_relay = publish(0, grad_x_ref)

    settle()

    def results(i, carry):
        rows = pl.ds(pl.multiple_of(i * BLK, BLK), BLK)
        far = pl.ds(pl.multiple_of(c * rows_half + i * BLK, BLK), BLK)
        values, e0, e1, wheres, first, second, on_u = facts(far)
        sums, _ = combine(wheres, gy_ref)
        h = h_ref[far, :]
        u = h * values[6] * gain_moe
        result = h + (sums + on_u * u + (first * values[3]) * vec0 + (second * values[5]) * vec1)
        half_ref[1, rows, :] = result.astype(BF16)
        return carry

    lax.fori_loop(0, rows_half // BLK, results, 0)
    result_copies, result_relay = publish(1, result_ref)

    stores = []
    if not gathered:
        for copy in sum_copies:
            copy.wait_recv()
        pieces = [
            (0, (0, kind, pl.ds(i * BLK, BLK)))
            for kind in range(2)
            for i in range(width // BLK)
        ] + [(1, (0, pl.ds(i * BLK, BLK))) for i in range(lands[1].shape[1] // BLK)]

        def fetch(i):
            which, where = pieces[i]
            return pltpu.make_async_copy(
                sum_refs[which].at[where], stages[which].at[i % 2], load.at[4 + i % 2]
            )

        def store(i):
            which, where = pieces[i]
            return pltpu.make_async_copy(
                stages[which].at[i % 2], total_refs[which].at[where], load.at[6 + i % 2]
            )

        fetch(0).start()
        for i, (which, where) in enumerate(pieces):
            if i + 1 < len(pieces):
                if i > 0:
                    store(i - 1).wait()
                fetch(i + 1).start()
            fetch(i).wait()
            stages[which][i % 2] += lands[which][where].astype(F32)
            store(i).start()
        stores = [store(len(pieces) - 2), store(len(pieces) - 1)]

    norm_copy.wait()
    row_ref[3:4, :] = norm_ref[0:1, :] + norm_in_ref[0:1, :]
    turned = jnp.concatenate([row_ref[...], jnp.zeros((LANES - 8, width), F32)], axis=0)
    turned = jnp.transpose(turned)
    lane = lax.broadcasted_iota(jnp.int32, (width, LANES), 1)
    lines = line_ref[...]
    for j, source in enumerate([3, 0, 1, 2]):
        lines = jnp.where(lane == columns + 4 + j, turned[:, source : source + 1], lines)
    line_ref[...] = lines
    if gathered:
        packs = [
            pltpu.make_async_copy(pack_ref, grads_ref, load.at[0]),
            pltpu.make_async_copy(line_ref, lines_ref, load.at[1]),
        ]
        for copy in packs:
            copy.start()
        for copy in packs:
            copy.wait()
    else:

        def send(j, carry):
            line_copy(j).start()
            return carry

        lax.fori_loop(1, n, send, 0)
        line_in_ref[d] = line_ref[slab(d), :]
        for s in range(2):
            for stage in range(2):
                for j in range(1, ring):
                    z_copy(s, stage, j).wait()

        def total(s):
            value = pack_ref[s, slab(d), :].astype(F32)
            for j in range(1, ring):
                value = value + z_in_ref[s, j].astype(F32)
            return value

        cross_ref[...] = total(1 - m).astype(BF16)
        cross_copy = remote(cross_ref, cross_in_ref, pair_send.at[3], pair_recv.at[3], across)
        cross_copy.start()
        grads_ref[...] = total(m)

        def arrive_lines(j, carry):
            line_copy(j).wait()
            return carry

        lax.fori_loop(1, n, arrive_lines, 0)
        value = line_in_ref[0]
        for e in range(1, n):
            value = value + line_in_ref[e]
        cross_line_ref[0] = value
        cross_line_copy = remote(
            cross_line_ref.at[0], cross_line_ref.at[1], pair_send.at[4], pair_recv.at[4], across
        )
        cross_line_copy.start()
        cross_copy.wait()
        grads_ref[...] += cross_in_ref[...].astype(F32)
        cross_line_copy.wait()
        lines_ref[...] = cross_line_ref[0] + cross_line_ref[1]

    for copies, relay in ((grad_x_copies, grad_x_relay), (result_copies, result_relay)):
        copies[0].wait_recv()
        relay.start()
    for copies, relay in ((grad_x_copies, grad_x_relay), (result_copies, result_relay)):
        copies[0].wait_send()
        copies[1].wait()
        copies[2].wait()
        relay.wait()
    logit_copy.wait()

    for copy in sum_copies:
        copy.wait_send()
    for copy in stores:
        copy.wait()

    def clear(j, carry):
        give(j).wait_send()
        return carry

    lax.fori_loop(1, n, clear, 0)

    def passed(j, carry):
        hand(j).wait_send()
        return carry

    lax.fori_loop(0, n, passed, 0)


def across_chips(value):
    return lax.ppermute(value, "tensor", [(0, 2), (2, 0), (1, 3), (3, 1)])


def across_cores(value):
    return lax.ppermute(value, "tensor", [(0, 1), (1, 0), (2, 3), (3, 2)])


def body(
    tokens,
    cotangent,
    prev_logits,
    routes,
    norm_attn,
    norm_moe,
    w_qkv,
    w_out,
    w_router,
    w_const,
    const_vec,
    w_in,
    w_down,
):
    rows, width = tokens.shape[1:]
    n = lax.axis_size("dp")
    experts = n
    columns = prev_logits.shape[2]
    capacity = 4 * max(1, 3 * rows // (4 * (experts + 4)))
    half = capacity // 2
    padded = -(-half // 16) * 16
    share = w_qkv.shape[2]
    local = 2 * share
    part = w_qkv.shape[1]
    t = lax.axis_index("tensor")
    m, c = t // 2, t % 2

    def mine(value):
        return lax.dynamic_index_in_dim(value, m, 0, keepdims=False)

    x, dy, choose = mine(tokens), mine(cotangent), mine(routes)
    cosine, sine = (jnp.asarray(v) for v in rope_constants())
    pairs = local // LANES

    wo_rows = w_out.T
    packed = jnp.concatenate(
        [w_qkv[i, :, :LANES] for i in range(3)]
        + [wo_rows[:, :LANES]]
        + [w_qkv[i, :, LANES:] for i in range(3)]
        + [
            wo_rows[:, LANES:],
            w_router,
            w_const,
            norm_attn[:, None],
            norm_moe[:, None],
            const_vec.T,
            jnp.zeros((part, LANES - columns - 8), BF16),
        ],
        axis=1,
    )
    gathered = part % 16 != 0
    if gathered:
        packed = lax.all_gather(packed, "dp", axis=0, tiled=True)
        other = across_chips(packed)
        packed = jnp.where(m == 0, jnp.stack([packed, other]), jnp.stack([other, packed]))
    spread_width = packed.shape[-1]
    front_outs = [
        struct((rows, width), BF16),
        struct((pairs, rows, LANES), BF16),
        struct((pairs, rows, LANES), BF16),
        struct((pairs, rows, LANES), BF16),
        struct((rows, width), BF16),
        struct((8, 8, rows), F32),
        struct((rows, width), F32),
        struct((rows, width), BF16),
        struct((rows, LANES), F32),
        struct((rows, LANES), F32),
        struct((width, width), BF16),
        struct((width, LANES), BF16),
        struct((LANES, width), F32),
        struct((2, width, spread_width), BF16),
        struct((n, padded, width), BF16),
        struct((n, 8, padded), F32),
    ]
    landing = [
        struct((n, padded, width), BF16),
    ] + [struct(w_in.shape, BF16)] * 3 + [struct(w_down.shape, BF16)] * 3
    dma = pltpu.SemaphoreType.DMA
    (
        a,
        q,
        k,
        v,
        o_all,
        lse,
        h,
        ub,
        stats,
        pos,
        wo_all,
        small_all,
        extra,
        spread,
        slots,
        gate_slots,
        dy_arrived,
        in_c,
        in_x,
        in_d,
        down_c,
        down_x,
        down_d,
    ) = pl.pallas_call(
        functools.partial(front_kernel, n, half, padded, gathered),
        out_shape=front_outs + landing,
        in_specs=[aspec()] * 4 + [vspec()] * 3 + [aspec()] * 2,
        out_specs=[vspec()] * len(front_outs) + [aspec()] * len(landing),
        scratch_shapes=[
            pltpu.VMEM((rows, width), BF16),
            pltpu.VMEM((rows, width), BF16),
            pltpu.VMEM((rows, columns), F32),
            pltpu.VMEM((rows, 2), jnp.int32),
            pltpu.VMEM((LANES, rows), F32),
            pltpu.VMEM((LANES, rows), F32),
            pltpu.VMEM((n, padded, width), BF16),
            dma((4,)),
            dma((8, n // 2)),
            dma((8, n // 2)),
            dma((n,)),
            dma((n,)),
            dma((1,)),
            dma((pairs + 1,)),
            dma((pairs + 1,)),
            dma((6,)),
            dma((6,)),
        ],
        compiler_params=pltpu.CompilerParams(
            collective_id=0, has_side_effects=True, vmem_limit_bytes=VMEM_LIMIT
        ),
        cost_estimate=pl.CostEstimate(
            flops=60_000_000_000, bytes_accessed=60_000_000, transcendentals=0
        ),
    )(tokens, cotangent, prev_logits, routes, packed, cosine, sine, w_in, w_down)

    hidden_width = w_in.shape[3]
    slots_all = experts * padded
    if gathered:
        chunk = min(256 if slots_all <= 1024 else 128, hidden_width)
        per = hidden_width // chunk

        def in_map(i):
            return lambda f: (0, 0, 0, jnp.clip(f - per * i, 0, per - 1))

        def down_map(i):
            return lambda f: (0, jnp.clip(f - per * i, 0, per - 1), 0)

        in_blocks = [pl.BlockSpec((1, 2, width, chunk), in_map(i)) for i in range(4)]
        down_blocks = [pl.BlockSpec((1, chunk, width), down_map(i)) for i in range(4)]
        expert_outs = (
            [
                struct((n, padded, width), BF16),
                struct((n, padded, width), BF16),
                struct((n, 8, padded), F32),
            ]
            + [struct(w_in.shape, BF16)] * 4
            + [struct(w_down.shape, BF16)] * 4
        )

        def whole(shape):
            return pl.BlockSpec(
                shape, lambda f: (0,) * len(shape), pipeline_mode=pl.Buffered(1)
            )

        parts = pl.pallas_call(
            functools.partial(expert_kernel, n, padded),
            grid=(4 * per,),
            out_shape=expert_outs,
            in_specs=[
                whole((slots_all, width)),
                whole((slots_all, width)),
                whole((n, 8, padded)),
            ]
            + in_blocks
            + down_blocks,
            out_specs=[
                whole((n, padded, width)),
                whole((n, padded, width)),
                whole((n, 8, padded)),
            ]
            + in_blocks
            + down_blocks,
            scratch_shapes=[
                pltpu.VMEM((width, slots_all), BF16),
                pltpu.VMEM((slots_all, width), BF16),
                pltpu.VMEM((slots_all, LANES), F32),
                pltpu.VMEM((slots_all, width), F32),
                pltpu.VMEM((slots_all, width), F32),
                pltpu.VMEM((2, width, chunk), BF16),
                pltpu.VMEM((chunk, width), BF16),
            ],
            compiler_params=pltpu.CompilerParams(vmem_limit_bytes=VMEM_LIMIT),
            cost_estimate=pl.CostEstimate(
                flops=18 * slots_all * width * 4 * hidden_width,
                bytes_accessed=30_000_000,
                transcendentals=0,
            ),
        )(
            lax.all_to_all(slots, "dp", split_axis=0, concat_axis=0, tiled=True).reshape(
                slots_all, width
            ),
            dy_arrived.reshape(slots_all, width),
            lax.all_to_all(gate_slots, "dp", split_axis=0, concat_axis=0, tiled=True),
            w_in,
            in_c,
            in_x,
            in_d,
            w_down,
            down_c,
            down_x,
            down_d,
        )
        gy, dx, dg = parts[0:3]
        gin, gdown = parts[3:7], parts[7:11]

        def everywhere(value):
            value = lax.all_to_all(value, "dp", split_axis=0, concat_axis=0, tiled=True)
            other = across_cores(value)
            return jnp.where(c == 0, jnp.stack([value, other]), jnp.stack([other, value]))

        dx_all, dg_all = everywhere(dx), everywhere(dg)

        def total(own, core, chip, diagonal):
            chip = (chip.astype(F32) + across_cores(diagonal).astype(F32)).astype(BF16)
            own = own.astype(F32) + across_cores(core).astype(F32)
            return own + across_chips(chip).astype(F32)

        grad_in, grad_down = total(*gin), total(*gdown)
        sums = []
    else:
        gy, *sums, dx_all, dg_all = pl.pallas_call(
            functools.partial(expert_exchange_kernel, n, padded),
            out_shape=[
                struct((n, padded, width), BF16),
                struct(w_in.shape, F32),
                struct(w_down.shape, F32),
                struct(w_in.shape, BF16),
                struct(w_down.shape, BF16),
                struct((2, n, padded, width), BF16),
                struct((2, n, 8, padded), F32),
            ],
            in_specs=[aspec()] * 11,
            out_specs=[vspec()] * 5 + [aspec()] * 2,
            scratch_shapes=[
                pltpu.VMEM((slots_all, width), BF16),
                pltpu.VMEM((width, slots_all), BF16),
                pltpu.VMEM((slots_all, width), BF16),
                pltpu.VMEM((slots_all, width), BF16),
                pltpu.VMEM((slots_all, LANES), F32),
                pltpu.VMEM((n, 8, padded), F32),
                pltpu.VMEM((4, 2, width, hidden_width), BF16),
                pltpu.VMEM((4 * hidden_width, width), BF16),
                pltpu.VMEM((slots_all, 4 * hidden_width), BF16),
                pltpu.VMEM((slots_all, 4 * hidden_width), BF16),
                pltpu.VMEM((slots_all, 4 * hidden_width), BF16),
                pltpu.VMEM((slots_all // 4, width), F32),
                pltpu.VMEM((slots_all, width), BF16),
                pltpu.VMEM((n, 8, padded), F32),
                pltpu.VMEM((2,) + w_in.shape[1:], BF16),
                pltpu.VMEM((2,) + w_down.shape[1:], BF16),
                dma((10 + n,)),
                dma((n,)),
                dma((n,)),
                dma((n,)),
                dma((n,)),
                dma((n,)),
                dma((n,)),
                dma((n,)),
                dma((n,)),
                dma((2, n)),
                dma((2, n)),
                dma((4,)),
                dma((4,)),
            ],
            compiler_params=pltpu.CompilerParams(
                collective_id=2, has_side_effects=True, vmem_limit_bytes=VMEM_LIMIT
            ),
            cost_estimate=pl.CostEstimate(
                flops=60_000_000_000, bytes_accessed=40_000_000, transcendentals=0
            ),
        )(
            slots,
            gate_slots,
            dy_arrived,
            w_in,
            in_c,
            in_x,
            in_d,
            w_down,
            down_c,
            down_x,
            down_d,
        )

    groups = 6 * LANES
    logit_rows = -(-columns // 8) * 8
    rear_outs = [
        struct((2, logit_rows, rows), F32),
        struct((2, width, groups), BF16) if gathered else struct((part, groups), F32),
        struct((width if gathered else part, LANES), F32),
    ]
    half_rows = rows // 2
    spread_n = 1 if gathered else n // 2
    line_n = 1 if gathered else n
    totals = [struct(w_in.shape, F32), struct(w_down.shape, F32)]
    totals = [] if gathered else totals
    staged = [
        pltpu.VMEM((2, BLK, hidden_width), F32),
        pltpu.VMEM((2, BLK, width), F32),
        pltpu.VMEM(w_in.shape, BF16),
        pltpu.VMEM(w_down.shape, BF16),
    ]
    staged = [] if gathered else staged
    results, input_grads, logits, grads, lines, *totals = pl.pallas_call(
        functools.partial(rear_kernel, n, half, padded, gathered, part),
        out_shape=[struct((2, rows, width), BF16)] * 2 + rear_outs + totals,
        in_specs=[aspec()] * (len(sums) + 1)
        + [vspec()] * 2
        + [aspec()] * 4
        + [vspec()] * 15,
        out_specs=[aspec()] * 2
        + [vspec()]
        + [aspec() if gathered else vspec()] * 2
        + [aspec()] * len(totals),
        scratch_shapes=[
            pltpu.VMEM((half_rows, width), BF16),
            pltpu.VMEM((rows, width), BF16),
            pltpu.VMEM((rows, 2), jnp.int32),
            pltpu.VMEM((rows, local), BF16),
            pltpu.VMEM((2, n, padded, width), BF16),
            pltpu.VMEM((half_rows, width), F32),
            pltpu.VMEM((rows, width), BF16),
            pltpu.VMEM((rows, local), BF16),
            pltpu.VMEM((rows, LANES), BF16),
            pltpu.VMEM((8, width), F32),
            pltpu.VMEM((2, rows, 5 * LANES), BF16),
            pltpu.VMEM((rows, LANES), F32),
            pltpu.VMEM((rows, LANES), F32),
            pltpu.VMEM((width, LANES), F32),
            pltpu.VMEM((2, width, groups), BF16),
            pltpu.VMEM((width, LANES), F32),
            pltpu.VMEM((2, spread_n, part, groups), BF16),
            pltpu.VMEM((2, spread_n, part, groups), BF16),
            pltpu.VMEM((line_n, part, LANES), F32),
            pltpu.VMEM((part, groups), BF16),
            pltpu.VMEM((part, groups), BF16),
            pltpu.VMEM((2, part, LANES), F32),
            pltpu.VMEM((half_rows, width), BF16),
            pltpu.VMEM((half_rows, width), BF16),
            pltpu.VMEM((half_rows, width), F32),
            pltpu.VMEM((8, width), F32),
            pltpu.VMEM((8, width), F32),
            pltpu.VMEM((2, half_rows, width), BF16),
            *staged,
            dma((8,)),
            dma((n,)),
            dma((n,)),
            dma((3,)),
            dma((n,)),
            dma((n,)),
            dma((4, 2, n // 2)),
            dma((4, 2, n // 2)),
            dma((n,)),
            dma((n,)),
            dma((5,)),
            dma((5,)),
            dma((2, 3)),
            dma((2, 3)),
            dma((2,)),
            dma((2,)),
        ],
        compiler_params=pltpu.CompilerParams(
            collective_id=1, has_side_effects=True, vmem_limit_bytes=VMEM_LIMIT
        ),
        cost_estimate=pl.CostEstimate(
            flops=100_000_000_000, bytes_accessed=60_000_000, transcendentals=0
        ),
    )(
        *sums,
        gy,
        dx_all,
        dg_all,
        tokens,
        cotangent,
        routes,
        o_all,
        h,
        ub,
        stats,
        pos,
        small_all,
        extra,
        wo_all,
        q,
        k,
        v,
        a,
        lse,
        spread,
        cosine,
        sine,
    )
    if not gathered:
        grad_in, grad_down = totals
    if gathered:
        grads = lax.psum_scatter(grads.astype(F32), "dp", scatter_dimension=1, tiled=True)
        lines = lax.psum_scatter(lines, "dp", scatter_dimension=0, tiled=True)
        other = lax.dynamic_index_in_dim(grads, 1 - m, 0, keepdims=False)
        grads = lax.dynamic_index_in_dim(grads, m, 0, keepdims=False) + across_chips(other)
        lines = lines + across_chips(lines)

    def heads(j):
        start = (4 + (j % 4) // 2) * LANES + (j % 2) * HD
        return jnp.concatenate(
            [grads[:, j * LANES : (j + 1) * LANES], grads[:, start : start + HD]], axis=1
        )

    return (
        results,
        input_grads,
        jnp.swapaxes(logits[:, :columns], 1, 2),
        lines[:, columns + 4],
        lines[:, columns + 5],
        jnp.stack([heads(i) for i in range(3)]),
        heads(3).T,
        lines[:, :columns],
        lines[:, columns : columns + 4],
        lines[:, columns + 6 : columns + 8].T,
        grad_in,
        grad_down,
    )


def solution(mesh):
    in_specs = (
        P(None, "dp", None),
        P(None, "dp", None),
        P(None, "dp", None),
        P(None, "dp", None),
        P("dp"),
        P("dp"),
        P(None, "dp", "tensor"),
        P("tensor", "dp"),
        P("dp", None),
        P("dp", None),
        P(None, "dp"),
        P("dp", None, None, "tensor"),
        P("dp", "tensor", None),
    )
    out_specs = (
        P(None, "dp", None),
        P(None, "dp", None),
        P(None, "dp", None),
        P("dp"),
        P("dp"),
        P(None, "dp", "tensor"),
        P("tensor", "dp"),
        P("dp", None),
        P("dp", None),
        P(None, "dp"),
        P("dp", None, None, "tensor"),
        P("dp", "tensor", None),
    )
    return jax.shard_map(body, mesh=mesh, in_specs=in_specs, out_specs=out_specs, check_vma=False)
```

```python
import functools

import jax
import jax.numpy as jnp
import numpy as np
from jax import lax
from jax.experimental import pallas as pl
from jax.experimental.pallas import tpu as pltpu
from jax.sharding import PartitionSpec as P

HD = 64
LEN = 1024
BLK = 256
EPSILON = 1e-06
LANES = 128
F32 = jnp.float32
BF16 = jnp.bfloat16
MESH = pl.DeviceIdType.MESH
VMEM_LIMIT = 60 * 1024 * 1024


def mm(a, b):
    return lax.dot_general(a, b, (((1,), (0,)), ((), ())), preferred_element_type=F32)


def mm_nt(a, b):
    return lax.dot_general(a, b, (((1,), (1,)), ((), ())), preferred_element_type=F32)


def mm_tn(a, b):
    return lax.dot_general(a, b, (((0,), (0,)), ((), ())), preferred_element_type=F32)


def vspec():
    return pl.BlockSpec(memory_space=pltpu.VMEM)


def aspec():
    return pl.BlockSpec(memory_space=pl.ANY)


def struct(shape, dtype):
    return jax.ShapeDtypeStruct(shape, dtype)


def greet(peers):
    barrier = pltpu.get_barrier_semaphore()
    for peer in peers:
        pl.semaphore_signal(barrier, inc=1, device_id=peer, device_id_type=MESH)
    pl.semaphore_wait(barrier, len(peers))


def remote(src, dst, send, recv, peer):
    return pltpu.make_async_remote_copy(
        src_ref=src,
        dst_ref=dst,
        send_sem=send,
        recv_sem=recv,
        device_id=peer,
        device_id_type=MESH,
    )


def plane_peers(n, d, t):
    return [(lax.rem(d + j, n), t) for j in range(1, n)]


def slot_hot(half, padded, base, places):
    rows = places.shape[1]
    slot = lax.broadcasted_iota(jnp.int32, (padded, rows), 0)
    wanted = jnp.where(slot < half, slot + base, -2).astype(F32)
    return (wanted == places).astype(F32).astype(BF16)


def rope_constants():
    half = HD // 2
    frequency = 10000.0 ** (-2.0 * np.arange(half) / HD)
    angle = np.arange(LEN)[:, None] * frequency[None, :]
    cosine, sine = np.cos(angle), np.sin(angle)
    cosine = np.concatenate([cosine, cosine, cosine, cosine], axis=1)
    sine = np.concatenate([-sine, sine, -sine, sine], axis=1)
    return cosine.astype(np.float32), sine.astype(np.float32)


def turn(field, cosine, sine):
    lane = lax.broadcasted_iota(jnp.int32, field.shape, 1)
    other = jnp.where(
        lax.rem(lane, HD) < HD // 2,
        pltpu.roll(field, LANES - HD // 2, 1),
        pltpu.roll(field, HD // 2, 1),
    )
    return field * cosine + other * sine


def pick(hot, values):
    return jnp.sum(jnp.where(hot, values, 0.0), axis=-1, keepdims=True)


def lane_ids(rows):
    return lax.broadcasted_iota(jnp.int32, (rows, LANES), 1)


def soft_pair(first, second):
    high = jnp.maximum(first, second)
    e0, e1 = jnp.exp(first - high), jnp.exp(second - high)
    return e0 / (e0 + e1), e1 / (e0 + e1)


def half_mask(rows):
    return lax.broadcasted_iota(jnp.int32, (rows, LANES), 1) < HD


def swap_halves(value):
    return pltpu.roll(value, HD, 1)


def front_kernel(
    n,
    half,
    padded,
    gathered,
    early,
    tokens_ref,
    cotangent_ref,
    routes_all_ref,
    prev_all_ref,
    heads_ref,
    out_ref,
    cos_ref,
    sin_ref,
    win_ref,
    *refs,
):
    tiny_refs, refs = refs[: 1 if gathered else 5], refs[1 if gathered else 5 :]
    late = refs[:6]
    h_ref, ub_ref, stat_ref, slot_ref, gate_ref, extra_ref = late
    stored = refs[6 : 6 + early]
    dy_arrived_ref, in_x_ref = refs[6 + early : 8 + early]
    refs = refs[8 + early :]
    kept, refs = refs[:early], refs[early:]
    a_ref, q_ref, k_ref, v_ref, o_ref, lse_ref, pos_ref, wo_ref, small_ref, spread_ref = kept
    x_ref, dy_ref, routes_ref, place_ref, gates_ref, dy_slot_ref = refs[:6]
    refs = refs[6:]
    load, pack_send, pack_recv, dy_send, dy_recv, stay = refs[:6]
    core_send, core_recv, w_send, w_recv, store_sem = refs[6:]

    def store(*which):
        for i in which:
            pltpu.make_async_copy(kept[i], stored[i], store_sem.at[i]).start()

    rows_all, width = x_ref.shape
    blocks = rows_all // BLK
    pairs = q_ref.shape[0]
    local = pairs * LANES
    columns = prev_all_ref.shape[0]
    d, t = lax.axis_index("dp"), lax.axis_index("tensor")
    m, c = lax.div(t, 2), lax.rem(t, 2)
    partner = (d, t + 1 - 2 * c)
    across = (d, lax.rem(t + 2, 4))
    loads = [
        pltpu.make_async_copy(src.at[m], dst, load.at[i])
        for i, (src, dst) in enumerate(
            [
                (routes_all_ref, routes_ref),
                (cotangent_ref, dy_ref),
                (tokens_ref, x_ref),
            ]
        )
    ]
    for copy in loads:
        copy.start()
    greet(plane_peers(n, d, t) + [partner, across])
    part = heads_ref.shape[1]

    def pack():
        side = lax.broadcasted_iota(jnp.int32, (part, part), 0)
        eye = jnp.where(side == lax.broadcasted_iota(jnp.int32, (part, part), 1), 1.0, 0.0)
        eye = eye.astype(BF16)
        wo = mm_nt(eye, out_ref[...])
        tiny = [ref[...].astype(F32) for ref in tiny_refs]
        tiny.append(jnp.zeros((LANES - columns - 8, part), F32))
        tiny = mm_nt(eye, jnp.concatenate(tiny, axis=0).astype(BF16))
        wide = [heads_ref[i].astype(F32) for i in range(3)] + [wo]
        firsts = [value[:, :LANES] for value in wide]
        odds = [
            jnp.concatenate([wide[i][:, LANES:], wide[i + 1][:, LANES:]], axis=1) for i in (0, 2)
        ]
        return jnp.concatenate(firsts + odds + [tiny], axis=1).astype(BF16)

    beside = (d + 1 - 2 * lax.rem(d, 2), t)
    lanes_a = pl.ds(0, 3 * LANES)
    lanes_b = pl.ds(3 * LANES, 4 * LANES)

    def behind(j):
        return lax.rem(d + n - 2 * j, n)

    def shard(chip, owner, lanes):
        return spread_ref.at[chip, pl.ds(pl.multiple_of(owner * part, part), part), lanes]

    def pass_on(chip, owner, lanes, row, j, peer):
        block = shard(chip, owner, lanes)
        return remote(block, block, pack_send.at[row, j], pack_recv.at[row, j], peer)

    def ahead(j):
        return (lax.rem(d + 2 * j, n), t)

    ring = n // 2
    if gathered:
        spread_ref[...] = tiny_refs[0][...]
    else:
        spread_ref[m, pl.ds(pl.multiple_of(d * part, part), part), :] = pack()
        a_x = pass_on(m, d, lanes_a, 4, 0, across)
        sends = [a_x]
        for j in range(1, ring):
            sends.append(pass_on(m, d, lanes_a, 0, j, ahead(j)))
            sends.append(pass_on(m, d, lanes_b, 4, j, ahead(j)))
        sends.append(pass_on(m, d, lanes_a, 2, 0, beside))
        sends.append(pass_on(m, d, lanes_b, 5, 0, beside))
        sends.append(pass_on(m, d, lanes_b, 6, 0, across))
        for copy in sends:
            copy.start()

    def relay_gather():
        if gathered:
            return
        a_x.wait_recv()
        more = [pass_on(1 - m, d, lanes_a, 1, j, ahead(j)) for j in range(1, ring)]
        more.append(pass_on(1 - m, d, lanes_a, 3, 0, beside))
        for copy in more:
            copy.start()
        sends.extend(more)
        for j in range(1, ring):
            pass_on(m, d, lanes_b, 4, j, ahead(j)).wait_recv()
            more = [
                pass_on(m, behind(j), lanes_b, 5, j, beside),
                pass_on(m, behind(j), lanes_b, 6, j, across),
            ]
            pass_on(m, d, lanes_a, 0, j, ahead(j)).wait_recv()
            more.append(pass_on(m, behind(j), lanes_a, 2, j, beside))
            for copy in more:
                copy.start()
            sends.extend(more)
        for j in range(1, ring):
            pass_on(1 - m, d, lanes_a, 1, j, ahead(j)).wait_recv()
            copy = pass_on(1 - m, behind(j), lanes_a, 3, j, beside)
            copy.start()
            sends.append(copy)
        for j in range(ring):
            pass_on(m, d, lanes_b, 5, j, beside).wait_recv()
            owner = lax.rem(beside[0] + n - 2 * j, n)
            copy = pass_on(m, owner, lanes_b, 7, j, across)
            copy.start()
            sends.append(copy)
        for j in range(ring):
            pass_on(m, d, lanes_a, 2, j, beside).wait_recv()
            pass_on(m, d, lanes_a, 3, j, beside).wait_recv()
            pass_on(m, d, lanes_b, 6, j, across).wait_recv()
            pass_on(m, d, lanes_b, 7, j, across).wait_recv()

    loads[0].wait()
    named = routes_ref[...].astype(F32)
    ids = lax.broadcasted_iota(jnp.int32, (LANES, rows_all), 0).astype(F32)
    hit = ((ids == named[0:1, :]) | (ids == named[1:2, :])) & (ids < float(n))
    before = lax.broadcasted_iota(jnp.int32, (rows_all, rows_all), 0) < lax.broadcasted_iota(
        jnp.int32, (rows_all, rows_all), 1
    )
    count = mm(hit.astype(F32).astype(BF16), before.astype(F32).astype(BF16))
    places = jnp.where(hit, count, -1.0)
    place_ref[...] = places
    pos_ref[...] = jnp.transpose(places)
    store(6)
    base = c * half

    def dy_copy(j):
        e = lax.rem(d + j, n)
        return remote(
            dy_slot_ref.at[e], dy_arrived_ref.at[d], dy_send.at[j], dy_recv.at[j], (e, t)
        )

    stays = [pltpu.make_async_copy(dy_slot_ref.at[d], dy_arrived_ref.at[d], stay.at[0])]
    loads[1].wait()

    def two_hot(i):
        return jnp.concatenate(
            [
                slot_hot(half, padded, base, place_ref[pl.ds(2 * i + side, 1), :])
                for side in range(2)
            ],
            axis=0,
        )

    def dy_step(i, carry):
        rows = mm(two_hot(i), dy_ref[...]).astype(BF16)
        for side in range(2):
            dy_slot_ref[2 * i + side] = rows[side * padded : (side + 1) * padded]
        return carry

    lax.fori_loop(0, n // 2, dy_step, 0)
    relay_gather()
    stays[0].start()

    def dy_start(j, carry):
        dy_copy(j).start()
        return carry

    lax.fori_loop(1, n, dy_start, 0)
    weight_copies = []
    if not gathered:
        weight_copies.append(remote(win_ref, in_x_ref, w_send.at[0], w_recv.at[0], across))
    for copy in weight_copies:
        copy.start()
    store(9)

    table = spread_ref[0, :, 6 * LANES : 7 * LANES]
    extra_ref[...] = jnp.transpose(table.astype(F32))
    keep = lax.broadcasted_iota(jnp.int32, (width, LANES), 1) < columns + 4
    small_ref[...] = jnp.where(keep, table, jnp.zeros_like(table))
    mask = half_mask(width)
    own = pl.multiple_of(c * local, LANES)
    wo_ref[:, pl.ds(own, LANES)] = spread_ref[0, :, 3 * LANES : 4 * LANES]
    wo_ref[:, pl.ds(own + LANES, LANES)] = spread_ref[1, :, 3 * LANES : 4 * LANES]
    wo_ref[:, pl.ds(own + 2 * LANES, LANES)] = jnp.where(
        mask,
        swap_halves(spread_ref[0, :, 5 * LANES : 6 * LANES].astype(F32)),
        spread_ref[1, :, 5 * LANES : 6 * LANES].astype(F32),
    ).astype(BF16)
    own_lanes = pl.ds(own, local)
    wo_copy = remote(
        wo_ref.at[:, own_lanes],
        wo_ref.at[:, own_lanes],
        core_send.at[pairs],
        core_recv.at[pairs],
        partner,
    )
    wo_copy.start()
    store(8)

    loads[2].wait()
    gain = extra_ref[columns + 4 : columns + 5, :]
    head = half_mask(BLK)

    def project(i, carry):
        rows = pl.ds(pl.multiple_of(i * BLK, BLK), BLK)
        x = x_ref[rows, :].astype(F32)
        r = lax.rsqrt(jnp.mean(x * x, axis=-1, keepdims=True) + EPSILON)
        a = (x * r * gain).astype(BF16)
        a_ref[rows, :] = a
        cosine, sine = cos_ref[rows, :], sin_ref[rows, :]

        def put(pair, q, k, v):
            q_ref[pair, rows, :] = turn(q, cosine, sine).astype(BF16) * BF16(HD**-0.5)
            k_ref[pair, rows, :] = turn(k, cosine, sine).astype(BF16)
            v_ref[pair, rows, :] = v.astype(BF16)

        odd = []
        for s in range(2):
            both = mm(a, spread_ref[s, :, 0 : 3 * LANES])
            put(s, *(both[:, j * LANES : (j + 1) * LANES] for j in range(3)))
            both = mm(a, spread_ref[s, :, 4 * LANES : 6 * LANES])
            odd.append((both[:, :LANES], both[:, LANES:]))
        put(
            2,
            jnp.where(head, odd[0][0], swap_halves(odd[1][0])),
            jnp.where(head, swap_halves(odd[0][0]), odd[1][0]),
            jnp.where(head, odd[0][1], swap_halves(odd[1][1])),
        )
        return carry

    lax.fori_loop(0, blocks, project, 0)
    store(0, 1, 2, 3)

    def o_copy(p):
        lanes = pl.ds(pl.multiple_of(own + p * LANES, LANES), LANES)
        return remote(
            o_ref.at[:, lanes], o_ref.at[:, lanes], core_send.at[p], core_recv.at[p], partner
        )

    def attend(p, carry):
        lanes = pl.ds(pl.multiple_of(own + p * LANES, LANES), LANES)
        for i in range(blocks):
            rows = pl.ds(i * BLK, BLK)
            seen = pl.ds(0, (i + 1) * BLK)
            q, k, v = q_ref[p, rows, :], k_ref[p, seen, :], v_ref[p, seen, :]
            halves = []
            for side in range(2):
                chosen = head if side == 0 else jnp.logical_not(head)
                s = mm_nt(jnp.where(chosen, q, jnp.zeros_like(q)), k)
                high = jnp.max(s, axis=-1, keepdims=True)
                e = jnp.exp(s - high)
                total = jnp.sum(e, axis=-1, keepdims=True)
                halves.append(mm(e.astype(BF16), v) * (1.0 / total))
                log_total = jnp.broadcast_to(high + jnp.log(total), (BLK, LANES))
                lse_ref[2 * p + side, :, rows] = jnp.transpose(log_total)[0:8, :]
            o_ref[rows, lanes] = jnp.where(head, halves[0], halves[1]).astype(BF16)
        o_copy(p).start()
        return carry

    lax.fori_loop(0, pairs, attend, 0)
    wo_copy.wait()
    for p in range(pairs):
        o_copy(p).wait()
    store(4, 5, 7)
    prev_lines = jnp.where(m == 0, prev_all_ref[:, 0, :], prev_all_ref[:, 1, :])
    spare = jnp.zeros((LANES - columns - 2, rows_all), F32)
    facts = jnp.concatenate([prev_lines, routes_ref[...].astype(F32), spare], axis=0)
    gates_ref[...] = facts

    gain_moe = extra_ref[columns + 5 : columns + 6, :]

    def middle(i, carry):
        rows = pl.ds(pl.multiple_of(i * BLK, BLK), BLK)
        z = mm_nt(o_ref[rows, :], wo_ref[...])
        h = x_ref[rows, :].astype(F32) + z
        r = lax.rsqrt(jnp.mean(h * h, axis=-1, keepdims=True) + EPSILON)
        ub = (h * r * gain_moe).astype(BF16)
        h_ref[rows, :] = h
        ub_ref[rows, :] = ub
        scores = mm(ub, small_ref[...])
        lane = lane_ids(BLK)
        facts = jnp.transpose(gates_ref[:, rows])
        e0 = facts[:, columns : columns + 1]
        e1 = facts[:, columns + 1 : columns + 2]
        hot0, hot1 = lane.astype(F32) == e0, lane.astype(F32) == e1
        logits = scores + facts
        g0, g1 = soft_pair(pick(hot0, logits), pick(hot1, logits))
        mix = [pick(lane == columns + j, scores) for j in range(4)]
        a00, a01 = soft_pair(mix[0], mix[1])
        a10, a11 = soft_pair(mix[2], mix[3])
        table = jnp.zeros((BLK, LANES), F32)
        for j, value in enumerate([g0, g1, a00, a01, a10, a11, r, e0, e1]):
            table = jnp.where(lane == j, value, table)
        stat_ref[rows, :] = table
        gates = jnp.where(hot0, g0, 0.0) + jnp.where(hot1, g1, 0.0)
        gates_ref[:, rows] = jnp.transpose(gates)
        return carry

    lax.fori_loop(0, blocks, middle, 0)
    piece = lax.broadcasted_iota(jnp.int32, (8, rows_all), 0)

    def slot_step(i, carry):
        hot = two_hot(i)
        rows = mm(hot, ub_ref[...]).astype(BF16)
        for side in range(2):
            e = 2 * i + side
            slot_ref[e] = rows[side * padded : (side + 1) * padded]
            gate = gates_ref[pl.ds(e, 1), :]
            high = gate.astype(BF16).astype(F32)
            mid = (gate - high).astype(BF16).astype(F32)
            low = gate - high - mid
            lines = jnp.where(piece == 0, high, jnp.where(piece == 1, mid, low))
            lines = jnp.where(piece < 3, lines, 0.0).astype(BF16)
            gate = mm_nt(lines, hot[side * padded : (side + 1) * padded])
            gate = jnp.sum(gate, axis=0, keepdims=True)
            gate_ref[e] = jnp.broadcast_to(gate, (8, padded))
        return carry

    lax.fori_loop(0, n // 2, slot_step, 0)
    def finish(j, carry):
        dy_copy(j).wait()
        return carry

    lax.fori_loop(1, n, finish, 0)
    for copy in stays:
        copy.wait()
    for copy in [] if gathered else sends:
        copy.wait_send()
    for copy in weight_copies:
        copy.wait()
    for i in range(early):
        pltpu.make_async_copy(kept[i], stored[i], store_sem.at[i]).wait()


def flip(value, index, size):
    bit = 1
    while bit < size:
        chosen = lax.rem(lax.div(index, bit), 2)
        value = value + chosen * (bit - 2 * bit * lax.rem(lax.div(value, bit), 2))
        bit *= 2
    return value


def expert_exchange_kernel(
    n,
    padded,
    slot_src_ref,
    gate_src_ref,
    dy_src_ref,
    in_own_ref,
    in_chip_ref,
    down_own_ref,
    gy_ref,
    own_in_ref,
    own_down_ref,
    chip_in_ref,
    far_down_ref,
    dx_all_ref,
    dg_all_ref,
    x_ref,
    xt_ref,
    dy_ref,
    scaled_ref,
    scale_ref,
    gate_ref,
    win_ref,
    wdown_ref,
    hidden_ref,
    dgate_ref,
    dup_ref,
    y_ref,
    dx_ref,
    dg_ref,
    land_in_ref,
    land_down_ref,
    chip_down_ref,
    load,
    slot_send,
    slot_recv,
    gate_send,
    gate_recv,
    dx_send,
    dx_recv,
    dg_send,
    dg_recv,
    pass_send,
    pass_recv,
    sum_send,
    sum_recv,
    w_send,
    w_recv,
):
    width = x_ref.shape[1]
    share = win_ref.shape[3]
    chunks = 4
    group = n // chunks
    span = group * padded
    block = 256
    d, t = lax.axis_index("dp"), lax.axis_index("tensor")
    c = lax.rem(t, 2)
    partner = (d, t + 1 - 2 * c)
    across = (d, lax.rem(t + 2, 4))
    greet(plane_peers(n, d, t) + [partner, across])

    def rows_of(i):
        return pl.ds(pl.multiple_of(i * padded, padded), padded)

    def slot_copy(i):
        e = flip(d, i, n)
        return remote(
            slot_src_ref.at[e], x_ref.at[rows_of(i)], slot_send.at[i], slot_recv.at[i], (e, t)
        )

    def gate_copy(i):
        e = flip(d, i, n)
        return remote(
            gate_src_ref.at[e], gate_ref.at[i], gate_send.at[i], gate_recv.at[i], (e, t)
        )

    def dx_copy(i):
        e = flip(d, i, n)
        return remote(
            dx_ref.at[rows_of(i)], dx_all_ref.at[c, d], dx_send.at[i], dx_recv.at[i], (e, t)
        )

    def dg_copy(i):
        e = flip(d, i, n)
        return remote(dg_ref.at[i], dg_all_ref.at[c, d], dg_send.at[i], dg_recv.at[i], (e, t))

    def hand(kind, i):
        ref = (dx_all_ref, dg_all_ref)[kind]
        block_ref = ref.at[c, flip(d, i, n)]
        return remote(
            block_ref, block_ref, pass_send.at[kind, i], pass_recv.at[kind, i], partner
        )

    def down_rows(s):
        return pl.ds(s * share, share)

    def send_chunk(k):
        for q in range(group):
            if k + q > 0:
                slot_copy(k * group + q).start()
                gate_copy(k * group + q).start()

    send_chunk(2)
    send_chunk(1)
    if group > 1:
        send_chunk(0)
    stays = [
        pltpu.make_async_copy(slot_src_ref.at[d], x_ref.at[rows_of(0)], load.at[0]),
        pltpu.make_async_copy(gate_src_ref.at[d], gate_ref.at[0], load.at[1]),
    ]
    own_loads = [
        pltpu.make_async_copy(in_own_ref.at[0], win_ref.at[0], load.at[2]),
        pltpu.make_async_copy(down_own_ref.at[0], wdown_ref.at[down_rows(0)], load.at[3]),
    ]
    chip_load = pltpu.make_async_copy(in_chip_ref.at[0], win_ref.at[2], load.at[4])
    weights = [
        remote(in_own_ref.at[0], win_ref.at[1], w_send.at[0], w_recv.at[0], partner),
        remote(
            down_own_ref.at[0], wdown_ref.at[down_rows(1)], w_send.at[1], w_recv.at[1], partner
        ),
        remote(in_chip_ref.at[0], win_ref.at[3], w_send.at[2], w_recv.at[2], partner),
        remote(
            down_own_ref.at[0], wdown_ref.at[down_rows(2)], w_send.at[3], w_recv.at[3], across
        ),
        remote(
            wdown_ref.at[down_rows(2)],
            wdown_ref.at[down_rows(3)],
            w_send.at[4],
            w_recv.at[4],
            partner,
        ),
    ]

    def dy_load(i):
        return pltpu.make_async_copy(
            dy_src_ref.at[flip(d, i, n)], dy_ref.at[rows_of(i)], load.at[10 + i]
        )

    for copy in [weights[3]] + stays + own_loads:
        copy.start()
    for i in range(n):
        dy_load(i).start()
    chip_load.start()
    for copy in weights[0:3]:
        copy.start()
    for copy in stays + own_loads:
        copy.wait()

    def take(k):
        rows = pl.ds(k * span, span)
        for q in range(group):
            i = k * group + q
            if i > 0:
                slot_copy(i).wait_recv()
                gate_copy(i).wait_recv()
            dy_load(i).wait()
            near = rows_of(i)
            line = jnp.broadcast_to(gate_ref[i, 0:1, :], (LANES, padded))
            scale = jnp.transpose(line)
            scale_ref[near, :] = scale
            scaled_ref[near, :] = (dy_ref[near, :].astype(F32) * scale[:, 0:1]).astype(BF16)
        xt_ref[:, rows] = jnp.transpose(x_ref[rows, :])

    per = share // block

    def units(first, last, chosen):
        def unit(u, carry):
            k = first + lax.div(u, 2 * per)
            b = lax.rem(u, 2 * per)
            s = chosen * 2 + lax.div(b, per)
            rows = pl.ds(pl.multiple_of(k * span, span), span)
            lanes = pl.ds(pl.multiple_of(lax.rem(b, per) * block, block), block)
            far = pl.ds(pl.multiple_of((chosen * 2 * per + b) * block, block), block)
            x = x_ref[rows, :]
            gate = mm(x, win_ref[s, 0, :, lanes])
            up = mm(x, win_ref[s, 1, :, lanes])
            grad = mm_nt(scaled_ref[rows, :], wdown_ref[far, :])
            sigma = 0.5 * jnp.tanh(0.5 * gate) + 0.5
            active = gate * sigma
            hidden_ref[rows, far] = (active * up).astype(BF16)
            dgate_ref[rows, far] = (grad * up * (sigma * (1.0 + gate * (1.0 - sigma)))).astype(
                BF16
            )
            dup_ref[rows, far] = (grad * active).astype(BF16)
            return carry

        lax.fori_loop(0, (last - first) * 2 * per, unit, 0)

    def close(k, carry):
        rows = pl.ds(pl.multiple_of(k * span, span), span)
        for j in range(width // block):
            lanes = pl.ds(j * block, block)
            total = jnp.zeros((span, block), F32)
            for s in range(4):
                far = pl.ds(s * share, share)
                total = total + mm_nt(dgate_ref[rows, far], win_ref[s, 0, lanes, :])
                total = total + mm_nt(dup_ref[rows, far], win_ref[s, 1, lanes, :])
            dx_ref[rows, lanes] = total.astype(BF16)
        for q in range(group):
            i = k * group + q

            @pl.when(i > 0)
            def _():
                dx_copy(i).start()

        for j in range(width // block):
            lanes = pl.ds(j * block, block)
            y_ref[:, lanes] = mm(hidden_ref[rows, :], wdown_ref[:, lanes])
        for q in range(group):
            i = k * group + q
            near = rows_of(i)
            y = y_ref[pl.ds(q * padded, padded), :]
            gy_ref[flip(d, i, n)] = (y * scale_ref[near, 0:1]).astype(BF16)
            dot = jnp.sum(y * dy_ref[near, :].astype(F32), axis=-1, keepdims=True)
            dg_ref[i] = jnp.transpose(jnp.broadcast_to(dot, (padded, LANES)))[0:8, :]

            @pl.when(i > 0)
            def _():
                dg_copy(i).start()

        return carry

    take(0)
    for copy in weights[0:2]:
        copy.wait_recv()
    units(0, 1, 0)
    take(1)
    units(1, 2, 0)
    take(2)
    send_chunk(3)
    units(2, 3, 0)
    chip_load.wait()
    weights[3].wait_recv()
    weights[4].start()
    weights[2].wait_recv()
    weights[4].wait_recv()
    units(0, 3, 1)
    lax.fori_loop(2, 3, close, 0)
    lax.fori_loop(0, 2, close, 0)
    take(3)
    units(3, 4, 0)
    units(3, 4, 1)
    lax.fori_loop(3, 4, close, 0)
    keeps = [
        pltpu.make_async_copy(dx_ref.at[rows_of(0)], dx_all_ref.at[c, d], load.at[0]),
        pltpu.make_async_copy(dg_ref.at[0], dg_all_ref.at[c, d], load.at[1]),
    ]
    for copy in keeps:
        copy.start()

    def forward(first, last):
        def step(i, carry):
            dx_copy(i).wait_recv()
            dg_copy(i).wait_recv()
            hand(0, i).start()
            hand(1, i).start()
            return carry

        lax.fori_loop(first, last, step, 0)

    def grad_in(s, kind, b):
        far = pl.ds(pl.multiple_of(s * share + b * block, block), block)
        return mm(xt_ref[...], (dgate_ref, dup_ref)[kind][:, far])

    def grad_down(s, b):
        far = pl.ds(pl.multiple_of(s * share + b * block, block), block)
        return mm_tn(hidden_ref[:, far], scaled_ref[...])

    def sum_copies(j):
        return [
            remote(win_ref.at[j], land_in_ref.at[j], sum_send.at[j], sum_recv.at[j], partner),
            remote(
                wdown_ref.at[pl.ds(j * share, share)],
                land_down_ref.at[j],
                sum_send.at[2 + j],
                sum_recv.at[2 + j],
                partner,
            ),
        ]

    for copy in weights:
        copy.wait_send()

    def down_sums(s, put):
        def unit(b, carry):
            put(pl.ds(pl.multiple_of(b * block, block), block), grad_down(s, b))
            return carry

        lax.fori_loop(0, per, unit, 0)

    def in_sums(s, put):
        def unit(b, carry):
            lanes = pl.ds(pl.multiple_of(b * block, block), block)
            for kind in range(2):
                put(kind, lanes, grad_in(s, kind, b))
            return carry

        lax.fori_loop(0, per, unit, 0)

    def leave_down(j, s):
        def put(rows, value):
            near = pl.multiple_of(rows.start + j * share, block)
            wdown_ref[pl.ds(near, block), :] = value.astype(BF16)

        down_sums(s, put)
        sum_copies(j)[1].start()

    def leave_in(j, s):
        def put(kind, lanes, value):
            win_ref[j, kind, :, lanes] = value.astype(BF16)

        in_sums(s, put)
        sum_copies(j)[0].start()

    leave_down(0, 3)
    leave_down(1, 1)
    sum_copies(0)[1].wait_recv()

    def chip_down(lanes, value):
        chip_down_ref[0, lanes, :] = (value + land_down_ref[0, lanes, :].astype(F32)).astype(BF16)

    down_sums(2, chip_down)
    far_copy = remote(chip_down_ref, far_down_ref, w_send.at[5], w_recv.at[5], across)
    far_copy.start()
    for copy in keeps:
        copy.wait()
    hand(0, 0).start()
    hand(1, 0).start()
    forward(1, 2 * group)
    leave_in(0, 3)
    leave_in(1, 1)
    sum_copies(0)[0].wait_recv()

    def chip_in(kind, lanes, value):
        chip_in_ref[0, kind, :, lanes] = (
            value + land_in_ref[0, kind, :, lanes].astype(F32)
        ).astype(BF16)

    in_sums(2, chip_in)
    for copy in sum_copies(1):
        copy.wait_recv()

    def own_in(kind, lanes, value):
        own_in_ref[0, kind, :, lanes] = value + land_in_ref[1, kind, :, lanes].astype(F32)

    def own_down(lanes, value):
        own_down_ref[0, lanes, :] = value + land_down_ref[1, lanes, :].astype(F32)

    in_sums(0, own_in)
    down_sums(0, own_down)
    forward(2 * group, n)

    def clear(i, carry):
        for copy in (slot_copy(i), gate_copy(i), dx_copy(i), dg_copy(i)):
            copy.wait_send()
        return carry

    lax.fori_loop(1, n, clear, 0)

    def passed(i, carry):
        hand(0, i).wait()
        hand(1, i).wait()
        return carry

    lax.fori_loop(0, n, passed, 0)
    for j in range(2):
        for copy in sum_copies(j):
            copy.wait_send()
    far_copy.wait()


def expert_kernel(
    sources,
    padded,
    x_ref,
    dy_ref,
    gate_ref,
    *refs,
):
    weights, outs = refs[:8], refs[8:19]
    in_refs, down_refs = weights[0:4], weights[4:8]
    gy_ref, dx_ref, dg_ref = outs[0:3]
    gin_refs, gdown_refs = outs[3:7], outs[7:11]
    xt_ref, scaled_ref, scale_ref, y_acc, dx_acc, win_ref, wdown_ref = refs[19:]
    step = pl.program_id(0)
    last = pl.num_programs(0) - 1

    @pl.when(step == 0)
    def _():
        xt_ref[...] = jnp.transpose(x_ref[...])
        for s in range(sources):
            rows = pl.ds(s * padded, padded)
            line = jnp.broadcast_to(gate_ref[s, 0:1, :], (LANES, padded))
            scale = jnp.transpose(line)
            scale_ref[rows, :] = scale
            scaled_ref[rows, :] = (dy_ref[rows, :].astype(F32) * scale[:, 0:1]).astype(BF16)
        y_acc[...] = jnp.zeros_like(y_acc)
        dx_acc[...] = jnp.zeros_like(dx_acc)

    per = pl.num_programs(0) // 4
    for i in range(4):

        @pl.when(lax.div(step, per) == i)
        def _():
            win_ref[...] = in_refs[i][0]
            wdown_ref[...] = down_refs[i][0]

    x = x_ref[...]
    gate = mm(x, win_ref[0])
    up = mm(x, win_ref[1])
    sigma = 1.0 / (1.0 + jnp.exp(-gate))
    active = gate * sigma
    hidden = (active * up).astype(BF16)
    y_acc[...] += mm(hidden, wdown_ref[...])
    scaled = scaled_ref[...]
    grad_hidden = mm_nt(scaled, wdown_ref[...])
    grad_gate = (grad_hidden * up * (sigma * (1.0 + gate * (1.0 - sigma)))).astype(BF16)
    grad_up = (grad_hidden * active).astype(BF16)
    dx_acc[...] += mm_nt(grad_gate, win_ref[0]) + mm_nt(grad_up, win_ref[1])
    xt = xt_ref[...]
    part_gate = mm(xt, grad_gate).astype(BF16)
    part_up = mm(xt, grad_up).astype(BF16)
    part_down = mm_tn(hidden, scaled).astype(BF16)
    for i in range(4):

        @pl.when(lax.div(step, per) == i)
        def _():
            gin_refs[i][0, 0] = part_gate
            gin_refs[i][0, 1] = part_up
            gdown_refs[i][0] = part_down

    @pl.when(step == last)
    def _():
        for s in range(sources):
            rows = pl.ds(s * padded, padded)
            y = y_acc[rows, :]
            gy_ref[s] = (y * scale_ref[rows, 0:1]).astype(BF16)
            dot = jnp.sum(y * dy_ref[rows, :].astype(F32), axis=-1, keepdims=True)
            dg_ref[s] = jnp.transpose(jnp.broadcast_to(dot, (padded, LANES)))[0:8, :]
            dx_ref[s] = dx_acc[rows, :].astype(BF16)


def rear_kernel(n, half, padded, gathered, part, *refs):
    crossing = 0 if gathered else 1
    chip_in_refs, refs = refs[:crossing], refs[crossing:]
    gy_src_ref, tokens_ref, cotangent_ref, o_all_ref = refs[:4]
    loaded, refs = refs[4:17], refs[17:]
    stat_ref, pos_ref, small_ref, extra_ref, dg_ref = refs[:5]
    result_ref, grad_x_ref, logit_ref, grads_ref, lines_ref = refs[5:10]
    far_in_refs, refs = refs[10 : 10 + crossing], refs[10 + crossing :]
    kept, refs = refs[:13], refs[13:]
    dx_ref, h_ref, wo_ref, ub_ref, q_ref, k_ref, v_ref = kept[:7]
    lse_ref, cos_ref, sin_ref, a_ref, spread_a_ref, spread_b_ref = kept[7:]
    x_ref, dy_ref, o_ref, gy_ref, dh_ref, dzb_ref, do_ref, low_ref, row_ref = refs[:9]
    dp_ref, dk_acc, dv_acc, wo_odd_ref, pack_ref, line_ref, y_in_ref, z_in_ref = refs[9:17]
    line_in_ref, cross_ref, cross_in_ref, cross_line_ref = refs[17:21]
    da_out_ref, da_in_ref, da_own_ref, norm_ref, norm_in_ref, half_ref = refs[21:27]
    load, fetch_sem, gy_send, gy_recv, stay, pass_send, pass_recv = refs[27:34]
    grad_send, grad_recv, line_send, line_recv, pair_send, pair_recv = refs[34:40]
    out_send, out_recv, sum_send, sum_recv = refs[40:]

    def fetch(i):
        src = loaded[i]
        if i == 11:
            src = src.at[:, :, pl.ds(0, 3 * LANES)]
        if i == 12:
            src = src.at[:, :, pl.ds(4 * LANES, 2 * LANES)]
        return pltpu.make_async_copy(src, kept[i], fetch_sem.at[i])

    rows_all, width = dy_ref.shape
    blocks = rows_all // BLK
    pairs = q_ref.shape[0]
    local = pairs * LANES
    columns = n + 4
    slots = n * padded
    d, t = lax.axis_index("dp"), lax.axis_index("tensor")
    m, c = lax.div(t, 2), lax.rem(t, 2)
    partner = (d, t + 1 - 2 * c)
    across = (d, lax.rem(t + 2, 4))
    rows_half = rows_all // 2
    own = pl.multiple_of(c * local, LANES)
    own_lanes = pl.ds(own, local)
    place = pl.ds(pl.multiple_of(c * rows_half, BLK), rows_half)
    loads = [
        pltpu.make_async_copy(src, dst, load.at[i])
        for i, (src, dst) in enumerate(
            [
                (cotangent_ref.at[m], dy_ref),
                (tokens_ref.at[m, place], x_ref),
                (o_all_ref.at[:, own_lanes], o_ref),
            ]
        )
    ]
    for i in range(2):
        fetch(i).start()
    for copy in loads:
        copy.start()
    for i in range(2, 13):
        fetch(i).start()
    greet(plane_peers(n, d, t) + [partner, across])

    sum_copies = [
        remote(src, land, sum_send.at[0], sum_recv.at[0], across)
        for src, land in zip(chip_in_refs, far_in_refs)
    ]
    for copy in sum_copies:
        copy.start()

    def give(j):
        s = lax.rem(d + j, n)
        return remote(gy_src_ref.at[s], gy_ref.at[c, d], gy_send.at[j], gy_recv.at[j], (s, t))

    def hand(j):
        block = gy_ref.at[c, lax.rem(d + n - j, n)]
        return remote(block, block, pass_send.at[j], pass_recv.at[j], partner)

    keep = pltpu.make_async_copy(gy_src_ref.at[d], gy_ref.at[c, d], stay.at[0])
    keep.start()

    def give_start(j, carry):
        give(j).start()
        return carry

    lax.fori_loop(1, n, give_start, 0)

    def collect():
        keep.wait()
        hand(0).start()

        def step(j, carry):
            give(j).wait_recv()
            hand(j).start()
            return carry

        lax.fori_loop(1, n, step, 0)

    def settle():
        def step(j, carry):
            hand(j).wait_recv()
            return carry

        lax.fori_loop(0, n, step, 0)

    row_ref[...] = jnp.zeros_like(row_ref)
    for copy in loads:
        copy.wait()
    for i in range(3):
        fetch(i).wait()

    gain_moe = extra_ref[columns + 5 : columns + 6, :]
    vec0 = extra_ref[columns + 6 : columns + 7, :]
    vec1 = extra_ref[columns + 7 : columns + 8, :]
    group = max(1, min(n, (1024 if slots <= 1024 else 512) // padded))
    span = group * padded

    def combine(wheres, ref, lines=None):
        total = jnp.zeros((BLK, width), F32)
        entries = [jnp.zeros((BLK, 1), F32) for _ in wheres]
        slot = lax.broadcasted_iota(jnp.int32, (BLK, span), 1)
        for side in range(2):
            for first in range(0, n, group):
                start = side * slots + first * padded
                hots = [slot == where - start for where in wheres]
                hot = jnp.where(hots[0] | hots[1], 1.0, 0.0).astype(BF16)
                block = ref[side, first : first + group].reshape(span, width)
                total = total + mm(hot, block)
                if lines is not None:
                    line = jnp.concatenate(
                        [lines[side, first + e, 0:1, :] for e in range(group)], axis=1
                    )
                    entries = [
                        entry + jnp.sum(jnp.where(one, line, 0.0), axis=-1, keepdims=True)
                        for entry, one in zip(entries, hots)
                    ]
        return total, entries

    def facts(rows):
        lane = lane_ids(BLK)
        stats = stat_ref[rows, :]
        values = [stats[:, j : j + 1] for j in range(7)]
        e0, e1 = stats[:, 7:8].astype(jnp.int32), stats[:, 8:9].astype(jnp.int32)
        wheres = []
        places = pos_ref[rows, :]
        for e in (e0, e1):
            place = pick(lane == e, places).astype(jnp.int32)
            side = (place >= half).astype(jnp.int32)
            where = side * (slots - half) + e * padded + place
            wheres.append(jnp.where(e < n, where, -1))
        g0, g1 = values[0:2]

        def named(number):
            return jnp.where(e0 == number, g0, 0.0) + jnp.where(e1 == number, g1, 0.0)

        copied, first, second = named(n + 1), named(n + 2), named(n + 3)
        on_u = copied + first * values[2] + second * values[4]
        return values, e0, e1, wheres, first, second, on_u

    def back(i, carry):
        rows = pl.ds(pl.multiple_of(i * BLK, BLK), BLK)
        values, e0, e1, wheres, first, second, on_u = facts(rows)
        g0, g1, a00, a01, a10, a11, r = values
        lane = lane_ids(BLK)
        grads, (f0, f1) = combine(wheres, dx_ref, dg_ref)
        h = h_ref[rows, :]
        normed = h * r
        u = normed * gain_moe
        dy = dy_ref[rows, :].astype(F32)
        s_u = jnp.sum(dy * u, axis=-1, keepdims=True)
        s_0 = jnp.sum(dy * vec0, axis=-1, keepdims=True)
        s_1 = jnp.sum(dy * vec1, axis=-1, keepdims=True)

        def other(e):
            value = jnp.where(e == n + 1, s_u, 0.0)
            value = jnp.where(e == n + 2, a00 * s_u + a01 * s_0, value)
            return jnp.where(e == n + 3, a10 * s_u + a11 * s_1, value)

        dg0, dg1 = f0 + other(e0), f1 + other(e1)
        mean = g0 * dg0 + g1 * dg1
        dl = jnp.where(lane == e0, g0 * (dg0 - mean), 0.0) + jnp.where(
            lane == e1, g1 * (dg1 - mean), 0.0
        )
        turned = jnp.transpose(dl)
        logit_ref[m, :, rows] = turned[0 : logit_ref.shape[1], :]
        d00, d01 = first * s_u, first * s_0
        d10, d11 = second * s_u, second * s_1
        m0 = a00 * d00 + a01 * d01
        m1 = a10 * d10 + a11 * d11
        low = dl
        for j, value in enumerate(
            [a00 * (d00 - m0), a01 * (d01 - m0), a10 * (d10 - m1), a11 * (d11 - m1)]
        ):
            low = jnp.where(lane == columns + j, value, low)
        low = low.astype(BF16)
        low_ref[rows, :] = low
        du = grads + mm_nt(low, small_ref[...]) + on_u * dy
        row_ref[0:1, :] += jnp.sum(du * normed, axis=0, keepdims=True)
        row_ref[1:2, :] += jnp.sum((first * a01) * dy, axis=0, keepdims=True)
        row_ref[2:3, :] += jnp.sum((second * a11) * dy, axis=0, keepdims=True)
        dn = du * gain_moe
        dh = dy + r * (dn - normed * jnp.mean(dn * normed, axis=-1, keepdims=True))

        @pl.when(lax.div(i, blocks // 2) == c)
        def _():
            near = pl.multiple_of(i * BLK - c * rows_half, BLK)
            dh_ref[pl.ds(near, BLK), :] = dh

        dzb = dh.astype(BF16)
        dzb_ref[rows, :] = dzb
        do_ref[rows, :] = mm(dzb, wo_ref[:, own_lanes]).astype(BF16)
        return carry

    lax.fori_loop(0, blocks, back, 0)
    logit_copy = remote(
        logit_ref.at[m], logit_ref.at[m], pair_send.at[0], pair_recv.at[0], across
    )
    logit_copy.start()

    fetch(3).wait()
    grad_wo = mm_tn(dzb_ref[...], o_ref[...])
    pack_ref[0, :, 3 * LANES : 4 * LANES] = grad_wo[:, 0:LANES].astype(BF16)
    pack_ref[1, :, 3 * LANES : 4 * LANES] = grad_wo[:, LANES : 2 * LANES].astype(BF16)
    wo_odd_ref[...] = grad_wo[:, 2 * LANES : 3 * LANES]
    line_ref[...] = mm_tn(ub_ref[...], low_ref[...])

    def slab(owner):
        return pl.ds(pl.multiple_of(owner * part, part), part)

    ring = n // 2
    y_own = lax.rem(d, 2)
    beside = (d + 1 - 2 * y_own, t)
    z_own = lax.div(d, 2)
    wide_lanes = (pl.ds(0, 4 * LANES), pl.ds(4 * LANES, 2 * LANES))

    def y_copy(s, stage, z):
        lanes = wide_lanes[stage]
        return remote(
            pack_ref.at[s, slab(2 * z + 1 - y_own), lanes],
            y_in_ref.at[s, z, :, lanes],
            grad_send.at[stage, s, z],
            grad_recv.at[stage, s, z],
            beside,
        )

    def z_copy(s, stage, j):
        lanes = wide_lanes[stage]
        z = lax.rem(z_own + j, ring)
        return remote(
            pack_ref.at[s, slab(2 * z + y_own), lanes],
            z_in_ref.at[s, j, :, lanes],
            grad_send.at[2 + stage, s, j],
            grad_recv.at[2 + stage, s, j],
            (2 * z + y_own, t),
        )

    def y_start(s, stage):
        for z in range(ring):
            y_copy(s, stage, z).start()

    def z_start(s, stage):
        lanes = wide_lanes[stage]
        for z in range(ring):
            y_copy(s, stage, z).wait()
            rows = slab(2 * z + y_own)
            value = pack_ref[s, rows, lanes].astype(F32) + y_in_ref[s, z, :, lanes].astype(F32)
            pack_ref[s, rows, lanes] = value.astype(BF16)
        for j in range(1, ring):
            z_copy(s, stage, j).start()

    def line_copy(j):
        e = lax.rem(d + j, n)
        return remote(
            line_ref.at[slab(e), :],
            line_in_ref.at[d],
            line_send.at[j],
            line_recv.at[j],
            (e, t),
        )

    head = half_mask(BLK)

    def attend_back(p):
        dk_acc[...] = jnp.zeros_like(dk_acc)
        dv_acc[...] = jnp.zeros_like(dv_acc)
        dq = []
        for i in range(blocks):
            rows = pl.ds(i * BLK, BLK)
            seen = pl.ds(0, (i + 1) * BLK)
            lanes = pl.ds(pl.multiple_of(p * LANES, LANES), LANES)
            q, do = q_ref[p, rows, :], do_ref[rows, lanes]
            k, v = k_ref[p, seen, :], v_ref[p, seen, :]
            zero = jnp.zeros_like(q)
            parts = []
            dk, dv = dk_acc[seen, :], dv_acc[seen, :]
            for side in range(2):
                chosen = head if side == 0 else jnp.logical_not(head)
                qm, dom = jnp.where(chosen, q, zero), jnp.where(chosen, do, zero)
                prob = jnp.exp(mm_nt(k, qm) - lse_ref[2 * p + side, 0:1, rows])
                grad_prob = mm_nt(v, dom)
                total = jnp.sum(prob * grad_prob, axis=0, keepdims=True)
                grad_score = (prob * (grad_prob - total)).astype(BF16)
                dv = dv + mm(prob.astype(BF16), dom)
                dk = dk + mm(grad_score, qm)
                parts.append(mm_tn(grad_score, k))
            dk_acc[seen, :] = dk
            dv_acc[seen, :] = dv
            value = jnp.where(head, parts[0], parts[1]) * (HD**-0.5)
            dq.append(turn(value, cos_ref[rows, :], -sin_ref[rows, :]))
        return (
            jnp.concatenate(dq, axis=0),
            turn(dk_acc[...], cos_ref[...], -sin_ref[...]),
            dv_acc[...],
        )

    def shard_step(i, carry):
        s = lax.rem(m + 1 + i, 2)
        for j, value in enumerate(attend_back(s)):
            dp_ref[s, :, j * LANES : (j + 1) * LANES] = value.astype(BF16)
        for j in range(3):
            lanes = pl.ds(j * LANES, LANES)
            pack_ref[s, :, lanes] = mm_tn(a_ref[...], dp_ref[s, :, lanes]).astype(BF16)
        if not gathered:
            y_start(s, 0)

            @pl.when(i == 1)
            def _():
                z_start(lax.rem(m + 1, 2), 0)

        return carry

    for i in range(4, 11):
        fetch(i).wait()
    lax.fori_loop(0, 2, shard_step, 0)
    collect()

    def publish(kind, out_ref):
        block = out_ref.at[m, place]
        copies = [
            remote(half_ref.at[kind], block, out_send.at[kind, 0], out_recv.at[kind, 0], across),
            remote(half_ref.at[kind], block, out_send.at[kind, 1], out_recv.at[kind, 1], partner),
            pltpu.make_async_copy(half_ref.at[kind], block, stay.at[1 + kind]),
        ]
        for copy in copies:
            copy.start()
        block = out_ref.at[1 - m, place]
        relay = remote(block, block, out_send.at[kind, 2], out_recv.at[kind, 2], partner)
        return copies, relay

    settle()

    def results(i, carry):
        rows = pl.ds(pl.multiple_of(i * BLK, BLK), BLK)
        far = pl.ds(pl.multiple_of(c * rows_half + i * BLK, BLK), BLK)
        values, e0, e1, wheres, first, second, on_u = facts(far)
        sums, _ = combine(wheres, gy_ref)
        h = h_ref[far, :]
        u = h * values[6] * gain_moe
        result = h + (sums + on_u * u + (first * values[3]) * vec0 + (second * values[5]) * vec1)
        half_ref[1, rows, :] = result.astype(BF16)
        return carry

    lax.fori_loop(0, rows_half // BLK, results, 0)
    result_copies, result_relay = publish(1, result_ref)

    dq, dk, dv = attend_back(2)
    wide = half_mask(rows_all)
    odd = [
        (jnp.where(wide, dq, swap_halves(dk)), jnp.where(wide, dv, 0.0)),
        (jnp.where(wide, swap_halves(dq), dk), jnp.where(wide, swap_halves(dv), 0.0)),
    ]
    tall = half_mask(width)
    for s in range(2):
        for j in range(2):
            dp_ref[s, :, (3 + j) * LANES : (4 + j) * LANES] = odd[s][j].astype(BF16)
    for s in range(2):
        pack_ref[s, :, 4 * LANES : 5 * LANES] = mm_tn(
            a_ref[...], dp_ref[s, :, 3 * LANES : 4 * LANES]
        ).astype(BF16)
        last = mm_tn(a_ref[...], dp_ref[s, :, 4 * LANES : 5 * LANES])
        side = wo_odd_ref[...]
        side = swap_halves(side) if s == 0 else side
        pack_ref[s, :, 5 * LANES : 6 * LANES] = jnp.where(tall, last, side).astype(BF16)
    if not gathered:
        y_start(0, 1)
        y_start(1, 1)
        z_start(m, 0)

    def da_rows(start):
        rows = pl.ds(pl.multiple_of(start, BLK), BLK)
        total = jnp.zeros((BLK, width), F32)
        for s in range(2):
            total = total + mm_nt(dp_ref[s, rows, 0 : 3 * LANES], spread_a_ref[s])
            total = total + mm_nt(dp_ref[s, rows, 3 * LANES : 5 * LANES], spread_b_ref[s])
        return total

    fetch(11).wait()
    fetch(12).wait()

    def da_other(i, carry):
        rows = pl.ds(pl.multiple_of(i * BLK, BLK), BLK)
        da_out_ref[rows, :] = da_rows((1 - c) * rows_half + i * BLK).astype(BF16)
        return carry

    lax.fori_loop(0, rows_half // BLK, da_other, 0)
    da_copy = remote(da_out_ref, da_in_ref, pair_send.at[1], pair_recv.at[1], partner)
    da_copy.start()

    def da_own(i, carry):
        rows = pl.ds(pl.multiple_of(i * BLK, BLK), BLK)
        da_own_ref[rows, :] = da_rows(c * rows_half + i * BLK)
        return carry

    lax.fori_loop(0, rows_half // BLK, da_own, 0)
    if not gathered:
        z_start(0, 1)
        z_start(1, 1)
    da_copy.wait()
    gain_attn = extra_ref[columns + 4 : columns + 5, :]
    norm_ref[...] = jnp.zeros_like(norm_ref)

    def finish(i, carry):
        rows = pl.ds(pl.multiple_of(i * BLK, BLK), BLK)
        x = x_ref[rows, :].astype(F32)
        r = lax.rsqrt(jnp.mean(x * x, axis=-1, keepdims=True) + EPSILON)
        normed = x * r
        da = da_own_ref[rows, :] + da_in_ref[rows, :].astype(F32)
        norm_ref[0:1, :] += jnp.sum(da * normed, axis=0, keepdims=True)
        dn = da * gain_attn
        grad = dh_ref[rows, :] + r * (dn - normed * jnp.mean(dn * normed, axis=-1, keepdims=True))
        half_ref[0, rows, :] = grad.astype(BF16)
        return carry

    lax.fori_loop(0, rows_half // BLK, finish, 0)
    norm_copy = remote(norm_ref, norm_in_ref, pair_send.at[2], pair_recv.at[2], partner)
    norm_copy.start()

    grad_x_copies, grad_x_relay = publish(0, grad_x_ref)

    norm_copy.wait()
    row_ref[3:4, :] = norm_ref[0:1, :] + norm_in_ref[0:1, :]
    turned = jnp.concatenate([row_ref[...], jnp.zeros((LANES - 8, width), F32)], axis=0)
    turned = jnp.transpose(turned)
    lane = lax.broadcasted_iota(jnp.int32, (width, LANES), 1)
    lines = line_ref[...]
    for j, source in enumerate([3, 0, 1, 2]):
        lines = jnp.where(lane == columns + 4 + j, turned[:, source : source + 1], lines)
    line_ref[...] = lines
    if gathered:
        packs = [
            pltpu.make_async_copy(pack_ref, grads_ref, load.at[0]),
            pltpu.make_async_copy(line_ref, lines_ref, load.at[1]),
        ]
        for copy in packs:
            copy.start()
        for copy in packs:
            copy.wait()
    else:

        def send(j, carry):
            line_copy(j).start()
            return carry

        lax.fori_loop(1, n, send, 0)
        line_in_ref[d] = line_ref[slab(d), :]
        for s in range(2):
            for stage in range(2):
                for j in range(1, ring):
                    z_copy(s, stage, j).wait()

        def total(s):
            value = pack_ref[s, slab(d), :].astype(F32)
            for j in range(1, ring):
                value = value + z_in_ref[s, j].astype(F32)
            return value

        cross_ref[...] = total(1 - m).astype(BF16)
        cross_copy = remote(cross_ref, cross_in_ref, pair_send.at[3], pair_recv.at[3], across)
        cross_copy.start()
        grads_ref[...] = total(m)

        def arrive_lines(j, carry):
            line_copy(j).wait()
            return carry

        lax.fori_loop(1, n, arrive_lines, 0)
        value = line_in_ref[0]
        for e in range(1, n):
            value = value + line_in_ref[e]
        cross_line_ref[0] = value
        cross_line_copy = remote(
            cross_line_ref.at[0], cross_line_ref.at[1], pair_send.at[4], pair_recv.at[4], across
        )
        cross_line_copy.start()
        cross_copy.wait()
        grads_ref[...] += cross_in_ref[...].astype(F32)
        cross_line_copy.wait()
        lines_ref[...] = cross_line_ref[0] + cross_line_ref[1]

    for copies, relay in ((grad_x_copies, grad_x_relay), (result_copies, result_relay)):
        copies[0].wait_recv()
        relay.start()
    for copies, relay in ((grad_x_copies, grad_x_relay), (result_copies, result_relay)):
        copies[0].wait_send()
        copies[1].wait()
        copies[2].wait()
        relay.wait()
    logit_copy.wait()

    for copy in sum_copies:
        copy.wait()

    def clear(j, carry):
        give(j).wait_send()
        return carry

    lax.fori_loop(1, n, clear, 0)

    def passed(j, carry):
        hand(j).wait_send()
        return carry

    lax.fori_loop(0, n, passed, 0)


def last_kernel(
    part,
    columns,
    results_ref,
    grad_x_ref,
    own_in_ref,
    far_in_ref,
    own_down_ref,
    far_down_ref,
    logit_ref,
    grads_ref,
    lines_ref,
    results_out,
    grad_x_out,
    in_out,
    down_out,
    logit_out,
    attn_out,
    moe_out,
    heads_out,
    out_out,
    router_out,
    const_out,
    vec_out,
):
    results_out[...] = results_ref[...]
    grad_x_out[...] = grad_x_ref[...]
    in_out[...] = own_in_ref[...] + far_in_ref[...].astype(F32)
    down_out[...] = own_down_ref[...] + far_down_ref[...].astype(F32)

    @pl.when(pl.program_id(0) == 0)
    def _():
        for m in range(2):
            logit_out[:, m, :] = logit_ref[m, 0:columns, :]
        firsts = [grads_ref[:, j * LANES : (j + 1) * LANES] for j in range(4)]
        odds = []
        for j in range(2):
            both = grads_ref[:, (4 + j) * LANES : (5 + j) * LANES]
            odds.extend([both, swap_halves(both)])
        for j in range(3):
            heads_out[j, :, 0:LANES] = firsts[j]
            heads_out[j, :, LANES : LANES + HD] = odds[j][:, 0:HD]
        spare = jnp.zeros((LANES - part, 2 * LANES), F32)
        rows = jnp.concatenate([firsts[3], odds[3]], axis=1)
        turned = jnp.transpose(jnp.concatenate([rows, spare], axis=0))
        out_out[...] = turned[0 : LANES + HD, 0:part]
        lines = jnp.concatenate([lines_ref[...], spare[:, 0:LANES]], axis=0)
        lines = jnp.transpose(lines)[:, 0:part]
        router_out[...] = lines[0:columns]
        const_out[...] = lines[columns : columns + 4]
        attn_out[...] = lines[columns + 4 : columns + 5]
        moe_out[...] = lines[columns + 5 : columns + 6]
        vec_out[...] = lines[columns + 6 : columns + 8]


def across_chips(value):
    return lax.ppermute(value, "tensor", [(0, 2), (2, 0), (1, 3), (3, 1)])


def across_cores(value):
    return lax.ppermute(value, "tensor", [(0, 1), (1, 0), (2, 3), (3, 2)])


def body(
    tokens,
    cotangent,
    prev_logits,
    routes,
    norm_attn,
    norm_moe,
    w_qkv,
    w_out,
    w_router,
    w_const,
    const_vec,
    w_in,
    w_down,
):
    rows, width = tokens.shape[1:]
    n = lax.axis_size("dp")
    experts = n
    columns = prev_logits.shape[2]
    capacity = 4 * max(1, 3 * rows // (4 * (experts + 4)))
    half = capacity // 2
    padded = -(-half // 16) * 16
    share = w_qkv.shape[2]
    local = 2 * share
    part = w_qkv.shape[1]
    t = lax.axis_index("tensor")
    m, c = t // 2, t % 2

    cosine, sine = (jnp.asarray(v) for v in rope_constants())
    pairs = local // LANES

    tinies = [w_router.T, w_const.T, norm_attn[None], norm_moe[None], const_vec]
    gathered = part % 16 != 0
    if gathered:
        wo_rows = w_out.T
        tiny = jnp.concatenate(
            tinies + [jnp.zeros((LANES - columns - 8, part), BF16)], axis=0
        )
        packed = jnp.concatenate(
            [w_qkv[i, :, :LANES] for i in range(3)]
            + [wo_rows[:, :LANES]]
            + [w_qkv[i, :, LANES:] for i in range(3)]
            + [wo_rows[:, LANES:], tiny.T],
            axis=1,
        )
    if gathered:
        packed = lax.all_gather(packed, "dp", axis=0, tiled=True)
        other = across_chips(packed)
        tinies = [jnp.where(m == 0, jnp.stack([packed, other]), jnp.stack([other, packed]))]
    late = [
        struct((rows, width), F32),
        struct((rows, width), BF16),
        struct((rows, LANES), F32),
        struct((n, padded, width), BF16),
        struct((n, 8, padded), F32),
        struct((LANES, width), F32),
    ]
    early = [
        struct((rows, width), BF16),
        struct((pairs, rows, LANES), BF16),
        struct((pairs, rows, LANES), BF16),
        struct((pairs, rows, LANES), BF16),
        struct((rows, width), BF16),
        struct((8, 8, rows), F32),
        struct((rows, LANES), F32),
        struct((width, width), BF16),
        struct((width, LANES), BF16),
        struct((2, width, 7 * LANES), BF16),
    ]
    landing = [struct((n, padded, width), BF16), struct(w_in.shape, BF16)]
    dma = pltpu.SemaphoreType.DMA
    outs = pl.pallas_call(
        functools.partial(front_kernel, n, half, padded, gathered, len(early)),
        out_shape=late + early + landing,
        in_specs=[aspec()] * 3 + [vspec()] * 5 + [aspec()] + [vspec()] * len(tinies),
        out_specs=[vspec()] * len(late) + [aspec()] * (len(early) + len(landing)),
        scratch_shapes=[pltpu.VMEM(o.shape, o.dtype) for o in early]
        + [
            pltpu.VMEM((rows, width), BF16),
            pltpu.VMEM((rows, width), BF16),
            pltpu.VMEM((2, rows), jnp.int32),
            pltpu.VMEM((LANES, rows), F32),
            pltpu.VMEM((LANES, rows), F32),
            pltpu.VMEM((n, padded, width), BF16),
            dma((3,)),
            dma((8, n // 2)),
            dma((8, n // 2)),
            dma((n,)),
            dma((n,)),
            dma((1,)),
            dma((pairs + 1,)),
            dma((pairs + 1,)),
            dma((1,)),
            dma((1,)),
            dma((len(early),)),
        ],
        compiler_params=pltpu.CompilerParams(
            collective_id=0, has_side_effects=True, vmem_limit_bytes=VMEM_LIMIT
        ),
        cost_estimate=pl.CostEstimate(
            flops=60_000_000_000, bytes_accessed=60_000_000, transcendentals=0
        ),
    )(
        tokens,
        cotangent,
        jnp.swapaxes(routes, 1, 2),
        jnp.transpose(prev_logits, (2, 0, 1)),
        w_qkv,
        w_out,
        cosine,
        sine,
        w_in,
        *tinies,
    )
    h, ub, stats, slots, gate_slots, extra = outs[:6]
    a, q, k, v, o_all, lse, pos, wo_all, small_all, spread, dy_arrived, in_x = outs[6:]

    hidden_width = w_in.shape[3]
    slots_all = experts * padded
    if gathered:
        in_x, down_x = across_chips(w_in), across_chips(w_down)
        in_c, down_c = across_cores(w_in), across_cores(w_down)
        in_d, down_d = across_cores(in_x), across_cores(down_x)
        chunk = min(256 if slots_all <= 1024 else 128, hidden_width)
        per = hidden_width // chunk

        def in_map(i):
            return lambda f: (0, 0, 0, jnp.clip(f - per * i, 0, per - 1))

        def down_map(i):
            return lambda f: (0, jnp.clip(f - per * i, 0, per - 1), 0)

        in_blocks = [pl.BlockSpec((1, 2, width, chunk), in_map(i)) for i in range(4)]
        down_blocks = [pl.BlockSpec((1, chunk, width), down_map(i)) for i in range(4)]
        expert_outs = (
            [
                struct((n, padded, width), BF16),
                struct((n, padded, width), BF16),
                struct((n, 8, padded), F32),
            ]
            + [struct(w_in.shape, BF16)] * 4
            + [struct(w_down.shape, BF16)] * 4
        )

        def whole(shape):
            return pl.BlockSpec(
                shape, lambda f: (0,) * len(shape), pipeline_mode=pl.Buffered(1)
            )

        parts = pl.pallas_call(
            functools.partial(expert_kernel, n, padded),
            grid=(4 * per,),
            out_shape=expert_outs,
            in_specs=[
                whole((slots_all, width)),
                whole((slots_all, width)),
                whole((n, 8, padded)),
            ]
            + in_blocks
            + down_blocks,
            out_specs=[
                whole((n, padded, width)),
                whole((n, padded, width)),
                whole((n, 8, padded)),
            ]
            + in_blocks
            + down_blocks,
            scratch_shapes=[
                pltpu.VMEM((width, slots_all), BF16),
                pltpu.VMEM((slots_all, width), BF16),
                pltpu.VMEM((slots_all, LANES), F32),
                pltpu.VMEM((slots_all, width), F32),
                pltpu.VMEM((slots_all, width), F32),
                pltpu.VMEM((2, width, chunk), BF16),
                pltpu.VMEM((chunk, width), BF16),
            ],
            compiler_params=pltpu.CompilerParams(vmem_limit_bytes=VMEM_LIMIT),
            cost_estimate=pl.CostEstimate(
                flops=18 * slots_all * width * 4 * hidden_width,
                bytes_accessed=30_000_000,
                transcendentals=0,
            ),
        )(
            lax.all_to_all(slots, "dp", split_axis=0, concat_axis=0, tiled=True).reshape(
                slots_all, width
            ),
            dy_arrived.reshape(slots_all, width),
            lax.all_to_all(gate_slots, "dp", split_axis=0, concat_axis=0, tiled=True),
            w_in,
            in_c,
            in_x,
            in_d,
            w_down,
            down_c,
            down_x,
            down_d,
        )
        gy, dx, dg = parts[0:3]
        gin, gdown = parts[3:7], parts[7:11]

        def everywhere(value):
            value = lax.all_to_all(value, "dp", split_axis=0, concat_axis=0, tiled=True)
            other = across_cores(value)
            return jnp.where(c == 0, jnp.stack([value, other]), jnp.stack([other, value]))

        dx_all, dg_all = everywhere(dx), everywhere(dg)

        def total(own, core, chip, diagonal):
            chip = (chip.astype(F32) + across_cores(diagonal).astype(F32)).astype(BF16)
            own = own.astype(F32) + across_cores(core).astype(F32)
            return own + across_chips(chip).astype(F32)

        grad_in, grad_down = total(*gin), total(*gdown)
        chip_in = []
    else:
        gy, own_in, own_down, chip_in, far_down, dx_all, dg_all = pl.pallas_call(
            functools.partial(expert_exchange_kernel, n, padded),
            out_shape=[
                struct((n, padded, width), BF16),
                struct(w_in.shape, F32),
                struct(w_down.shape, F32),
                struct(w_in.shape, BF16),
                struct(w_down.shape, BF16),
                struct((2, n, padded, width), BF16),
                struct((2, n, 8, padded), F32),
            ],
            in_specs=[aspec()] * 6,
            out_specs=[vspec()] * 4 + [aspec()] * 3,
            scratch_shapes=[
                pltpu.VMEM((slots_all, width), BF16),
                pltpu.VMEM((width, slots_all), BF16),
                pltpu.VMEM((slots_all, width), BF16),
                pltpu.VMEM((slots_all, width), BF16),
                pltpu.VMEM((slots_all, LANES), F32),
                pltpu.VMEM((n, 8, padded), F32),
                pltpu.VMEM((4, 2, width, hidden_width), BF16),
                pltpu.VMEM((4 * hidden_width, width), BF16),
                pltpu.VMEM((slots_all, 4 * hidden_width), BF16),
                pltpu.VMEM((slots_all, 4 * hidden_width), BF16),
                pltpu.VMEM((slots_all, 4 * hidden_width), BF16),
                pltpu.VMEM((slots_all // 4, width), F32),
                pltpu.VMEM((slots_all, width), BF16),
                pltpu.VMEM((n, 8, padded), F32),
                pltpu.VMEM((2,) + w_in.shape[1:], BF16),
                pltpu.VMEM((2,) + w_down.shape[1:], BF16),
                pltpu.VMEM(w_down.shape, BF16),
                dma((10 + n,)),
                dma((n,)),
                dma((n,)),
                dma((n,)),
                dma((n,)),
                dma((n,)),
                dma((n,)),
                dma((n,)),
                dma((n,)),
                dma((2, n)),
                dma((2, n)),
                dma((4,)),
                dma((4,)),
                dma((6,)),
                dma((6,)),
            ],
            compiler_params=pltpu.CompilerParams(
                collective_id=2, has_side_effects=True, vmem_limit_bytes=VMEM_LIMIT
            ),
            cost_estimate=pl.CostEstimate(
                flops=60_000_000_000, bytes_accessed=40_000_000, transcendentals=0
            ),
        )(
            slots,
            gate_slots,
            dy_arrived,
            w_in,
            in_x,
            w_down,
        )
        chip_in = [chip_in]

    groups = 6 * LANES
    logit_rows = -(-columns // 8) * 8
    rear_outs = [
        struct((2, logit_rows, rows), F32),
        struct((2, width, groups), BF16) if gathered else struct((part, groups), F32),
        struct((width if gathered else part, LANES), F32),
    ]
    half_rows = rows // 2
    spread_n = 1 if gathered else n // 2
    line_n = 1 if gathered else n
    kept = [
        struct((2, n, padded, width), BF16),
        struct((rows, width), F32),
        struct((width, width), BF16),
        struct((rows, width), BF16),
        struct((pairs, rows, LANES), BF16),
        struct((pairs, rows, LANES), BF16),
        struct((pairs, rows, LANES), BF16),
        struct((8, 8, rows), F32),
        struct((rows, LANES), F32),
        struct((rows, LANES), F32),
        struct((rows, width), BF16),
        struct((2, width, 3 * LANES), BF16),
        struct((2, width, 2 * LANES), BF16),
    ]
    results, input_grads, logits, grads, lines, *far_in = pl.pallas_call(
        functools.partial(rear_kernel, n, half, padded, gathered, part),
        out_shape=[struct((2, rows, width), BF16)] * 2
        + rear_outs
        + [struct(w_in.shape, BF16)] * len(chip_in),
        in_specs=[aspec()] * (len(chip_in) + 4 + len(kept)) + [vspec()] * 5,
        out_specs=[aspec()] * 2
        + [vspec()]
        + [aspec() if gathered else vspec()] * 2
        + [aspec()] * len(chip_in),
        scratch_shapes=[pltpu.VMEM(o.shape, o.dtype) for o in kept]
        + [
            pltpu.VMEM((half_rows, width), BF16),
            pltpu.VMEM((rows, width), BF16),
            pltpu.VMEM((rows, local), BF16),
            pltpu.VMEM((2, n, padded, width), BF16),
            pltpu.VMEM((half_rows, width), F32),
            pltpu.VMEM((rows, width), BF16),
            pltpu.VMEM((rows, local), BF16),
            pltpu.VMEM((rows, LANES), BF16),
            pltpu.VMEM((8, width), F32),
            pltpu.VMEM((2, rows, 5 * LANES), BF16),
            pltpu.VMEM((rows, LANES), F32),
            pltpu.VMEM((rows, LANES), F32),
            pltpu.VMEM((width, LANES), F32),
            pltpu.VMEM((2, width, groups), BF16),
            pltpu.VMEM((width, LANES), F32),
            pltpu.VMEM((2, spread_n, part, groups), BF16),
            pltpu.VMEM((2, spread_n, part, groups), BF16),
            pltpu.VMEM((line_n, part, LANES), F32),
            pltpu.VMEM((part, groups), BF16),
            pltpu.VMEM((part, groups), BF16),
            pltpu.VMEM((2, part, LANES), F32),
            pltpu.VMEM((half_rows, width), BF16),
            pltpu.VMEM((half_rows, width), BF16),
            pltpu.VMEM((half_rows, width), F32),
            pltpu.VMEM((8, width), F32),
            pltpu.VMEM((8, width), F32),
            pltpu.VMEM((2, half_rows, width), BF16),
            dma((3,)),
            dma((len(kept),)),
            dma((n,)),
            dma((n,)),
            dma((3,)),
            dma((n,)),
            dma((n,)),
            dma((4, 2, n // 2)),
            dma((4, 2, n // 2)),
            dma((n,)),
            dma((n,)),
            dma((5,)),
            dma((5,)),
            dma((2, 3)),
            dma((2, 3)),
            dma((1,)),
            dma((1,)),
        ],
        compiler_params=pltpu.CompilerParams(
            collective_id=1, has_side_effects=True, vmem_limit_bytes=VMEM_LIMIT
        ),
        cost_estimate=pl.CostEstimate(
            flops=100_000_000_000, bytes_accessed=60_000_000, transcendentals=0
        ),
    )(
        *chip_in,
        gy,
        tokens,
        cotangent,
        o_all,
        dx_all,
        h,
        wo_all,
        ub,
        q,
        k,
        v,
        lse,
        cosine,
        sine,
        a,
        spread,
        spread,
        stats,
        pos,
        small_all,
        extra,
        dg_all,
    )
    if not gathered:
        steps = 8

        def split(value, axis):
            block = list(value.shape)
            block[axis] //= steps

            def index(i):
                where = [0] * len(block)
                where[axis] = i
                return tuple(where)

            return pl.BlockSpec(tuple(block), index)

        def full(value):
            return pl.BlockSpec(value.shape, lambda i: (0,) * len(value.shape))

        large = [
            (results, 1),
            (input_grads, 1),
            (own_in, 2),
            (far_in[0], 2),
            (own_down, 1),
            (far_down, 1),
        ]
        tinies = [
            struct((columns, 2, rows), F32),
            struct((1, part), F32),
            struct((1, part), F32),
            struct((3, part, share), F32),
            struct((share, part), F32),
            struct((columns, part), F32),
            struct((4, part), F32),
            struct((2, part), F32),
        ]
        final = [large[0], large[1], large[2], large[4]]
        done = pl.pallas_call(
            functools.partial(last_kernel, part, columns),
            grid=(steps,),
            out_shape=[struct(v.shape, v.dtype) for v, _ in final] + tinies,
            in_specs=[split(v, axis) for v, axis in large]
            + [full(v) for v in (logits, grads, lines)],
            out_specs=[split(v, axis) for v, axis in final] + [full(v) for v in tinies],
            compiler_params=pltpu.CompilerParams(vmem_limit_bytes=VMEM_LIMIT),
        )(*(v for v, _ in large), logits, grads, lines)
        results, input_grads, grad_in, grad_down, logits = done[:5]
        gain_attn, gain_moe, heads, out, router, const, vec = done[5:]
        return (
            results,
            input_grads,
            jnp.transpose(logits, (1, 2, 0)),
            gain_attn[0],
            gain_moe[0],
            heads,
            out,
            router.T,
            const.T,
            vec,
            grad_in,
            grad_down,
        )
    grads = lax.psum_scatter(grads.astype(F32), "dp", scatter_dimension=1, tiled=True)
    lines = lax.psum_scatter(lines, "dp", scatter_dimension=0, tiled=True)
    other = lax.dynamic_index_in_dim(grads, 1 - m, 0, keepdims=False)
    grads = lax.dynamic_index_in_dim(grads, m, 0, keepdims=False) + across_chips(other)
    lines = lines + across_chips(lines)

    def heads(j):
        start = (4 + (j % 4) // 2) * LANES + (j % 2) * HD
        return jnp.concatenate(
            [grads[:, j * LANES : (j + 1) * LANES], grads[:, start : start + HD]], axis=1
        )

    return (
        results,
        input_grads,
        jnp.swapaxes(logits[:, :columns], 1, 2),
        lines[:, columns + 4],
        lines[:, columns + 5],
        jnp.stack([heads(i) for i in range(3)]),
        heads(3).T,
        lines[:, :columns],
        lines[:, columns : columns + 4],
        lines[:, columns + 6 : columns + 8].T,
        grad_in,
        grad_down,
    )


def solution(mesh):
    in_specs = (
        P(None, "dp", None),
        P(None, "dp", None),
        P(None, "dp", None),
        P(None, "dp", None),
        P("dp"),
        P("dp"),
        P(None, "dp", "tensor"),
        P("tensor", "dp"),
        P("dp", None),
        P("dp", None),
        P(None, "dp"),
        P("dp", None, None, "tensor"),
        P("dp", "tensor", None),
    )
    out_specs = (
        P(None, "dp", None),
        P(None, "dp", None),
        P(None, "dp", None),
        P("dp"),
        P("dp"),
        P(None, "dp", "tensor"),
        P("tensor", "dp"),
        P("dp", None),
        P("dp", None),
        P(None, "dp"),
        P("dp", None, None, "tensor"),
        P("dp", "tensor", None),
    )
    return jax.shard_map(body, mesh=mesh, in_specs=in_specs, out_specs=out_specs, check_vma=False)
```

```python
import functools

import jax
import jax.numpy as jnp
import numpy as np
from jax import lax
from jax.experimental import pallas as pl
from jax.experimental.pallas import tpu as pltpu
from jax.sharding import PartitionSpec as P

HD = 64
LEN = 1024
BLK = 256
EPSILON = 1e-06
LANES = 128
F32 = jnp.float32
BF16 = jnp.bfloat16
MESH = pl.DeviceIdType.MESH
VMEM_LIMIT = 60 * 1024 * 1024


def mm(a, b):
    return lax.dot_general(a, b, (((1,), (0,)), ((), ())), preferred_element_type=F32)


def mm_nt(a, b):
    return lax.dot_general(a, b, (((1,), (1,)), ((), ())), preferred_element_type=F32)


def mm_tn(a, b):
    return lax.dot_general(a, b, (((0,), (0,)), ((), ())), preferred_element_type=F32)


def vspec():
    return pl.BlockSpec(memory_space=pltpu.VMEM)


def aspec():
    return pl.BlockSpec(memory_space=pl.ANY)


def struct(shape, dtype):
    return jax.ShapeDtypeStruct(shape, dtype)


def greet(peers):
    barrier = pltpu.get_barrier_semaphore()
    for peer in peers:
        pl.semaphore_signal(barrier, inc=1, device_id=peer, device_id_type=MESH)
    pl.semaphore_wait(barrier, len(peers))


def remote(src, dst, send, recv, peer):
    return pltpu.make_async_remote_copy(
        src_ref=src,
        dst_ref=dst,
        send_sem=send,
        recv_sem=recv,
        device_id=peer,
        device_id_type=MESH,
    )


def plane_peers(n, d, t):
    return [(lax.rem(d + j, n), t) for j in range(1, n)]


def slot_hot(half, padded, base, places):
    rows = places.shape[1]
    slot = lax.broadcasted_iota(jnp.int32, (padded, rows), 0)
    wanted = jnp.where(slot < half, slot + base, -2).astype(F32)
    return (wanted == places).astype(F32).astype(BF16)


def rope_constants():
    half = HD // 2
    frequency = 10000.0 ** (-2.0 * np.arange(half) / HD)
    angle = np.arange(LEN)[:, None] * frequency[None, :]
    cosine, sine = np.cos(angle), np.sin(angle)
    cosine = np.concatenate([cosine, cosine, cosine, cosine], axis=1)
    sine = np.concatenate([-sine, sine, -sine, sine], axis=1)
    return cosine.astype(np.float32), sine.astype(np.float32)


def turn(field, cosine, sine):
    lane = lax.broadcasted_iota(jnp.int32, field.shape, 1)
    other = jnp.where(
        lax.rem(lane, HD) < HD // 2,
        pltpu.roll(field, LANES - HD // 2, 1),
        pltpu.roll(field, HD // 2, 1),
    )
    return field * cosine + other * sine


def pick(hot, values):
    return jnp.sum(jnp.where(hot, values, 0.0), axis=-1, keepdims=True)


def lane_ids(rows):
    return lax.broadcasted_iota(jnp.int32, (rows, LANES), 1)


def soft_pair(first, second):
    high = jnp.maximum(first, second)
    e0, e1 = jnp.exp(first - high), jnp.exp(second - high)
    return e0 / (e0 + e1), e1 / (e0 + e1)


def half_mask(rows):
    return lax.broadcasted_iota(jnp.int32, (rows, LANES), 1) < HD


def swap_halves(value):
    return pltpu.roll(value, HD, 1)


def front_kernel(
    n,
    half,
    padded,
    gathered,
    early,
    tokens_ref,
    cotangent_ref,
    routes_all_ref,
    prev_all_ref,
    heads_ref,
    out_ref,
    cos_ref,
    sin_ref,
    win_ref,
    *refs,
):
    tiny_refs, refs = refs[: 1 if gathered else 5], refs[1 if gathered else 5 :]
    slot_ref, gate_ref, extra_ref = refs[:3]
    stored = refs[3 : 3 + early]
    dy_arrived_ref, in_x_ref = refs[3 + early : 5 + early]
    refs = refs[5 + early :]
    kept, refs = refs[:early], refs[early:]
    a_ref, q_ref, k_ref, v_ref, o_ref, lse_ref, pos_ref, wo_ref, small_ref, spread_ref = kept[:10]
    h_ref, ub_ref, stat_ref = kept[10:]
    x_ref, dy_ref, routes_ref, place_ref, gates_ref, dy_slot_ref = refs[:6]
    refs = refs[6:]
    load, pack_send, pack_recv, dy_send, dy_recv, stay = refs[:6]
    core_send, core_recv, w_send, w_recv, store_sem = refs[6:]

    def store(*which):
        for i in which:
            pltpu.make_async_copy(kept[i], stored[i], store_sem.at[i]).start()

    rows_all, width = x_ref.shape
    blocks = rows_all // BLK
    pairs = q_ref.shape[0]
    local = pairs * LANES
    columns = prev_all_ref.shape[0]
    d, t = lax.axis_index("dp"), lax.axis_index("tensor")
    m, c = lax.div(t, 2), lax.rem(t, 2)
    partner = (d, t + 1 - 2 * c)
    across = (d, lax.rem(t + 2, 4))
    loads = [
        pltpu.make_async_copy(src.at[m], dst, load.at[i])
        for i, (src, dst) in enumerate(
            [
                (routes_all_ref, routes_ref),
                (cotangent_ref, dy_ref),
                (tokens_ref, x_ref),
            ]
        )
    ]
    for copy in loads:
        copy.start()
    greet(plane_peers(n, d, t) + [partner, across])
    part = heads_ref.shape[1]

    def pack():
        side = lax.broadcasted_iota(jnp.int32, (part, part), 0)
        eye = jnp.where(side == lax.broadcasted_iota(jnp.int32, (part, part), 1), 1.0, 0.0)
        eye = eye.astype(BF16)
        wo = mm_nt(eye, out_ref[...])
        tiny = [ref[...].astype(F32) for ref in tiny_refs]
        tiny.append(jnp.zeros((LANES - columns - 8, part), F32))
        tiny = mm_nt(eye, jnp.concatenate(tiny, axis=0).astype(BF16))
        wide = [heads_ref[i].astype(F32) for i in range(3)] + [wo]
        firsts = [value[:, :LANES] for value in wide]
        odds = [
            jnp.concatenate([wide[i][:, LANES:], wide[i + 1][:, LANES:]], axis=1) for i in (0, 2)
        ]
        return jnp.concatenate(firsts + odds + [tiny], axis=1).astype(BF16)

    beside = (d + 1 - 2 * lax.rem(d, 2), t)
    lanes_a = pl.ds(0, 3 * LANES)
    lanes_b = pl.ds(3 * LANES, 4 * LANES)

    def behind(j):
        return lax.rem(d + n - 2 * j, n)

    def shard(chip, owner, lanes):
        return spread_ref.at[chip, pl.ds(pl.multiple_of(owner * part, part), part), lanes]

    def pass_on(chip, owner, lanes, row, j, peer):
        block = shard(chip, owner, lanes)
        return remote(block, block, pack_send.at[row, j], pack_recv.at[row, j], peer)

    def ahead(j):
        return (lax.rem(d + 2 * j, n), t)

    ring = n // 2
    if gathered:
        spread_ref[...] = tiny_refs[0][...]
    else:
        spread_ref[m, pl.ds(pl.multiple_of(d * part, part), part), :] = pack()
        a_x = pass_on(m, d, lanes_a, 4, 0, across)
        sends = [a_x]
        for j in range(1, ring):
            sends.append(pass_on(m, d, lanes_a, 0, j, ahead(j)))
            sends.append(pass_on(m, d, lanes_b, 4, j, ahead(j)))
        sends.append(pass_on(m, d, lanes_a, 2, 0, beside))
        sends.append(pass_on(m, d, lanes_b, 5, 0, beside))
        sends.append(pass_on(m, d, lanes_b, 6, 0, across))
        for copy in sends:
            copy.start()

    def relay_gather(after_z, after_x):
        if gathered:
            after_z()
            after_x()
            return
        a_x.wait_recv()
        more = [pass_on(1 - m, d, lanes_a, 1, j, ahead(j)) for j in range(1, ring)]
        more.append(pass_on(1 - m, d, lanes_a, 3, 0, beside))
        for copy in more:
            copy.start()
        sends.extend(more)
        for j in range(1, ring):
            pass_on(m, d, lanes_b, 4, j, ahead(j)).wait_recv()
            more = [
                pass_on(m, behind(j), lanes_b, 5, j, beside),
                pass_on(m, behind(j), lanes_b, 6, j, across),
            ]
            pass_on(m, d, lanes_a, 0, j, ahead(j)).wait_recv()
            more.append(pass_on(m, behind(j), lanes_a, 2, j, beside))
            for copy in more:
                copy.start()
            sends.extend(more)
        for j in range(1, ring):
            pass_on(1 - m, d, lanes_a, 1, j, ahead(j)).wait_recv()
            copy = pass_on(1 - m, behind(j), lanes_a, 3, j, beside)
            copy.start()
            sends.append(copy)
        after_z()
        for j in range(ring):
            pass_on(m, d, lanes_b, 5, j, beside).wait_recv()
            owner = lax.rem(beside[0] + n - 2 * j, n)
            copy = pass_on(m, owner, lanes_b, 7, j, across)
            copy.start()
            sends.append(copy)
        after_x()
        for j in range(ring):
            pass_on(m, d, lanes_a, 2, j, beside).wait_recv()
            pass_on(m, d, lanes_a, 3, j, beside).wait_recv()
            pass_on(m, d, lanes_b, 6, j, across).wait_recv()
            pass_on(m, d, lanes_b, 7, j, across).wait_recv()

    loads[0].wait()
    named = routes_ref[...].astype(F32)
    ids = lax.broadcasted_iota(jnp.int32, (LANES, rows_all), 0).astype(F32)
    hit = ((ids == named[0:1, :]) | (ids == named[1:2, :])) & (ids < float(n))
    before = lax.broadcasted_iota(jnp.int32, (rows_all, rows_all), 0) < lax.broadcasted_iota(
        jnp.int32, (rows_all, rows_all), 1
    )
    count = mm(hit.astype(F32).astype(BF16), before.astype(F32).astype(BF16))
    places = jnp.where(hit, count, -1.0)
    place_ref[...] = places
    pos_ref[...] = jnp.transpose(places)
    store(6)
    base = c * half

    def dy_copy(j):
        e = lax.rem(d + j, n)
        return remote(
            dy_slot_ref.at[e], dy_arrived_ref.at[d], dy_send.at[j], dy_recv.at[j], (e, t)
        )

    stays = [pltpu.make_async_copy(dy_slot_ref.at[d], dy_arrived_ref.at[d], stay.at[0])]
    loads[1].wait()

    def two_hot(i):
        return jnp.concatenate(
            [
                slot_hot(half, padded, base, place_ref[pl.ds(2 * i + side, 1), :])
                for side in range(2)
            ],
            axis=0,
        )

    def dy_step(i, carry):
        rows = mm(two_hot(i), dy_ref[...]).astype(BF16)
        for side in range(2):
            dy_slot_ref[2 * i + side] = rows[side * padded : (side + 1) * padded]
        return carry

    lax.fori_loop(0, n // 2, dy_step, 0)
    weight_copies = []
    if not gathered:
        weight_copies.append(remote(win_ref, in_x_ref, w_send.at[0], w_recv.at[0], across))

    def dy_start(j, carry):
        dy_copy(j).start()
        return carry

    relay_gather(
        lambda: lax.fori_loop(1, n, dy_start, 0), lambda: [c.start() for c in weight_copies]
    )
    stays[0].start()
    store(9)

    table = spread_ref[0, :, 6 * LANES : 7 * LANES]
    extra_ref[...] = jnp.transpose(table.astype(F32))
    keep = lax.broadcasted_iota(jnp.int32, (width, LANES), 1) < columns + 4
    small_ref[...] = jnp.where(keep, table, jnp.zeros_like(table))
    mask = half_mask(width)
    own = pl.multiple_of(c * local, LANES)
    wo_ref[:, pl.ds(own, LANES)] = spread_ref[0, :, 3 * LANES : 4 * LANES]
    wo_ref[:, pl.ds(own + LANES, LANES)] = spread_ref[1, :, 3 * LANES : 4 * LANES]
    wo_ref[:, pl.ds(own + 2 * LANES, LANES)] = jnp.where(
        mask,
        swap_halves(spread_ref[0, :, 5 * LANES : 6 * LANES].astype(F32)),
        spread_ref[1, :, 5 * LANES : 6 * LANES].astype(F32),
    ).astype(BF16)
    own_lanes = pl.ds(own, local)
    wo_copy = remote(
        wo_ref.at[:, own_lanes],
        wo_ref.at[:, own_lanes],
        core_send.at[pairs],
        core_recv.at[pairs],
        partner,
    )
    wo_copy.start()
    store(8)

    loads[2].wait()
    gain = extra_ref[columns + 4 : columns + 5, :]
    head = half_mask(BLK)

    def project(i, carry):
        rows = pl.ds(pl.multiple_of(i * BLK, BLK), BLK)
        x = x_ref[rows, :].astype(F32)
        r = lax.rsqrt(jnp.mean(x * x, axis=-1, keepdims=True) + EPSILON)
        a = (x * r * gain).astype(BF16)
        a_ref[rows, :] = a
        cosine, sine = cos_ref[rows, :], sin_ref[rows, :]

        def put(pair, q, k, v):
            q_ref[pair, rows, :] = turn(q, cosine, sine).astype(BF16) * BF16(HD**-0.5)
            k_ref[pair, rows, :] = turn(k, cosine, sine).astype(BF16)
            v_ref[pair, rows, :] = v.astype(BF16)

        odd = []
        for s in range(2):
            both = mm(a, spread_ref[s, :, 0 : 3 * LANES])
            put(s, *(both[:, j * LANES : (j + 1) * LANES] for j in range(3)))
            both = mm(a, spread_ref[s, :, 4 * LANES : 6 * LANES])
            odd.append((both[:, :LANES], both[:, LANES:]))
        put(
            2,
            jnp.where(head, odd[0][0], swap_halves(odd[1][0])),
            jnp.where(head, swap_halves(odd[0][0]), odd[1][0]),
            jnp.where(head, odd[0][1], swap_halves(odd[1][1])),
        )
        return carry

    lax.fori_loop(0, blocks, project, 0)
    store(0, 1, 2, 3)

    def o_copy(p):
        lanes = pl.ds(pl.multiple_of(own + p * LANES, LANES), LANES)
        return remote(
            o_ref.at[:, lanes], o_ref.at[:, lanes], core_send.at[p], core_recv.at[p], partner
        )

    def attend(p, carry):
        lanes = pl.ds(pl.multiple_of(own + p * LANES, LANES), LANES)
        for i in range(blocks):
            rows = pl.ds(i * BLK, BLK)
            seen = pl.ds(0, (i + 1) * BLK)
            q, k, v = q_ref[p, rows, :], k_ref[p, seen, :], v_ref[p, seen, :]
            halves = []
            for side in range(2):
                chosen = head if side == 0 else jnp.logical_not(head)
                s = mm_nt(jnp.where(chosen, q, jnp.zeros_like(q)), k)
                high = jnp.max(s, axis=-1, keepdims=True)
                e = jnp.exp(s - high)
                total = jnp.sum(e, axis=-1, keepdims=True)
                halves.append(mm(e.astype(BF16), v) * (1.0 / total))
                log_total = jnp.broadcast_to(high + jnp.log(total), (BLK, LANES))
                lse_ref[2 * p + side, :, rows] = jnp.transpose(log_total)[0:8, :]
            o_ref[rows, lanes] = jnp.where(head, halves[0], halves[1]).astype(BF16)
        o_copy(p).start()
        return carry

    lax.fori_loop(0, pairs, attend, 0)
    wo_copy.wait()
    for p in range(pairs):
        o_copy(p).wait()
    store(4, 5, 7)
    prev_lines = jnp.where(m == 0, prev_all_ref[:, 0, :], prev_all_ref[:, 1, :])
    spare = jnp.zeros((LANES - columns - 2, rows_all), F32)
    facts = jnp.concatenate([prev_lines, routes_ref[...].astype(F32), spare], axis=0)
    gates_ref[...] = facts

    gain_moe = extra_ref[columns + 5 : columns + 6, :]

    def middle(i, carry):
        rows = pl.ds(pl.multiple_of(i * BLK, BLK), BLK)
        z = mm_nt(o_ref[rows, :], wo_ref[...])
        h = x_ref[rows, :].astype(F32) + z
        r = lax.rsqrt(jnp.mean(h * h, axis=-1, keepdims=True) + EPSILON)
        ub = (h * r * gain_moe).astype(BF16)
        h_ref[rows, :] = h
        ub_ref[rows, :] = ub
        scores = mm(ub, small_ref[...])
        lane = lane_ids(BLK)
        facts = jnp.transpose(gates_ref[:, rows])
        e0 = facts[:, columns : columns + 1]
        e1 = facts[:, columns + 1 : columns + 2]
        hot0, hot1 = lane.astype(F32) == e0, lane.astype(F32) == e1
        logits = scores + facts
        g0, g1 = soft_pair(pick(hot0, logits), pick(hot1, logits))
        mix = [pick(lane == columns + j, scores) for j in range(4)]
        a00, a01 = soft_pair(mix[0], mix[1])
        a10, a11 = soft_pair(mix[2], mix[3])
        table = jnp.zeros((BLK, LANES), F32)
        for j, value in enumerate([g0, g1, a00, a01, a10, a11, r, e0, e1]):
            table = jnp.where(lane == j, value, table)
        stat_ref[rows, :] = table
        gates = jnp.where(hot0, g0, 0.0) + jnp.where(hot1, g1, 0.0)
        gates_ref[:, rows] = jnp.transpose(gates)
        return carry

    lax.fori_loop(0, blocks, middle, 0)
    store(10, 11, 12)
    piece = lax.broadcasted_iota(jnp.int32, (8, rows_all), 0)

    def slot_step(i, carry):
        hot = two_hot(i)
        rows = mm(hot, ub_ref[...]).astype(BF16)
        for side in range(2):
            e = 2 * i + side
            slot_ref[e] = rows[side * padded : (side + 1) * padded]
            gate = gates_ref[pl.ds(e, 1), :]
            high = gate.astype(BF16).astype(F32)
            mid = (gate - high).astype(BF16).astype(F32)
            low = gate - high - mid
            lines = jnp.where(piece == 0, high, jnp.where(piece == 1, mid, low))
            lines = jnp.where(piece < 3, lines, 0.0).astype(BF16)
            gate = mm_nt(lines, hot[side * padded : (side + 1) * padded])
            gate = jnp.sum(gate, axis=0, keepdims=True)
            gate_ref[e] = jnp.broadcast_to(gate, (8, padded))
        return carry

    lax.fori_loop(0, n // 2, slot_step, 0)
    def finish(j, carry):
        dy_copy(j).wait()
        return carry

    lax.fori_loop(1, n, finish, 0)
    for copy in stays:
        copy.wait()
    for copy in [] if gathered else sends:
        copy.wait_send()
    for copy in weight_copies:
        copy.wait()
    for i in range(early):
        pltpu.make_async_copy(kept[i], stored[i], store_sem.at[i]).wait()


def flip(value, index, size):
    bit = 1
    while bit < size:
        chosen = lax.rem(lax.div(index, bit), 2)
        value = value + chosen * (bit - 2 * bit * lax.rem(lax.div(value, bit), 2))
        bit *= 2
    return value


def expert_exchange_kernel(
    n,
    padded,
    slot_src_ref,
    gate_src_ref,
    dy_src_ref,
    in_own_ref,
    in_chip_ref,
    down_own_ref,
    gy_out_ref,
    own_in_out_ref,
    own_down_out_ref,
    chip_in_out_ref,
    far_down_ref,
    dx_all_ref,
    dg_all_ref,
    gy_ref,
    own_in_ref,
    own_down_ref,
    chip_in_ref,
    x_ref,
    xt_ref,
    dy_ref,
    scaled_ref,
    scale_ref,
    gate_ref,
    win_ref,
    wdown_ref,
    hidden_ref,
    dgate_ref,
    dup_ref,
    y_ref,
    dx_ref,
    dg_ref,
    land_in_ref,
    land_down_ref,
    chip_down_ref,
    load,
    slot_send,
    slot_recv,
    gate_send,
    gate_recv,
    dx_send,
    dx_recv,
    dg_send,
    dg_recv,
    pass_send,
    pass_recv,
    sum_send,
    sum_recv,
    w_send,
    w_recv,
    store_sem,
):
    width = x_ref.shape[1]
    share = win_ref.shape[3]
    chunks = 4
    group = n // chunks
    span = group * padded
    block = 256
    d, t = lax.axis_index("dp"), lax.axis_index("tensor")
    c = lax.rem(t, 2)
    partner = (d, t + 1 - 2 * c)
    across = (d, lax.rem(t + 2, 4))
    stores = [
        pltpu.make_async_copy(src, dst, store_sem.at[i])
        for i, (src, dst) in enumerate(
            [
                (gy_ref, gy_out_ref),
                (chip_in_ref, chip_in_out_ref),
                (own_in_ref, own_in_out_ref),
                (own_down_ref, own_down_out_ref),
            ]
        )
    ]
    greet(plane_peers(n, d, t) + [partner, across])

    def rows_of(i):
        return pl.ds(pl.multiple_of(i * padded, padded), padded)

    def slot_copy(i):
        e = flip(d, i, n)
        return remote(
            slot_src_ref.at[e], x_ref.at[rows_of(i)], slot_send.at[i], slot_recv.at[i], (e, t)
        )

    def gate_copy(i):
        e = flip(d, i, n)
        return remote(
            gate_src_ref.at[e], gate_ref.at[i], gate_send.at[i], gate_recv.at[i], (e, t)
        )

    def dx_copy(i):
        e = flip(d, i, n)
        return remote(
            dx_ref.at[rows_of(i)], dx_all_ref.at[c, d], dx_send.at[i], dx_recv.at[i], (e, t)
        )

    def dg_copy(i):
        e = flip(d, i, n)
        return remote(dg_ref.at[i], dg_all_ref.at[c, d], dg_send.at[i], dg_recv.at[i], (e, t))

    def hand(kind, i):
        ref = (dx_all_ref, dg_all_ref)[kind]
        block_ref = ref.at[c, flip(d, i, n)]
        return remote(
            block_ref, block_ref, pass_send.at[kind, i], pass_recv.at[kind, i], partner
        )

    def down_rows(s):
        return pl.ds(s * share, share)

    def send_chunk(k):
        for q in range(group):
            if k + q > 0:
                slot_copy(k * group + q).start()
                gate_copy(k * group + q).start()

    send_chunk(2)
    send_chunk(1)
    if group > 1:
        send_chunk(0)
    stays = [
        pltpu.make_async_copy(slot_src_ref.at[d], x_ref.at[rows_of(0)], load.at[0]),
        pltpu.make_async_copy(gate_src_ref.at[d], gate_ref.at[0], load.at[1]),
    ]
    own_loads = [
        pltpu.make_async_copy(in_own_ref.at[0], win_ref.at[0], load.at[2]),
        pltpu.make_async_copy(down_own_ref.at[0], wdown_ref.at[down_rows(0)], load.at[3]),
    ]
    chip_load = pltpu.make_async_copy(in_chip_ref.at[0], win_ref.at[2], load.at[4])
    weights = [
        remote(in_own_ref.at[0], win_ref.at[1], w_send.at[0], w_recv.at[0], partner),
        remote(
            down_own_ref.at[0], wdown_ref.at[down_rows(1)], w_send.at[1], w_recv.at[1], partner
        ),
        remote(in_chip_ref.at[0], win_ref.at[3], w_send.at[2], w_recv.at[2], partner),
        remote(
            down_own_ref.at[0], wdown_ref.at[down_rows(2)], w_send.at[3], w_recv.at[3], across
        ),
        remote(
            wdown_ref.at[down_rows(2)],
            wdown_ref.at[down_rows(3)],
            w_send.at[4],
            w_recv.at[4],
            partner,
        ),
    ]

    def dy_load(i):
        return pltpu.make_async_copy(
            dy_src_ref.at[flip(d, i, n)], dy_ref.at[rows_of(i)], load.at[10 + i]
        )

    for copy in [weights[3]] + stays + own_loads:
        copy.start()
    for i in range(n):
        dy_load(i).start()
    chip_load.start()
    for copy in weights[0:3]:
        copy.start()
    for copy in stays + own_loads:
        copy.wait()

    def take(k):
        rows = pl.ds(k * span, span)
        for q in range(group):
            i = k * group + q
            if i > 0:
                slot_copy(i).wait_recv()
                gate_copy(i).wait_recv()
            dy_load(i).wait()
            near = rows_of(i)
            line = jnp.broadcast_to(gate_ref[i, 0:1, :], (LANES, padded))
            scale = jnp.transpose(line)
            scale_ref[near, :] = scale
            scaled_ref[near, :] = (dy_ref[near, :].astype(F32) * scale[:, 0:1]).astype(BF16)
        xt_ref[:, rows] = jnp.transpose(x_ref[rows, :])

    per = share // block

    def units(first, last, chosen):
        def unit(u, carry):
            k = first + lax.div(u, 2 * per)
            b = lax.rem(u, 2 * per)
            s = chosen * 2 + lax.div(b, per)
            rows = pl.ds(pl.multiple_of(k * span, span), span)
            lanes = pl.ds(pl.multiple_of(lax.rem(b, per) * block, block), block)
            far = pl.ds(pl.multiple_of((chosen * 2 * per + b) * block, block), block)
            x = x_ref[rows, :]
            gate = mm(x, win_ref[s, 0, :, lanes])
            up = mm(x, win_ref[s, 1, :, lanes])
            grad = mm_nt(scaled_ref[rows, :], wdown_ref[far, :])
            sigma = 0.5 * jnp.tanh(0.5 * gate) + 0.5
            active = gate * sigma
            hidden_ref[rows, far] = (active * up).astype(BF16)
            dgate_ref[rows, far] = (grad * up * (sigma * (1.0 + gate * (1.0 - sigma)))).astype(
                BF16
            )
            dup_ref[rows, far] = (grad * active).astype(BF16)
            return carry

        lax.fori_loop(0, (last - first) * 2 * per, unit, 0)

    def close(k, carry):
        rows = pl.ds(pl.multiple_of(k * span, span), span)
        for j in range(width // block):
            lanes = pl.ds(j * block, block)
            total = jnp.zeros((span, block), F32)
            for s in range(4):
                far = pl.ds(s * share, share)
                total = total + mm_nt(dgate_ref[rows, far], win_ref[s, 0, lanes, :])
                total = total + mm_nt(dup_ref[rows, far], win_ref[s, 1, lanes, :])
            dx_ref[rows, lanes] = total.astype(BF16)
        for q in range(group):
            i = k * group + q

            @pl.when(i > 0)
            def _():
                dx_copy(i).start()

        for j in range(width // block):
            lanes = pl.ds(j * block, block)
            y_ref[:, lanes] = mm(hidden_ref[rows, :], wdown_ref[:, lanes])
        for q in range(group):
            i = k * group + q
            near = rows_of(i)
            y = y_ref[pl.ds(q * padded, padded), :]
            gy_ref[flip(d, i, n)] = (y * scale_ref[near, 0:1]).astype(BF16)
            dot = jnp.sum(y * dy_ref[near, :].astype(F32), axis=-1, keepdims=True)
            dg_ref[i] = jnp.transpose(jnp.broadcast_to(dot, (padded, LANES)))[0:8, :]

            @pl.when(i > 0)
            def _():
                dg_copy(i).start()

        return carry

    take(0)
    for copy in weights[0:2]:
        copy.wait_recv()
    units(0, 1, 0)
    take(1)
    units(1, 2, 0)
    take(2)
    send_chunk(3)
    units(2, 3, 0)
    chip_load.wait()
    weights[3].wait_recv()
    weights[4].start()
    weights[2].wait_recv()
    weights[4].wait_recv()
    units(0, 3, 1)
    lax.fori_loop(2, 3, close, 0)
    lax.fori_loop(0, 2, close, 0)
    take(3)
    units(3, 4, 0)
    units(3, 4, 1)
    lax.fori_loop(3, 4, close, 0)
    stores[0].start()
    keeps = [
        pltpu.make_async_copy(dx_ref.at[rows_of(0)], dx_all_ref.at[c, d], load.at[0]),
        pltpu.make_async_copy(dg_ref.at[0], dg_all_ref.at[c, d], load.at[1]),
    ]
    for copy in keeps:
        copy.start()

    def forward(first, last):
        def step(i, carry):
            dx_copy(i).wait_recv()
            dg_copy(i).wait_recv()
            hand(0, i).start()
            hand(1, i).start()
            return carry

        lax.fori_loop(first, last, step, 0)

    def grad_in(s, kind, b):
        far = pl.ds(pl.multiple_of(s * share + b * block, block), block)
        return mm(xt_ref[...], (dgate_ref, dup_ref)[kind][:, far])

    def grad_down(s, b):
        far = pl.ds(pl.multiple_of(s * share + b * block, block), block)
        return mm_tn(hidden_ref[:, far], scaled_ref[...])

    def sum_copies(j):
        return [
            remote(win_ref.at[j], land_in_ref.at[j], sum_send.at[j], sum_recv.at[j], partner),
            remote(
                wdown_ref.at[pl.ds(j * share, share)],
                land_down_ref.at[j],
                sum_send.at[2 + j],
                sum_recv.at[2 + j],
                partner,
            ),
        ]

    for copy in weights:
        copy.wait_send()

    def down_sums(s, put):
        def unit(b, carry):
            put(pl.ds(pl.multiple_of(b * block, block), block), grad_down(s, b))
            return carry

        lax.fori_loop(0, per, unit, 0)

    def in_sums(s, put):
        def unit(b, carry):
            lanes = pl.ds(pl.multiple_of(b * block, block), block)
            for kind in range(2):
                put(kind, lanes, grad_in(s, kind, b))
            return carry

        lax.fori_loop(0, per, unit, 0)

    def leave_down(j, s):
        def put(rows, value):
            near = pl.multiple_of(rows.start + j * share, block)
            wdown_ref[pl.ds(near, block), :] = value.astype(BF16)

        down_sums(s, put)
        sum_copies(j)[1].start()

    def leave_in(j, s):
        def put(kind, lanes, value):
            win_ref[j, kind, :, lanes] = value.astype(BF16)

        in_sums(s, put)
        sum_copies(j)[0].start()

    leave_down(0, 3)
    leave_down(1, 1)
    sum_copies(0)[1].wait_recv()

    def chip_down(lanes, value):
        chip_down_ref[0, lanes, :] = (value + land_down_ref[0, lanes, :].astype(F32)).astype(BF16)

    down_sums(2, chip_down)
    far_copy = remote(chip_down_ref, far_down_ref, w_send.at[5], w_recv.at[5], across)
    far_copy.start()
    for copy in keeps:
        copy.wait()
    hand(0, 0).start()
    hand(1, 0).start()
    forward(1, 2 * group)
    leave_in(0, 3)
    leave_in(1, 1)
    sum_copies(0)[0].wait_recv()

    def chip_in(kind, lanes, value):
        chip_in_ref[0, kind, :, lanes] = (
            value + land_in_ref[0, kind, :, lanes].astype(F32)
        ).astype(BF16)

    in_sums(2, chip_in)
    stores[1].start()
    for copy in sum_copies(1):
        copy.wait_recv()

    def own_in(kind, lanes, value):
        own_in_ref[0, kind, :, lanes] = value + land_in_ref[1, kind, :, lanes].astype(F32)

    def own_down(lanes, value):
        own_down_ref[0, lanes, :] = value + land_down_ref[1, lanes, :].astype(F32)

    in_sums(0, own_in)
    stores[2].start()
    down_sums(0, own_down)
    stores[3].start()
    forward(2 * group, n)

    def clear(i, carry):
        for copy in (slot_copy(i), gate_copy(i), dx_copy(i), dg_copy(i)):
            copy.wait_send()
        return carry

    lax.fori_loop(1, n, clear, 0)

    def passed(i, carry):
        hand(0, i).wait()
        hand(1, i).wait()
        return carry

    lax.fori_loop(0, n, passed, 0)
    for j in range(2):
        for copy in sum_copies(j):
            copy.wait_send()
    far_copy.wait()
    for copy in stores:
        copy.wait()


def expert_kernel(
    sources,
    padded,
    x_ref,
    dy_ref,
    gate_ref,
    *refs,
):
    weights, outs = refs[:8], refs[8:19]
    in_refs, down_refs = weights[0:4], weights[4:8]
    gy_ref, dx_ref, dg_ref = outs[0:3]
    gin_refs, gdown_refs = outs[3:7], outs[7:11]
    xt_ref, scaled_ref, scale_ref, y_acc, dx_acc, win_ref, wdown_ref = refs[19:]
    step = pl.program_id(0)
    last = pl.num_programs(0) - 1

    @pl.when(step == 0)
    def _():
        xt_ref[...] = jnp.transpose(x_ref[...])
        for s in range(sources):
            rows = pl.ds(s * padded, padded)
            line = jnp.broadcast_to(gate_ref[s, 0:1, :], (LANES, padded))
            scale = jnp.transpose(line)
            scale_ref[rows, :] = scale
            scaled_ref[rows, :] = (dy_ref[rows, :].astype(F32) * scale[:, 0:1]).astype(BF16)
        y_acc[...] = jnp.zeros_like(y_acc)
        dx_acc[...] = jnp.zeros_like(dx_acc)

    per = pl.num_programs(0) // 4
    for i in range(4):

        @pl.when(lax.div(step, per) == i)
        def _():
            win_ref[...] = in_refs[i][0]
            wdown_ref[...] = down_refs[i][0]

    x = x_ref[...]
    gate = mm(x, win_ref[0])
    up = mm(x, win_ref[1])
    sigma = 1.0 / (1.0 + jnp.exp(-gate))
    active = gate * sigma
    hidden = (active * up).astype(BF16)
    y_acc[...] += mm(hidden, wdown_ref[...])
    scaled = scaled_ref[...]
    grad_hidden = mm_nt(scaled, wdown_ref[...])
    grad_gate = (grad_hidden * up * (sigma * (1.0 + gate * (1.0 - sigma)))).astype(BF16)
    grad_up = (grad_hidden * active).astype(BF16)
    dx_acc[...] += mm_nt(grad_gate, win_ref[0]) + mm_nt(grad_up, win_ref[1])
    xt = xt_ref[...]
    part_gate = mm(xt, grad_gate).astype(BF16)
    part_up = mm(xt, grad_up).astype(BF16)
    part_down = mm_tn(hidden, scaled).astype(BF16)
    for i in range(4):

        @pl.when(lax.div(step, per) == i)
        def _():
            gin_refs[i][0, 0] = part_gate
            gin_refs[i][0, 1] = part_up
            gdown_refs[i][0] = part_down

    @pl.when(step == last)
    def _():
        for s in range(sources):
            rows = pl.ds(s * padded, padded)
            y = y_acc[rows, :]
            gy_ref[s] = (y * scale_ref[rows, 0:1]).astype(BF16)
            dot = jnp.sum(y * dy_ref[rows, :].astype(F32), axis=-1, keepdims=True)
            dg_ref[s] = jnp.transpose(jnp.broadcast_to(dot, (padded, LANES)))[0:8, :]
            dx_ref[s] = dx_acc[rows, :].astype(BF16)


def rear_kernel(n, half, padded, gathered, part, *refs):
    crossing = 0 if gathered else 1
    chip_in_refs, refs = refs[:crossing], refs[crossing:]
    gy_src_ref, tokens_ref, cotangent_ref, o_all_ref = refs[:4]
    loaded, refs = refs[4:17], refs[17:]
    stat_ref, pos_ref, small_ref, extra_ref, dg_ref = refs[:5]
    result_ref, grad_x_ref, logit_ref, grads_ref, lines_ref = refs[5:10]
    far_in_refs, refs = refs[10 : 10 + crossing], refs[10 + crossing :]
    kept, refs = refs[:13], refs[13:]
    dx_ref, h_ref, wo_ref, ub_ref, q_ref, k_ref, v_ref = kept[:7]
    lse_ref, cos_ref, sin_ref, a_ref, spread_a_ref, spread_b_ref = kept[7:]
    x_ref, dy_ref, o_ref, gy_ref, dh_ref, dzb_ref, do_ref, low_ref, row_ref = refs[:9]
    dp_ref, dk_acc, dv_acc, wo_odd_ref, pack_ref, line_ref, y_in_ref, z_in_ref = refs[9:17]
    line_in_ref, cross_ref, cross_in_ref, cross_line_ref = refs[17:21]
    da_out_ref, da_in_ref, da_own_ref, norm_ref, norm_in_ref, half_ref = refs[21:27]
    load, fetch_sem, gy_send, gy_recv, stay, pass_send, pass_recv = refs[27:34]
    grad_send, grad_recv, line_send, line_recv, pair_send, pair_recv = refs[34:40]
    out_send, out_recv, sum_send, sum_recv = refs[40:]

    def fetch(i):
        src = loaded[i]
        if i == 11:
            src = src.at[:, :, pl.ds(0, 3 * LANES)]
        if i == 12:
            src = src.at[:, :, pl.ds(4 * LANES, 2 * LANES)]
        return pltpu.make_async_copy(src, kept[i], fetch_sem.at[i])

    rows_all, width = dy_ref.shape
    blocks = rows_all // BLK
    pairs = q_ref.shape[0]
    local = pairs * LANES
    columns = n + 4
    slots = n * padded
    d, t = lax.axis_index("dp"), lax.axis_index("tensor")
    m, c = lax.div(t, 2), lax.rem(t, 2)
    partner = (d, t + 1 - 2 * c)
    across = (d, lax.rem(t + 2, 4))
    rows_half = rows_all // 2
    own = pl.multiple_of(c * local, LANES)
    own_lanes = pl.ds(own, local)
    place = pl.ds(pl.multiple_of(c * rows_half, BLK), rows_half)
    loads = [
        pltpu.make_async_copy(src, dst, load.at[i])
        for i, (src, dst) in enumerate(
            [
                (cotangent_ref.at[m], dy_ref),
                (tokens_ref.at[m, place], x_ref),
                (o_all_ref.at[:, own_lanes], o_ref),
            ]
        )
    ]
    for i in range(2):
        fetch(i).start()
    for copy in loads:
        copy.start()
    for i in range(2, 13):
        fetch(i).start()
    greet(plane_peers(n, d, t) + [partner, across])

    sum_copies = [
        remote(src, land, sum_send.at[0], sum_recv.at[0], across)
        for src, land in zip(chip_in_refs, far_in_refs)
    ]
    for copy in sum_copies:
        copy.start()

    def give(j):
        s = lax.rem(d + j, n)
        return remote(gy_src_ref.at[s], gy_ref.at[c, d], gy_send.at[j], gy_recv.at[j], (s, t))

    def hand(j):
        block = gy_ref.at[c, lax.rem(d + n - j, n)]
        return remote(block, block, pass_send.at[j], pass_recv.at[j], partner)

    keep = pltpu.make_async_copy(gy_src_ref.at[d], gy_ref.at[c, d], stay.at[0])
    keep.start()

    def give_start(j, carry):
        give(j).start()
        return carry

    lax.fori_loop(1, n, give_start, 0)

    def collect():
        keep.wait()
        hand(0).start()

        def step(j, carry):
            give(j).wait_recv()
            hand(j).start()
            return carry

        lax.fori_loop(1, n, step, 0)

    def settle():
        def step(j, carry):
            hand(j).wait_recv()
            return carry

        lax.fori_loop(0, n, step, 0)

    row_ref[...] = jnp.zeros_like(row_ref)
    for copy in loads:
        copy.wait()
    for i in range(3):
        fetch(i).wait()

    gain_moe = extra_ref[columns + 5 : columns + 6, :]
    vec0 = extra_ref[columns + 6 : columns + 7, :]
    vec1 = extra_ref[columns + 7 : columns + 8, :]
    group = max(1, min(n, (1024 if slots <= 1024 else 512) // padded))
    span = group * padded

    def combine(wheres, ref, lines=None):
        total = jnp.zeros((BLK, width), F32)
        entries = [jnp.zeros((BLK, 1), F32) for _ in wheres]
        slot = lax.broadcasted_iota(jnp.int32, (BLK, span), 1)
        for side in range(2):
            for first in range(0, n, group):
                start = side * slots + first * padded
                hots = [slot == where - start for where in wheres]
                hot = jnp.where(hots[0] | hots[1], 1.0, 0.0).astype(BF16)
                block = ref[side, first : first + group].reshape(span, width)
                total = total + mm(hot, block)
                if lines is not None:
                    line = jnp.concatenate(
                        [lines[side, first + e, 0:1, :] for e in range(group)], axis=1
                    )
                    entries = [
                        entry + jnp.sum(jnp.where(one, line, 0.0), axis=-1, keepdims=True)
                        for entry, one in zip(entries, hots)
                    ]
        return total, entries

    def facts(rows):
        lane = lane_ids(BLK)
        stats = stat_ref[rows, :]
        values = [stats[:, j : j + 1] for j in range(7)]
        e0, e1 = stats[:, 7:8].astype(jnp.int32), stats[:, 8:9].astype(jnp.int32)
        wheres = []
        places = pos_ref[rows, :]
        for e in (e0, e1):
            place = pick(lane == e, places).astype(jnp.int32)
            side = (place >= half).astype(jnp.int32)
            where = side * (slots - half) + e * padded + place
            wheres.append(jnp.where(e < n, where, -1))
        g0, g1 = values[0:2]

        def named(number):
            return jnp.where(e0 == number, g0, 0.0) + jnp.where(e1 == number, g1, 0.0)

        copied, first, second = named(n + 1), named(n + 2), named(n + 3)
        on_u = copied + first * values[2] + second * values[4]
        return values, e0, e1, wheres, first, second, on_u

    def back(i, carry):
        rows = pl.ds(pl.multiple_of(i * BLK, BLK), BLK)
        values, e0, e1, wheres, first, second, on_u = facts(rows)
        g0, g1, a00, a01, a10, a11, r = values
        lane = lane_ids(BLK)
        grads, (f0, f1) = combine(wheres, dx_ref, dg_ref)
        h = h_ref[rows, :]
        normed = h * r
        u = normed * gain_moe
        dy = dy_ref[rows, :].astype(F32)
        s_u = jnp.sum(dy * u, axis=-1, keepdims=True)
        s_0 = jnp.sum(dy * vec0, axis=-1, keepdims=True)
        s_1 = jnp.sum(dy * vec1, axis=-1, keepdims=True)

        def other(e):
            value = jnp.where(e == n + 1, s_u, 0.0)
            value = jnp.where(e == n + 2, a00 * s_u + a01 * s_0, value)
            return jnp.where(e == n + 3, a10 * s_u + a11 * s_1, value)

        dg0, dg1 = f0 + other(e0), f1 + other(e1)
        mean = g0 * dg0 + g1 * dg1
        dl = jnp.where(lane == e0, g0 * (dg0 - mean), 0.0) + jnp.where(
            lane == e1, g1 * (dg1 - mean), 0.0
        )
        turned = jnp.transpose(dl)
        logit_ref[m, :, rows] = turned[0 : logit_ref.shape[1], :]
        d00, d01 = first * s_u, first * s_0
        d10, d11 = second * s_u, second * s_1
        m0 = a00 * d00 + a01 * d01
        m1 = a10 * d10 + a11 * d11
        low = dl
        for j, value in enumerate(
            [a00 * (d00 - m0), a01 * (d01 - m0), a10 * (d10 - m1), a11 * (d11 - m1)]
        ):
            low = jnp.where(lane == columns + j, value, low)
        low = low.astype(BF16)
        low_ref[rows, :] = low
        du = grads + mm_nt(low, small_ref[...]) + on_u * dy
        row_ref[0:1, :] += jnp.sum(du * normed, axis=0, keepdims=True)
        row_ref[1:2, :] += jnp.sum((first * a01) * dy, axis=0, keepdims=True)
        row_ref[2:3, :] += jnp.sum((second * a11) * dy, axis=0, keepdims=True)
        dn = du * gain_moe
        dh = dy + r * (dn - normed * jnp.mean(dn * normed, axis=-1, keepdims=True))

        @pl.when(lax.div(i, blocks // 2) == c)
        def _():
            near = pl.multiple_of(i * BLK - c * rows_half, BLK)
            dh_ref[pl.ds(near, BLK), :] = dh

        dzb = dh.astype(BF16)
        dzb_ref[rows, :] = dzb
        do_ref[rows, :] = mm(dzb, wo_ref[:, own_lanes]).astype(BF16)
        return carry

    lax.fori_loop(0, blocks, back, 0)
    logit_copy = remote(
        logit_ref.at[m], logit_ref.at[m], pair_send.at[0], pair_recv.at[0], across
    )
    logit_copy.start()

    fetch(3).wait()
    grad_wo = mm_tn(dzb_ref[...], o_ref[...])
    pack_ref[0, :, 3 * LANES : 4 * LANES] = grad_wo[:, 0:LANES].astype(BF16)
    pack_ref[1, :, 3 * LANES : 4 * LANES] = grad_wo[:, LANES : 2 * LANES].astype(BF16)
    wo_odd_ref[...] = grad_wo[:, 2 * LANES : 3 * LANES]
    line_ref[...] = mm_tn(ub_ref[...], low_ref[...])

    def slab(owner):
        return pl.ds(pl.multiple_of(owner * part, part), part)

    ring = n // 2
    y_own = lax.rem(d, 2)
    beside = (d + 1 - 2 * y_own, t)
    z_own = lax.div(d, 2)
    wide_lanes = (pl.ds(0, 4 * LANES), pl.ds(4 * LANES, 2 * LANES))

    def y_copy(s, stage, z):
        lanes = wide_lanes[stage]
        return remote(
            pack_ref.at[s, slab(2 * z + 1 - y_own), lanes],
            y_in_ref.at[s, z, :, lanes],
            grad_send.at[stage, s, z],
            grad_recv.at[stage, s, z],
            beside,
        )

    def z_copy(s, stage, j):
        lanes = wide_lanes[stage]
        z = lax.rem(z_own + j, ring)
        return remote(
            pack_ref.at[s, slab(2 * z + y_own), lanes],
            z_in_ref.at[s, j, :, lanes],
            grad_send.at[2 + stage, s, j],
            grad_recv.at[2 + stage, s, j],
            (2 * z + y_own, t),
        )

    def y_start(s, stage):
        for z in range(ring):
            y_copy(s, stage, z).start()

    def z_start(s, stage):
        lanes = wide_lanes[stage]
        for z in range(ring):
            y_copy(s, stage, z).wait()
            rows = slab(2 * z + y_own)
            value = pack_ref[s, rows, lanes].astype(F32) + y_in_ref[s, z, :, lanes].astype(F32)
            pack_ref[s, rows, lanes] = value.astype(BF16)
        for j in range(1, ring):
            z_copy(s, stage, j).start()

    def line_copy(j):
        e = lax.rem(d + j, n)
        return remote(
            line_ref.at[slab(e), :],
            line_in_ref.at[d],
            line_send.at[j],
            line_recv.at[j],
            (e, t),
        )

    head = half_mask(BLK)

    def attend_back(p):
        dk_acc[...] = jnp.zeros_like(dk_acc)
        dv_acc[...] = jnp.zeros_like(dv_acc)
        dq = []
        for i in range(blocks):
            rows = pl.ds(i * BLK, BLK)
            seen = pl.ds(0, (i + 1) * BLK)
            lanes = pl.ds(pl.multiple_of(p * LANES, LANES), LANES)
            q, do = q_ref[p, rows, :], do_ref[rows, lanes]
            k, v = k_ref[p, seen, :], v_ref[p, seen, :]
            zero = jnp.zeros_like(q)
            parts = []
            dk, dv = dk_acc[seen, :], dv_acc[seen, :]
            for side in range(2):
                chosen = head if side == 0 else jnp.logical_not(head)
                qm, dom = jnp.where(chosen, q, zero), jnp.where(chosen, do, zero)
                prob = jnp.exp(mm_nt(k, qm) - lse_ref[2 * p + side, 0:1, rows])
                grad_prob = mm_nt(v, dom)
                total = jnp.sum(prob * grad_prob, axis=0, keepdims=True)
                grad_score = (prob * (grad_prob - total)).astype(BF16)
                dv = dv + mm(prob.astype(BF16), dom)
                dk = dk + mm(grad_score, qm)
                parts.append(mm_tn(grad_score, k))
            dk_acc[seen, :] = dk
            dv_acc[seen, :] = dv
            value = jnp.where(head, parts[0], parts[1]) * (HD**-0.5)
            dq.append(turn(value, cos_ref[rows, :], -sin_ref[rows, :]))
        return (
            jnp.concatenate(dq, axis=0),
            turn(dk_acc[...], cos_ref[...], -sin_ref[...]),
            dv_acc[...],
        )

    def shard_step(i, carry):
        s = lax.rem(m + 1 + i, 2)
        for j, value in enumerate(attend_back(s)):
            dp_ref[s, :, j * LANES : (j + 1) * LANES] = value.astype(BF16)
        for j in range(3):
            lanes = pl.ds(j * LANES, LANES)
            pack_ref[s, :, lanes] = mm_tn(a_ref[...], dp_ref[s, :, lanes]).astype(BF16)
        if not gathered:
            y_start(s, 0)

            @pl.when(i == 1)
            def _():
                z_start(lax.rem(m + 1, 2), 0)

        return carry

    for i in range(4, 11):
        fetch(i).wait()
    lax.fori_loop(0, 2, shard_step, 0)
    collect()

    def publish(kind, out_ref):
        block = out_ref.at[m, place]
        copies = [
            remote(half_ref.at[kind], block, out_send.at[kind, 0], out_recv.at[kind, 0], across),
            remote(half_ref.at[kind], block, out_send.at[kind, 1], out_recv.at[kind, 1], partner),
            pltpu.make_async_copy(half_ref.at[kind], block, stay.at[1 + kind]),
        ]
        for copy in copies:
            copy.start()
        block = out_ref.at[1 - m, place]
        relay = remote(block, block, out_send.at[kind, 2], out_recv.at[kind, 2], partner)
        return copies, relay

    settle()

    def results(i, carry):
        rows = pl.ds(pl.multiple_of(i * BLK, BLK), BLK)
        far = pl.ds(pl.multiple_of(c * rows_half + i * BLK, BLK), BLK)
        values, e0, e1, wheres, first, second, on_u = facts(far)
        sums, _ = combine(wheres, gy_ref)
        h = h_ref[far, :]
        u = h * values[6] * gain_moe
        result = h + (sums + on_u * u + (first * values[3]) * vec0 + (second * values[5]) * vec1)
        half_ref[1, rows, :] = result.astype(BF16)
        return carry

    lax.fori_loop(0, rows_half // BLK, results, 0)
    result_copies, result_relay = publish(1, result_ref)

    dq, dk, dv = attend_back(2)
    wide = half_mask(rows_all)
    odd = [
        (jnp.where(wide, dq, swap_halves(dk)), jnp.where(wide, dv, 0.0)),
        (jnp.where(wide, swap_halves(dq), dk), jnp.where(wide, swap_halves(dv), 0.0)),
    ]
    tall = half_mask(width)
    for s in range(2):
        for j in range(2):
            dp_ref[s, :, (3 + j) * LANES : (4 + j) * LANES] = odd[s][j].astype(BF16)
    for s in range(2):
        pack_ref[s, :, 4 * LANES : 5 * LANES] = mm_tn(
            a_ref[...], dp_ref[s, :, 3 * LANES : 4 * LANES]
        ).astype(BF16)
        last = mm_tn(a_ref[...], dp_ref[s, :, 4 * LANES : 5 * LANES])
        side = wo_odd_ref[...]
        side = swap_halves(side) if s == 0 else side
        pack_ref[s, :, 5 * LANES : 6 * LANES] = jnp.where(tall, last, side).astype(BF16)
    if not gathered:
        y_start(0, 1)
        y_start(1, 1)
        z_start(m, 0)

    def da_rows(start):
        rows = pl.ds(pl.multiple_of(start, BLK), BLK)
        total = jnp.zeros((BLK, width), F32)
        for s in range(2):
            total = total + mm_nt(dp_ref[s, rows, 0 : 3 * LANES], spread_a_ref[s])
            total = total + mm_nt(dp_ref[s, rows, 3 * LANES : 5 * LANES], spread_b_ref[s])
        return total

    fetch(11).wait()
    fetch(12).wait()

    def da_other(i, carry):
        rows = pl.ds(pl.multiple_of(i * BLK, BLK), BLK)
        da_out_ref[rows, :] = da_rows((1 - c) * rows_half + i * BLK).astype(BF16)
        return carry

    lax.fori_loop(0, rows_half // BLK, da_other, 0)
    da_copy = remote(da_out_ref, da_in_ref, pair_send.at[1], pair_recv.at[1], partner)
    da_copy.start()

    def da_own(i, carry):
        rows = pl.ds(pl.multiple_of(i * BLK, BLK), BLK)
        da_own_ref[rows, :] = da_rows(c * rows_half + i * BLK)
        return carry

    lax.fori_loop(0, rows_half // BLK, da_own, 0)
    if not gathered:
        z_start(0, 1)
        z_start(1, 1)
    da_copy.wait()
    gain_attn = extra_ref[columns + 4 : columns + 5, :]
    norm_ref[...] = jnp.zeros_like(norm_ref)

    def finish(i, carry):
        rows = pl.ds(pl.multiple_of(i * BLK, BLK), BLK)
        x = x_ref[rows, :].astype(F32)
        r = lax.rsqrt(jnp.mean(x * x, axis=-1, keepdims=True) + EPSILON)
        normed = x * r
        da = da_own_ref[rows, :] + da_in_ref[rows, :].astype(F32)
        norm_ref[0:1, :] += jnp.sum(da * normed, axis=0, keepdims=True)
        dn = da * gain_attn
        grad = dh_ref[rows, :] + r * (dn - normed * jnp.mean(dn * normed, axis=-1, keepdims=True))
        half_ref[0, rows, :] = grad.astype(BF16)
        return carry

    lax.fori_loop(0, rows_half // BLK, finish, 0)
    norm_copy = remote(norm_ref, norm_in_ref, pair_send.at[2], pair_recv.at[2], partner)
    norm_copy.start()

    grad_x_copies, grad_x_relay = publish(0, grad_x_ref)

    norm_copy.wait()
    row_ref[3:4, :] = norm_ref[0:1, :] + norm_in_ref[0:1, :]
    turned = jnp.concatenate([row_ref[...], jnp.zeros((LANES - 8, width), F32)], axis=0)
    turned = jnp.transpose(turned)
    lane = lax.broadcasted_iota(jnp.int32, (width, LANES), 1)
    lines = line_ref[...]
    for j, source in enumerate([3, 0, 1, 2]):
        lines = jnp.where(lane == columns + 4 + j, turned[:, source : source + 1], lines)
    line_ref[...] = lines
    if gathered:
        packs = [
            pltpu.make_async_copy(pack_ref, grads_ref, load.at[0]),
            pltpu.make_async_copy(line_ref, lines_ref, load.at[1]),
        ]
        for copy in packs:
            copy.start()
        for copy in packs:
            copy.wait()
    else:

        def send(j, carry):
            line_copy(j).start()
            return carry

        lax.fori_loop(1, n, send, 0)
        line_in_ref[d] = line_ref[slab(d), :]
        for s in range(2):
            for stage in range(2):
                for j in range(1, ring):
                    z_copy(s, stage, j).wait()

        def total(s):
            value = pack_ref[s, slab(d), :].astype(F32)
            for j in range(1, ring):
                value = value + z_in_ref[s, j].astype(F32)
            return value

        cross_ref[...] = total(1 - m).astype(BF16)
        cross_copy = remote(cross_ref, cross_in_ref, pair_send.at[3], pair_recv.at[3], across)
        cross_copy.start()
        grads_ref[...] = total(m)
        result_copies[0].wait_recv()
        result_relay.start()

        def arrive_lines(j, carry):
            line_copy(j).wait()
            return carry

        lax.fori_loop(1, n, arrive_lines, 0)
        value = line_in_ref[0]
        for e in range(1, n):
            value = value + line_in_ref[e]
        cross_line_ref[0] = value
        cross_line_copy = remote(
            cross_line_ref.at[0], cross_line_ref.at[1], pair_send.at[4], pair_recv.at[4], across
        )
        cross_line_copy.start()
        cross_copy.wait()
        grads_ref[...] += cross_in_ref[...].astype(F32)
        cross_line_copy.wait()
        lines_ref[...] = cross_line_ref[0] + cross_line_ref[1]

    grad_x_copies[0].wait_recv()
    grad_x_relay.start()
    if gathered:
        result_copies[0].wait_recv()
        result_relay.start()
    for copies, relay in ((grad_x_copies, grad_x_relay), (result_copies, result_relay)):
        copies[0].wait_send()
        copies[1].wait()
        copies[2].wait()
        relay.wait()
    logit_copy.wait()

    for copy in sum_copies:
        copy.wait()

    def clear(j, carry):
        give(j).wait_send()
        return carry

    lax.fori_loop(1, n, clear, 0)

    def passed(j, carry):
        hand(j).wait_send()
        return carry

    lax.fori_loop(0, n, passed, 0)


def last_kernel(
    part,
    columns,
    results_ref,
    grad_x_ref,
    own_in_ref,
    far_in_ref,
    own_down_ref,
    far_down_ref,
    logit_ref,
    grads_ref,
    lines_ref,
    results_out,
    grad_x_out,
    in_out,
    down_out,
    logit_out,
    attn_out,
    moe_out,
    heads_out,
    out_out,
    router_out,
    const_out,
    vec_out,
):
    results_out[...] = results_ref[...]
    grad_x_out[...] = grad_x_ref[...]
    in_out[...] = own_in_ref[...] + far_in_ref[...].astype(F32)
    down_out[...] = own_down_ref[...] + far_down_ref[...].astype(F32)

    @pl.when(pl.program_id(0) == 0)
    def _():
        for m in range(2):
            logit_out[:, m, :] = logit_ref[m, 0:columns, :]
        firsts = [grads_ref[:, j * LANES : (j + 1) * LANES] for j in range(4)]
        odds = []
        for j in range(2):
            both = grads_ref[:, (4 + j) * LANES : (5 + j) * LANES]
            odds.extend([both, swap_halves(both)])
        for j in range(3):
            heads_out[j, :, 0:LANES] = firsts[j]
            heads_out[j, :, LANES : LANES + HD] = odds[j][:, 0:HD]
        spare = jnp.zeros((LANES - part, 2 * LANES), F32)
        rows = jnp.concatenate([firsts[3], odds[3]], axis=1)
        turned = jnp.transpose(jnp.concatenate([rows, spare], axis=0))
        out_out[...] = turned[0 : LANES + HD, 0:part]
        lines = jnp.concatenate([lines_ref[...], spare[:, 0:LANES]], axis=0)
        lines = jnp.transpose(lines)[:, 0:part]
        router_out[...] = lines[0:columns]
        const_out[...] = lines[columns : columns + 4]
        attn_out[...] = lines[columns + 4 : columns + 5]
        moe_out[...] = lines[columns + 5 : columns + 6]
        vec_out[...] = lines[columns + 6 : columns + 8]


def across_chips(value):
    return lax.ppermute(value, "tensor", [(0, 2), (2, 0), (1, 3), (3, 1)])


def across_cores(value):
    return lax.ppermute(value, "tensor", [(0, 1), (1, 0), (2, 3), (3, 2)])


def body(
    tokens,
    cotangent,
    prev_logits,
    routes,
    norm_attn,
    norm_moe,
    w_qkv,
    w_out,
    w_router,
    w_const,
    const_vec,
    w_in,
    w_down,
):
    rows, width = tokens.shape[1:]
    n = lax.axis_size("dp")
    experts = n
    columns = prev_logits.shape[2]
    capacity = 4 * max(1, 3 * rows // (4 * (experts + 4)))
    half = capacity // 2
    padded = -(-half // 16) * 16
    share = w_qkv.shape[2]
    local = 2 * share
    part = w_qkv.shape[1]
    t = lax.axis_index("tensor")
    m, c = t // 2, t % 2

    cosine, sine = (jnp.asarray(v) for v in rope_constants())
    pairs = local // LANES

    tinies = [w_router.T, w_const.T, norm_attn[None], norm_moe[None], const_vec]
    gathered = part % 16 != 0
    if gathered:
        wo_rows = w_out.T
        tiny = jnp.concatenate(
            tinies + [jnp.zeros((LANES - columns - 8, part), BF16)], axis=0
        )
        packed = jnp.concatenate(
            [w_qkv[i, :, :LANES] for i in range(3)]
            + [wo_rows[:, :LANES]]
            + [w_qkv[i, :, LANES:] for i in range(3)]
            + [wo_rows[:, LANES:], tiny.T],
            axis=1,
        )
    if gathered:
        packed = lax.all_gather(packed, "dp", axis=0, tiled=True)
        other = across_chips(packed)
        tinies = [jnp.where(m == 0, jnp.stack([packed, other]), jnp.stack([other, packed]))]
    late = [
        struct((n, padded, width), BF16),
        struct((n, 8, padded), F32),
        struct((LANES, width), F32),
    ]
    early = [
        struct((rows, width), BF16),
        struct((pairs, rows, LANES), BF16),
        struct((pairs, rows, LANES), BF16),
        struct((pairs, rows, LANES), BF16),
        struct((rows, width), BF16),
        struct((8, 8, rows), F32),
        struct((rows, LANES), F32),
        struct((width, width), BF16),
        struct((width, LANES), BF16),
        struct((2, width, 7 * LANES), BF16),
        struct((rows, width), F32),
        struct((rows, width), BF16),
        struct((rows, LANES), F32),
    ]
    landing = [struct((n, padded, width), BF16), struct(w_in.shape, BF16)]
    dma = pltpu.SemaphoreType.DMA
    outs = pl.pallas_call(
        functools.partial(front_kernel, n, half, padded, gathered, len(early)),
        out_shape=late + early + landing,
        in_specs=[aspec()] * 3 + [vspec()] * 5 + [aspec()] + [vspec()] * len(tinies),
        out_specs=[vspec()] * len(late) + [aspec()] * (len(early) + len(landing)),
        scratch_shapes=[pltpu.VMEM(o.shape, o.dtype) for o in early]
        + [
            pltpu.VMEM((rows, width), BF16),
            pltpu.VMEM((rows, width), BF16),
            pltpu.VMEM((2, rows), jnp.int32),
            pltpu.VMEM((LANES, rows), F32),
            pltpu.VMEM((LANES, rows), F32),
            pltpu.VMEM((n, padded, width), BF16),
            dma((3,)),
            dma((8, n // 2)),
            dma((8, n // 2)),
            dma((n,)),
            dma((n,)),
            dma((1,)),
            dma((pairs + 1,)),
            dma((pairs + 1,)),
            dma((1,)),
            dma((1,)),
            dma((len(early),)),
        ],
        compiler_params=pltpu.CompilerParams(
            collective_id=0, has_side_effects=True, vmem_limit_bytes=VMEM_LIMIT
        ),
        cost_estimate=pl.CostEstimate(
            flops=60_000_000_000, bytes_accessed=60_000_000, transcendentals=0
        ),
    )(
        tokens,
        cotangent,
        jnp.swapaxes(routes, 1, 2),
        jnp.transpose(prev_logits, (2, 0, 1)),
        w_qkv,
        w_out,
        cosine,
        sine,
        w_in,
        *tinies,
    )
    slots, gate_slots, extra, a, q, k, v, o_all, lse, pos = outs[:10]
    wo_all, small_all, spread, h, ub, stats, dy_arrived, in_x = outs[10:]

    hidden_width = w_in.shape[3]
    slots_all = experts * padded
    if gathered:
        in_x, down_x = across_chips(w_in), across_chips(w_down)
        in_c, down_c = across_cores(w_in), across_cores(w_down)
        in_d, down_d = across_cores(in_x), across_cores(down_x)
        chunk = min(256 if slots_all <= 1024 else 128, hidden_width)
        per = hidden_width // chunk

        def in_map(i):
            return lambda f: (0, 0, 0, jnp.clip(f - per * i, 0, per - 1))

        def down_map(i):
            return lambda f: (0, jnp.clip(f - per * i, 0, per - 1), 0)

        in_blocks = [pl.BlockSpec((1, 2, width, chunk), in_map(i)) for i in range(4)]
        down_blocks = [pl.BlockSpec((1, chunk, width), down_map(i)) for i in range(4)]
        expert_outs = (
            [
                struct((n, padded, width), BF16),
                struct((n, padded, width), BF16),
                struct((n, 8, padded), F32),
            ]
            + [struct(w_in.shape, BF16)] * 4
            + [struct(w_down.shape, BF16)] * 4
        )

        def whole(shape):
            return pl.BlockSpec(
                shape, lambda f: (0,) * len(shape), pipeline_mode=pl.Buffered(1)
            )

        parts = pl.pallas_call(
            functools.partial(expert_kernel, n, padded),
            grid=(4 * per,),
            out_shape=expert_outs,
            in_specs=[
                whole((slots_all, width)),
                whole((slots_all, width)),
                whole((n, 8, padded)),
            ]
            + in_blocks
            + down_blocks,
            out_specs=[
                whole((n, padded, width)),
                whole((n, padded, width)),
                whole((n, 8, padded)),
            ]
            + in_blocks
            + down_blocks,
            scratch_shapes=[
                pltpu.VMEM((width, slots_all), BF16),
                pltpu.VMEM((slots_all, width), BF16),
                pltpu.VMEM((slots_all, LANES), F32),
                pltpu.VMEM((slots_all, width), F32),
                pltpu.VMEM((slots_all, width), F32),
                pltpu.VMEM((2, width, chunk), BF16),
                pltpu.VMEM((chunk, width), BF16),
            ],
            compiler_params=pltpu.CompilerParams(vmem_limit_bytes=VMEM_LIMIT),
            cost_estimate=pl.CostEstimate(
                flops=18 * slots_all * width * 4 * hidden_width,
                bytes_accessed=30_000_000,
                transcendentals=0,
            ),
        )(
            lax.all_to_all(slots, "dp", split_axis=0, concat_axis=0, tiled=True).reshape(
                slots_all, width
            ),
            dy_arrived.reshape(slots_all, width),
            lax.all_to_all(gate_slots, "dp", split_axis=0, concat_axis=0, tiled=True),
            w_in,
            in_c,
            in_x,
            in_d,
            w_down,
            down_c,
            down_x,
            down_d,
        )
        gy, dx, dg = parts[0:3]
        gin, gdown = parts[3:7], parts[7:11]

        def everywhere(value):
            value = lax.all_to_all(value, "dp", split_axis=0, concat_axis=0, tiled=True)
            other = across_cores(value)
            return jnp.where(c == 0, jnp.stack([value, other]), jnp.stack([other, value]))

        dx_all, dg_all = everywhere(dx), everywhere(dg)

        def total(own, core, chip, diagonal):
            chip = (chip.astype(F32) + across_cores(diagonal).astype(F32)).astype(BF16)
            own = own.astype(F32) + across_cores(core).astype(F32)
            return own + across_chips(chip).astype(F32)

        grad_in, grad_down = total(*gin), total(*gdown)
        chip_in = []
    else:
        gy, own_in, own_down, chip_in, far_down, dx_all, dg_all = pl.pallas_call(
            functools.partial(expert_exchange_kernel, n, padded),
            out_shape=[
                struct((n, padded, width), BF16),
                struct(w_in.shape, F32),
                struct(w_down.shape, F32),
                struct(w_in.shape, BF16),
                struct(w_down.shape, BF16),
                struct((2, n, padded, width), BF16),
                struct((2, n, 8, padded), F32),
            ],
            in_specs=[aspec()] * 6,
            out_specs=[aspec()] * 7,
            scratch_shapes=[
                pltpu.VMEM((n, padded, width), BF16),
                pltpu.VMEM(w_in.shape, F32),
                pltpu.VMEM(w_down.shape, F32),
                pltpu.VMEM(w_in.shape, BF16),
                pltpu.VMEM((slots_all, width), BF16),
                pltpu.VMEM((width, slots_all), BF16),
                pltpu.VMEM((slots_all, width), BF16),
                pltpu.VMEM((slots_all, width), BF16),
                pltpu.VMEM((slots_all, LANES), F32),
                pltpu.VMEM((n, 8, padded), F32),
                pltpu.VMEM((4, 2, width, hidden_width), BF16),
                pltpu.VMEM((4 * hidden_width, width), BF16),
                pltpu.VMEM((slots_all, 4 * hidden_width), BF16),
                pltpu.VMEM((slots_all, 4 * hidden_width), BF16),
                pltpu.VMEM((slots_all, 4 * hidden_width), BF16),
                pltpu.VMEM((slots_all // 4, width), F32),
                pltpu.VMEM((slots_all, width), BF16),
                pltpu.VMEM((n, 8, padded), F32),
                pltpu.VMEM((2,) + w_in.shape[1:], BF16),
                pltpu.VMEM((2,) + w_down.shape[1:], BF16),
                pltpu.VMEM(w_down.shape, BF16),
                dma((10 + n,)),
                dma((n,)),
                dma((n,)),
                dma((n,)),
                dma((n,)),
                dma((n,)),
                dma((n,)),
                dma((n,)),
                dma((n,)),
                dma((2, n)),
                dma((2, n)),
                dma((4,)),
                dma((4,)),
                dma((6,)),
                dma((6,)),
                dma((4,)),
            ],
            compiler_params=pltpu.CompilerParams(
                collective_id=2, has_side_effects=True, vmem_limit_bytes=VMEM_LIMIT
            ),
            cost_estimate=pl.CostEstimate(
                flops=60_000_000_000, bytes_accessed=40_000_000, transcendentals=0
            ),
        )(
            slots,
            gate_slots,
            dy_arrived,
            w_in,
            in_x,
            w_down,
        )
        chip_in = [chip_in]

    groups = 6 * LANES
    logit_rows = -(-columns // 8) * 8
    rear_outs = [
        struct((2, logit_rows, rows), F32),
        struct((2, width, groups), BF16) if gathered else struct((part, groups), F32),
        struct((width if gathered else part, LANES), F32),
    ]
    half_rows = rows // 2
    spread_n = 1 if gathered else n // 2
    line_n = 1 if gathered else n
    kept = [
        struct((2, n, padded, width), BF16),
        struct((rows, width), F32),
        struct((width, width), BF16),
        struct((rows, width), BF16),
        struct((pairs, rows, LANES), BF16),
        struct((pairs, rows, LANES), BF16),
        struct((pairs, rows, LANES), BF16),
        struct((8, 8, rows), F32),
        struct((rows, LANES), F32),
        struct((rows, LANES), F32),
        struct((rows, width), BF16),
        struct((2, width, 3 * LANES), BF16),
        struct((2, width, 2 * LANES), BF16),
    ]
    results, input_grads, logits, grads, lines, *far_in = pl.pallas_call(
        functools.partial(rear_kernel, n, half, padded, gathered, part),
        out_shape=[struct((2, rows, width), BF16)] * 2
        + rear_outs
        + [struct(w_in.shape, BF16)] * len(chip_in),
        in_specs=[aspec()] * (len(chip_in) + 4 + len(kept)) + [vspec()] * 5,
        out_specs=[aspec()] * 2
        + [vspec()]
        + [aspec() if gathered else vspec()] * 2
        + [aspec()] * len(chip_in),
        scratch_shapes=[pltpu.VMEM(o.shape, o.dtype) for o in kept]
        + [
            pltpu.VMEM((half_rows, width), BF16),
            pltpu.VMEM((rows, width), BF16),
            pltpu.VMEM((rows, local), BF16),
            pltpu.VMEM((2, n, padded, width), BF16),
            pltpu.VMEM((half_rows, width), F32),
            pltpu.VMEM((rows, width), BF16),
            pltpu.VMEM((rows, local), BF16),
            pltpu.VMEM((rows, LANES), BF16),
            pltpu.VMEM((8, width), F32),
            pltpu.VMEM((2, rows, 5 * LANES), BF16),
            pltpu.VMEM((rows, LANES), F32),
            pltpu.VMEM((rows, LANES), F32),
            pltpu.VMEM((width, LANES), F32),
            pltpu.VMEM((2, width, groups), BF16),
            pltpu.VMEM((width, LANES), F32),
            pltpu.VMEM((2, spread_n, part, groups), BF16),
            pltpu.VMEM((2, spread_n, part, groups), BF16),
            pltpu.VMEM((line_n, part, LANES), F32),
            pltpu.VMEM((part, groups), BF16),
            pltpu.VMEM((part, groups), BF16),
            pltpu.VMEM((2, part, LANES), F32),
            pltpu.VMEM((half_rows, width), BF16),
            pltpu.VMEM((half_rows, width), BF16),
            pltpu.VMEM((half_rows, width), F32),
            pltpu.VMEM((8, width), F32),
            pltpu.VMEM((8, width), F32),
            pltpu.VMEM((2, half_rows, width), BF16),
            dma((3,)),
            dma((len(kept),)),
            dma((n,)),
            dma((n,)),
            dma((3,)),
            dma((n,)),
            dma((n,)),
            dma((4, 2, n // 2)),
            dma((4, 2, n // 2)),
            dma((n,)),
            dma((n,)),
            dma((5,)),
            dma((5,)),
            dma((2, 3)),
            dma((2, 3)),
            dma((1,)),
            dma((1,)),
        ],
        compiler_params=pltpu.CompilerParams(
            collective_id=1, has_side_effects=True, vmem_limit_bytes=VMEM_LIMIT
        ),
        cost_estimate=pl.CostEstimate(
            flops=100_000_000_000, bytes_accessed=60_000_000, transcendentals=0
        ),
    )(
        *chip_in,
        gy,
        tokens,
        cotangent,
        o_all,
        dx_all,
        h,
        wo_all,
        ub,
        q,
        k,
        v,
        lse,
        cosine,
        sine,
        a,
        spread,
        spread,
        stats,
        pos,
        small_all,
        extra,
        dg_all,
    )
    if not gathered:
        steps = 8

        def split(value, axis):
            block = list(value.shape)
            block[axis] //= steps

            def index(i):
                where = [0] * len(block)
                where[axis] = i
                return tuple(where)

            return pl.BlockSpec(tuple(block), index)

        def full(value):
            return pl.BlockSpec(value.shape, lambda i: (0,) * len(value.shape))

        large = [
            (results, 1),
            (input_grads, 1),
            (own_in, 2),
            (far_in[0], 2),
            (own_down, 1),
            (far_down, 1),
        ]
        tinies = [
            struct((columns, 2, rows), F32),
            struct((1, part), F32),
            struct((1, part), F32),
            struct((3, part, share), F32),
            struct((share, part), F32),
            struct((columns, part), F32),
            struct((4, part), F32),
            struct((2, part), F32),
        ]
        final = [large[0], large[1], large[2], large[4]]
        done = pl.pallas_call(
            functools.partial(last_kernel, part, columns),
            grid=(steps,),
            out_shape=[struct(v.shape, v.dtype) for v, _ in final] + tinies,
            in_specs=[split(v, axis) for v, axis in large]
            + [full(v) for v in (logits, grads, lines)],
            out_specs=[split(v, axis) for v, axis in final] + [full(v) for v in tinies],
            compiler_params=pltpu.CompilerParams(vmem_limit_bytes=VMEM_LIMIT),
        )(*(v for v, _ in large), logits, grads, lines)
        results, input_grads, grad_in, grad_down, logits = done[:5]
        gain_attn, gain_moe, heads, out, router, const, vec = done[5:]
        return (
            results,
            input_grads,
            jnp.transpose(logits, (1, 2, 0)),
            gain_attn[0],
            gain_moe[0],
            heads,
            out,
            router.T,
            const.T,
            vec,
            grad_in,
            grad_down,
        )
    grads = lax.psum_scatter(grads.astype(F32), "dp", scatter_dimension=1, tiled=True)
    lines = lax.psum_scatter(lines, "dp", scatter_dimension=0, tiled=True)
    other = lax.dynamic_index_in_dim(grads, 1 - m, 0, keepdims=False)
    grads = lax.dynamic_index_in_dim(grads, m, 0, keepdims=False) + across_chips(other)
    lines = lines + across_chips(lines)

    def heads(j):
        start = (4 + (j % 4) // 2) * LANES + (j % 2) * HD
        return jnp.concatenate(
            [grads[:, j * LANES : (j + 1) * LANES], grads[:, start : start + HD]], axis=1
        )

    return (
        results,
        input_grads,
        jnp.swapaxes(logits[:, :columns], 1, 2),
        lines[:, columns + 4],
        lines[:, columns + 5],
        jnp.stack([heads(i) for i in range(3)]),
        heads(3).T,
        lines[:, :columns],
        lines[:, columns : columns + 4],
        lines[:, columns + 6 : columns + 8].T,
        grad_in,
        grad_down,
    )


def solution(mesh):
    in_specs = (
        P(None, "dp", None),
        P(None, "dp", None),
        P(None, "dp", None),
        P(None, "dp", None),
        P("dp"),
        P("dp"),
        P(None, "dp", "tensor"),
        P("tensor", "dp"),
        P("dp", None),
        P("dp", None),
        P(None, "dp"),
        P("dp", None, None, "tensor"),
        P("dp", "tensor", None),
    )
    out_specs = (
        P(None, "dp", None),
        P(None, "dp", None),
        P(None, "dp", None),
        P("dp"),
        P("dp"),
        P(None, "dp", "tensor"),
        P("tensor", "dp"),
        P("dp", None),
        P("dp", None),
        P(None, "dp"),
        P("dp", None, None, "tensor"),
        P("dp", "tensor", None),
    )
    return jax.shard_map(body, mesh=mesh, in_specs=in_specs, out_specs=out_specs, check_vma=False)
```

```python
import functools

import jax
import jax.numpy as jnp
import numpy as np
from jax import lax
from jax.experimental import pallas as pl
from jax.experimental.pallas import tpu as pltpu
from jax.sharding import PartitionSpec as P

HD = 64
LEN = 1024
BLK = 256
EPSILON = 1e-06
LANES = 128
F32 = jnp.float32
BF16 = jnp.bfloat16
MESH = pl.DeviceIdType.MESH
VMEM_LIMIT = 60 * 1024 * 1024


def mm(a, b):
    return lax.dot_general(a, b, (((1,), (0,)), ((), ())), preferred_element_type=F32)


def mm_nt(a, b):
    return lax.dot_general(a, b, (((1,), (1,)), ((), ())), preferred_element_type=F32)


def mm_tn(a, b):
    return lax.dot_general(a, b, (((0,), (0,)), ((), ())), preferred_element_type=F32)


def vspec():
    return pl.BlockSpec(memory_space=pltpu.VMEM)


def aspec():
    return pl.BlockSpec(memory_space=pl.ANY)


def struct(shape, dtype):
    return jax.ShapeDtypeStruct(shape, dtype)


def greet(peers):
    barrier = pltpu.get_barrier_semaphore()
    for peer in peers:
        pl.semaphore_signal(barrier, inc=1, device_id=peer, device_id_type=MESH)
    pl.semaphore_wait(barrier, len(peers))


def remote(src, dst, send, recv, peer):
    return pltpu.make_async_remote_copy(
        src_ref=src,
        dst_ref=dst,
        send_sem=send,
        recv_sem=recv,
        device_id=peer,
        device_id_type=MESH,
    )


def plane_peers(n, d, t):
    return [(lax.rem(d + j, n), t) for j in range(1, n)]


def slot_hot(half, padded, base, places):
    rows = places.shape[1]
    slot = lax.broadcasted_iota(jnp.int32, (padded, rows), 0)
    wanted = jnp.where(slot < half, slot + base, -2).astype(F32)
    return (wanted == places).astype(F32).astype(BF16)


def rope_constants():
    half = HD // 2
    frequency = 10000.0 ** (-2.0 * np.arange(half) / HD)
    angle = np.arange(LEN)[:, None] * frequency[None, :]
    cosine, sine = np.cos(angle), np.sin(angle)
    cosine = np.concatenate([cosine, cosine, cosine, cosine], axis=1)
    sine = np.concatenate([-sine, sine, -sine, sine], axis=1)
    return cosine.astype(np.float32), sine.astype(np.float32)


def turn(field, cosine, sine):
    lane = lax.broadcasted_iota(jnp.int32, field.shape, 1)
    other = jnp.where(
        lax.rem(lane, HD) < HD // 2,
        pltpu.roll(field, LANES - HD // 2, 1),
        pltpu.roll(field, HD // 2, 1),
    )
    return field * cosine + other * sine


def pick(hot, values):
    return jnp.sum(jnp.where(hot, values, 0.0), axis=-1, keepdims=True)


def lane_ids(rows):
    return lax.broadcasted_iota(jnp.int32, (rows, LANES), 1)


def soft_pair(first, second):
    high = jnp.maximum(first, second)
    e0, e1 = jnp.exp(first - high), jnp.exp(second - high)
    return e0 / (e0 + e1), e1 / (e0 + e1)


def half_mask(rows):
    return lax.broadcasted_iota(jnp.int32, (rows, LANES), 1) < HD


def swap_halves(value):
    return pltpu.roll(value, HD, 1)


def front_kernel(
    n,
    half,
    padded,
    gathered,
    early,
    tokens_ref,
    cotangent_ref,
    routes_all_ref,
    prev_all_ref,
    heads_ref,
    out_ref,
    cos_ref,
    sin_ref,
    win_ref,
    *refs,
):
    tiny_refs, refs = refs[: 1 if gathered else 5], refs[1 if gathered else 5 :]
    slot_ref, gate_ref, extra_ref = refs[:3]
    stored = refs[3 : 3 + early]
    dy_arrived_ref, in_x_ref = refs[3 + early : 5 + early]
    refs = refs[5 + early :]
    kept, refs = refs[:early], refs[early:]
    a_ref, q_ref, k_ref, v_ref, o_ref, lse_ref, pos_ref, wo_ref, small_ref, spread_ref = kept[:10]
    h_ref, ub_ref, stat_ref = kept[10:]
    x_ref, dy_ref, routes_ref, place_ref, gates_ref, dy_slot_ref = refs[:6]
    refs = refs[6:]
    load, pack_send, pack_recv, dy_send, dy_recv, stay = refs[:6]
    core_send, core_recv, w_send, w_recv, store_sem = refs[6:]

    def store(*which):
        for i in which:
            pltpu.make_async_copy(kept[i], stored[i], store_sem.at[i]).start()

    rows_all, width = x_ref.shape
    blocks = rows_all // BLK
    pairs = q_ref.shape[0]
    local = pairs * LANES
    columns = prev_all_ref.shape[0]
    d, t = lax.axis_index("dp"), lax.axis_index("tensor")
    m, c = lax.div(t, 2), lax.rem(t, 2)
    partner = (d, t + 1 - 2 * c)
    across = (d, lax.rem(t + 2, 4))
    loads = [
        pltpu.make_async_copy(src.at[m], dst, load.at[i])
        for i, (src, dst) in enumerate(
            [
                (routes_all_ref, routes_ref),
                (cotangent_ref, dy_ref),
                (tokens_ref, x_ref),
            ]
        )
    ]
    for copy in loads:
        copy.start()
    greet(plane_peers(n, d, t) + [partner, across])
    part = heads_ref.shape[1]

    def pack():
        side = lax.broadcasted_iota(jnp.int32, (part, part), 0)
        eye = jnp.where(side == lax.broadcasted_iota(jnp.int32, (part, part), 1), 1.0, 0.0)
        eye = eye.astype(BF16)
        wo = mm_nt(eye, out_ref[...])
        tiny = [ref[...].astype(F32) for ref in tiny_refs]
        tiny.append(jnp.zeros((LANES - columns - 8, part), F32))
        tiny = mm_nt(eye, jnp.concatenate(tiny, axis=0).astype(BF16))
        wide = [heads_ref[i].astype(F32) for i in range(3)] + [wo]
        firsts = [value[:, :LANES] for value in wide]
        odds = [
            jnp.concatenate([wide[i][:, LANES:], wide[i + 1][:, LANES:]], axis=1) for i in (0, 2)
        ]
        return jnp.concatenate(firsts + odds + [tiny], axis=1).astype(BF16)

    beside = (d + 1 - 2 * lax.rem(d, 2), t)
    lanes_a = pl.ds(0, 3 * LANES)
    lanes_b = pl.ds(3 * LANES, 4 * LANES)

    def behind(j):
        return lax.rem(d + n - 2 * j, n)

    def shard(chip, owner, lanes):
        return spread_ref.at[chip, pl.ds(pl.multiple_of(owner * part, part), part), lanes]

    def pass_on(chip, owner, lanes, row, j, peer):
        block = shard(chip, owner, lanes)
        return remote(block, block, pack_send.at[row, j], pack_recv.at[row, j], peer)

    def ahead(j):
        return (lax.rem(d + 2 * j, n), t)

    ring = n // 2
    if gathered:
        spread_ref[...] = tiny_refs[0][...]
    else:
        spread_ref[m, pl.ds(pl.multiple_of(d * part, part), part), :] = pack()
        a_x = pass_on(m, d, lanes_a, 4, 0, across)
        sends = [a_x]
        for j in range(1, ring):
            sends.append(pass_on(m, d, lanes_a, 0, j, ahead(j)))
            sends.append(pass_on(m, d, lanes_b, 4, j, ahead(j)))
        sends.append(pass_on(m, d, lanes_a, 2, 0, beside))
        sends.append(pass_on(m, d, lanes_b, 5, 0, beside))
        sends.append(pass_on(m, d, lanes_b, 6, 0, across))
        for copy in sends:
            copy.start()

    def relay_gather(after_z, after_x):
        if gathered:
            after_z()
            after_x()
            return
        a_x.wait_recv()
        more = [pass_on(1 - m, d, lanes_a, 1, j, ahead(j)) for j in range(1, ring)]
        more.append(pass_on(1 - m, d, lanes_a, 3, 0, beside))
        for copy in more:
            copy.start()
        sends.extend(more)
        for j in range(1, ring):
            pass_on(m, d, lanes_b, 4, j, ahead(j)).wait_recv()
            more = [
                pass_on(m, behind(j), lanes_b, 5, j, beside),
                pass_on(m, behind(j), lanes_b, 6, j, across),
            ]
            pass_on(m, d, lanes_a, 0, j, ahead(j)).wait_recv()
            more.append(pass_on(m, behind(j), lanes_a, 2, j, beside))
            for copy in more:
                copy.start()
            sends.extend(more)
        for j in range(1, ring):
            pass_on(1 - m, d, lanes_a, 1, j, ahead(j)).wait_recv()
            copy = pass_on(1 - m, behind(j), lanes_a, 3, j, beside)
            copy.start()
            sends.append(copy)
        after_z()
        for j in range(ring):
            pass_on(m, d, lanes_b, 5, j, beside).wait_recv()
            owner = lax.rem(beside[0] + n - 2 * j, n)
            copy = pass_on(m, owner, lanes_b, 7, j, across)
            copy.start()
            sends.append(copy)
        after_x()
        for j in range(ring):
            pass_on(m, d, lanes_a, 2, j, beside).wait_recv()
            pass_on(m, d, lanes_a, 3, j, beside).wait_recv()
            pass_on(m, d, lanes_b, 6, j, across).wait_recv()
            pass_on(m, d, lanes_b, 7, j, across).wait_recv()

    loads[0].wait()
    named = routes_ref[...].astype(F32)
    ids = lax.broadcasted_iota(jnp.int32, (LANES, rows_all), 0).astype(F32)
    hit = ((ids == named[0:1, :]) | (ids == named[1:2, :])) & (ids < float(n))
    before = lax.broadcasted_iota(jnp.int32, (rows_all, rows_all), 0) < lax.broadcasted_iota(
        jnp.int32, (rows_all, rows_all), 1
    )
    count = mm(hit.astype(F32).astype(BF16), before.astype(F32).astype(BF16))
    places = jnp.where(hit, count, -1.0)
    place_ref[...] = places
    pos_ref[...] = jnp.transpose(places)
    store(6)
    base = c * half

    def dy_copy(j):
        e = lax.rem(d + j, n)
        return remote(
            dy_slot_ref.at[e], dy_arrived_ref.at[d], dy_send.at[j], dy_recv.at[j], (e, t)
        )

    stays = [pltpu.make_async_copy(dy_slot_ref.at[d], dy_arrived_ref.at[d], stay.at[0])]
    loads[1].wait()

    def two_hot(i):
        return jnp.concatenate(
            [
                slot_hot(half, padded, base, place_ref[pl.ds(2 * i + side, 1), :])
                for side in range(2)
            ],
            axis=0,
        )

    def dy_step(i, carry):
        rows = mm(two_hot(i), dy_ref[...]).astype(BF16)
        for side in range(2):
            dy_slot_ref[2 * i + side] = rows[side * padded : (side + 1) * padded]
        return carry

    lax.fori_loop(0, n // 2, dy_step, 0)
    weight_copies = []
    if not gathered:
        weight_copies.append(remote(win_ref, in_x_ref, w_send.at[0], w_recv.at[0], across))

    def dy_start(j, carry):
        dy_copy(j).start()
        return carry

    relay_gather(
        lambda: lax.fori_loop(1, n, dy_start, 0), lambda: [c.start() for c in weight_copies]
    )
    stays[0].start()
    store(9)

    table = spread_ref[0, :, 6 * LANES : 7 * LANES]
    extra_ref[...] = jnp.transpose(table.astype(F32))
    keep = lax.broadcasted_iota(jnp.int32, (width, LANES), 1) < columns + 4
    small_ref[...] = jnp.where(keep, table, jnp.zeros_like(table))
    mask = half_mask(width)
    own = pl.multiple_of(c * local, LANES)
    wo_ref[:, pl.ds(own, LANES)] = spread_ref[0, :, 3 * LANES : 4 * LANES]
    wo_ref[:, pl.ds(own + LANES, LANES)] = spread_ref[1, :, 3 * LANES : 4 * LANES]
    wo_ref[:, pl.ds(own + 2 * LANES, LANES)] = jnp.where(
        mask,
        swap_halves(spread_ref[0, :, 5 * LANES : 6 * LANES].astype(F32)),
        spread_ref[1, :, 5 * LANES : 6 * LANES].astype(F32),
    ).astype(BF16)
    own_lanes = pl.ds(own, local)
    wo_copy = remote(
        wo_ref.at[:, own_lanes],
        wo_ref.at[:, own_lanes],
        core_send.at[pairs],
        core_recv.at[pairs],
        partner,
    )
    wo_copy.start()
    store(8)

    loads[2].wait()
    gain = extra_ref[columns + 4 : columns + 5, :]
    head = half_mask(BLK)

    def project(i, carry):
        rows = pl.ds(pl.multiple_of(i * BLK, BLK), BLK)
        x = x_ref[rows, :].astype(F32)
        r = lax.rsqrt(jnp.mean(x * x, axis=-1, keepdims=True) + EPSILON)
        a = (x * r * gain).astype(BF16)
        a_ref[rows, :] = a
        cosine, sine = cos_ref[rows, :], sin_ref[rows, :]

        def put(pair, q, k, v):
            q_ref[pair, rows, :] = turn(q, cosine, sine).astype(BF16) * BF16(HD**-0.5)
            k_ref[pair, rows, :] = turn(k, cosine, sine).astype(BF16)
            v_ref[pair, rows, :] = v.astype(BF16)

        odd = []
        for s in range(2):
            both = mm(a, spread_ref[s, :, 0 : 3 * LANES])
            put(s, *(both[:, j * LANES : (j + 1) * LANES] for j in range(3)))
            both = mm(a, spread_ref[s, :, 4 * LANES : 6 * LANES])
            odd.append((both[:, :LANES], both[:, LANES:]))
        put(
            2,
            jnp.where(head, odd[0][0], swap_halves(odd[1][0])),
            jnp.where(head, swap_halves(odd[0][0]), odd[1][0]),
            jnp.where(head, odd[0][1], swap_halves(odd[1][1])),
        )
        return carry

    lax.fori_loop(0, blocks, project, 0)
    store(0, 1, 2, 3)

    def o_copy(p):
        lanes = pl.ds(pl.multiple_of(own + p * LANES, LANES), LANES)
        return remote(
            o_ref.at[:, lanes], o_ref.at[:, lanes], core_send.at[p], core_recv.at[p], partner
        )

    def attend(p, carry):
        lanes = pl.ds(pl.multiple_of(own + p * LANES, LANES), LANES)
        for i in range(blocks):
            rows = pl.ds(i * BLK, BLK)
            seen = pl.ds(0, (i + 1) * BLK)
            q, k, v = q_ref[p, rows, :], k_ref[p, seen, :], v_ref[p, seen, :]
            halves = []
            for side in range(2):
                chosen = head if side == 0 else jnp.logical_not(head)
                s = mm_nt(jnp.where(chosen, q, jnp.zeros_like(q)), k)
                high = jnp.max(s, axis=-1, keepdims=True)
                e = jnp.exp(s - high)
                total = jnp.sum(e, axis=-1, keepdims=True)
                halves.append(mm(e.astype(BF16), v) * (1.0 / total))
                log_total = jnp.broadcast_to(high + jnp.log(total), (BLK, LANES))
                lse_ref[2 * p + side, :, rows] = jnp.transpose(log_total)[0:8, :]
            o_ref[rows, lanes] = jnp.where(head, halves[0], halves[1]).astype(BF16)
        o_copy(p).start()
        return carry

    lax.fori_loop(0, pairs, attend, 0)
    wo_copy.wait()
    for p in range(pairs):
        o_copy(p).wait()
    store(4, 5, 7)
    prev_lines = jnp.where(m == 0, prev_all_ref[:, 0, :], prev_all_ref[:, 1, :])
    spare = jnp.zeros((LANES - columns - 2, rows_all), F32)
    facts = jnp.concatenate([prev_lines, routes_ref[...].astype(F32), spare], axis=0)
    gates_ref[...] = facts

    gain_moe = extra_ref[columns + 5 : columns + 6, :]

    def middle(i, carry):
        rows = pl.ds(pl.multiple_of(i * BLK, BLK), BLK)
        z = mm_nt(o_ref[rows, :], wo_ref[...])
        h = x_ref[rows, :].astype(F32) + z
        r = lax.rsqrt(jnp.mean(h * h, axis=-1, keepdims=True) + EPSILON)
        ub = (h * r * gain_moe).astype(BF16)
        h_ref[rows, :] = h
        ub_ref[rows, :] = ub
        scores = mm(ub, small_ref[...])
        lane = lane_ids(BLK)
        facts = jnp.transpose(gates_ref[:, rows])
        e0 = facts[:, columns : columns + 1]
        e1 = facts[:, columns + 1 : columns + 2]
        hot0, hot1 = lane.astype(F32) == e0, lane.astype(F32) == e1
        logits = scores + facts
        g0, g1 = soft_pair(pick(hot0, logits), pick(hot1, logits))
        mix = [pick(lane == columns + j, scores) for j in range(4)]
        a00, a01 = soft_pair(mix[0], mix[1])
        a10, a11 = soft_pair(mix[2], mix[3])
        table = jnp.zeros((BLK, LANES), F32)
        for j, value in enumerate([g0, g1, a00, a01, a10, a11, r, e0, e1]):
            table = jnp.where(lane == j, value, table)
        stat_ref[rows, :] = table
        gates = jnp.where(hot0, g0, 0.0) + jnp.where(hot1, g1, 0.0)
        gates_ref[:, rows] = jnp.transpose(gates)
        return carry

    lax.fori_loop(0, blocks, middle, 0)
    store(10, 11, 12)
    piece = lax.broadcasted_iota(jnp.int32, (8, rows_all), 0)

    def slot_step(i, carry):
        hot = two_hot(i)
        rows = mm(hot, ub_ref[...]).astype(BF16)
        for side in range(2):
            e = 2 * i + side
            slot_ref[e] = rows[side * padded : (side + 1) * padded]
            gate = gates_ref[pl.ds(e, 1), :]
            high = gate.astype(BF16).astype(F32)
            mid = (gate - high).astype(BF16).astype(F32)
            low = gate - high - mid
            lines = jnp.where(piece == 0, high, jnp.where(piece == 1, mid, low))
            lines = jnp.where(piece < 3, lines, 0.0).astype(BF16)
            gate = mm_nt(lines, hot[side * padded : (side + 1) * padded])
            gate = jnp.sum(gate, axis=0, keepdims=True)
            gate_ref[e] = jnp.broadcast_to(gate, (8, padded))
        return carry

    lax.fori_loop(0, n // 2, slot_step, 0)
    def finish(j, carry):
        dy_copy(j).wait()
        return carry

    lax.fori_loop(1, n, finish, 0)
    for copy in stays:
        copy.wait()
    for copy in [] if gathered else sends:
        copy.wait_send()
    for copy in weight_copies:
        copy.wait()
    for i in range(early):
        pltpu.make_async_copy(kept[i], stored[i], store_sem.at[i]).wait()


def flip(value, index, size):
    bit = 1
    while bit < size:
        chosen = lax.rem(lax.div(index, bit), 2)
        value = value + chosen * (bit - 2 * bit * lax.rem(lax.div(value, bit), 2))
        bit *= 2
    return value


def expert_exchange_kernel(
    n,
    padded,
    slot_src_ref,
    gate_src_ref,
    dy_src_ref,
    in_own_ref,
    in_chip_ref,
    down_own_ref,
    gy_out_ref,
    own_in_out_ref,
    own_down_out_ref,
    chip_in_out_ref,
    far_down_ref,
    dx_all_ref,
    dg_all_ref,
    gy_ref,
    own_in_ref,
    own_down_ref,
    chip_in_ref,
    x_ref,
    xt_ref,
    dy_ref,
    scaled_ref,
    scale_ref,
    gate_ref,
    win_ref,
    wdown_ref,
    hidden_ref,
    dgate_ref,
    dup_ref,
    y_ref,
    dx_ref,
    dg_ref,
    land_in_ref,
    land_down_ref,
    chip_down_ref,
    load,
    slot_send,
    slot_recv,
    gate_send,
    gate_recv,
    dx_send,
    dx_recv,
    dg_send,
    dg_recv,
    pass_send,
    pass_recv,
    sum_send,
    sum_recv,
    w_send,
    w_recv,
    store_sem,
):
    width = x_ref.shape[1]
    share = win_ref.shape[3]
    chunks = 4
    group = n // chunks
    span = group * padded
    block = 256
    d, t = lax.axis_index("dp"), lax.axis_index("tensor")
    c = lax.rem(t, 2)
    partner = (d, t + 1 - 2 * c)
    across = (d, lax.rem(t + 2, 4))
    stores = [
        pltpu.make_async_copy(src, dst, store_sem.at[i])
        for i, (src, dst) in enumerate(
            [
                (gy_ref, gy_out_ref),
                (chip_in_ref, chip_in_out_ref),
                (own_in_ref, own_in_out_ref),
                (own_down_ref, own_down_out_ref),
            ]
        )
    ]
    greet(plane_peers(n, d, t) + [partner, across])

    def rows_of(i):
        return pl.ds(pl.multiple_of(i * padded, padded), padded)

    def slot_copy(i):
        e = flip(d, i, n)
        return remote(
            slot_src_ref.at[e], x_ref.at[rows_of(i)], slot_send.at[i], slot_recv.at[i], (e, t)
        )

    def gate_copy(i):
        e = flip(d, i, n)
        return remote(
            gate_src_ref.at[e], gate_ref.at[i], gate_send.at[i], gate_recv.at[i], (e, t)
        )

    def dx_copy(i):
        e = flip(d, i, n)
        return remote(
            dx_ref.at[rows_of(i)], dx_all_ref.at[c, d], dx_send.at[i], dx_recv.at[i], (e, t)
        )

    def dg_copy(i):
        e = flip(d, i, n)
        return remote(dg_ref.at[i], dg_all_ref.at[c, d], dg_send.at[i], dg_recv.at[i], (e, t))

    def hand(kind, i):
        ref = (dx_all_ref, dg_all_ref)[kind]
        block_ref = ref.at[c, flip(d, i, n)]
        return remote(
            block_ref, block_ref, pass_send.at[kind, i], pass_recv.at[kind, i], partner
        )

    def down_rows(s):
        return pl.ds(s * share, share)

    def send_chunk(k):
        for q in range(group):
            if k + q > 0:
                slot_copy(k * group + q).start()
                gate_copy(k * group + q).start()

    send_chunk(2)
    send_chunk(1)
    if group > 1:
        send_chunk(0)
    stays = [
        pltpu.make_async_copy(slot_src_ref.at[d], x_ref.at[rows_of(0)], load.at[0]),
        pltpu.make_async_copy(gate_src_ref.at[d], gate_ref.at[0], load.at[1]),
    ]
    own_loads = [
        pltpu.make_async_copy(in_own_ref.at[0], win_ref.at[0], load.at[2]),
        pltpu.make_async_copy(down_own_ref.at[0], wdown_ref.at[down_rows(0)], load.at[3]),
    ]
    chip_load = pltpu.make_async_copy(in_chip_ref.at[0], win_ref.at[2], load.at[4])
    weights = [
        remote(in_own_ref.at[0], win_ref.at[1], w_send.at[0], w_recv.at[0], partner),
        remote(
            down_own_ref.at[0], wdown_ref.at[down_rows(1)], w_send.at[1], w_recv.at[1], partner
        ),
        remote(in_chip_ref.at[0], win_ref.at[3], w_send.at[2], w_recv.at[2], partner),
        remote(
            down_own_ref.at[0], wdown_ref.at[down_rows(2)], w_send.at[3], w_recv.at[3], across
        ),
        remote(
            wdown_ref.at[down_rows(2)],
            wdown_ref.at[down_rows(3)],
            w_send.at[4],
            w_recv.at[4],
            partner,
        ),
    ]

    def dy_load(i):
        return pltpu.make_async_copy(
            dy_src_ref.at[flip(d, i, n)], dy_ref.at[rows_of(i)], load.at[10 + i]
        )

    for copy in [weights[3]] + stays + own_loads:
        copy.start()
    for i in range(n):
        dy_load(i).start()
    chip_load.start()
    for copy in weights[0:3]:
        copy.start()
    for copy in stays + own_loads:
        copy.wait()

    def take(k):
        rows = pl.ds(k * span, span)
        for q in range(group):
            i = k * group + q
            if i > 0:
                slot_copy(i).wait_recv()
                gate_copy(i).wait_recv()
            dy_load(i).wait()
            near = rows_of(i)
            line = jnp.broadcast_to(gate_ref[i, 0:1, :], (LANES, padded))
            scale = jnp.transpose(line)
            scale_ref[near, :] = scale
            scaled_ref[near, :] = (dy_ref[near, :].astype(F32) * scale[:, 0:1]).astype(BF16)
        xt_ref[:, rows] = jnp.transpose(x_ref[rows, :])

    per = share // block

    def units(first, last, chosen):
        def unit(u, carry):
            k = first + lax.div(u, 2 * per)
            b = lax.rem(u, 2 * per)
            s = chosen * 2 + lax.div(b, per)
            rows = pl.ds(pl.multiple_of(k * span, span), span)
            lanes = pl.ds(pl.multiple_of(lax.rem(b, per) * block, block), block)
            far = pl.ds(pl.multiple_of((chosen * 2 * per + b) * block, block), block)
            x = x_ref[rows, :]
            gate = mm(x, win_ref[s, 0, :, lanes])
            up = mm(x, win_ref[s, 1, :, lanes])
            grad = mm_nt(scaled_ref[rows, :], wdown_ref[far, :])
            sigma = 0.5 * jnp.tanh(0.5 * gate) + 0.5
            active = gate * sigma
            hidden_ref[rows, far] = (active * up).astype(BF16)
            dgate_ref[rows, far] = (grad * up * (sigma * (1.0 + gate * (1.0 - sigma)))).astype(
                BF16
            )
            dup_ref[rows, far] = (grad * active).astype(BF16)
            return carry

        lax.fori_loop(0, (last - first) * 2 * per, unit, 0)

    def close(k, carry):
        rows = pl.ds(pl.multiple_of(k * span, span), span)
        for j in range(width // block):
            lanes = pl.ds(j * block, block)
            total = jnp.zeros((span, block), F32)
            for s in range(4):
                far = pl.ds(s * share, share)
                total = total + mm_nt(dgate_ref[rows, far], win_ref[s, 0, lanes, :])
                total = total + mm_nt(dup_ref[rows, far], win_ref[s, 1, lanes, :])
            dx_ref[rows, lanes] = total.astype(BF16)
        for q in range(group):
            i = k * group + q

            @pl.when(i > 0)
            def _():
                dx_copy(i).start()

        for j in range(width // block):
            lanes = pl.ds(j * block, block)
            y_ref[:, lanes] = mm(hidden_ref[rows, :], wdown_ref[:, lanes])
        for q in range(group):
            i = k * group + q
            near = rows_of(i)
            y = y_ref[pl.ds(q * padded, padded), :]
            gy_ref[flip(d, i, n)] = (y * scale_ref[near, 0:1]).astype(BF16)
            dot = jnp.sum(y * dy_ref[near, :].astype(F32), axis=-1, keepdims=True)
            dg_ref[i] = jnp.transpose(jnp.broadcast_to(dot, (padded, LANES)))[0:8, :]

            @pl.when(i > 0)
            def _():
                dg_copy(i).start()

        return carry

    take(0)
    for copy in weights[0:2]:
        copy.wait_recv()
    units(0, 1, 0)
    take(1)
    units(1, 2, 0)
    take(2)
    send_chunk(3)
    units(2, 3, 0)
    chip_load.wait()
    weights[3].wait_recv()
    weights[4].start()
    weights[2].wait_recv()
    weights[4].wait_recv()
    units(0, 3, 1)
    lax.fori_loop(2, 3, close, 0)
    lax.fori_loop(0, 2, close, 0)
    take(3)
    units(3, 4, 0)
    units(3, 4, 1)
    lax.fori_loop(3, 4, close, 0)
    stores[0].start()
    keeps = [
        pltpu.make_async_copy(dx_ref.at[rows_of(0)], dx_all_ref.at[c, d], load.at[0]),
        pltpu.make_async_copy(dg_ref.at[0], dg_all_ref.at[c, d], load.at[1]),
    ]
    for copy in keeps:
        copy.start()

    def forward(first, last):
        def step(i, carry):
            dx_copy(i).wait_recv()
            dg_copy(i).wait_recv()
            hand(0, i).start()
            hand(1, i).start()
            return carry

        lax.fori_loop(first, last, step, 0)

    def grad_in(s, kind, b):
        far = pl.ds(pl.multiple_of(s * share + b * block, block), block)
        return mm(xt_ref[...], (dgate_ref, dup_ref)[kind][:, far])

    def grad_down(s, b):
        far = pl.ds(pl.multiple_of(s * share + b * block, block), block)
        return mm_tn(hidden_ref[:, far], scaled_ref[...])

    def sum_copies(j):
        return [
            remote(win_ref.at[j], land_in_ref.at[j], sum_send.at[j], sum_recv.at[j], partner),
            remote(
                wdown_ref.at[pl.ds(j * share, share)],
                land_down_ref.at[j],
                sum_send.at[2 + j],
                sum_recv.at[2 + j],
                partner,
            ),
        ]

    for copy in weights:
        copy.wait_send()

    def down_sums(s, put):
        def unit(b, carry):
            put(pl.ds(pl.multiple_of(b * block, block), block), grad_down(s, b))
            return carry

        lax.fori_loop(0, per, unit, 0)

    def in_sums(s, put):
        def unit(b, carry):
            lanes = pl.ds(pl.multiple_of(b * block, block), block)
            for kind in range(2):
                put(kind, lanes, grad_in(s, kind, b))
            return carry

        lax.fori_loop(0, per, unit, 0)

    def leave_down(j, s):
        def put(rows, value):
            near = pl.multiple_of(rows.start + j * share, block)
            wdown_ref[pl.ds(near, block), :] = value.astype(BF16)

        down_sums(s, put)
        sum_copies(j)[1].start()

    def leave_in(j, s):
        def put(kind, lanes, value):
            win_ref[j, kind, :, lanes] = value.astype(BF16)

        in_sums(s, put)
        sum_copies(j)[0].start()

    leave_down(0, 3)
    leave_down(1, 1)
    sum_copies(0)[1].wait_recv()

    def chip_down(lanes, value):
        chip_down_ref[0, lanes, :] = (value + land_down_ref[0, lanes, :].astype(F32)).astype(BF16)

    down_sums(2, chip_down)
    far_copy = remote(chip_down_ref, far_down_ref, w_send.at[5], w_recv.at[5], across)
    far_copy.start()
    for copy in keeps:
        copy.wait()
    hand(0, 0).start()
    hand(1, 0).start()
    forward(1, 2 * group)
    leave_in(0, 3)
    leave_in(1, 1)
    sum_copies(0)[0].wait_recv()

    def chip_in(kind, lanes, value):
        chip_in_ref[0, kind, :, lanes] = (
            value + land_in_ref[0, kind, :, lanes].astype(F32)
        ).astype(BF16)

    in_sums(2, chip_in)
    stores[1].start()
    for copy in sum_copies(1):
        copy.wait_recv()

    def own_in(kind, lanes, value):
        own_in_ref[0, kind, :, lanes] = value + land_in_ref[1, kind, :, lanes].astype(F32)

    def own_down(lanes, value):
        own_down_ref[0, lanes, :] = value + land_down_ref[1, lanes, :].astype(F32)

    in_sums(0, own_in)
    stores[2].start()
    down_sums(0, own_down)
    stores[3].start()
    forward(2 * group, n)

    def clear(i, carry):
        for copy in (slot_copy(i), gate_copy(i), dx_copy(i), dg_copy(i)):
            copy.wait_send()
        return carry

    lax.fori_loop(1, n, clear, 0)

    def passed(i, carry):
        hand(0, i).wait()
        hand(1, i).wait()
        return carry

    lax.fori_loop(0, n, passed, 0)
    for j in range(2):
        for copy in sum_copies(j):
            copy.wait_send()
    far_copy.wait()
    for copy in stores:
        copy.wait()


def expert_kernel(
    sources,
    padded,
    x_ref,
    dy_ref,
    gate_ref,
    *refs,
):
    weights, outs = refs[:8], refs[8:19]
    in_refs, down_refs = weights[0:4], weights[4:8]
    gy_ref, dx_ref, dg_ref = outs[0:3]
    gin_refs, gdown_refs = outs[3:7], outs[7:11]
    xt_ref, scaled_ref, scale_ref, y_acc, dx_acc, win_ref, wdown_ref = refs[19:]
    step = pl.program_id(0)
    last = pl.num_programs(0) - 1

    @pl.when(step == 0)
    def _():
        xt_ref[...] = jnp.transpose(x_ref[...])
        for s in range(sources):
            rows = pl.ds(s * padded, padded)
            line = jnp.broadcast_to(gate_ref[s, 0:1, :], (LANES, padded))
            scale = jnp.transpose(line)
            scale_ref[rows, :] = scale
            scaled_ref[rows, :] = (dy_ref[rows, :].astype(F32) * scale[:, 0:1]).astype(BF16)
        y_acc[...] = jnp.zeros_like(y_acc)
        dx_acc[...] = jnp.zeros_like(dx_acc)

    per = pl.num_programs(0) // 4
    for i in range(4):

        @pl.when(lax.div(step, per) == i)
        def _():
            win_ref[...] = in_refs[i][0]
            wdown_ref[...] = down_refs[i][0]

    x = x_ref[...]
    gate = mm(x, win_ref[0])
    up = mm(x, win_ref[1])
    sigma = 1.0 / (1.0 + jnp.exp(-gate))
    active = gate * sigma
    hidden = (active * up).astype(BF16)
    y_acc[...] += mm(hidden, wdown_ref[...])
    scaled = scaled_ref[...]
    grad_hidden = mm_nt(scaled, wdown_ref[...])
    grad_gate = (grad_hidden * up * (sigma * (1.0 + gate * (1.0 - sigma)))).astype(BF16)
    grad_up = (grad_hidden * active).astype(BF16)
    dx_acc[...] += mm_nt(grad_gate, win_ref[0]) + mm_nt(grad_up, win_ref[1])
    xt = xt_ref[...]
    part_gate = mm(xt, grad_gate).astype(BF16)
    part_up = mm(xt, grad_up).astype(BF16)
    part_down = mm_tn(hidden, scaled).astype(BF16)
    for i in range(4):

        @pl.when(lax.div(step, per) == i)
        def _():
            gin_refs[i][0, 0] = part_gate
            gin_refs[i][0, 1] = part_up
            gdown_refs[i][0] = part_down

    @pl.when(step == last)
    def _():
        for s in range(sources):
            rows = pl.ds(s * padded, padded)
            y = y_acc[rows, :]
            gy_ref[s] = (y * scale_ref[rows, 0:1]).astype(BF16)
            dot = jnp.sum(y * dy_ref[rows, :].astype(F32), axis=-1, keepdims=True)
            dg_ref[s] = jnp.transpose(jnp.broadcast_to(dot, (padded, LANES)))[0:8, :]
            dx_ref[s] = dx_acc[rows, :].astype(BF16)


def rear_kernel(n, half, padded, gathered, part, *refs):
    crossing = 0 if gathered else 1
    chip_in_refs, refs = refs[:crossing], refs[crossing:]
    gy_src_ref, tokens_ref, cotangent_ref, o_all_ref = refs[:4]
    loaded, refs = refs[4:17], refs[17:]
    stat_ref, pos_ref, small_ref, extra_ref, dg_ref = refs[:5]
    result_ref, grad_x_ref, logit_ref, grads_ref, lines_ref = refs[5:10]
    far_in_refs, refs = refs[10 : 10 + crossing], refs[10 + crossing :]
    kept, refs = refs[:13], refs[13:]
    dx_ref, h_ref, wo_ref, ub_ref, q_ref, k_ref, v_ref = kept[:7]
    lse_ref, cos_ref, sin_ref, a_ref, spread_a_ref, spread_b_ref = kept[7:]
    x_ref, dy_ref, o_ref, gy_ref, dh_ref, dzb_ref, do_ref, low_ref, row_ref = refs[:9]
    dp_ref, dk_acc, dv_acc, wo_odd_ref, pack_ref, line_ref, y_in_ref, z_in_ref = refs[9:17]
    line_in_ref, cross_ref, cross_in_ref, cross_line_ref = refs[17:21]
    da_out_ref, da_in_ref, da_own_ref, norm_ref, norm_in_ref, half_ref = refs[21:27]
    load, fetch_sem, gy_send, gy_recv, stay, pass_send, pass_recv = refs[27:34]
    grad_send, grad_recv, line_send, line_recv, pair_send, pair_recv = refs[34:40]
    out_send, out_recv, sum_send, sum_recv = refs[40:]

    def fetch(i):
        src = loaded[i]
        if i == 11:
            src = src.at[:, :, pl.ds(0, 3 * LANES)]
        if i == 12:
            src = src.at[:, :, pl.ds(4 * LANES, 2 * LANES)]
        return pltpu.make_async_copy(src, kept[i], fetch_sem.at[i])

    rows_all, width = dy_ref.shape
    blocks = rows_all // BLK
    pairs = q_ref.shape[0]
    local = pairs * LANES
    columns = n + 4
    slots = n * padded
    d, t = lax.axis_index("dp"), lax.axis_index("tensor")
    m, c = lax.div(t, 2), lax.rem(t, 2)
    partner = (d, t + 1 - 2 * c)
    across = (d, lax.rem(t + 2, 4))
    rows_half = rows_all // 2
    own = pl.multiple_of(c * local, LANES)
    own_lanes = pl.ds(own, local)
    place = pl.ds(pl.multiple_of(c * rows_half, BLK), rows_half)
    loads = [
        pltpu.make_async_copy(src, dst, load.at[i])
        for i, (src, dst) in enumerate(
            [
                (cotangent_ref.at[m], dy_ref),
                (tokens_ref.at[m, place], x_ref),
                (o_all_ref.at[:, own_lanes], o_ref),
            ]
        )
    ]
    for i in range(2):
        fetch(i).start()
    for copy in loads:
        copy.start()
    for i in range(2, 13):
        fetch(i).start()
    greet(plane_peers(n, d, t) + [partner, across])

    sum_copies = [
        remote(src, land, sum_send.at[0], sum_recv.at[0], across)
        for src, land in zip(chip_in_refs, far_in_refs)
    ]
    for copy in sum_copies:
        copy.start()

    def give(j):
        s = lax.rem(d + j, n)
        return remote(gy_src_ref.at[s], gy_ref.at[c, d], gy_send.at[j], gy_recv.at[j], (s, t))

    def hand(j):
        block = gy_ref.at[c, lax.rem(d + n - j, n)]
        return remote(block, block, pass_send.at[j], pass_recv.at[j], partner)

    keep = pltpu.make_async_copy(gy_src_ref.at[d], gy_ref.at[c, d], stay.at[0])
    keep.start()

    def give_start(j, carry):
        give(j).start()
        return carry

    lax.fori_loop(1, n, give_start, 0)

    def collect():
        keep.wait()
        hand(0).start()

        def step(j, carry):
            give(j).wait_recv()
            hand(j).start()
            return carry

        lax.fori_loop(1, n, step, 0)

    def settle():
        def step(j, carry):
            hand(j).wait_recv()
            return carry

        lax.fori_loop(0, n, step, 0)

    row_ref[...] = jnp.zeros_like(row_ref)
    for copy in loads:
        copy.wait()
    for i in range(3):
        fetch(i).wait()

    gain_moe = extra_ref[columns + 5 : columns + 6, :]
    vec0 = extra_ref[columns + 6 : columns + 7, :]
    vec1 = extra_ref[columns + 7 : columns + 8, :]
    group = max(1, min(n, (1024 if slots <= 1024 else 512) // padded))
    span = group * padded

    def combine(wheres, ref, lines=None):
        total = jnp.zeros((BLK, width), F32)
        entries = [jnp.zeros((BLK, 1), F32) for _ in wheres]
        slot = lax.broadcasted_iota(jnp.int32, (BLK, span), 1)
        for side in range(2):
            for first in range(0, n, group):
                start = side * slots + first * padded
                hots = [slot == where - start for where in wheres]
                hot = jnp.where(hots[0] | hots[1], 1.0, 0.0).astype(BF16)
                block = ref[side, first : first + group].reshape(span, width)
                total = total + mm(hot, block)
                if lines is not None:
                    line = jnp.concatenate(
                        [lines[side, first + e, 0:1, :] for e in range(group)], axis=1
                    )
                    entries = [
                        entry + jnp.sum(jnp.where(one, line, 0.0), axis=-1, keepdims=True)
                        for entry, one in zip(entries, hots)
                    ]
        return total, entries

    def facts(rows):
        lane = lane_ids(BLK)
        stats = stat_ref[rows, :]
        values = [stats[:, j : j + 1] for j in range(7)]
        e0, e1 = stats[:, 7:8].astype(jnp.int32), stats[:, 8:9].astype(jnp.int32)
        wheres = []
        places = pos_ref[rows, :]
        for e in (e0, e1):
            place = pick(lane == e, places).astype(jnp.int32)
            side = (place >= half).astype(jnp.int32)
            where = side * (slots - half) + e * padded + place
            wheres.append(jnp.where(e < n, where, -1))
        g0, g1 = values[0:2]

        def named(number):
            return jnp.where(e0 == number, g0, 0.0) + jnp.where(e1 == number, g1, 0.0)

        copied, first, second = named(n + 1), named(n + 2), named(n + 3)
        on_u = copied + first * values[2] + second * values[4]
        return values, e0, e1, wheres, first, second, on_u

    def back(i, carry):
        rows = pl.ds(pl.multiple_of(i * BLK, BLK), BLK)
        values, e0, e1, wheres, first, second, on_u = facts(rows)
        g0, g1, a00, a01, a10, a11, r = values
        lane = lane_ids(BLK)
        grads, (f0, f1) = combine(wheres, dx_ref, dg_ref)
        h = h_ref[rows, :]
        normed = h * r
        u = normed * gain_moe
        dy = dy_ref[rows, :].astype(F32)
        s_u = jnp.sum(dy * u, axis=-1, keepdims=True)
        s_0 = jnp.sum(dy * vec0, axis=-1, keepdims=True)
        s_1 = jnp.sum(dy * vec1, axis=-1, keepdims=True)

        def other(e):
            value = jnp.where(e == n + 1, s_u, 0.0)
            value = jnp.where(e == n + 2, a00 * s_u + a01 * s_0, value)
            return jnp.where(e == n + 3, a10 * s_u + a11 * s_1, value)

        dg0, dg1 = f0 + other(e0), f1 + other(e1)
        mean = g0 * dg0 + g1 * dg1
        dl = jnp.where(lane == e0, g0 * (dg0 - mean), 0.0) + jnp.where(
            lane == e1, g1 * (dg1 - mean), 0.0
        )
        turned = jnp.transpose(dl)
        logit_ref[m, :, rows] = turned[0 : logit_ref.shape[1], :]
        d00, d01 = first * s_u, first * s_0
        d10, d11 = second * s_u, second * s_1
        m0 = a00 * d00 + a01 * d01
        m1 = a10 * d10 + a11 * d11
        low = dl
        for j, value in enumerate(
            [a00 * (d00 - m0), a01 * (d01 - m0), a10 * (d10 - m1), a11 * (d11 - m1)]
        ):
            low = jnp.where(lane == columns + j, value, low)
        low = low.astype(BF16)
        low_ref[rows, :] = low
        du = grads + mm_nt(low, small_ref[...]) + on_u * dy
        row_ref[0:1, :] += jnp.sum(du * normed, axis=0, keepdims=True)
        row_ref[1:2, :] += jnp.sum((first * a01) * dy, axis=0, keepdims=True)
        row_ref[2:3, :] += jnp.sum((second * a11) * dy, axis=0, keepdims=True)
        dn = du * gain_moe
        dh = dy + r * (dn - normed * jnp.mean(dn * normed, axis=-1, keepdims=True))

        @pl.when(lax.div(i, blocks // 2) == c)
        def _():
            near = pl.multiple_of(i * BLK - c * rows_half, BLK)
            dh_ref[pl.ds(near, BLK), :] = dh

        dzb = dh.astype(BF16)
        dzb_ref[rows, :] = dzb
        do_ref[rows, :] = mm(dzb, wo_ref[:, own_lanes]).astype(BF16)
        return carry

    lax.fori_loop(0, blocks, back, 0)
    logit_copy = remote(
        logit_ref.at[m], logit_ref.at[m], pair_send.at[0], pair_recv.at[0], across
    )
    logit_copy.start()

    fetch(3).wait()
    grad_wo = mm_tn(dzb_ref[...], o_ref[...])
    pack_ref[0, :, 3 * LANES : 4 * LANES] = grad_wo[:, 0:LANES].astype(BF16)
    pack_ref[1, :, 3 * LANES : 4 * LANES] = grad_wo[:, LANES : 2 * LANES].astype(BF16)
    wo_odd_ref[...] = grad_wo[:, 2 * LANES : 3 * LANES]
    line_ref[...] = mm_tn(ub_ref[...], low_ref[...])

    def slab(owner):
        return pl.ds(pl.multiple_of(owner * part, part), part)

    ring = n // 2
    y_own = lax.rem(d, 2)
    beside = (d + 1 - 2 * y_own, t)
    z_own = lax.div(d, 2)
    wide_lanes = (pl.ds(0, 3 * LANES), pl.ds(3 * LANES, 3 * LANES))

    def y_copy(s, stage, z):
        lanes = wide_lanes[stage]
        return remote(
            pack_ref.at[s, slab(2 * z + 1 - y_own), lanes],
            y_in_ref.at[s, z, :, lanes],
            grad_send.at[stage, s, z],
            grad_recv.at[stage, s, z],
            beside,
        )

    def z_copy(s, stage, j):
        lanes = wide_lanes[stage]
        z = lax.rem(z_own + j, ring)
        return remote(
            pack_ref.at[s, slab(2 * z + y_own), lanes],
            z_in_ref.at[s, j, :, lanes],
            grad_send.at[2 + stage, s, j],
            grad_recv.at[2 + stage, s, j],
            (2 * z + y_own, t),
        )

    def y_start(s, stage):
        for z in range(ring):
            y_copy(s, stage, z).start()

    def z_start(s, stage):
        lanes = wide_lanes[stage]
        for z in range(ring):
            y_copy(s, stage, z).wait()
            rows = slab(2 * z + y_own)
            value = pack_ref[s, rows, lanes].astype(F32) + y_in_ref[s, z, :, lanes].astype(F32)
            pack_ref[s, rows, lanes] = value.astype(BF16)
        for j in range(1, ring):
            z_copy(s, stage, j).start()

    def line_copy(j):
        e = lax.rem(d + j, n)
        return remote(
            line_ref.at[slab(e), :],
            line_in_ref.at[d],
            line_send.at[j],
            line_recv.at[j],
            (e, t),
        )

    head = half_mask(BLK)

    def attend_back(p):
        dk_acc[...] = jnp.zeros_like(dk_acc)
        dv_acc[...] = jnp.zeros_like(dv_acc)
        dq = []
        for i in range(blocks):
            rows = pl.ds(i * BLK, BLK)
            seen = pl.ds(0, (i + 1) * BLK)
            lanes = pl.ds(pl.multiple_of(p * LANES, LANES), LANES)
            q, do = q_ref[p, rows, :], do_ref[rows, lanes]
            k, v = k_ref[p, seen, :], v_ref[p, seen, :]
            zero = jnp.zeros_like(q)
            parts = []
            dk, dv = dk_acc[seen, :], dv_acc[seen, :]
            for side in range(2):
                chosen = head if side == 0 else jnp.logical_not(head)
                qm, dom = jnp.where(chosen, q, zero), jnp.where(chosen, do, zero)
                prob = jnp.exp(mm_nt(k, qm) - lse_ref[2 * p + side, 0:1, rows])
                grad_prob = mm_nt(v, dom)
                total = jnp.sum(prob * grad_prob, axis=0, keepdims=True)
                grad_score = (prob * (grad_prob - total)).astype(BF16)
                dv = dv + mm(prob.astype(BF16), dom)
                dk = dk + mm(grad_score, qm)
                parts.append(mm_tn(grad_score, k))
            dk_acc[seen, :] = dk
            dv_acc[seen, :] = dv
            value = jnp.where(head, parts[0], parts[1]) * (HD**-0.5)
            dq.append(turn(value, cos_ref[rows, :], -sin_ref[rows, :]))
        return (
            jnp.concatenate(dq, axis=0),
            turn(dk_acc[...], cos_ref[...], -sin_ref[...]),
            dv_acc[...],
        )

    for i in range(4, 11):
        fetch(i).wait()
    dq, dk, dv = attend_back(2)
    wide = half_mask(rows_all)
    odd = [
        (jnp.where(wide, dq, swap_halves(dk)), jnp.where(wide, dv, 0.0)),
        (jnp.where(wide, swap_halves(dq), dk), jnp.where(wide, swap_halves(dv), 0.0)),
    ]
    tall = half_mask(width)
    for s in range(2):
        for j in range(2):
            dp_ref[s, :, (3 + j) * LANES : (4 + j) * LANES] = odd[s][j].astype(BF16)
    for s in range(2):
        pack_ref[s, :, 4 * LANES : 5 * LANES] = mm_tn(
            a_ref[...], dp_ref[s, :, 3 * LANES : 4 * LANES]
        ).astype(BF16)
        last = mm_tn(a_ref[...], dp_ref[s, :, 4 * LANES : 5 * LANES])
        side = wo_odd_ref[...]
        side = swap_halves(side) if s == 0 else side
        pack_ref[s, :, 5 * LANES : 6 * LANES] = jnp.where(tall, last, side).astype(BF16)
    if not gathered:
        y_start(0, 1)
        y_start(1, 1)

    def shard_step(i, carry):
        s = lax.rem(m + 1 + i, 2)
        for j, value in enumerate(attend_back(s)):
            dp_ref[s, :, j * LANES : (j + 1) * LANES] = value.astype(BF16)
        for j in range(3):
            lanes = pl.ds(j * LANES, LANES)
            pack_ref[s, :, lanes] = mm_tn(a_ref[...], dp_ref[s, :, lanes]).astype(BF16)
        if not gathered:
            y_start(s, 0)
        return carry

    lax.fori_loop(0, 2, shard_step, 0)
    if not gathered:
        z_start(0, 1)
        z_start(1, 1)
    collect()

    def publish(kind, out_ref):
        block = out_ref.at[m, place]
        copies = [
            remote(half_ref.at[kind], block, out_send.at[kind, 0], out_recv.at[kind, 0], across),
            remote(half_ref.at[kind], block, out_send.at[kind, 1], out_recv.at[kind, 1], partner),
            pltpu.make_async_copy(half_ref.at[kind], block, stay.at[1 + kind]),
        ]
        for copy in copies:
            copy.start()
        block = out_ref.at[1 - m, place]
        relay = remote(block, block, out_send.at[kind, 2], out_recv.at[kind, 2], partner)
        return copies, relay

    settle()

    def results(i, carry):
        rows = pl.ds(pl.multiple_of(i * BLK, BLK), BLK)
        far = pl.ds(pl.multiple_of(c * rows_half + i * BLK, BLK), BLK)
        values, e0, e1, wheres, first, second, on_u = facts(far)
        sums, _ = combine(wheres, gy_ref)
        h = h_ref[far, :]
        u = h * values[6] * gain_moe
        result = h + (sums + on_u * u + (first * values[3]) * vec0 + (second * values[5]) * vec1)
        half_ref[1, rows, :] = result.astype(BF16)
        return carry

    lax.fori_loop(0, rows_half // BLK, results, 0)
    result_copies, result_relay = publish(1, result_ref)

    if not gathered:
        z_start(1 - m, 0)

    def da_rows(start):
        rows = pl.ds(pl.multiple_of(start, BLK), BLK)
        total = jnp.zeros((BLK, width), F32)
        for s in range(2):
            total = total + mm_nt(dp_ref[s, rows, 0 : 3 * LANES], spread_a_ref[s])
            total = total + mm_nt(dp_ref[s, rows, 3 * LANES : 5 * LANES], spread_b_ref[s])
        return total

    fetch(11).wait()
    fetch(12).wait()

    def da_other(i, carry):
        rows = pl.ds(pl.multiple_of(i * BLK, BLK), BLK)
        da_out_ref[rows, :] = da_rows((1 - c) * rows_half + i * BLK).astype(BF16)
        return carry

    lax.fori_loop(0, rows_half // BLK, da_other, 0)
    da_copy = remote(da_out_ref, da_in_ref, pair_send.at[1], pair_recv.at[1], partner)
    da_copy.start()

    def da_own(i, carry):
        rows = pl.ds(pl.multiple_of(i * BLK, BLK), BLK)
        da_own_ref[rows, :] = da_rows(c * rows_half + i * BLK)
        return carry

    lax.fori_loop(0, rows_half // BLK, da_own, 0)
    if not gathered:
        z_start(m, 0)
    da_copy.wait()
    gain_attn = extra_ref[columns + 4 : columns + 5, :]
    norm_ref[...] = jnp.zeros_like(norm_ref)

    def finish(i, carry):
        rows = pl.ds(pl.multiple_of(i * BLK, BLK), BLK)
        x = x_ref[rows, :].astype(F32)
        r = lax.rsqrt(jnp.mean(x * x, axis=-1, keepdims=True) + EPSILON)
        normed = x * r
        da = da_own_ref[rows, :] + da_in_ref[rows, :].astype(F32)
        norm_ref[0:1, :] += jnp.sum(da * normed, axis=0, keepdims=True)
        dn = da * gain_attn
        grad = dh_ref[rows, :] + r * (dn - normed * jnp.mean(dn * normed, axis=-1, keepdims=True))
        half_ref[0, rows, :] = grad.astype(BF16)
        return carry

    lax.fori_loop(0, rows_half // BLK, finish, 0)
    norm_copy = remote(norm_ref, norm_in_ref, pair_send.at[2], pair_recv.at[2], partner)
    norm_copy.start()

    grad_x_copies, grad_x_relay = publish(0, grad_x_ref)

    norm_copy.wait()
    row_ref[3:4, :] = norm_ref[0:1, :] + norm_in_ref[0:1, :]
    turned = jnp.concatenate([row_ref[...], jnp.zeros((LANES - 8, width), F32)], axis=0)
    turned = jnp.transpose(turned)
    lane = lax.broadcasted_iota(jnp.int32, (width, LANES), 1)
    lines = line_ref[...]
    for j, source in enumerate([3, 0, 1, 2]):
        lines = jnp.where(lane == columns + 4 + j, turned[:, source : source + 1], lines)
    line_ref[...] = lines
    if gathered:
        packs = [
            pltpu.make_async_copy(pack_ref, grads_ref, load.at[0]),
            pltpu.make_async_copy(line_ref, lines_ref, load.at[1]),
        ]
        for copy in packs:
            copy.start()
        for copy in packs:
            copy.wait()
    else:

        def send(j, carry):
            line_copy(j).start()
            return carry

        lax.fori_loop(1, n, send, 0)
        line_in_ref[d] = line_ref[slab(d), :]
        for s, stage in ((0, 1), (1, 1), (1 - m, 0)):
            for j in range(1, ring):
                z_copy(s, stage, j).wait()

        def total(s):
            value = pack_ref[s, slab(d), :].astype(F32)
            for j in range(1, ring):
                value = value + z_in_ref[s, j].astype(F32)
            return value

        cross_ref[...] = total(1 - m).astype(BF16)
        cross_copy = remote(cross_ref, cross_in_ref, pair_send.at[3], pair_recv.at[3], across)
        cross_copy.start()
        for j in range(1, ring):
            z_copy(m, 0, j).wait()
        grads_ref[...] = total(m)
        result_copies[0].wait_recv()
        result_relay.start()

        def arrive_lines(j, carry):
            line_copy(j).wait()
            return carry

        lax.fori_loop(1, n, arrive_lines, 0)
        value = line_in_ref[0]
        for e in range(1, n):
            value = value + line_in_ref[e]
        cross_line_ref[0] = value
        cross_line_copy = remote(
            cross_line_ref.at[0], cross_line_ref.at[1], pair_send.at[4], pair_recv.at[4], across
        )
        cross_line_copy.start()
        cross_copy.wait()
        grads_ref[...] += cross_in_ref[...].astype(F32)
        cross_line_copy.wait()
        lines_ref[...] = cross_line_ref[0] + cross_line_ref[1]

    grad_x_copies[0].wait_recv()
    grad_x_relay.start()
    if gathered:
        result_copies[0].wait_recv()
        result_relay.start()
    for copies, relay in ((grad_x_copies, grad_x_relay), (result_copies, result_relay)):
        copies[0].wait_send()
        copies[1].wait()
        copies[2].wait()
        relay.wait()
    logit_copy.wait()

    for copy in sum_copies:
        copy.wait()

    def clear(j, carry):
        give(j).wait_send()
        return carry

    lax.fori_loop(1, n, clear, 0)

    def passed(j, carry):
        hand(j).wait_send()
        return carry

    lax.fori_loop(0, n, passed, 0)


def last_kernel(
    part,
    columns,
    results_ref,
    grad_x_ref,
    own_in_ref,
    far_in_ref,
    own_down_ref,
    far_down_ref,
    logit_ref,
    grads_ref,
    lines_ref,
    results_out,
    grad_x_out,
    in_out,
    down_out,
    logit_out,
    attn_out,
    moe_out,
    heads_out,
    out_out,
    router_out,
    const_out,
    vec_out,
):
    results_out[...] = results_ref[...]
    grad_x_out[...] = grad_x_ref[...]
    in_out[...] = own_in_ref[...] + far_in_ref[...].astype(F32)
    down_out[...] = own_down_ref[...] + far_down_ref[...].astype(F32)

    @pl.when(pl.program_id(0) == 0)
    def _():
        for m in range(2):
            logit_out[:, m, :] = logit_ref[m, 0:columns, :]
        firsts = [grads_ref[:, j * LANES : (j + 1) * LANES] for j in range(4)]
        odds = []
        for j in range(2):
            both = grads_ref[:, (4 + j) * LANES : (5 + j) * LANES]
            odds.extend([both, swap_halves(both)])
        for j in range(3):
            heads_out[j, :, 0:LANES] = firsts[j]
            heads_out[j, :, LANES : LANES + HD] = odds[j][:, 0:HD]
        spare = jnp.zeros((LANES - part, 2 * LANES), F32)
        rows = jnp.concatenate([firsts[3], odds[3]], axis=1)
        turned = jnp.transpose(jnp.concatenate([rows, spare], axis=0))
        out_out[...] = turned[0 : LANES + HD, 0:part]
        lines = jnp.concatenate([lines_ref[...], spare[:, 0:LANES]], axis=0)
        lines = jnp.transpose(lines)[:, 0:part]
        router_out[...] = lines[0:columns]
        const_out[...] = lines[columns : columns + 4]
        attn_out[...] = lines[columns + 4 : columns + 5]
        moe_out[...] = lines[columns + 5 : columns + 6]
        vec_out[...] = lines[columns + 6 : columns + 8]


def across_chips(value):
    return lax.ppermute(value, "tensor", [(0, 2), (2, 0), (1, 3), (3, 1)])


def across_cores(value):
    return lax.ppermute(value, "tensor", [(0, 1), (1, 0), (2, 3), (3, 2)])


def body(
    tokens,
    cotangent,
    prev_logits,
    routes,
    norm_attn,
    norm_moe,
    w_qkv,
    w_out,
    w_router,
    w_const,
    const_vec,
    w_in,
    w_down,
):
    rows, width = tokens.shape[1:]
    n = lax.axis_size("dp")
    experts = n
    columns = prev_logits.shape[2]
    capacity = 4 * max(1, 3 * rows // (4 * (experts + 4)))
    half = capacity // 2
    padded = -(-half // 16) * 16
    share = w_qkv.shape[2]
    local = 2 * share
    part = w_qkv.shape[1]
    t = lax.axis_index("tensor")
    m, c = t // 2, t % 2

    cosine, sine = (jnp.asarray(v) for v in rope_constants())
    pairs = local // LANES

    tinies = [w_router.T, w_const.T, norm_attn[None], norm_moe[None], const_vec]
    gathered = part % 16 != 0
    if gathered:
        wo_rows = w_out.T
        tiny = jnp.concatenate(
            tinies + [jnp.zeros((LANES - columns - 8, part), BF16)], axis=0
        )
        packed = jnp.concatenate(
            [w_qkv[i, :, :LANES] for i in range(3)]
            + [wo_rows[:, :LANES]]
            + [w_qkv[i, :, LANES:] for i in range(3)]
            + [wo_rows[:, LANES:], tiny.T],
            axis=1,
        )
    if gathered:
        packed = lax.all_gather(packed, "dp", axis=0, tiled=True)
        other = across_chips(packed)
        tinies = [jnp.where(m == 0, jnp.stack([packed, other]), jnp.stack([other, packed]))]
    late = [
        struct((n, padded, width), BF16),
        struct((n, 8, padded), F32),
        struct((LANES, width), F32),
    ]
    early = [
        struct((rows, width), BF16),
        struct((pairs, rows, LANES), BF16),
        struct((pairs, rows, LANES), BF16),
        struct((pairs, rows, LANES), BF16),
        struct((rows, width), BF16),
        struct((8, 8, rows), F32),
        struct((rows, LANES), F32),
        struct((width, width), BF16),
        struct((width, LANES), BF16),
        struct((2, width, 7 * LANES), BF16),
        struct((rows, width), F32),
        struct((rows, width), BF16),
        struct((rows, LANES), F32),
    ]
    landing = [struct((n, padded, width), BF16), struct(w_in.shape, BF16)]
    dma = pltpu.SemaphoreType.DMA
    outs = pl.pallas_call(
        functools.partial(front_kernel, n, half, padded, gathered, len(early)),
        out_shape=late + early + landing,
        in_specs=[aspec()] * 3 + [vspec()] * 5 + [aspec()] + [vspec()] * len(tinies),
        out_specs=[vspec()] * len(late) + [aspec()] * (len(early) + len(landing)),
        scratch_shapes=[pltpu.VMEM(o.shape, o.dtype) for o in early]
        + [
            pltpu.VMEM((rows, width), BF16),
            pltpu.VMEM((rows, width), BF16),
            pltpu.VMEM((2, rows), jnp.int32),
            pltpu.VMEM((LANES, rows), F32),
            pltpu.VMEM((LANES, rows), F32),
            pltpu.VMEM((n, padded, width), BF16),
            dma((3,)),
            dma((8, n // 2)),
            dma((8, n // 2)),
            dma((n,)),
            dma((n,)),
            dma((1,)),
            dma((pairs + 1,)),
            dma((pairs + 1,)),
            dma((1,)),
            dma((1,)),
            dma((len(early),)),
        ],
        compiler_params=pltpu.CompilerParams(
            collective_id=0, has_side_effects=True, vmem_limit_bytes=VMEM_LIMIT
        ),
        cost_estimate=pl.CostEstimate(
            flops=60_000_000_000, bytes_accessed=60_000_000, transcendentals=0
        ),
    )(
        tokens,
        cotangent,
        jnp.swapaxes(routes, 1, 2),
        jnp.transpose(prev_logits, (2, 0, 1)),
        w_qkv,
        w_out,
        cosine,
        sine,
        w_in,
        *tinies,
    )
    slots, gate_slots, extra, a, q, k, v, o_all, lse, pos = outs[:10]
    wo_all, small_all, spread, h, ub, stats, dy_arrived, in_x = outs[10:]

    hidden_width = w_in.shape[3]
    slots_all = experts * padded
    if gathered:
        in_x, down_x = across_chips(w_in), across_chips(w_down)
        in_c, down_c = across_cores(w_in), across_cores(w_down)
        in_d, down_d = across_cores(in_x), across_cores(down_x)
        chunk = min(256 if slots_all <= 1024 else 128, hidden_width)
        per = hidden_width // chunk

        def in_map(i):
            return lambda f: (0, 0, 0, jnp.clip(f - per * i, 0, per - 1))

        def down_map(i):
            return lambda f: (0, jnp.clip(f - per * i, 0, per - 1), 0)

        in_blocks = [pl.BlockSpec((1, 2, width, chunk), in_map(i)) for i in range(4)]
        down_blocks = [pl.BlockSpec((1, chunk, width), down_map(i)) for i in range(4)]
        expert_outs = (
            [
                struct((n, padded, width), BF16),
                struct((n, padded, width), BF16),
                struct((n, 8, padded), F32),
            ]
            + [struct(w_in.shape, BF16)] * 4
            + [struct(w_down.shape, BF16)] * 4
        )

        def whole(shape):
            return pl.BlockSpec(
                shape, lambda f: (0,) * len(shape), pipeline_mode=pl.Buffered(1)
            )

        parts = pl.pallas_call(
            functools.partial(expert_kernel, n, padded),
            grid=(4 * per,),
            out_shape=expert_outs,
            in_specs=[
                whole((slots_all, width)),
                whole((slots_all, width)),
                whole((n, 8, padded)),
            ]
            + in_blocks
            + down_blocks,
            out_specs=[
                whole((n, padded, width)),
                whole((n, padded, width)),
                whole((n, 8, padded)),
            ]
            + in_blocks
            + down_blocks,
            scratch_shapes=[
                pltpu.VMEM((width, slots_all), BF16),
                pltpu.VMEM((slots_all, width), BF16),
                pltpu.VMEM((slots_all, LANES), F32),
                pltpu.VMEM((slots_all, width), F32),
                pltpu.VMEM((slots_all, width), F32),
                pltpu.VMEM((2, width, chunk), BF16),
                pltpu.VMEM((chunk, width), BF16),
            ],
            compiler_params=pltpu.CompilerParams(vmem_limit_bytes=VMEM_LIMIT),
            cost_estimate=pl.CostEstimate(
                flops=18 * slots_all * width * 4 * hidden_width,
                bytes_accessed=30_000_000,
                transcendentals=0,
            ),
        )(
            lax.all_to_all(slots, "dp", split_axis=0, concat_axis=0, tiled=True).reshape(
                slots_all, width
            ),
            dy_arrived.reshape(slots_all, width),
            lax.all_to_all(gate_slots, "dp", split_axis=0, concat_axis=0, tiled=True),
            w_in,
            in_c,
            in_x,
            in_d,
            w_down,
            down_c,
            down_x,
            down_d,
        )
        gy, dx, dg = parts[0:3]
        gin, gdown = parts[3:7], parts[7:11]

        def everywhere(value):
            value = lax.all_to_all(value, "dp", split_axis=0, concat_axis=0, tiled=True)
            other = across_cores(value)
            return jnp.where(c == 0, jnp.stack([value, other]), jnp.stack([other, value]))

        dx_all, dg_all = everywhere(dx), everywhere(dg)

        def total(own, core, chip, diagonal):
            chip = (chip.astype(F32) + across_cores(diagonal).astype(F32)).astype(BF16)
            own = own.astype(F32) + across_cores(core).astype(F32)
            return own + across_chips(chip).astype(F32)

        grad_in, grad_down = total(*gin), total(*gdown)
        chip_in = []
    else:
        gy, own_in, own_down, chip_in, far_down, dx_all, dg_all = pl.pallas_call(
            functools.partial(expert_exchange_kernel, n, padded),
            out_shape=[
                struct((n, padded, width), BF16),
                struct(w_in.shape, F32),
                struct(w_down.shape, F32),
                struct(w_in.shape, BF16),
                struct(w_down.shape, BF16),
                struct((2, n, padded, width), BF16),
                struct((2, n, 8, padded), F32),
            ],
            in_specs=[aspec()] * 6,
            out_specs=[aspec()] * 7,
            scratch_shapes=[
                pltpu.VMEM((n, padded, width), BF16),
                pltpu.VMEM(w_in.shape, F32),
                pltpu.VMEM(w_down.shape, F32),
                pltpu.VMEM(w_in.shape, BF16),
                pltpu.VMEM((slots_all, width), BF16),
                pltpu.VMEM((width, slots_all), BF16),
                pltpu.VMEM((slots_all, width), BF16),
                pltpu.VMEM((slots_all, width), BF16),
                pltpu.VMEM((slots_all, LANES), F32),
                pltpu.VMEM((n, 8, padded), F32),
                pltpu.VMEM((4, 2, width, hidden_width), BF16),
                pltpu.VMEM((4 * hidden_width, width), BF16),
                pltpu.VMEM((slots_all, 4 * hidden_width), BF16),
                pltpu.VMEM((slots_all, 4 * hidden_width), BF16),
                pltpu.VMEM((slots_all, 4 * hidden_width), BF16),
                pltpu.VMEM((slots_all // 4, width), F32),
                pltpu.VMEM((slots_all, width), BF16),
                pltpu.VMEM((n, 8, padded), F32),
                pltpu.VMEM((2,) + w_in.shape[1:], BF16),
                pltpu.VMEM((2,) + w_down.shape[1:], BF16),
                pltpu.VMEM(w_down.shape, BF16),
                dma((10 + n,)),
                dma((n,)),
                dma((n,)),
                dma((n,)),
                dma((n,)),
                dma((n,)),
                dma((n,)),
                dma((n,)),
                dma((n,)),
                dma((2, n)),
                dma((2, n)),
                dma((4,)),
                dma((4,)),
                dma((6,)),
                dma((6,)),
                dma((4,)),
            ],
            compiler_params=pltpu.CompilerParams(
                collective_id=2, has_side_effects=True, vmem_limit_bytes=VMEM_LIMIT
            ),
            cost_estimate=pl.CostEstimate(
                flops=60_000_000_000, bytes_accessed=40_000_000, transcendentals=0
            ),
        )(
            slots,
            gate_slots,
            dy_arrived,
            w_in,
            in_x,
            w_down,
        )
        chip_in = [chip_in]

    groups = 6 * LANES
    logit_rows = -(-columns // 8) * 8
    rear_outs = [
        struct((2, logit_rows, rows), F32),
        struct((2, width, groups), BF16) if gathered else struct((part, groups), F32),
        struct((width if gathered else part, LANES), F32),
    ]
    half_rows = rows // 2
    spread_n = 1 if gathered else n // 2
    line_n = 1 if gathered else n
    kept = [
        struct((2, n, padded, width), BF16),
        struct((rows, width), F32),
        struct((width, width), BF16),
        struct((rows, width), BF16),
        struct((pairs, rows, LANES), BF16),
        struct((pairs, rows, LANES), BF16),
        struct((pairs, rows, LANES), BF16),
        struct((8, 8, rows), F32),
        struct((rows, LANES), F32),
        struct((rows, LANES), F32),
        struct((rows, width), BF16),
        struct((2, width, 3 * LANES), BF16),
        struct((2, width, 2 * LANES), BF16),
    ]
    results, input_grads, logits, grads, lines, *far_in = pl.pallas_call(
        functools.partial(rear_kernel, n, half, padded, gathered, part),
        out_shape=[struct((2, rows, width), BF16)] * 2
        + rear_outs
        + [struct(w_in.shape, BF16)] * len(chip_in),
        in_specs=[aspec()] * (len(chip_in) + 4 + len(kept)) + [vspec()] * 5,
        out_specs=[aspec()] * 2
        + [vspec()]
        + [aspec() if gathered else vspec()] * 2
        + [aspec()] * len(chip_in),
        scratch_shapes=[pltpu.VMEM(o.shape, o.dtype) for o in kept]
        + [
            pltpu.VMEM((half_rows, width), BF16),
            pltpu.VMEM((rows, width), BF16),
            pltpu.VMEM((rows, local), BF16),
            pltpu.VMEM((2, n, padded, width), BF16),
            pltpu.VMEM((half_rows, width), F32),
            pltpu.VMEM((rows, width), BF16),
            pltpu.VMEM((rows, local), BF16),
            pltpu.VMEM((rows, LANES), BF16),
            pltpu.VMEM((8, width), F32),
            pltpu.VMEM((2, rows, 5 * LANES), BF16),
            pltpu.VMEM((rows, LANES), F32),
            pltpu.VMEM((rows, LANES), F32),
            pltpu.VMEM((width, LANES), F32),
            pltpu.VMEM((2, width, groups), BF16),
            pltpu.VMEM((width, LANES), F32),
            pltpu.VMEM((2, spread_n, part, groups), BF16),
            pltpu.VMEM((2, spread_n, part, groups), BF16),
            pltpu.VMEM((line_n, part, LANES), F32),
            pltpu.VMEM((part, groups), BF16),
            pltpu.VMEM((part, groups), BF16),
            pltpu.VMEM((2, part, LANES), F32),
            pltpu.VMEM((half_rows, width), BF16),
            pltpu.VMEM((half_rows, width), BF16),
            pltpu.VMEM((half_rows, width), F32),
            pltpu.VMEM((8, width), F32),
            pltpu.VMEM((8, width), F32),
            pltpu.VMEM((2, half_rows, width), BF16),
            dma((3,)),
            dma((len(kept),)),
            dma((n,)),
            dma((n,)),
            dma((3,)),
            dma((n,)),
            dma((n,)),
            dma((4, 2, n // 2)),
            dma((4, 2, n // 2)),
            dma((n,)),
            dma((n,)),
            dma((5,)),
            dma((5,)),
            dma((2, 3)),
            dma((2, 3)),
            dma((1,)),
            dma((1,)),
        ],
        compiler_params=pltpu.CompilerParams(
            collective_id=1, has_side_effects=True, vmem_limit_bytes=VMEM_LIMIT
        ),
        cost_estimate=pl.CostEstimate(
            flops=100_000_000_000, bytes_accessed=60_000_000, transcendentals=0
        ),
    )(
        *chip_in,
        gy,
        tokens,
        cotangent,
        o_all,
        dx_all,
        h,
        wo_all,
        ub,
        q,
        k,
        v,
        lse,
        cosine,
        sine,
        a,
        spread,
        spread,
        stats,
        pos,
        small_all,
        extra,
        dg_all,
    )
    if not gathered:
        steps = 4

        def split(value, axis):
            block = list(value.shape)
            block[axis] //= steps

            def index(i):
                where = [0] * len(block)
                where[axis] = i
                return tuple(where)

            return pl.BlockSpec(tuple(block), index)

        def full(value):
            return pl.BlockSpec(value.shape, lambda i: (0,) * len(value.shape))

        large = [
            (results, 1),
            (input_grads, 1),
            (own_in, 2),
            (far_in[0], 2),
            (own_down, 1),
            (far_down, 1),
        ]
        tinies = [
            struct((columns, 2, rows), F32),
            struct((1, part), F32),
            struct((1, part), F32),
            struct((3, part, share), F32),
            struct((share, part), F32),
            struct((columns, part), F32),
            struct((4, part), F32),
            struct((2, part), F32),
        ]
        final = [large[0], large[1], large[2], large[4]]
        done = pl.pallas_call(
            functools.partial(last_kernel, part, columns),
            grid=(steps,),
            out_shape=[struct(v.shape, v.dtype) for v, _ in final] + tinies,
            in_specs=[split(v, axis) for v, axis in large]
            + [full(v) for v in (logits, grads, lines)],
            out_specs=[split(v, axis) for v, axis in final] + [full(v) for v in tinies],
            compiler_params=pltpu.CompilerParams(vmem_limit_bytes=VMEM_LIMIT),
        )(*(v for v, _ in large), logits, grads, lines)
        results, input_grads, grad_in, grad_down, logits = done[:5]
        gain_attn, gain_moe, heads, out, router, const, vec = done[5:]
        return (
            results,
            input_grads,
            jnp.transpose(logits, (1, 2, 0)),
            gain_attn[0],
            gain_moe[0],
            heads,
            out,
            router.T,
            const.T,
            vec,
            grad_in,
            grad_down,
        )
    grads = lax.psum_scatter(grads.astype(F32), "dp", scatter_dimension=1, tiled=True)
    lines = lax.psum_scatter(lines, "dp", scatter_dimension=0, tiled=True)
    other = lax.dynamic_index_in_dim(grads, 1 - m, 0, keepdims=False)
    grads = lax.dynamic_index_in_dim(grads, m, 0, keepdims=False) + across_chips(other)
    lines = lines + across_chips(lines)

    def heads(j):
        start = (4 + (j % 4) // 2) * LANES + (j % 2) * HD
        return jnp.concatenate(
            [grads[:, j * LANES : (j + 1) * LANES], grads[:, start : start + HD]], axis=1
        )

    return (
        results,
        input_grads,
        jnp.swapaxes(logits[:, :columns], 1, 2),
        lines[:, columns + 4],
        lines[:, columns + 5],
        jnp.stack([heads(i) for i in range(3)]),
        heads(3).T,
        lines[:, :columns],
        lines[:, columns : columns + 4],
        lines[:, columns + 6 : columns + 8].T,
        grad_in,
        grad_down,
    )


def solution(mesh):
    in_specs = (
        P(None, "dp", None),
        P(None, "dp", None),
        P(None, "dp", None),
        P(None, "dp", None),
        P("dp"),
        P("dp"),
        P(None, "dp", "tensor"),
        P("tensor", "dp"),
        P("dp", None),
        P("dp", None),
        P(None, "dp"),
        P("dp", None, None, "tensor"),
        P("dp", "tensor", None),
    )
    out_specs = (
        P(None, "dp", None),
        P(None, "dp", None),
        P(None, "dp", None),
        P("dp"),
        P("dp"),
        P(None, "dp", "tensor"),
        P("tensor", "dp"),
        P("dp", None),
        P("dp", None),
        P(None, "dp"),
        P("dp", None, None, "tensor"),
        P("dp", "tensor", None),
    )
    return jax.shard_map(body, mesh=mesh, in_specs=in_specs, out_specs=out_specs, check_vma=False)
```

```python
import functools

import jax
import jax.numpy as jnp
import numpy as np
from jax import lax
from jax.experimental import pallas as pl
from jax.experimental.pallas import tpu as pltpu
from jax.sharding import PartitionSpec as P

HD = 64
LEN = 1024
BLK = 256
EPSILON = 1e-06
LANES = 128
F32 = jnp.float32
BF16 = jnp.bfloat16
MESH = pl.DeviceIdType.MESH
VMEM_LIMIT = 60 * 1024 * 1024


def mm(a, b):
    return lax.dot_general(a, b, (((1,), (0,)), ((), ())), preferred_element_type=F32)


def mm_nt(a, b):
    return lax.dot_general(a, b, (((1,), (1,)), ((), ())), preferred_element_type=F32)


def mm_tn(a, b):
    return lax.dot_general(a, b, (((0,), (0,)), ((), ())), preferred_element_type=F32)


def vspec():
    return pl.BlockSpec(memory_space=pltpu.VMEM)


def aspec():
    return pl.BlockSpec(memory_space=pl.ANY)


def struct(shape, dtype):
    return jax.ShapeDtypeStruct(shape, dtype)


def greet(peers):
    barrier = pltpu.get_barrier_semaphore()
    for peer in peers:
        pl.semaphore_signal(barrier, inc=1, device_id=peer, device_id_type=MESH)
    pl.semaphore_wait(barrier, len(peers))


def remote(src, dst, send, recv, peer):
    return pltpu.make_async_remote_copy(
        src_ref=src,
        dst_ref=dst,
        send_sem=send,
        recv_sem=recv,
        device_id=peer,
        device_id_type=MESH,
    )


def plane_peers(n, d, t):
    return [(lax.rem(d + j, n), t) for j in range(1, n)]


def slot_hot(half, padded, base, places):
    rows = places.shape[1]
    slot = lax.broadcasted_iota(jnp.int32, (padded, rows), 0)
    wanted = jnp.where(slot < half, slot + base, -2).astype(F32)
    return (wanted == places).astype(F32).astype(BF16)


def rope_constants():
    half = HD // 2
    frequency = 10000.0 ** (-2.0 * np.arange(half) / HD)
    angle = np.arange(LEN)[:, None] * frequency[None, :]
    cosine, sine = np.cos(angle), np.sin(angle)
    cosine = np.concatenate([cosine, cosine, cosine, cosine], axis=1)
    sine = np.concatenate([-sine, sine, -sine, sine], axis=1)
    return cosine.astype(np.float32), sine.astype(np.float32)


def turn(field, cosine, sine):
    lane = lax.broadcasted_iota(jnp.int32, field.shape, 1)
    other = jnp.where(
        lax.rem(lane, HD) < HD // 2,
        pltpu.roll(field, LANES - HD // 2, 1),
        pltpu.roll(field, HD // 2, 1),
    )
    return field * cosine + other * sine


def pick(hot, values):
    return jnp.sum(jnp.where(hot, values, 0.0), axis=-1, keepdims=True)


def lane_ids(rows):
    return lax.broadcasted_iota(jnp.int32, (rows, LANES), 1)


def soft_pair(first, second):
    high = jnp.maximum(first, second)
    e0, e1 = jnp.exp(first - high), jnp.exp(second - high)
    return e0 / (e0 + e1), e1 / (e0 + e1)


def half_mask(rows):
    return lax.broadcasted_iota(jnp.int32, (rows, LANES), 1) < HD


def swap_halves(value):
    return pltpu.roll(value, HD, 1)


def front_kernel(
    n,
    half,
    padded,
    gathered,
    early,
    tokens_ref,
    cotangent_ref,
    routes_all_ref,
    prev_all_ref,
    heads_ref,
    out_ref,
    cos_ref,
    sin_ref,
    win_ref,
    *refs,
):
    tiny_refs, refs = refs[: 1 if gathered else 5], refs[1 if gathered else 5 :]
    slot_ref, gate_ref, extra_ref = refs[:3]
    stored = refs[3 : 3 + early]
    dy_arrived_ref, in_x_ref = refs[3 + early : 5 + early]
    refs = refs[5 + early :]
    kept, refs = refs[:early], refs[early:]
    a_ref, q_ref, k_ref, v_ref, o_ref, lse_ref, pos_ref, wo_ref, small_ref, spread_ref = kept[:10]
    h_ref, ub_ref, stat_ref = kept[10:]
    x_ref, dy_ref, routes_ref, place_ref, gates_ref, dy_slot_ref = refs[:6]
    refs = refs[6:]
    load, pack_send, pack_recv, dy_send, dy_recv, stay = refs[:6]
    core_send, core_recv, w_send, w_recv, store_sem = refs[6:]

    def store(*which):
        for i in which:
            pltpu.make_async_copy(kept[i], stored[i], store_sem.at[i]).start()

    rows_all, width = x_ref.shape
    blocks = rows_all // BLK
    pairs = q_ref.shape[0]
    local = pairs * LANES
    columns = prev_all_ref.shape[0]
    d, t = lax.axis_index("dp"), lax.axis_index("tensor")
    m, c = lax.div(t, 2), lax.rem(t, 2)
    partner = (d, t + 1 - 2 * c)
    across = (d, lax.rem(t + 2, 4))
    loads = [
        pltpu.make_async_copy(src.at[m], dst, load.at[i])
        for i, (src, dst) in enumerate(
            [
                (routes_all_ref, routes_ref),
                (cotangent_ref, dy_ref),
                (tokens_ref, x_ref),
            ]
        )
    ]
    for copy in loads:
        copy.start()
    greet(plane_peers(n, d, t) + [partner, across])
    part = heads_ref.shape[1]

    def pack():
        side = lax.broadcasted_iota(jnp.int32, (part, part), 0)
        eye = jnp.where(side == lax.broadcasted_iota(jnp.int32, (part, part), 1), 1.0, 0.0)
        eye = eye.astype(BF16)
        wo = mm_nt(eye, out_ref[...])
        tiny = [ref[...].astype(F32) for ref in tiny_refs]
        tiny.append(jnp.zeros((LANES - columns - 8, part), F32))
        tiny = mm_nt(eye, jnp.concatenate(tiny, axis=0).astype(BF16))
        wide = [heads_ref[i].astype(F32) for i in range(3)] + [wo]
        firsts = [value[:, :LANES] for value in wide]
        odds = [
            jnp.concatenate([wide[i][:, LANES:], wide[i + 1][:, LANES:]], axis=1) for i in (0, 2)
        ]
        return jnp.concatenate(firsts + odds + [tiny], axis=1).astype(BF16)

    beside = (d + 1 - 2 * lax.rem(d, 2), t)
    lanes_a = pl.ds(0, 3 * LANES)
    lanes_b = pl.ds(3 * LANES, 4 * LANES)

    def behind(j):
        return lax.rem(d + n - 2 * j, n)

    def shard(chip, owner, lanes):
        return spread_ref.at[chip, pl.ds(pl.multiple_of(owner * part, part), part), lanes]

    def pass_on(chip, owner, lanes, row, j, peer):
        block = shard(chip, owner, lanes)
        return remote(block, block, pack_send.at[row, j], pack_recv.at[row, j], peer)

    def ahead(j):
        return (lax.rem(d + 2 * j, n), t)

    ring = n // 2
    if gathered:
        spread_ref[...] = tiny_refs[0][...]
    else:
        spread_ref[m, pl.ds(pl.multiple_of(d * part, part), part), :] = pack()
        a_x = pass_on(m, d, lanes_a, 4, 0, across)
        sends = [a_x]
        for j in range(1, ring):
            sends.append(pass_on(m, d, lanes_a, 0, j, ahead(j)))
            sends.append(pass_on(m, d, lanes_b, 4, j, ahead(j)))
        sends.append(pass_on(m, d, lanes_a, 2, 0, beside))
        sends.append(pass_on(m, d, lanes_b, 5, 0, beside))
        sends.append(pass_on(m, d, lanes_b, 6, 0, across))
        for copy in sends:
            copy.start()

    def relay_gather(after_z, after_x):
        if gathered:
            after_z()
            after_x()
            return
        a_x.wait_recv()
        more = [pass_on(1 - m, d, lanes_a, 1, j, ahead(j)) for j in range(1, ring)]
        more.append(pass_on(1 - m, d, lanes_a, 3, 0, beside))
        for copy in more:
            copy.start()
        sends.extend(more)
        for j in range(1, ring):
            pass_on(m, d, lanes_b, 4, j, ahead(j)).wait_recv()
            more = [
                pass_on(m, behind(j), lanes_b, 5, j, beside),
                pass_on(m, behind(j), lanes_b, 6, j, across),
            ]
            pass_on(m, d, lanes_a, 0, j, ahead(j)).wait_recv()
            more.append(pass_on(m, behind(j), lanes_a, 2, j, beside))
            for copy in more:
                copy.start()
            sends.extend(more)
        for j in range(1, ring):
            pass_on(1 - m, d, lanes_a, 1, j, ahead(j)).wait_recv()
            copy = pass_on(1 - m, behind(j), lanes_a, 3, j, beside)
            copy.start()
            sends.append(copy)
        after_z()
        for j in range(ring):
            pass_on(m, d, lanes_b, 5, j, beside).wait_recv()
            owner = lax.rem(beside[0] + n - 2 * j, n)
            copy = pass_on(m, owner, lanes_b, 7, j, across)
            copy.start()
            sends.append(copy)
        after_x()
        for j in range(ring):
            pass_on(m, d, lanes_a, 2, j, beside).wait_recv()
            pass_on(m, d, lanes_a, 3, j, beside).wait_recv()
            pass_on(m, d, lanes_b, 6, j, across).wait_recv()
            pass_on(m, d, lanes_b, 7, j, across).wait_recv()

    loads[0].wait()
    named = routes_ref[...].astype(F32)
    ids = lax.broadcasted_iota(jnp.int32, (LANES, rows_all), 0).astype(F32)
    hit = ((ids == named[0:1, :]) | (ids == named[1:2, :])) & (ids < float(n))
    before = lax.broadcasted_iota(jnp.int32, (rows_all, rows_all), 0) < lax.broadcasted_iota(
        jnp.int32, (rows_all, rows_all), 1
    )
    count = mm(hit.astype(F32).astype(BF16), before.astype(F32).astype(BF16))
    places = jnp.where(hit, count, -1.0)
    place_ref[...] = places
    pos_ref[...] = jnp.transpose(places)
    store(6)
    base = c * half

    def dy_copy(j):
        e = lax.rem(d + j, n)
        return remote(
            dy_slot_ref.at[e], dy_arrived_ref.at[d], dy_send.at[j], dy_recv.at[j], (e, t)
        )

    stays = [pltpu.make_async_copy(dy_slot_ref.at[d], dy_arrived_ref.at[d], stay.at[0])]
    loads[1].wait()

    def two_hot(i):
        return jnp.concatenate(
            [
                slot_hot(half, padded, base, place_ref[pl.ds(2 * i + side, 1), :])
                for side in range(2)
            ],
            axis=0,
        )

    def dy_step(i, carry):
        rows = mm(two_hot(i), dy_ref[...]).astype(BF16)
        for side in range(2):
            dy_slot_ref[2 * i + side] = rows[side * padded : (side + 1) * padded]
        return carry

    lax.fori_loop(0, n // 2, dy_step, 0)
    weight_copies = []
    if not gathered:
        weight_copies.append(remote(win_ref, in_x_ref, w_send.at[0], w_recv.at[0], across))

    def dy_start(j, carry):
        dy_copy(j).start()
        return carry

    relay_gather(
        lambda: lax.fori_loop(1, n, dy_start, 0), lambda: [c.start() for c in weight_copies]
    )
    stays[0].start()
    store(9)

    table = spread_ref[0, :, 6 * LANES : 7 * LANES]
    extra_ref[...] = jnp.transpose(table.astype(F32))
    keep = lax.broadcasted_iota(jnp.int32, (width, LANES), 1) < columns + 4
    small_ref[...] = jnp.where(keep, table, jnp.zeros_like(table))
    mask = half_mask(width)
    own = pl.multiple_of(c * local, LANES)
    wo_ref[:, pl.ds(own, LANES)] = spread_ref[0, :, 3 * LANES : 4 * LANES]
    wo_ref[:, pl.ds(own + LANES, LANES)] = spread_ref[1, :, 3 * LANES : 4 * LANES]
    wo_ref[:, pl.ds(own + 2 * LANES, LANES)] = jnp.where(
        mask,
        swap_halves(spread_ref[0, :, 5 * LANES : 6 * LANES].astype(F32)),
        spread_ref[1, :, 5 * LANES : 6 * LANES].astype(F32),
    ).astype(BF16)
    own_lanes = pl.ds(own, local)
    wo_copy = remote(
        wo_ref.at[:, own_lanes],
        wo_ref.at[:, own_lanes],
        core_send.at[pairs],
        core_recv.at[pairs],
        partner,
    )
    wo_copy.start()
    store(8)

    loads[2].wait()
    gain = extra_ref[columns + 4 : columns + 5, :]
    head = half_mask(BLK)

    def project(i, carry):
        rows = pl.ds(pl.multiple_of(i * BLK, BLK), BLK)
        x = x_ref[rows, :].astype(F32)
        r = lax.rsqrt(jnp.mean(x * x, axis=-1, keepdims=True) + EPSILON)
        a = (x * r * gain).astype(BF16)
        a_ref[rows, :] = a
        cosine, sine = cos_ref[rows, :], sin_ref[rows, :]

        def put(pair, q, k, v):
            q_ref[pair, rows, :] = turn(q, cosine, sine).astype(BF16) * BF16(HD**-0.5)
            k_ref[pair, rows, :] = turn(k, cosine, sine).astype(BF16)
            v_ref[pair, rows, :] = v.astype(BF16)

        odd = []
        for s in range(2):
            both = mm(a, spread_ref[s, :, 0 : 3 * LANES])
            put(s, *(both[:, j * LANES : (j + 1) * LANES] for j in range(3)))
            both = mm(a, spread_ref[s, :, 4 * LANES : 6 * LANES])
            odd.append((both[:, :LANES], both[:, LANES:]))
        put(
            2,
            jnp.where(head, odd[0][0], swap_halves(odd[1][0])),
            jnp.where(head, swap_halves(odd[0][0]), odd[1][0]),
            jnp.where(head, odd[0][1], swap_halves(odd[1][1])),
        )
        return carry

    lax.fori_loop(0, blocks, project, 0)
    store(0, 1, 2, 3)

    def o_copy(p):
        lanes = pl.ds(pl.multiple_of(own + p * LANES, LANES), LANES)
        return remote(
            o_ref.at[:, lanes], o_ref.at[:, lanes], core_send.at[p], core_recv.at[p], partner
        )

    def attend(p, carry):
        lanes = pl.ds(pl.multiple_of(own + p * LANES, LANES), LANES)
        for i in range(blocks):
            rows = pl.ds(i * BLK, BLK)
            seen = pl.ds(0, (i + 1) * BLK)
            q, k, v = q_ref[p, rows, :], k_ref[p, seen, :], v_ref[p, seen, :]
            halves = []
            for side in range(2):
                chosen = head if side == 0 else jnp.logical_not(head)
                s = mm_nt(jnp.where(chosen, q, jnp.zeros_like(q)), k)
                high = jnp.max(s, axis=-1, keepdims=True)
                e = jnp.exp(s - high)
                total = jnp.sum(e, axis=-1, keepdims=True)
                halves.append(mm(e.astype(BF16), v) * (1.0 / total))
                log_total = jnp.broadcast_to(high + jnp.log(total), (BLK, LANES))
                lse_ref[2 * p + side, :, rows] = jnp.transpose(log_total)[0:8, :]
            o_ref[rows, lanes] = jnp.where(head, halves[0], halves[1]).astype(BF16)
        o_copy(p).start()
        return carry

    lax.fori_loop(0, pairs, attend, 0)
    wo_copy.wait()
    for p in range(pairs):
        o_copy(p).wait()
    store(4, 5, 7)
    prev_lines = jnp.where(m == 0, prev_all_ref[:, 0, :], prev_all_ref[:, 1, :])
    spare = jnp.zeros((LANES - columns - 2, rows_all), F32)
    facts = jnp.concatenate([prev_lines, routes_ref[...].astype(F32), spare], axis=0)
    gates_ref[...] = facts

    gain_moe = extra_ref[columns + 5 : columns + 6, :]

    def middle(i, carry):
        rows = pl.ds(pl.multiple_of(i * BLK, BLK), BLK)
        z = mm_nt(o_ref[rows, :], wo_ref[...])
        h = x_ref[rows, :].astype(F32) + z
        r = lax.rsqrt(jnp.mean(h * h, axis=-1, keepdims=True) + EPSILON)
        ub = (h * r * gain_moe).astype(BF16)
        h_ref[rows, :] = h
        ub_ref[rows, :] = ub
        scores = mm(ub, small_ref[...])
        lane = lane_ids(BLK)
        facts = jnp.transpose(gates_ref[:, rows])
        e0 = facts[:, columns : columns + 1]
        e1 = facts[:, columns + 1 : columns + 2]
        hot0, hot1 = lane.astype(F32) == e0, lane.astype(F32) == e1
        logits = scores + facts
        g0, g1 = soft_pair(pick(hot0, logits), pick(hot1, logits))
        mix = [pick(lane == columns + j, scores) for j in range(4)]
        a00, a01 = soft_pair(mix[0], mix[1])
        a10, a11 = soft_pair(mix[2], mix[3])
        table = jnp.zeros((BLK, LANES), F32)
        for j, value in enumerate([g0, g1, a00, a01, a10, a11, r, e0, e1]):
            table = jnp.where(lane == j, value, table)
        stat_ref[rows, :] = table
        gates = jnp.where(hot0, g0, 0.0) + jnp.where(hot1, g1, 0.0)
        gates_ref[:, rows] = jnp.transpose(gates)
        return carry

    lax.fori_loop(0, blocks, middle, 0)
    store(10, 11, 12)
    piece = lax.broadcasted_iota(jnp.int32, (8, rows_all), 0)

    def slot_step(i, carry):
        hot = two_hot(i)
        rows = mm(hot, ub_ref[...]).astype(BF16)
        for side in range(2):
            e = 2 * i + side
            slot_ref[e] = rows[side * padded : (side + 1) * padded]
            gate = gates_ref[pl.ds(e, 1), :]
            high = gate.astype(BF16).astype(F32)
            mid = (gate - high).astype(BF16).astype(F32)
            low = gate - high - mid
            lines = jnp.where(piece == 0, high, jnp.where(piece == 1, mid, low))
            lines = jnp.where(piece < 3, lines, 0.0).astype(BF16)
            gate = mm_nt(lines, hot[side * padded : (side + 1) * padded])
            gate = jnp.sum(gate, axis=0, keepdims=True)
            gate_ref[e] = jnp.broadcast_to(gate, (8, padded))
        return carry

    lax.fori_loop(0, n // 2, slot_step, 0)
    def finish(j, carry):
        dy_copy(j).wait()
        return carry

    lax.fori_loop(1, n, finish, 0)
    for copy in stays:
        copy.wait()
    for copy in [] if gathered else sends:
        copy.wait_send()
    for copy in weight_copies:
        copy.wait()
    for i in range(early):
        pltpu.make_async_copy(kept[i], stored[i], store_sem.at[i]).wait()


def flip(value, index, size):
    bit = 1
    while bit < size:
        chosen = lax.rem(lax.div(index, bit), 2)
        value = value + chosen * (bit - 2 * bit * lax.rem(lax.div(value, bit), 2))
        bit *= 2
    return value


def expert_exchange_kernel(
    n,
    padded,
    slot_src_ref,
    gate_src_ref,
    dy_src_ref,
    in_own_ref,
    in_chip_ref,
    down_own_ref,
    gy_out_ref,
    own_in_out_ref,
    own_down_out_ref,
    chip_in_out_ref,
    far_down_ref,
    dx_all_ref,
    dg_all_ref,
    gy_ref,
    own_in_ref,
    own_down_ref,
    chip_in_ref,
    x_ref,
    xt_ref,
    dy_ref,
    scaled_ref,
    scale_ref,
    gate_ref,
    win_ref,
    wdown_ref,
    hidden_ref,
    dgate_ref,
    dup_ref,
    y_ref,
    dx_ref,
    dg_ref,
    land_in_ref,
    land_down_ref,
    chip_down_ref,
    load,
    slot_send,
    slot_recv,
    gate_send,
    gate_recv,
    dx_send,
    dx_recv,
    dg_send,
    dg_recv,
    pass_send,
    pass_recv,
    sum_send,
    sum_recv,
    w_send,
    w_recv,
    store_sem,
):
    width = x_ref.shape[1]
    share = win_ref.shape[3]
    chunks = 4
    group = n // chunks
    span = group * padded
    block = 256
    d, t = lax.axis_index("dp"), lax.axis_index("tensor")
    c = lax.rem(t, 2)
    partner = (d, t + 1 - 2 * c)
    across = (d, lax.rem(t + 2, 4))
    stores = [
        pltpu.make_async_copy(src, dst, store_sem.at[i])
        for i, (src, dst) in enumerate(
            [
                (gy_ref, gy_out_ref),
                (chip_in_ref, chip_in_out_ref),
                (own_in_ref, own_in_out_ref),
                (own_down_ref, own_down_out_ref),
            ]
        )
    ]
    greet(plane_peers(n, d, t) + [partner, across])

    def rows_of(i):
        return pl.ds(pl.multiple_of(i * padded, padded), padded)

    def slot_copy(i):
        e = flip(d, i, n)
        return remote(
            slot_src_ref.at[e], x_ref.at[rows_of(i)], slot_send.at[i], slot_recv.at[i], (e, t)
        )

    def gate_copy(i):
        e = flip(d, i, n)
        return remote(
            gate_src_ref.at[e], gate_ref.at[i], gate_send.at[i], gate_recv.at[i], (e, t)
        )

    def dx_copy(i):
        e = flip(d, i, n)
        return remote(
            dx_ref.at[rows_of(i)], dx_all_ref.at[c, d], dx_send.at[i], dx_recv.at[i], (e, t)
        )

    def dg_copy(i):
        e = flip(d, i, n)
        return remote(dg_ref.at[i], dg_all_ref.at[c, d], dg_send.at[i], dg_recv.at[i], (e, t))

    def hand(kind, i):
        ref = (dx_all_ref, dg_all_ref)[kind]
        block_ref = ref.at[c, flip(d, i, n)]
        return remote(
            block_ref, block_ref, pass_send.at[kind, i], pass_recv.at[kind, i], partner
        )

    def down_rows(s):
        return pl.ds(s * share, share)

    def send_chunk(k):
        for q in range(group):
            if k + q > 0:
                slot_copy(k * group + q).start()
                gate_copy(k * group + q).start()

    send_chunk(2)
    send_chunk(1)
    if group > 1:
        send_chunk(0)
    stays = [
        pltpu.make_async_copy(slot_src_ref.at[d], x_ref.at[rows_of(0)], load.at[0]),
        pltpu.make_async_copy(gate_src_ref.at[d], gate_ref.at[0], load.at[1]),
    ]
    own_loads = [
        pltpu.make_async_copy(in_own_ref.at[0], win_ref.at[0], load.at[2]),
        pltpu.make_async_copy(down_own_ref.at[0], wdown_ref.at[down_rows(0)], load.at[3]),
    ]
    chip_load = pltpu.make_async_copy(in_chip_ref.at[0], win_ref.at[2], load.at[4])
    weights = [
        remote(in_own_ref.at[0], win_ref.at[1], w_send.at[0], w_recv.at[0], partner),
        remote(
            down_own_ref.at[0], wdown_ref.at[down_rows(1)], w_send.at[1], w_recv.at[1], partner
        ),
        remote(in_chip_ref.at[0], win_ref.at[3], w_send.at[2], w_recv.at[2], partner),
        remote(
            down_own_ref.at[0], wdown_ref.at[down_rows(2)], w_send.at[3], w_recv.at[3], across
        ),
        remote(
            wdown_ref.at[down_rows(2)],
            wdown_ref.at[down_rows(3)],
            w_send.at[4],
            w_recv.at[4],
            partner,
        ),
    ]

    def dy_load(i):
        return pltpu.make_async_copy(
            dy_src_ref.at[flip(d, i, n)], dy_ref.at[rows_of(i)], load.at[10 + i]
        )

    for copy in [weights[3]] + stays + own_loads:
        copy.start()
    for i in range(n):
        dy_load(i).start()
    chip_load.start()
    for copy in weights[0:3]:
        copy.start()
    for copy in stays + own_loads:
        copy.wait()

    def take(k):
        rows = pl.ds(k * span, span)
        for q in range(group):
            i = k * group + q
            if i > 0:
                slot_copy(i).wait_recv()
                gate_copy(i).wait_recv()
            dy_load(i).wait()
            near = rows_of(i)
            line = jnp.broadcast_to(gate_ref[i, 0:1, :], (LANES, padded))
            scale = jnp.transpose(line)
            scale_ref[near, :] = scale
            scaled_ref[near, :] = (dy_ref[near, :].astype(F32) * scale[:, 0:1]).astype(BF16)
        xt_ref[:, rows] = jnp.transpose(x_ref[rows, :])

    per = share // block

    def units(first, last, chosen):
        def unit(u, carry):
            k = first + lax.div(u, 2 * per)
            b = lax.rem(u, 2 * per)
            s = chosen * 2 + lax.div(b, per)
            rows = pl.ds(pl.multiple_of(k * span, span), span)
            lanes = pl.ds(pl.multiple_of(lax.rem(b, per) * block, block), block)
            far = pl.ds(pl.multiple_of((chosen * 2 * per + b) * block, block), block)
            x = x_ref[rows, :]
            gate = mm(x, win_ref[s, 0, :, lanes])
            up = mm(x, win_ref[s, 1, :, lanes])
            grad = mm_nt(scaled_ref[rows, :], wdown_ref[far, :])
            sigma = 0.5 * jnp.tanh(0.5 * gate) + 0.5
            active = gate * sigma
            hidden_ref[rows, far] = (active * up).astype(BF16)
            dgate_ref[rows, far] = (grad * up * (sigma * (1.0 + gate * (1.0 - sigma)))).astype(
                BF16
            )
            dup_ref[rows, far] = (grad * active).astype(BF16)
            return carry

        lax.fori_loop(0, (last - first) * 2 * per, unit, 0)

    def close(k, carry):
        rows = pl.ds(pl.multiple_of(k * span, span), span)
        for j in range(width // block):
            lanes = pl.ds(j * block, block)
            total = jnp.zeros((span, block), F32)
            for s in range(4):
                far = pl.ds(s * share, share)
                total = total + mm_nt(dgate_ref[rows, far], win_ref[s, 0, lanes, :])
                total = total + mm_nt(dup_ref[rows, far], win_ref[s, 1, lanes, :])
            dx_ref[rows, lanes] = total.astype(BF16)
        for q in range(group):
            i = k * group + q

            @pl.when(i > 0)
            def _():
                dx_copy(i).start()

        for j in range(width // block):
            lanes = pl.ds(j * block, block)
            y_ref[:, lanes] = mm(hidden_ref[rows, :], wdown_ref[:, lanes])
        for q in range(group):
            i = k * group + q
            near = rows_of(i)
            y = y_ref[pl.ds(q * padded, padded), :]
            gy_ref[flip(d, i, n)] = (y * scale_ref[near, 0:1]).astype(BF16)
            dot = jnp.sum(y * dy_ref[near, :].astype(F32), axis=-1, keepdims=True)
            dg_ref[i] = jnp.transpose(jnp.broadcast_to(dot, (padded, LANES)))[0:8, :]

            @pl.when(i > 0)
            def _():
                dg_copy(i).start()

        return carry

    take(0)
    for copy in weights[0:2]:
        copy.wait_recv()
    units(0, 1, 0)
    take(1)
    units(1, 2, 0)
    take(2)
    send_chunk(3)
    units(2, 3, 0)
    chip_load.wait()
    weights[3].wait_recv()
    weights[4].start()
    weights[2].wait_recv()
    weights[4].wait_recv()
    units(0, 3, 1)
    lax.fori_loop(2, 3, close, 0)
    lax.fori_loop(0, 2, close, 0)
    take(3)
    units(3, 4, 0)
    units(3, 4, 1)
    lax.fori_loop(3, 4, close, 0)
    stores[0].start()
    keeps = [
        pltpu.make_async_copy(dx_ref.at[rows_of(0)], dx_all_ref.at[c, d], load.at[0]),
        pltpu.make_async_copy(dg_ref.at[0], dg_all_ref.at[c, d], load.at[1]),
    ]
    for copy in keeps:
        copy.start()

    def forward(first, last):
        def step(i, carry):
            dx_copy(i).wait_recv()
            dg_copy(i).wait_recv()
            hand(0, i).start()
            hand(1, i).start()
            return carry

        lax.fori_loop(first, last, step, 0)

    def grad_in(s, kind, b):
        far = pl.ds(pl.multiple_of(s * share + b * block, block), block)
        return mm(xt_ref[...], (dgate_ref, dup_ref)[kind][:, far])

    def grad_down(s, b):
        far = pl.ds(pl.multiple_of(s * share + b * block, block), block)
        return mm_tn(hidden_ref[:, far], scaled_ref[...])

    def sum_copies(j):
        return [
            remote(win_ref.at[j], land_in_ref.at[j], sum_send.at[j], sum_recv.at[j], partner),
            remote(
                wdown_ref.at[pl.ds(j * share, share)],
                land_down_ref.at[j],
                sum_send.at[2 + j],
                sum_recv.at[2 + j],
                partner,
            ),
        ]

    for copy in weights:
        copy.wait_send()

    def down_sums(s, put):
        def unit(b, carry):
            put(pl.ds(pl.multiple_of(b * block, block), block), grad_down(s, b))
            return carry

        lax.fori_loop(0, per, unit, 0)

    def in_sums(s, put):
        def unit(b, carry):
            lanes = pl.ds(pl.multiple_of(b * block, block), block)
            for kind in range(2):
                put(kind, lanes, grad_in(s, kind, b))
            return carry

        lax.fori_loop(0, per, unit, 0)

    def leave_down(j, s):
        def put(rows, value):
            near = pl.multiple_of(rows.start + j * share, block)
            wdown_ref[pl.ds(near, block), :] = value.astype(BF16)

        down_sums(s, put)
        sum_copies(j)[1].start()

    def leave_in(j, s):
        def put(kind, lanes, value):
            win_ref[j, kind, :, lanes] = value.astype(BF16)

        in_sums(s, put)
        sum_copies(j)[0].start()

    leave_down(0, 3)
    leave_down(1, 1)
    sum_copies(0)[1].wait_recv()

    def chip_down(lanes, value):
        chip_down_ref[0, lanes, :] = (value + land_down_ref[0, lanes, :].astype(F32)).astype(BF16)

    down_sums(2, chip_down)
    far_copy = remote(chip_down_ref, far_down_ref, w_send.at[5], w_recv.at[5], across)
    far_copy.start()
    for copy in keeps:
        copy.wait()
    hand(0, 0).start()
    hand(1, 0).start()
    forward(1, 2 * group)
    leave_in(0, 3)
    leave_in(1, 1)
    sum_copies(0)[0].wait_recv()

    def chip_in(kind, lanes, value):
        chip_in_ref[0, kind, :, lanes] = (
            value + land_in_ref[0, kind, :, lanes].astype(F32)
        ).astype(BF16)

    in_sums(2, chip_in)
    stores[1].start()
    for copy in sum_copies(1):
        copy.wait_recv()

    def own_in(kind, lanes, value):
        own_in_ref[0, kind, :, lanes] = value + land_in_ref[1, kind, :, lanes].astype(F32)

    def own_down(lanes, value):
        own_down_ref[0, lanes, :] = value + land_down_ref[1, lanes, :].astype(F32)

    in_sums(0, own_in)
    stores[2].start()
    down_sums(0, own_down)
    stores[3].start()
    forward(2 * group, n)

    def clear(i, carry):
        for copy in (slot_copy(i), gate_copy(i), dx_copy(i), dg_copy(i)):
            copy.wait_send()
        return carry

    lax.fori_loop(1, n, clear, 0)

    def passed(i, carry):
        hand(0, i).wait()
        hand(1, i).wait()
        return carry

    lax.fori_loop(0, n, passed, 0)
    for j in range(2):
        for copy in sum_copies(j):
            copy.wait_send()
    far_copy.wait()
    for copy in stores:
        copy.wait()


def expert_kernel(
    sources,
    padded,
    x_ref,
    dy_ref,
    gate_ref,
    *refs,
):
    weights, outs = refs[:8], refs[8:19]
    in_refs, down_refs = weights[0:4], weights[4:8]
    gy_ref, dx_ref, dg_ref = outs[0:3]
    gin_refs, gdown_refs = outs[3:7], outs[7:11]
    xt_ref, scaled_ref, scale_ref, y_acc, dx_acc, win_ref, wdown_ref = refs[19:]
    step = pl.program_id(0)
    last = pl.num_programs(0) - 1

    @pl.when(step == 0)
    def _():
        xt_ref[...] = jnp.transpose(x_ref[...])
        for s in range(sources):
            rows = pl.ds(s * padded, padded)
            line = jnp.broadcast_to(gate_ref[s, 0:1, :], (LANES, padded))
            scale = jnp.transpose(line)
            scale_ref[rows, :] = scale
            scaled_ref[rows, :] = (dy_ref[rows, :].astype(F32) * scale[:, 0:1]).astype(BF16)
        y_acc[...] = jnp.zeros_like(y_acc)
        dx_acc[...] = jnp.zeros_like(dx_acc)

    per = pl.num_programs(0) // 4
    for i in range(4):

        @pl.when(lax.div(step, per) == i)
        def _():
            win_ref[...] = in_refs[i][0]
            wdown_ref[...] = down_refs[i][0]

    x = x_ref[...]
    gate = mm(x, win_ref[0])
    up = mm(x, win_ref[1])
    sigma = 1.0 / (1.0 + jnp.exp(-gate))
    active = gate * sigma
    hidden = (active * up).astype(BF16)
    y_acc[...] += mm(hidden, wdown_ref[...])
    scaled = scaled_ref[...]
    grad_hidden = mm_nt(scaled, wdown_ref[...])
    grad_gate = (grad_hidden * up * (sigma * (1.0 + gate * (1.0 - sigma)))).astype(BF16)
    grad_up = (grad_hidden * active).astype(BF16)
    dx_acc[...] += mm_nt(grad_gate, win_ref[0]) + mm_nt(grad_up, win_ref[1])
    xt = xt_ref[...]
    part_gate = mm(xt, grad_gate).astype(BF16)
    part_up = mm(xt, grad_up).astype(BF16)
    part_down = mm_tn(hidden, scaled).astype(BF16)
    for i in range(4):

        @pl.when(lax.div(step, per) == i)
        def _():
            gin_refs[i][0, 0] = part_gate
            gin_refs[i][0, 1] = part_up
            gdown_refs[i][0] = part_down

    @pl.when(step == last)
    def _():
        for s in range(sources):
            rows = pl.ds(s * padded, padded)
            y = y_acc[rows, :]
            gy_ref[s] = (y * scale_ref[rows, 0:1]).astype(BF16)
            dot = jnp.sum(y * dy_ref[rows, :].astype(F32), axis=-1, keepdims=True)
            dg_ref[s] = jnp.transpose(jnp.broadcast_to(dot, (padded, LANES)))[0:8, :]
            dx_ref[s] = dx_acc[rows, :].astype(BF16)


def rear_kernel(n, half, padded, gathered, part, *refs):
    crossing = 0 if gathered else 1
    chip_in_refs, refs = refs[:crossing], refs[crossing:]
    gy_src_ref, tokens_ref, cotangent_ref, o_all_ref = refs[:4]
    loaded, refs = refs[4:17], refs[17:]
    stat_ref, pos_ref, small_ref, extra_ref, dg_ref = refs[:5]
    result_ref, grad_x_ref, logit_ref, grads_ref, lines_ref, norm_out_ref = refs[5:11]
    far_in_refs, refs = refs[11 : 11 + crossing], refs[11 + crossing :]
    kept, refs = refs[:13], refs[13:]
    dx_ref, h_ref, wo_ref, ub_ref, q_ref, k_ref, v_ref = kept[:7]
    lse_ref, cos_ref, sin_ref, a_ref, spread_a_ref, spread_b_ref = kept[7:]
    x_ref, dy_ref, o_ref, gy_ref, dh_ref, dzb_ref, do_ref, low_ref, row_ref = refs[:9]
    dp_ref, dk_acc, dv_acc, wo_odd_ref, pack_ref, line_ref, y_in_ref, z_in_ref = refs[9:17]
    line_in_ref, cross_ref, cross_in_ref, cross_line_ref = refs[17:21]
    da_out_ref, da_in_ref, da_own_ref, norm_ref, norm_in_ref, half_ref = refs[21:27]
    norm_line_ref, norm_all_ref, norm_cross_ref = refs[27:30]
    load, fetch_sem, gy_send, gy_recv, stay, pass_send, pass_recv = refs[30:37]
    grad_send, grad_recv, line_send, line_recv, pair_send, pair_recv = refs[37:43]
    out_send, out_recv, sum_send, sum_recv, norm_send, norm_recv = refs[43:]

    def fetch(i):
        src = loaded[i]
        if i == 11:
            src = src.at[:, :, pl.ds(0, 3 * LANES)]
        if i == 12:
            src = src.at[:, :, pl.ds(4 * LANES, 2 * LANES)]
        return pltpu.make_async_copy(src, kept[i], fetch_sem.at[i])

    rows_all, width = dy_ref.shape
    blocks = rows_all // BLK
    pairs = q_ref.shape[0]
    local = pairs * LANES
    columns = n + 4
    slots = n * padded
    d, t = lax.axis_index("dp"), lax.axis_index("tensor")
    m, c = lax.div(t, 2), lax.rem(t, 2)
    partner = (d, t + 1 - 2 * c)
    across = (d, lax.rem(t + 2, 4))
    rows_half = rows_all // 2
    own = pl.multiple_of(c * local, LANES)
    own_lanes = pl.ds(own, local)
    place = pl.ds(pl.multiple_of(c * rows_half, BLK), rows_half)
    loads = [
        pltpu.make_async_copy(src, dst, load.at[i])
        for i, (src, dst) in enumerate(
            [
                (cotangent_ref.at[m], dy_ref),
                (tokens_ref.at[m, place], x_ref),
                (o_all_ref.at[:, own_lanes], o_ref),
            ]
        )
    ]
    for i in range(2):
        fetch(i).start()
    for copy in loads:
        copy.start()
    for i in range(2, 13):
        fetch(i).start()
    greet(plane_peers(n, d, t) + [partner, across])

    sum_copies = [
        remote(src, land, sum_send.at[0], sum_recv.at[0], across)
        for src, land in zip(chip_in_refs, far_in_refs)
    ]
    for copy in sum_copies:
        copy.start()

    def give(j):
        s = lax.rem(d + j, n)
        return remote(gy_src_ref.at[s], gy_ref.at[c, d], gy_send.at[j], gy_recv.at[j], (s, t))

    def hand(j):
        block = gy_ref.at[c, lax.rem(d + n - j, n)]
        return remote(block, block, pass_send.at[j], pass_recv.at[j], partner)

    keep = pltpu.make_async_copy(gy_src_ref.at[d], gy_ref.at[c, d], stay.at[0])
    keep.start()

    def give_start(j, carry):
        give(j).start()
        return carry

    lax.fori_loop(1, n, give_start, 0)

    def collect():
        keep.wait()
        hand(0).start()

        def step(j, carry):
            give(j).wait_recv()
            hand(j).start()
            return carry

        lax.fori_loop(1, n, step, 0)

    def settle():
        def step(j, carry):
            hand(j).wait_recv()
            return carry

        lax.fori_loop(0, n, step, 0)

    row_ref[...] = jnp.zeros_like(row_ref)
    for copy in loads:
        copy.wait()
    for i in range(3):
        fetch(i).wait()

    gain_moe = extra_ref[columns + 5 : columns + 6, :]
    vec0 = extra_ref[columns + 6 : columns + 7, :]
    vec1 = extra_ref[columns + 7 : columns + 8, :]
    group = max(1, min(n, (1024 if slots <= 1024 else 512) // padded))
    span = group * padded

    def combine(wheres, ref, lines=None):
        total = jnp.zeros((BLK, width), F32)
        entries = [jnp.zeros((BLK, 1), F32) for _ in wheres]
        slot = lax.broadcasted_iota(jnp.int32, (BLK, span), 1)
        for side in range(2):
            for first in range(0, n, group):
                start = side * slots + first * padded
                hots = [slot == where - start for where in wheres]
                hot = jnp.where(hots[0] | hots[1], 1.0, 0.0).astype(BF16)
                block = ref[side, first : first + group].reshape(span, width)
                total = total + mm(hot, block)
                if lines is not None:
                    line = jnp.concatenate(
                        [lines[side, first + e, 0:1, :] for e in range(group)], axis=1
                    )
                    entries = [
                        entry + jnp.sum(jnp.where(one, line, 0.0), axis=-1, keepdims=True)
                        for entry, one in zip(entries, hots)
                    ]
        return total, entries

    def facts(rows):
        lane = lane_ids(BLK)
        stats = stat_ref[rows, :]
        values = [stats[:, j : j + 1] for j in range(7)]
        e0, e1 = stats[:, 7:8].astype(jnp.int32), stats[:, 8:9].astype(jnp.int32)
        wheres = []
        places = pos_ref[rows, :]
        for e in (e0, e1):
            place = pick(lane == e, places).astype(jnp.int32)
            side = (place >= half).astype(jnp.int32)
            where = side * (slots - half) + e * padded + place
            wheres.append(jnp.where(e < n, where, -1))
        g0, g1 = values[0:2]

        def named(number):
            return jnp.where(e0 == number, g0, 0.0) + jnp.where(e1 == number, g1, 0.0)

        copied, first, second = named(n + 1), named(n + 2), named(n + 3)
        on_u = copied + first * values[2] + second * values[4]
        return values, e0, e1, wheres, first, second, on_u

    def back(i, carry):
        rows = pl.ds(pl.multiple_of(i * BLK, BLK), BLK)
        values, e0, e1, wheres, first, second, on_u = facts(rows)
        g0, g1, a00, a01, a10, a11, r = values
        lane = lane_ids(BLK)
        grads, (f0, f1) = combine(wheres, dx_ref, dg_ref)
        h = h_ref[rows, :]
        normed = h * r
        u = normed * gain_moe
        dy = dy_ref[rows, :].astype(F32)
        s_u = jnp.sum(dy * u, axis=-1, keepdims=True)
        s_0 = jnp.sum(dy * vec0, axis=-1, keepdims=True)
        s_1 = jnp.sum(dy * vec1, axis=-1, keepdims=True)

        def other(e):
            value = jnp.where(e == n + 1, s_u, 0.0)
            value = jnp.where(e == n + 2, a00 * s_u + a01 * s_0, value)
            return jnp.where(e == n + 3, a10 * s_u + a11 * s_1, value)

        dg0, dg1 = f0 + other(e0), f1 + other(e1)
        mean = g0 * dg0 + g1 * dg1
        dl = jnp.where(lane == e0, g0 * (dg0 - mean), 0.0) + jnp.where(
            lane == e1, g1 * (dg1 - mean), 0.0
        )
        turned = jnp.transpose(dl)
        logit_ref[m, :, rows] = turned[0 : logit_ref.shape[1], :]
        d00, d01 = first * s_u, first * s_0
        d10, d11 = second * s_u, second * s_1
        m0 = a00 * d00 + a01 * d01
        m1 = a10 * d10 + a11 * d11
        low = dl
        for j, value in enumerate(
            [a00 * (d00 - m0), a01 * (d01 - m0), a10 * (d10 - m1), a11 * (d11 - m1)]
        ):
            low = jnp.where(lane == columns + j, value, low)
        low = low.astype(BF16)
        low_ref[rows, :] = low
        du = grads + mm_nt(low, small_ref[...]) + on_u * dy
        row_ref[0:1, :] += jnp.sum(du * normed, axis=0, keepdims=True)
        row_ref[1:2, :] += jnp.sum((first * a01) * dy, axis=0, keepdims=True)
        row_ref[2:3, :] += jnp.sum((second * a11) * dy, axis=0, keepdims=True)
        dn = du * gain_moe
        dh = dy + r * (dn - normed * jnp.mean(dn * normed, axis=-1, keepdims=True))

        @pl.when(lax.div(i, blocks // 2) == c)
        def _():
            near = pl.multiple_of(i * BLK - c * rows_half, BLK)
            dh_ref[pl.ds(near, BLK), :] = dh

        dzb = dh.astype(BF16)
        dzb_ref[rows, :] = dzb
        do_ref[rows, :] = mm(dzb, wo_ref[:, own_lanes]).astype(BF16)
        return carry

    lax.fori_loop(0, blocks, back, 0)
    logit_copy = remote(
        logit_ref.at[m], logit_ref.at[m], pair_send.at[0], pair_recv.at[0], across
    )
    logit_copy.start()

    fetch(3).wait()
    grad_wo = mm_tn(dzb_ref[...], o_ref[...])
    pack_ref[0, :, 3 * LANES : 4 * LANES] = grad_wo[:, 0:LANES].astype(BF16)
    pack_ref[1, :, 3 * LANES : 4 * LANES] = grad_wo[:, LANES : 2 * LANES].astype(BF16)
    wo_odd_ref[...] = grad_wo[:, 2 * LANES : 3 * LANES]
    lines = mm_tn(ub_ref[...], low_ref[...])
    lane_of = lax.broadcasted_iota(jnp.int32, (width, LANES), 1)
    turned = jnp.concatenate([row_ref[...], jnp.zeros((LANES - 8, width), F32)], axis=0)
    turned = jnp.transpose(turned)
    for j in range(3):
        lines = jnp.where(lane_of == columns + 5 + j, turned[:, j : j + 1], lines)
    line_ref[...] = lines

    def slab(owner):
        return pl.ds(pl.multiple_of(owner * part, part), part)

    ring = n // 2
    y_own = lax.rem(d, 2)
    beside = (d + 1 - 2 * y_own, t)
    z_own = lax.div(d, 2)
    wide_lanes = (pl.ds(0, 3 * LANES), pl.ds(3 * LANES, 3 * LANES))

    def y_copy(s, stage, z):
        lanes = wide_lanes[stage]
        return remote(
            pack_ref.at[s, slab(2 * z + 1 - y_own), lanes],
            y_in_ref.at[s, z, :, lanes],
            grad_send.at[stage, s, z],
            grad_recv.at[stage, s, z],
            beside,
        )

    def z_copy(s, stage, j):
        lanes = wide_lanes[stage]
        z = lax.rem(z_own + j, ring)
        return remote(
            pack_ref.at[s, slab(2 * z + y_own), lanes],
            z_in_ref.at[s, j, :, lanes],
            grad_send.at[2 + stage, s, j],
            grad_recv.at[2 + stage, s, j],
            (2 * z + y_own, t),
        )

    def y_start(s, stage):
        for z in range(ring):
            y_copy(s, stage, z).start()

    def z_start(s, stage):
        lanes = wide_lanes[stage]
        for z in range(ring):
            y_copy(s, stage, z).wait()
            rows = slab(2 * z + y_own)
            value = pack_ref[s, rows, lanes].astype(F32) + y_in_ref[s, z, :, lanes].astype(F32)
            pack_ref[s, rows, lanes] = value.astype(BF16)
        for j in range(1, ring):
            z_copy(s, stage, j).start()

    def line_copy(j):
        e = lax.rem(d + j, n)
        return remote(
            line_ref.at[slab(e), :],
            line_in_ref.at[d],
            line_send.at[j],
            line_recv.at[j],
            (e, t),
        )

    head = half_mask(BLK)

    def attend_back(p):
        dk_acc[...] = jnp.zeros_like(dk_acc)
        dv_acc[...] = jnp.zeros_like(dv_acc)
        dq = []
        for i in range(blocks):
            rows = pl.ds(i * BLK, BLK)
            seen = pl.ds(0, (i + 1) * BLK)
            lanes = pl.ds(pl.multiple_of(p * LANES, LANES), LANES)
            q, do = q_ref[p, rows, :], do_ref[rows, lanes]
            k, v = k_ref[p, seen, :], v_ref[p, seen, :]
            zero = jnp.zeros_like(q)
            parts = []
            dk, dv = dk_acc[seen, :], dv_acc[seen, :]
            for side in range(2):
                chosen = head if side == 0 else jnp.logical_not(head)
                qm, dom = jnp.where(chosen, q, zero), jnp.where(chosen, do, zero)
                prob = jnp.exp(mm_nt(k, qm) - lse_ref[2 * p + side, 0:1, rows])
                grad_prob = mm_nt(v, dom)
                total = jnp.sum(prob * grad_prob, axis=0, keepdims=True)
                grad_score = (prob * (grad_prob - total)).astype(BF16)
                dv = dv + mm(prob.astype(BF16), dom)
                dk = dk + mm(grad_score, qm)
                parts.append(mm_tn(grad_score, k))
            dk_acc[seen, :] = dk
            dv_acc[seen, :] = dv
            value = jnp.where(head, parts[0], parts[1]) * (HD**-0.5)
            dq.append(turn(value, cos_ref[rows, :], -sin_ref[rows, :]))
        return (
            jnp.concatenate(dq, axis=0),
            turn(dk_acc[...], cos_ref[...], -sin_ref[...]),
            dv_acc[...],
        )

    if not gathered:

        def send_line(j, carry):
            line_copy(j).start()
            return carry

        lax.fori_loop(1, n, send_line, 0)
        line_in_ref[d] = line_ref[slab(d), :]

    for i in range(4, 11):
        fetch(i).wait()
    dq, dk, dv = attend_back(2)
    wide = half_mask(rows_all)
    odd = [
        (jnp.where(wide, dq, swap_halves(dk)), jnp.where(wide, dv, 0.0)),
        (jnp.where(wide, swap_halves(dq), dk), jnp.where(wide, swap_halves(dv), 0.0)),
    ]
    tall = half_mask(width)
    for s in range(2):
        for j in range(2):
            dp_ref[s, :, (3 + j) * LANES : (4 + j) * LANES] = odd[s][j].astype(BF16)
    for s in range(2):
        pack_ref[s, :, 4 * LANES : 5 * LANES] = mm_tn(
            a_ref[...], dp_ref[s, :, 3 * LANES : 4 * LANES]
        ).astype(BF16)
        last = mm_tn(a_ref[...], dp_ref[s, :, 4 * LANES : 5 * LANES])
        side = wo_odd_ref[...]
        side = swap_halves(side) if s == 0 else side
        pack_ref[s, :, 5 * LANES : 6 * LANES] = jnp.where(tall, last, side).astype(BF16)
    if not gathered:
        y_start(0, 1)
        y_start(1, 1)

    def shard_step(i, carry):
        s = lax.rem(m + 1 + i, 2)
        for j, value in enumerate(attend_back(s)):
            dp_ref[s, :, j * LANES : (j + 1) * LANES] = value.astype(BF16)
        for j in range(3):
            lanes = pl.ds(j * LANES, LANES)
            pack_ref[s, :, lanes] = mm_tn(a_ref[...], dp_ref[s, :, lanes]).astype(BF16)
        if not gathered:
            y_start(s, 0)
        return carry

    lax.fori_loop(0, 2, shard_step, 0)
    if not gathered:
        z_start(0, 1)
        z_start(1, 1)

        def arrive_lines(j, carry):
            line_copy(j).wait()
            return carry

        lax.fori_loop(1, n, arrive_lines, 0)
        value = line_in_ref[0]
        for e in range(1, n):
            value = value + line_in_ref[e]
        cross_line_ref[0] = value
        cross_line_copy = remote(
            cross_line_ref.at[0], cross_line_ref.at[1], pair_send.at[4], pair_recv.at[4], across
        )
        cross_line_copy.start()
    collect()

    def publish(kind, out_ref):
        block = out_ref.at[m, place]
        copies = [
            remote(half_ref.at[kind], block, out_send.at[kind, 0], out_recv.at[kind, 0], across),
            remote(half_ref.at[kind], block, out_send.at[kind, 1], out_recv.at[kind, 1], partner),
            pltpu.make_async_copy(half_ref.at[kind], block, stay.at[1 + kind]),
        ]
        for copy in copies:
            copy.start()
        block = out_ref.at[1 - m, place]
        relay = remote(block, block, out_send.at[kind, 2], out_recv.at[kind, 2], partner)
        return copies, relay

    settle()

    def results(i, carry):
        rows = pl.ds(pl.multiple_of(i * BLK, BLK), BLK)
        far = pl.ds(pl.multiple_of(c * rows_half + i * BLK, BLK), BLK)
        values, e0, e1, wheres, first, second, on_u = facts(far)
        sums, _ = combine(wheres, gy_ref)
        h = h_ref[far, :]
        u = h * values[6] * gain_moe
        result = h + (sums + on_u * u + (first * values[3]) * vec0 + (second * values[5]) * vec1)
        half_ref[1, rows, :] = result.astype(BF16)
        return carry

    lax.fori_loop(0, rows_half // BLK, results, 0)
    result_copies, result_relay = publish(1, result_ref)

    if not gathered:
        z_start(1 - m, 0)

    def da_rows(start):
        rows = pl.ds(pl.multiple_of(start, BLK), BLK)
        total = jnp.zeros((BLK, width), F32)
        for s in range(2):
            total = total + mm_nt(dp_ref[s, rows, 0 : 3 * LANES], spread_a_ref[s])
            total = total + mm_nt(dp_ref[s, rows, 3 * LANES : 5 * LANES], spread_b_ref[s])
        return total

    fetch(11).wait()
    fetch(12).wait()

    def da_other(i, carry):
        rows = pl.ds(pl.multiple_of(i * BLK, BLK), BLK)
        da_out_ref[rows, :] = da_rows((1 - c) * rows_half + i * BLK).astype(BF16)
        return carry

    lax.fori_loop(0, rows_half // BLK, da_other, 0)
    da_copy = remote(da_out_ref, da_in_ref, pair_send.at[1], pair_recv.at[1], partner)
    da_copy.start()

    def da_own(i, carry):
        rows = pl.ds(pl.multiple_of(i * BLK, BLK), BLK)
        da_own_ref[rows, :] = da_rows(c * rows_half + i * BLK)
        return carry

    lax.fori_loop(0, rows_half // BLK, da_own, 0)
    if not gathered:
        z_start(m, 0)
    da_copy.wait()
    gain_attn = extra_ref[columns + 4 : columns + 5, :]
    norm_ref[...] = jnp.zeros_like(norm_ref)

    def finish(i, carry):
        rows = pl.ds(pl.multiple_of(i * BLK, BLK), BLK)
        x = x_ref[rows, :].astype(F32)
        r = lax.rsqrt(jnp.mean(x * x, axis=-1, keepdims=True) + EPSILON)
        normed = x * r
        da = da_own_ref[rows, :] + da_in_ref[rows, :].astype(F32)
        norm_ref[0:1, :] += jnp.sum(da * normed, axis=0, keepdims=True)
        dn = da * gain_attn
        grad = dh_ref[rows, :] + r * (dn - normed * jnp.mean(dn * normed, axis=-1, keepdims=True))
        half_ref[0, rows, :] = grad.astype(BF16)
        return carry

    lax.fori_loop(0, rows_half // BLK, finish, 0)
    norm_copy = remote(norm_ref, norm_in_ref, pair_send.at[2], pair_recv.at[2], partner)
    norm_copy.start()

    grad_x_copies, grad_x_relay = publish(0, grad_x_ref)

    norm_copy.wait()
    norm = norm_ref[...] + norm_in_ref[...]
    if gathered:
        turned = jnp.concatenate([norm, jnp.zeros((LANES - 8, width), F32)], axis=0)
        turned = jnp.transpose(turned)
        line_ref[...] = jnp.where(lane_of == columns + 4, turned[:, 0:1], line_ref[...])
        norm_out_ref[...] = jnp.zeros_like(norm_out_ref)
        packs = [
            pltpu.make_async_copy(pack_ref, grads_ref, load.at[0]),
            pltpu.make_async_copy(line_ref, lines_ref, load.at[1]),
        ]
        for copy in packs:
            copy.start()
        for copy in packs:
            copy.wait()
    else:
        norm_line_ref[...] = jnp.zeros_like(norm_line_ref)
        for j in range(width // LANES):
            norm_line_ref[j : j + 1, :] = norm[0:1, j * LANES : (j + 1) * LANES]

        def norm_give(j):
            e = lax.rem(d + j, n)
            return remote(
                norm_line_ref, norm_all_ref.at[d], norm_send.at[j], norm_recv.at[j], (e, t)
            )

        def norm_start(j, carry):
            norm_give(j).start()
            return carry

        lax.fori_loop(1, n, norm_start, 0)
        norm_all_ref[d] = norm_line_ref[...]

        def norm_wait(j, carry):
            norm_give(j).wait()
            return carry

        lax.fori_loop(1, n, norm_wait, 0)
        value = norm_all_ref[0]
        for e in range(1, n):
            value = value + norm_all_ref[e]
        norm_cross_ref[0] = value
        norm_cross_copy = remote(
            norm_cross_ref.at[0], norm_cross_ref.at[1], pair_send.at[5], pair_recv.at[5], across
        )
        norm_cross_copy.start()
        for s, stage in ((0, 1), (1, 1), (1 - m, 0)):
            for j in range(1, ring):
                z_copy(s, stage, j).wait()

        def total(s):
            value = pack_ref[s, slab(d), :].astype(F32)
            for j in range(1, ring):
                value = value + z_in_ref[s, j].astype(F32)
            return value

        cross_ref[...] = total(1 - m).astype(BF16)
        cross_copy = remote(cross_ref, cross_in_ref, pair_send.at[3], pair_recv.at[3], across)
        cross_copy.start()
        for j in range(1, ring):
            z_copy(m, 0, j).wait()
        grads_ref[...] = total(m)
        result_copies[0].wait_recv()
        result_relay.start()

        cross_copy.wait()
        grads_ref[...] += cross_in_ref[...].astype(F32)
        cross_line_copy.wait()
        lines_ref[...] = cross_line_ref[0] + cross_line_ref[1]
        norm_cross_copy.wait()
        norm_out_ref[...] = norm_cross_ref[0] + norm_cross_ref[1]

    grad_x_copies[0].wait_recv()
    grad_x_relay.start()
    if gathered:
        result_copies[0].wait_recv()
        result_relay.start()
    for copies, relay in ((grad_x_copies, grad_x_relay), (result_copies, result_relay)):
        copies[0].wait_send()
        copies[1].wait()
        copies[2].wait()
        relay.wait()
    logit_copy.wait()

    for copy in sum_copies:
        copy.wait()

    def clear(j, carry):
        give(j).wait_send()
        return carry

    lax.fori_loop(1, n, clear, 0)

    def passed(j, carry):
        hand(j).wait_send()
        return carry

    lax.fori_loop(0, n, passed, 0)


def last_kernel(
    part,
    columns,
    results_ref,
    grad_x_ref,
    own_in_ref,
    far_in_ref,
    own_down_ref,
    far_down_ref,
    logit_ref,
    grads_ref,
    lines_ref,
    norm_ref,
    results_out,
    grad_x_out,
    in_out,
    down_out,
    logit_out,
    attn_out,
    moe_out,
    heads_out,
    out_out,
    router_out,
    const_out,
    vec_out,
):
    results_out[...] = results_ref[...]
    grad_x_out[...] = grad_x_ref[...]
    in_out[...] = own_in_ref[...] + far_in_ref[...].astype(F32)
    down_out[...] = own_down_ref[...] + far_down_ref[...].astype(F32)

    @pl.when(pl.program_id(0) == 0)
    def _():
        for m in range(2):
            logit_out[:, m, :] = logit_ref[m, 0:columns, :]
        firsts = [grads_ref[:, j * LANES : (j + 1) * LANES] for j in range(4)]
        odds = []
        for j in range(2):
            both = grads_ref[:, (4 + j) * LANES : (5 + j) * LANES]
            odds.extend([both, swap_halves(both)])
        for j in range(3):
            heads_out[j, :, 0:LANES] = firsts[j]
            heads_out[j, :, LANES : LANES + HD] = odds[j][:, 0:HD]
        spare = jnp.zeros((LANES - part, 2 * LANES), F32)
        rows = jnp.concatenate([firsts[3], odds[3]], axis=1)
        turned = jnp.transpose(jnp.concatenate([rows, spare], axis=0))
        out_out[...] = turned[0 : LANES + HD, 0:part]
        lines = jnp.concatenate([lines_ref[...], spare[:, 0:LANES]], axis=0)
        lines = jnp.transpose(lines)[:, 0:part]
        router_out[...] = lines[0:columns]
        const_out[...] = lines[columns : columns + 4]
        norm = jnp.concatenate([norm_ref[...], jnp.zeros((LANES - 8, LANES), F32)], axis=0)
        norm = jnp.transpose(norm)
        place = lax.broadcasted_iota(jnp.int32, (LANES, part), 0)
        wanted = lax.broadcasted_iota(jnp.int32, (LANES, part), 1) + lax.axis_index("dp") * part
        total = jnp.zeros((1, part), F32)
        for j in range(results_ref.shape[2] // LANES):
            chosen = jnp.where(place + j * LANES == wanted, norm[:, j : j + 1], 0.0)
            total = total + jnp.sum(chosen, axis=0, keepdims=True)
        attn_out[...] = total
        moe_out[...] = lines[columns + 5 : columns + 6]
        vec_out[...] = lines[columns + 6 : columns + 8]


def across_chips(value):
    return lax.ppermute(value, "tensor", [(0, 2), (2, 0), (1, 3), (3, 1)])


def across_cores(value):
    return lax.ppermute(value, "tensor", [(0, 1), (1, 0), (2, 3), (3, 2)])


def body(
    tokens,
    cotangent,
    prev_logits,
    routes,
    norm_attn,
    norm_moe,
    w_qkv,
    w_out,
    w_router,
    w_const,
    const_vec,
    w_in,
    w_down,
):
    rows, width = tokens.shape[1:]
    n = lax.axis_size("dp")
    experts = n
    columns = prev_logits.shape[2]
    capacity = 4 * max(1, 3 * rows // (4 * (experts + 4)))
    half = capacity // 2
    padded = -(-half // 16) * 16
    share = w_qkv.shape[2]
    local = 2 * share
    part = w_qkv.shape[1]
    t = lax.axis_index("tensor")
    m, c = t // 2, t % 2

    cosine, sine = (jnp.asarray(v) for v in rope_constants())
    pairs = local // LANES

    tinies = [w_router.T, w_const.T, norm_attn[None], norm_moe[None], const_vec]
    gathered = part % 16 != 0
    if gathered:
        wo_rows = w_out.T
        tiny = jnp.concatenate(
            tinies + [jnp.zeros((LANES - columns - 8, part), BF16)], axis=0
        )
        packed = jnp.concatenate(
            [w_qkv[i, :, :LANES] for i in range(3)]
            + [wo_rows[:, :LANES]]
            + [w_qkv[i, :, LANES:] for i in range(3)]
            + [wo_rows[:, LANES:], tiny.T],
            axis=1,
        )
    if gathered:
        packed = lax.all_gather(packed, "dp", axis=0, tiled=True)
        other = across_chips(packed)
        tinies = [jnp.where(m == 0, jnp.stack([packed, other]), jnp.stack([other, packed]))]
    late = [
        struct((n, padded, width), BF16),
        struct((n, 8, padded), F32),
        struct((LANES, width), F32),
    ]
    early = [
        struct((rows, width), BF16),
        struct((pairs, rows, LANES), BF16),
        struct((pairs, rows, LANES), BF16),
        struct((pairs, rows, LANES), BF16),
        struct((rows, width), BF16),
        struct((8, 8, rows), F32),
        struct((rows, LANES), F32),
        struct((width, width), BF16),
        struct((width, LANES), BF16),
        struct((2, width, 7 * LANES), BF16),
        struct((rows, width), F32),
        struct((rows, width), BF16),
        struct((rows, LANES), F32),
    ]
    landing = [struct((n, padded, width), BF16), struct(w_in.shape, BF16)]
    dma = pltpu.SemaphoreType.DMA
    outs = pl.pallas_call(
        functools.partial(front_kernel, n, half, padded, gathered, len(early)),
        out_shape=late + early + landing,
        in_specs=[aspec()] * 3 + [vspec()] * 5 + [aspec()] + [vspec()] * len(tinies),
        out_specs=[vspec()] * len(late) + [aspec()] * (len(early) + len(landing)),
        scratch_shapes=[pltpu.VMEM(o.shape, o.dtype) for o in early]
        + [
            pltpu.VMEM((rows, width), BF16),
            pltpu.VMEM((rows, width), BF16),
            pltpu.VMEM((2, rows), jnp.int32),
            pltpu.VMEM((LANES, rows), F32),
            pltpu.VMEM((LANES, rows), F32),
            pltpu.VMEM((n, padded, width), BF16),
            dma((3,)),
            dma((8, n // 2)),
            dma((8, n // 2)),
            dma((n,)),
            dma((n,)),
            dma((1,)),
            dma((pairs + 1,)),
            dma((pairs + 1,)),
            dma((1,)),
            dma((1,)),
            dma((len(early),)),
        ],
        compiler_params=pltpu.CompilerParams(
            collective_id=0, has_side_effects=True, vmem_limit_bytes=VMEM_LIMIT
        ),
        cost_estimate=pl.CostEstimate(
            flops=60_000_000_000, bytes_accessed=60_000_000, transcendentals=0
        ),
    )(
        tokens,
        cotangent,
        jnp.swapaxes(routes, 1, 2),
        jnp.transpose(prev_logits, (2, 0, 1)),
        w_qkv,
        w_out,
        cosine,
        sine,
        w_in,
        *tinies,
    )
    slots, gate_slots, extra, a, q, k, v, o_all, lse, pos = outs[:10]
    wo_all, small_all, spread, h, ub, stats, dy_arrived, in_x = outs[10:]

    hidden_width = w_in.shape[3]
    slots_all = experts * padded
    if gathered:
        in_x, down_x = across_chips(w_in), across_chips(w_down)
        in_c, down_c = across_cores(w_in), across_cores(w_down)
        in_d, down_d = across_cores(in_x), across_cores(down_x)
        chunk = min(256 if slots_all <= 1024 else 128, hidden_width)
        per = hidden_width // chunk

        def in_map(i):
            return lambda f: (0, 0, 0, jnp.clip(f - per * i, 0, per - 1))

        def down_map(i):
            return lambda f: (0, jnp.clip(f - per * i, 0, per - 1), 0)

        in_blocks = [pl.BlockSpec((1, 2, width, chunk), in_map(i)) for i in range(4)]
        down_blocks = [pl.BlockSpec((1, chunk, width), down_map(i)) for i in range(4)]
        expert_outs = (
            [
                struct((n, padded, width), BF16),
                struct((n, padded, width), BF16),
                struct((n, 8, padded), F32),
            ]
            + [struct(w_in.shape, BF16)] * 4
            + [struct(w_down.shape, BF16)] * 4
        )

        def whole(shape):
            return pl.BlockSpec(
                shape, lambda f: (0,) * len(shape), pipeline_mode=pl.Buffered(1)
            )

        parts = pl.pallas_call(
            functools.partial(expert_kernel, n, padded),
            grid=(4 * per,),
            out_shape=expert_outs,
            in_specs=[
                whole((slots_all, width)),
                whole((slots_all, width)),
                whole((n, 8, padded)),
            ]
            + in_blocks
            + down_blocks,
            out_specs=[
                whole((n, padded, width)),
                whole((n, padded, width)),
                whole((n, 8, padded)),
            ]
            + in_blocks
            + down_blocks,
            scratch_shapes=[
                pltpu.VMEM((width, slots_all), BF16),
                pltpu.VMEM((slots_all, width), BF16),
                pltpu.VMEM((slots_all, LANES), F32),
                pltpu.VMEM((slots_all, width), F32),
                pltpu.VMEM((slots_all, width), F32),
                pltpu.VMEM((2, width, chunk), BF16),
                pltpu.VMEM((chunk, width), BF16),
            ],
            compiler_params=pltpu.CompilerParams(vmem_limit_bytes=VMEM_LIMIT),
            cost_estimate=pl.CostEstimate(
                flops=18 * slots_all * width * 4 * hidden_width,
                bytes_accessed=30_000_000,
                transcendentals=0,
            ),
        )(
            lax.all_to_all(slots, "dp", split_axis=0, concat_axis=0, tiled=True).reshape(
                slots_all, width
            ),
            dy_arrived.reshape(slots_all, width),
            lax.all_to_all(gate_slots, "dp", split_axis=0, concat_axis=0, tiled=True),
            w_in,
            in_c,
            in_x,
            in_d,
            w_down,
            down_c,
            down_x,
            down_d,
        )
        gy, dx, dg = parts[0:3]
        gin, gdown = parts[3:7], parts[7:11]

        def everywhere(value):
            value = lax.all_to_all(value, "dp", split_axis=0, concat_axis=0, tiled=True)
            other = across_cores(value)
            return jnp.where(c == 0, jnp.stack([value, other]), jnp.stack([other, value]))

        dx_all, dg_all = everywhere(dx), everywhere(dg)

        def total(own, core, chip, diagonal):
            chip = (chip.astype(F32) + across_cores(diagonal).astype(F32)).astype(BF16)
            own = own.astype(F32) + across_cores(core).astype(F32)
            return own + across_chips(chip).astype(F32)

        grad_in, grad_down = total(*gin), total(*gdown)
        chip_in = []
    else:
        gy, own_in, own_down, chip_in, far_down, dx_all, dg_all = pl.pallas_call(
            functools.partial(expert_exchange_kernel, n, padded),
            out_shape=[
                struct((n, padded, width), BF16),
                struct(w_in.shape, F32),
                struct(w_down.shape, F32),
                struct(w_in.shape, BF16),
                struct(w_down.shape, BF16),
                struct((2, n, padded, width), BF16),
                struct((2, n, 8, padded), F32),
            ],
            in_specs=[aspec()] * 6,
            out_specs=[aspec()] * 7,
            scratch_shapes=[
                pltpu.VMEM((n, padded, width), BF16),
                pltpu.VMEM(w_in.shape, F32),
                pltpu.VMEM(w_down.shape, F32),
                pltpu.VMEM(w_in.shape, BF16),
                pltpu.VMEM((slots_all, width), BF16),
                pltpu.VMEM((width, slots_all), BF16),
                pltpu.VMEM((slots_all, width), BF16),
                pltpu.VMEM((slots_all, width), BF16),
                pltpu.VMEM((slots_all, LANES), F32),
                pltpu.VMEM((n, 8, padded), F32),
                pltpu.VMEM((4, 2, width, hidden_width), BF16),
                pltpu.VMEM((4 * hidden_width, width), BF16),
                pltpu.VMEM((slots_all, 4 * hidden_width), BF16),
                pltpu.VMEM((slots_all, 4 * hidden_width), BF16),
                pltpu.VMEM((slots_all, 4 * hidden_width), BF16),
                pltpu.VMEM((slots_all // 4, width), F32),
                pltpu.VMEM((slots_all, width), BF16),
                pltpu.VMEM((n, 8, padded), F32),
                pltpu.VMEM((2,) + w_in.shape[1:], BF16),
                pltpu.VMEM((2,) + w_down.shape[1:], BF16),
                pltpu.VMEM(w_down.shape, BF16),
                dma((10 + n,)),
                dma((n,)),
                dma((n,)),
                dma((n,)),
                dma((n,)),
                dma((n,)),
                dma((n,)),
                dma((n,)),
                dma((n,)),
                dma((2, n)),
                dma((2, n)),
                dma((4,)),
                dma((4,)),
                dma((6,)),
                dma((6,)),
                dma((4,)),
            ],
            compiler_params=pltpu.CompilerParams(
                collective_id=2, has_side_effects=True, vmem_limit_bytes=VMEM_LIMIT
            ),
            cost_estimate=pl.CostEstimate(
                flops=60_000_000_000, bytes_accessed=40_000_000, transcendentals=0
            ),
        )(
            slots,
            gate_slots,
            dy_arrived,
            w_in,
            in_x,
            w_down,
        )
        chip_in = [chip_in]

    groups = 6 * LANES
    logit_rows = -(-columns // 8) * 8
    rear_outs = [
        struct((2, logit_rows, rows), F32),
        struct((2, width, groups), BF16) if gathered else struct((part, groups), F32),
        struct((width if gathered else part, LANES), F32),
        struct((8, LANES), F32),
    ]
    half_rows = rows // 2
    spread_n = 1 if gathered else n // 2
    line_n = 1 if gathered else n
    kept = [
        struct((2, n, padded, width), BF16),
        struct((rows, width), F32),
        struct((width, width), BF16),
        struct((rows, width), BF16),
        struct((pairs, rows, LANES), BF16),
        struct((pairs, rows, LANES), BF16),
        struct((pairs, rows, LANES), BF16),
        struct((8, 8, rows), F32),
        struct((rows, LANES), F32),
        struct((rows, LANES), F32),
        struct((rows, width), BF16),
        struct((2, width, 3 * LANES), BF16),
        struct((2, width, 2 * LANES), BF16),
    ]
    results, input_grads, logits, grads, lines, norm_line, *far_in = pl.pallas_call(
        functools.partial(rear_kernel, n, half, padded, gathered, part),
        out_shape=[struct((2, rows, width), BF16)] * 2
        + rear_outs
        + [struct(w_in.shape, BF16)] * len(chip_in),
        in_specs=[aspec()] * (len(chip_in) + 4 + len(kept)) + [vspec()] * 5,
        out_specs=[aspec()] * 2
        + [vspec()]
        + [aspec() if gathered else vspec()] * 2
        + [vspec()]
        + [aspec()] * len(chip_in),
        scratch_shapes=[pltpu.VMEM(o.shape, o.dtype) for o in kept]
        + [
            pltpu.VMEM((half_rows, width), BF16),
            pltpu.VMEM((rows, width), BF16),
            pltpu.VMEM((rows, local), BF16),
            pltpu.VMEM((2, n, padded, width), BF16),
            pltpu.VMEM((half_rows, width), F32),
            pltpu.VMEM((rows, width), BF16),
            pltpu.VMEM((rows, local), BF16),
            pltpu.VMEM((rows, LANES), BF16),
            pltpu.VMEM((8, width), F32),
            pltpu.VMEM((2, rows, 5 * LANES), BF16),
            pltpu.VMEM((rows, LANES), F32),
            pltpu.VMEM((rows, LANES), F32),
            pltpu.VMEM((width, LANES), F32),
            pltpu.VMEM((2, width, groups), BF16),
            pltpu.VMEM((width, LANES), F32),
            pltpu.VMEM((2, spread_n, part, groups), BF16),
            pltpu.VMEM((2, spread_n, part, groups), BF16),
            pltpu.VMEM((line_n, part, LANES), F32),
            pltpu.VMEM((part, groups), BF16),
            pltpu.VMEM((part, groups), BF16),
            pltpu.VMEM((2, part, LANES), F32),
            pltpu.VMEM((half_rows, width), BF16),
            pltpu.VMEM((half_rows, width), BF16),
            pltpu.VMEM((half_rows, width), F32),
            pltpu.VMEM((8, width), F32),
            pltpu.VMEM((8, width), F32),
            pltpu.VMEM((2, half_rows, width), BF16),
            pltpu.VMEM((8, LANES), F32),
            pltpu.VMEM((line_n, 8, LANES), F32),
            pltpu.VMEM((2, 8, LANES), F32),
            dma((3,)),
            dma((len(kept),)),
            dma((n,)),
            dma((n,)),
            dma((3,)),
            dma((n,)),
            dma((n,)),
            dma((4, 2, n // 2)),
            dma((4, 2, n // 2)),
            dma((n,)),
            dma((n,)),
            dma((6,)),
            dma((6,)),
            dma((2, 3)),
            dma((2, 3)),
            dma((1,)),
            dma((1,)),
            dma((n,)),
            dma((n,)),
        ],
        compiler_params=pltpu.CompilerParams(
            collective_id=1, has_side_effects=True, vmem_limit_bytes=VMEM_LIMIT
        ),
        cost_estimate=pl.CostEstimate(
            flops=100_000_000_000, bytes_accessed=60_000_000, transcendentals=0
        ),
    )(
        *chip_in,
        gy,
        tokens,
        cotangent,
        o_all,
        dx_all,
        h,
        wo_all,
        ub,
        q,
        k,
        v,
        lse,
        cosine,
        sine,
        a,
        spread,
        spread,
        stats,
        pos,
        small_all,
        extra,
        dg_all,
    )
    if not gathered:
        steps = 4

        def split(value, axis):
            block = list(value.shape)
            block[axis] //= steps

            def index(i):
                where = [0] * len(block)
                where[axis] = i
                return tuple(where)

            return pl.BlockSpec(tuple(block), index)

        def full(value):
            return pl.BlockSpec(value.shape, lambda i: (0,) * len(value.shape))

        large = [
            (results, 1),
            (input_grads, 1),
            (own_in, 2),
            (far_in[0], 2),
            (own_down, 1),
            (far_down, 1),
        ]
        tinies = [
            struct((columns, 2, rows), F32),
            struct((1, part), F32),
            struct((1, part), F32),
            struct((3, part, share), F32),
            struct((share, part), F32),
            struct((columns, part), F32),
            struct((4, part), F32),
            struct((2, part), F32),
        ]
        final = [large[0], large[1], large[2], large[4]]
        done = pl.pallas_call(
            functools.partial(last_kernel, part, columns),
            grid=(steps,),
            out_shape=[struct(v.shape, v.dtype) for v, _ in final] + tinies,
            in_specs=[split(v, axis) for v, axis in large]
            + [full(v) for v in (logits, grads, lines, norm_line)],
            out_specs=[split(v, axis) for v, axis in final] + [full(v) for v in tinies],
            compiler_params=pltpu.CompilerParams(vmem_limit_bytes=VMEM_LIMIT),
        )(*(v for v, _ in large), logits, grads, lines, norm_line)
        results, input_grads, grad_in, grad_down, logits = done[:5]
        gain_attn, gain_moe, heads, out, router, const, vec = done[5:]
        return (
            results,
            input_grads,
            jnp.transpose(logits, (1, 2, 0)),
            gain_attn[0],
            gain_moe[0],
            heads,
            out,
            router.T,
            const.T,
            vec,
            grad_in,
            grad_down,
        )
    grads = lax.psum_scatter(grads.astype(F32), "dp", scatter_dimension=1, tiled=True)
    lines = lax.psum_scatter(lines, "dp", scatter_dimension=0, tiled=True)
    other = lax.dynamic_index_in_dim(grads, 1 - m, 0, keepdims=False)
    grads = lax.dynamic_index_in_dim(grads, m, 0, keepdims=False) + across_chips(other)
    lines = lines + across_chips(lines)

    def heads(j):
        start = (4 + (j % 4) // 2) * LANES + (j % 2) * HD
        return jnp.concatenate(
            [grads[:, j * LANES : (j + 1) * LANES], grads[:, start : start + HD]], axis=1
        )

    return (
        results,
        input_grads,
        jnp.swapaxes(logits[:, :columns], 1, 2),
        lines[:, columns + 4],
        lines[:, columns + 5],
        jnp.stack([heads(i) for i in range(3)]),
        heads(3).T,
        lines[:, :columns],
        lines[:, columns : columns + 4],
        lines[:, columns + 6 : columns + 8].T,
        grad_in,
        grad_down,
    )


def solution(mesh):
    in_specs = (
        P(None, "dp", None),
        P(None, "dp", None),
        P(None, "dp", None),
        P(None, "dp", None),
        P("dp"),
        P("dp"),
        P(None, "dp", "tensor"),
        P("tensor", "dp"),
        P("dp", None),
        P("dp", None),
        P(None, "dp"),
        P("dp", None, None, "tensor"),
        P("dp", "tensor", None),
    )
    out_specs = (
        P(None, "dp", None),
        P(None, "dp", None),
        P(None, "dp", None),
        P("dp"),
        P("dp"),
        P(None, "dp", "tensor"),
        P("tensor", "dp"),
        P("dp", None),
        P("dp", None),
        P(None, "dp"),
        P("dp", None, None, "tensor"),
        P("dp", "tensor", None),
    )
    return jax.shard_map(body, mesh=mesh, in_specs=in_specs, out_specs=out_specs, check_vma=False)
```

```python
import functools

import jax
import jax.numpy as jnp
import numpy as np
from jax import lax
from jax.experimental import pallas as pl
from jax.experimental.pallas import tpu as pltpu
from jax.sharding import PartitionSpec as P

HD = 64
LEN = 1024
BLK = 256
EPSILON = 1e-06
LANES = 128
F32 = jnp.float32
BF16 = jnp.bfloat16
MESH = pl.DeviceIdType.MESH
VMEM_LIMIT = 60 * 1024 * 1024


def mm(a, b):
    return lax.dot_general(a, b, (((1,), (0,)), ((), ())), preferred_element_type=F32)


def mm_nt(a, b):
    return lax.dot_general(a, b, (((1,), (1,)), ((), ())), preferred_element_type=F32)


def mm_tn(a, b):
    return lax.dot_general(a, b, (((0,), (0,)), ((), ())), preferred_element_type=F32)


def vspec():
    return pl.BlockSpec(memory_space=pltpu.VMEM)


def aspec():
    return pl.BlockSpec(memory_space=pl.ANY)


def struct(shape, dtype):
    return jax.ShapeDtypeStruct(shape, dtype)


def greet(peers):
    barrier = pltpu.get_barrier_semaphore()
    for peer in peers:
        pl.semaphore_signal(barrier, inc=1, device_id=peer, device_id_type=MESH)
    pl.semaphore_wait(barrier, len(peers))


def remote(src, dst, send, recv, peer):
    return pltpu.make_async_remote_copy(
        src_ref=src,
        dst_ref=dst,
        send_sem=send,
        recv_sem=recv,
        device_id=peer,
        device_id_type=MESH,
    )


def plane_peers(n, d, t):
    return [(lax.rem(d + j, n), t) for j in range(1, n)]


def slot_hot(half, padded, base, places):
    rows = places.shape[1]
    slot = lax.broadcasted_iota(jnp.int32, (padded, rows), 0)
    wanted = jnp.where(slot < half, slot + base, -2).astype(F32)
    return (wanted == places).astype(F32).astype(BF16)


def rope_constants():
    half = HD // 2
    frequency = 10000.0 ** (-2.0 * np.arange(half) / HD)
    angle = np.arange(LEN)[:, None] * frequency[None, :]
    cosine, sine = np.cos(angle), np.sin(angle)
    cosine = np.concatenate([cosine, cosine, cosine, cosine], axis=1)
    sine = np.concatenate([-sine, sine, -sine, sine], axis=1)
    return cosine.astype(np.float32), sine.astype(np.float32)


def turn(field, cosine, sine):
    lane = lax.broadcasted_iota(jnp.int32, field.shape, 1)
    other = jnp.where(
        lax.rem(lane, HD) < HD // 2,
        pltpu.roll(field, LANES - HD // 2, 1),
        pltpu.roll(field, HD // 2, 1),
    )
    return field * cosine + other * sine


def pick(hot, values):
    return jnp.sum(jnp.where(hot, values, 0.0), axis=-1, keepdims=True)


def lane_ids(rows):
    return lax.broadcasted_iota(jnp.int32, (rows, LANES), 1)


def soft_pair(first, second):
    high = jnp.maximum(first, second)
    e0, e1 = jnp.exp(first - high), jnp.exp(second - high)
    return e0 / (e0 + e1), e1 / (e0 + e1)


def half_mask(rows):
    return lax.broadcasted_iota(jnp.int32, (rows, LANES), 1) < HD


def swap_halves(value):
    return pltpu.roll(value, HD, 1)


def front_kernel(
    n,
    half,
    padded,
    gathered,
    early,
    tokens_ref,
    cotangent_ref,
    routes_all_ref,
    prev_all_ref,
    heads_ref,
    out_ref,
    cos_ref,
    sin_ref,
    win_ref,
    *refs,
):
    tiny_refs, refs = refs[: 1 if gathered else 5], refs[1 if gathered else 5 :]
    slot_ref, gate_ref, extra_ref = refs[:3]
    stored = refs[3 : 3 + early]
    dy_arrived_ref, in_x_ref = refs[3 + early : 5 + early]
    refs = refs[5 + early :]
    kept, refs = refs[:early], refs[early:]
    a_ref, q_ref, k_ref, v_ref, o_ref, lse_ref, pos_ref, wo_ref, small_ref, spread_ref = kept[:10]
    h_ref, ub_ref, stat_ref = kept[10:]
    x_ref, dy_ref, routes_ref, place_ref, gates_ref, dy_slot_ref = refs[:6]
    refs = refs[6:]
    load, pack_send, pack_recv, dy_send, dy_recv, stay = refs[:6]
    core_send, core_recv, w_send, w_recv, store_sem = refs[6:]

    def store(*which):
        for i in which:
            pltpu.make_async_copy(kept[i], stored[i], store_sem.at[i]).start()

    rows_all, width = x_ref.shape
    blocks = rows_all // BLK
    pairs = q_ref.shape[0]
    local = pairs * LANES
    columns = prev_all_ref.shape[0]
    d, t = lax.axis_index("dp"), lax.axis_index("tensor")
    m, c = lax.div(t, 2), lax.rem(t, 2)
    partner = (d, t + 1 - 2 * c)
    across = (d, lax.rem(t + 2, 4))
    loads = [
        pltpu.make_async_copy(src.at[m], dst, load.at[i])
        for i, (src, dst) in enumerate(
            [
                (routes_all_ref, routes_ref),
                (cotangent_ref, dy_ref),
                (tokens_ref, x_ref),
            ]
        )
    ]
    for copy in loads:
        copy.start()
    greet(plane_peers(n, d, t) + [partner, across])
    part = heads_ref.shape[1]

    def pack():
        side = lax.broadcasted_iota(jnp.int32, (part, part), 0)
        eye = jnp.where(side == lax.broadcasted_iota(jnp.int32, (part, part), 1), 1.0, 0.0)
        eye = eye.astype(BF16)
        wo = mm_nt(eye, out_ref[...])
        tiny = [ref[...].astype(F32) for ref in tiny_refs]
        tiny.append(jnp.zeros((LANES - columns - 8, part), F32))
        tiny = mm_nt(eye, jnp.concatenate(tiny, axis=0).astype(BF16))
        wide = [heads_ref[i].astype(F32) for i in range(3)] + [wo]
        firsts = [value[:, :LANES] for value in wide]
        odds = [
            jnp.concatenate([wide[i][:, LANES:], wide[i + 1][:, LANES:]], axis=1) for i in (0, 2)
        ]
        return jnp.concatenate(firsts + odds + [tiny], axis=1).astype(BF16)

    beside = (d + 1 - 2 * lax.rem(d, 2), t)
    lanes_a = pl.ds(0, 3 * LANES)
    lanes_b = pl.ds(3 * LANES, 4 * LANES)

    def behind(j):
        return lax.rem(d + n - 2 * j, n)

    def shard(chip, owner, lanes):
        return spread_ref.at[chip, pl.ds(pl.multiple_of(owner * part, part), part), lanes]

    def pass_on(chip, owner, lanes, row, j, peer):
        block = shard(chip, owner, lanes)
        return remote(block, block, pack_send.at[row, j], pack_recv.at[row, j], peer)

    def ahead(j):
        return (lax.rem(d + 2 * j, n), t)

    ring = n // 2
    if gathered:
        spread_ref[...] = tiny_refs[0][...]
    else:
        spread_ref[m, pl.ds(pl.multiple_of(d * part, part), part), :] = pack()
        a_x = pass_on(m, d, lanes_a, 4, 0, across)
        sends = [a_x]
        for j in range(1, ring):
            sends.append(pass_on(m, d, lanes_a, 0, j, ahead(j)))
            sends.append(pass_on(m, d, lanes_b, 4, j, ahead(j)))
        sends.append(pass_on(m, d, lanes_a, 2, 0, beside))
        sends.append(pass_on(m, d, lanes_b, 5, 0, beside))
        sends.append(pass_on(m, d, lanes_b, 6, 0, across))
        for copy in sends:
            copy.start()

    def relay_gather(after_z, after_x):
        if gathered:
            after_z()
            after_x()
            return
        a_x.wait_recv()
        more = [pass_on(1 - m, d, lanes_a, 1, j, ahead(j)) for j in range(1, ring)]
        more.append(pass_on(1 - m, d, lanes_a, 3, 0, beside))
        for copy in more:
            copy.start()
        sends.extend(more)
        for j in range(1, ring):
            pass_on(m, d, lanes_b, 4, j, ahead(j)).wait_recv()
            more = [
                pass_on(m, behind(j), lanes_b, 5, j, beside),
                pass_on(m, behind(j), lanes_b, 6, j, across),
            ]
            pass_on(m, d, lanes_a, 0, j, ahead(j)).wait_recv()
            more.append(pass_on(m, behind(j), lanes_a, 2, j, beside))
            for copy in more:
                copy.start()
            sends.extend(more)
        for j in range(1, ring):
            pass_on(1 - m, d, lanes_a, 1, j, ahead(j)).wait_recv()
            copy = pass_on(1 - m, behind(j), lanes_a, 3, j, beside)
            copy.start()
            sends.append(copy)
        after_z()
        for j in range(ring):
            pass_on(m, d, lanes_b, 5, j, beside).wait_recv()
            owner = lax.rem(beside[0] + n - 2 * j, n)
            copy = pass_on(m, owner, lanes_b, 7, j, across)
            copy.start()
            sends.append(copy)
        after_x()
        for j in range(ring):
            pass_on(m, d, lanes_a, 2, j, beside).wait_recv()
            pass_on(m, d, lanes_a, 3, j, beside).wait_recv()
            pass_on(m, d, lanes_b, 6, j, across).wait_recv()
            pass_on(m, d, lanes_b, 7, j, across).wait_recv()

    loads[0].wait()
    named = routes_ref[...].astype(F32)
    ids = lax.broadcasted_iota(jnp.int32, (LANES, rows_all), 0).astype(F32)
    hit = ((ids == named[0:1, :]) | (ids == named[1:2, :])) & (ids < float(n))
    before = lax.broadcasted_iota(jnp.int32, (rows_all, rows_all), 0) < lax.broadcasted_iota(
        jnp.int32, (rows_all, rows_all), 1
    )
    count = mm(hit.astype(F32).astype(BF16), before.astype(F32).astype(BF16))
    places = jnp.where(hit, count, -1.0)
    place_ref[...] = places
    pos_ref[...] = jnp.transpose(places)
    store(6)
    base = c * half

    def dy_copy(j):
        e = lax.rem(d + j, n)
        return remote(
            dy_slot_ref.at[e], dy_arrived_ref.at[d], dy_send.at[j], dy_recv.at[j], (e, t)
        )

    stays = [pltpu.make_async_copy(dy_slot_ref.at[d], dy_arrived_ref.at[d], stay.at[0])]
    loads[1].wait()

    def two_hot(i):
        return jnp.concatenate(
            [
                slot_hot(half, padded, base, place_ref[pl.ds(2 * i + side, 1), :])
                for side in range(2)
            ],
            axis=0,
        )

    def dy_step(i, carry):
        rows = mm(two_hot(i), dy_ref[...]).astype(BF16)
        for side in range(2):
            dy_slot_ref[2 * i + side] = rows[side * padded : (side + 1) * padded]
        return carry

    lax.fori_loop(0, n // 2, dy_step, 0)
    weight_copies = []
    if not gathered:
        weight_copies.append(remote(win_ref, in_x_ref, w_send.at[0], w_recv.at[0], across))

    def dy_start(j, carry):
        dy_copy(j).start()
        return carry

    relay_gather(
        lambda: lax.fori_loop(1, n, dy_start, 0), lambda: [c.start() for c in weight_copies]
    )
    stays[0].start()
    store(9)

    table = spread_ref[0, :, 6 * LANES : 7 * LANES]
    extra_ref[...] = jnp.transpose(table.astype(F32))
    keep = lax.broadcasted_iota(jnp.int32, (width, LANES), 1) < columns + 4
    small_ref[...] = jnp.where(keep, table, jnp.zeros_like(table))
    mask = half_mask(width)
    own = pl.multiple_of(c * local, LANES)
    wo_ref[:, pl.ds(own, LANES)] = spread_ref[0, :, 3 * LANES : 4 * LANES]
    wo_ref[:, pl.ds(own + LANES, LANES)] = spread_ref[1, :, 3 * LANES : 4 * LANES]
    wo_ref[:, pl.ds(own + 2 * LANES, LANES)] = jnp.where(
        mask,
        swap_halves(spread_ref[0, :, 5 * LANES : 6 * LANES].astype(F32)),
        spread_ref[1, :, 5 * LANES : 6 * LANES].astype(F32),
    ).astype(BF16)
    own_lanes = pl.ds(own, local)
    wo_copy = remote(
        wo_ref.at[:, own_lanes],
        wo_ref.at[:, own_lanes],
        core_send.at[pairs],
        core_recv.at[pairs],
        partner,
    )
    wo_copy.start()
    store(8)

    loads[2].wait()
    gain = extra_ref[columns + 4 : columns + 5, :]
    head = half_mask(BLK)

    def project(i, carry):
        rows = pl.ds(pl.multiple_of(i * BLK, BLK), BLK)
        x = x_ref[rows, :].astype(F32)
        r = lax.rsqrt(jnp.mean(x * x, axis=-1, keepdims=True) + EPSILON)
        a = (x * r * gain).astype(BF16)
        a_ref[rows, :] = a
        cosine, sine = cos_ref[rows, :], sin_ref[rows, :]

        def put(pair, q, k, v):
            q_ref[pair, rows, :] = turn(q, cosine, sine).astype(BF16) * BF16(HD**-0.5)
            k_ref[pair, rows, :] = turn(k, cosine, sine).astype(BF16)
            v_ref[pair, rows, :] = v.astype(BF16)

        odd = []
        for s in range(2):
            both = mm(a, spread_ref[s, :, 0 : 3 * LANES])
            put(s, *(both[:, j * LANES : (j + 1) * LANES] for j in range(3)))
            both = mm(a, spread_ref[s, :, 4 * LANES : 6 * LANES])
            odd.append((both[:, :LANES], both[:, LANES:]))
        put(
            2,
            jnp.where(head, odd[0][0], swap_halves(odd[1][0])),
            jnp.where(head, swap_halves(odd[0][0]), odd[1][0]),
            jnp.where(head, odd[0][1], swap_halves(odd[1][1])),
        )
        return carry

    lax.fori_loop(0, blocks, project, 0)
    store(0, 1, 2, 3)

    def o_copy(p):
        lanes = pl.ds(pl.multiple_of(own + p * LANES, LANES), LANES)
        return remote(
            o_ref.at[:, lanes], o_ref.at[:, lanes], core_send.at[p], core_recv.at[p], partner
        )

    def attend(p, carry):
        lanes = pl.ds(pl.multiple_of(own + p * LANES, LANES), LANES)
        for i in range(blocks):
            rows = pl.ds(i * BLK, BLK)
            seen = pl.ds(0, (i + 1) * BLK)
            q, k, v = q_ref[p, rows, :], k_ref[p, seen, :], v_ref[p, seen, :]
            halves = []
            for side in range(2):
                chosen = head if side == 0 else jnp.logical_not(head)
                s = mm_nt(jnp.where(chosen, q, jnp.zeros_like(q)), k)
                high = jnp.max(s, axis=-1, keepdims=True)
                e = jnp.exp(s - high)
                total = jnp.sum(e, axis=-1, keepdims=True)
                halves.append(mm(e.astype(BF16), v) * (1.0 / total))
                log_total = jnp.broadcast_to(high + jnp.log(total), (BLK, LANES))
                lse_ref[2 * p + side, :, rows] = jnp.transpose(log_total)[0:8, :]
            o_ref[rows, lanes] = jnp.where(head, halves[0], halves[1]).astype(BF16)
        o_copy(p).start()
        return carry

    lax.fori_loop(0, pairs, attend, 0)
    wo_copy.wait()
    for p in range(pairs):
        o_copy(p).wait()
    store(4, 5, 7)
    prev_lines = jnp.where(m == 0, prev_all_ref[:, 0, :], prev_all_ref[:, 1, :])
    spare = jnp.zeros((LANES - columns - 2, rows_all), F32)
    facts = jnp.concatenate([prev_lines, routes_ref[...].astype(F32), spare], axis=0)
    gates_ref[...] = facts

    gain_moe = extra_ref[columns + 5 : columns + 6, :]

    def middle(i, carry):
        rows = pl.ds(pl.multiple_of(i * BLK, BLK), BLK)
        z = mm_nt(o_ref[rows, :], wo_ref[...])
        h = x_ref[rows, :].astype(F32) + z
        r = lax.rsqrt(jnp.mean(h * h, axis=-1, keepdims=True) + EPSILON)
        ub = (h * r * gain_moe).astype(BF16)
        h_ref[rows, :] = h
        ub_ref[rows, :] = ub
        scores = mm(ub, small_ref[...])
        lane = lane_ids(BLK)
        facts = jnp.transpose(gates_ref[:, rows])
        e0 = facts[:, columns : columns + 1]
        e1 = facts[:, columns + 1 : columns + 2]
        hot0, hot1 = lane.astype(F32) == e0, lane.astype(F32) == e1
        logits = scores + facts
        g0, g1 = soft_pair(pick(hot0, logits), pick(hot1, logits))
        mix = [pick(lane == columns + j, scores) for j in range(4)]
        a00, a01 = soft_pair(mix[0], mix[1])
        a10, a11 = soft_pair(mix[2], mix[3])
        table = jnp.zeros((BLK, LANES), F32)
        for j, value in enumerate([g0, g1, a00, a01, a10, a11, r, e0, e1]):
            table = jnp.where(lane == j, value, table)
        stat_ref[rows, :] = table
        gates = jnp.where(hot0, g0, 0.0) + jnp.where(hot1, g1, 0.0)
        gates_ref[:, rows] = jnp.transpose(gates)
        return carry

    lax.fori_loop(0, blocks, middle, 0)
    store(10, 11, 12)
    piece = lax.broadcasted_iota(jnp.int32, (8, rows_all), 0)

    def slot_step(i, carry):
        hot = two_hot(i)
        rows = mm(hot, ub_ref[...]).astype(BF16)
        for side in range(2):
            e = 2 * i + side
            slot_ref[e] = rows[side * padded : (side + 1) * padded]
            gate = gates_ref[pl.ds(e, 1), :]
            high = gate.astype(BF16).astype(F32)
            mid = (gate - high).astype(BF16).astype(F32)
            low = gate - high - mid
            lines = jnp.where(piece == 0, high, jnp.where(piece == 1, mid, low))
            lines = jnp.where(piece < 3, lines, 0.0).astype(BF16)
            gate = mm_nt(lines, hot[side * padded : (side + 1) * padded])
            gate = jnp.sum(gate, axis=0, keepdims=True)
            gate_ref[e] = jnp.broadcast_to(gate, (8, padded))
        return carry

    lax.fori_loop(0, n // 2, slot_step, 0)
    def finish(j, carry):
        dy_copy(j).wait()
        return carry

    lax.fori_loop(1, n, finish, 0)
    for copy in stays:
        copy.wait()
    for copy in [] if gathered else sends:
        copy.wait_send()
    for copy in weight_copies:
        copy.wait()
    for i in range(early):
        pltpu.make_async_copy(kept[i], stored[i], store_sem.at[i]).wait()


def flip(value, index, size):
    bit = 1
    while bit < size:
        chosen = lax.rem(lax.div(index, bit), 2)
        value = value + chosen * (bit - 2 * bit * lax.rem(lax.div(value, bit), 2))
        bit *= 2
    return value


def expert_exchange_kernel(
    n,
    padded,
    slot_src_ref,
    gate_src_ref,
    dy_src_ref,
    in_own_ref,
    in_chip_ref,
    down_own_ref,
    gy_out_ref,
    own_in_out_ref,
    own_down_out_ref,
    chip_in_out_ref,
    far_down_ref,
    dx_all_ref,
    dg_all_ref,
    gy_ref,
    own_in_ref,
    own_down_ref,
    chip_in_ref,
    x_ref,
    xt_ref,
    dy_ref,
    scaled_ref,
    scale_ref,
    gate_ref,
    win_ref,
    wdown_ref,
    hidden_ref,
    dgate_ref,
    dup_ref,
    y_ref,
    dx_ref,
    dg_ref,
    land_in_ref,
    land_down_ref,
    chip_down_ref,
    load,
    slot_send,
    slot_recv,
    gate_send,
    gate_recv,
    dx_send,
    dx_recv,
    dg_send,
    dg_recv,
    pass_send,
    pass_recv,
    sum_send,
    sum_recv,
    w_send,
    w_recv,
    store_sem,
):
    width = x_ref.shape[1]
    share = win_ref.shape[3]
    chunks = 4
    group = n // chunks
    span = group * padded
    block = 256
    d, t = lax.axis_index("dp"), lax.axis_index("tensor")
    c = lax.rem(t, 2)
    partner = (d, t + 1 - 2 * c)
    across = (d, lax.rem(t + 2, 4))
    stores = [
        pltpu.make_async_copy(src, dst, store_sem.at[i])
        for i, (src, dst) in enumerate(
            [
                (gy_ref, gy_out_ref),
                (chip_in_ref, chip_in_out_ref),
                (own_in_ref, own_in_out_ref),
                (own_down_ref, own_down_out_ref),
            ]
        )
    ]
    greet(plane_peers(n, d, t) + [partner, across])

    def rows_of(i):
        return pl.ds(pl.multiple_of(i * padded, padded), padded)

    def slot_copy(i):
        e = flip(d, i, n)
        return remote(
            slot_src_ref.at[e], x_ref.at[rows_of(i)], slot_send.at[i], slot_recv.at[i], (e, t)
        )

    def gate_copy(i):
        e = flip(d, i, n)
        return remote(
            gate_src_ref.at[e], gate_ref.at[i], gate_send.at[i], gate_recv.at[i], (e, t)
        )

    def dx_copy(i):
        e = flip(d, i, n)
        return remote(
            dx_ref.at[rows_of(i)], dx_all_ref.at[c, d], dx_send.at[i], dx_recv.at[i], (e, t)
        )

    def dg_copy(i):
        e = flip(d, i, n)
        return remote(dg_ref.at[i], dg_all_ref.at[c, d], dg_send.at[i], dg_recv.at[i], (e, t))

    def hand(kind, i):
        ref = (dx_all_ref, dg_all_ref)[kind]
        block_ref = ref.at[c, flip(d, i, n)]
        return remote(
            block_ref, block_ref, pass_send.at[kind, i], pass_recv.at[kind, i], partner
        )

    def down_rows(s):
        return pl.ds(s * share, share)

    def send_chunk(k):
        for q in range(group):
            if k + q > 0:
                slot_copy(k * group + q).start()
                gate_copy(k * group + q).start()

    send_chunk(2)
    send_chunk(1)
    if group > 1:
        send_chunk(0)
    stays = [
        pltpu.make_async_copy(slot_src_ref.at[d], x_ref.at[rows_of(0)], load.at[0]),
        pltpu.make_async_copy(gate_src_ref.at[d], gate_ref.at[0], load.at[1]),
    ]
    own_loads = [
        pltpu.make_async_copy(in_own_ref.at[0], win_ref.at[0], load.at[2]),
        pltpu.make_async_copy(down_own_ref.at[0], wdown_ref.at[down_rows(0)], load.at[3]),
    ]
    chip_load = pltpu.make_async_copy(in_chip_ref.at[0], win_ref.at[2], load.at[4])
    weights = [
        remote(in_own_ref.at[0], win_ref.at[1], w_send.at[0], w_recv.at[0], partner),
        remote(
            down_own_ref.at[0], wdown_ref.at[down_rows(1)], w_send.at[1], w_recv.at[1], partner
        ),
        remote(in_chip_ref.at[0], win_ref.at[3], w_send.at[2], w_recv.at[2], partner),
        remote(
            down_own_ref.at[0], wdown_ref.at[down_rows(2)], w_send.at[3], w_recv.at[3], across
        ),
        remote(
            wdown_ref.at[down_rows(2)],
            wdown_ref.at[down_rows(3)],
            w_send.at[4],
            w_recv.at[4],
            partner,
        ),
    ]

    def dy_load(i):
        return pltpu.make_async_copy(
            dy_src_ref.at[flip(d, i, n)], dy_ref.at[rows_of(i)], load.at[10 + i]
        )

    for copy in [weights[3]] + stays + own_loads:
        copy.start()
    for i in range(n):
        dy_load(i).start()
    chip_load.start()
    for copy in weights[0:3]:
        copy.start()
    for copy in stays + own_loads:
        copy.wait()

    def take(k):
        rows = pl.ds(k * span, span)
        for q in range(group):
            i = k * group + q
            if i > 0:
                slot_copy(i).wait_recv()
                gate_copy(i).wait_recv()
            dy_load(i).wait()
            near = rows_of(i)
            line = jnp.broadcast_to(gate_ref[i, 0:1, :], (LANES, padded))
            scale = jnp.transpose(line)
            scale_ref[near, :] = scale
            scaled_ref[near, :] = (dy_ref[near, :].astype(F32) * scale[:, 0:1]).astype(BF16)
        xt_ref[:, rows] = jnp.transpose(x_ref[rows, :])

    per = share // block

    def units(first, last, chosen):
        def unit(u, carry):
            k = first + lax.div(u, 2 * per)
            b = lax.rem(u, 2 * per)
            s = chosen * 2 + lax.div(b, per)
            rows = pl.ds(pl.multiple_of(k * span, span), span)
            lanes = pl.ds(pl.multiple_of(lax.rem(b, per) * block, block), block)
            far = pl.ds(pl.multiple_of((chosen * 2 * per + b) * block, block), block)
            x = x_ref[rows, :]
            gate = mm(x, win_ref[s, 0, :, lanes])
            up = mm(x, win_ref[s, 1, :, lanes])
            grad = mm_nt(scaled_ref[rows, :], wdown_ref[far, :])
            sigma = 0.5 * jnp.tanh(0.5 * gate) + 0.5
            active = gate * sigma
            hidden_ref[rows, far] = (active * up).astype(BF16)
            dgate_ref[rows, far] = (grad * up * (sigma * (1.0 + gate * (1.0 - sigma)))).astype(
                BF16
            )
            dup_ref[rows, far] = (grad * active).astype(BF16)
            return carry

        lax.fori_loop(0, (last - first) * 2 * per, unit, 0)

    def close(k, carry):
        rows = pl.ds(pl.multiple_of(k * span, span), span)
        for j in range(width // block):
            lanes = pl.ds(j * block, block)
            total = jnp.zeros((span, block), F32)
            for s in range(4):
                far = pl.ds(s * share, share)
                total = total + mm_nt(dgate_ref[rows, far], win_ref[s, 0, lanes, :])
                total = total + mm_nt(dup_ref[rows, far], win_ref[s, 1, lanes, :])
            dx_ref[rows, lanes] = total.astype(BF16)
        for q in range(group):
            i = k * group + q

            @pl.when(i > 0)
            def _():
                dx_copy(i).start()

        for j in range(width // block):
            lanes = pl.ds(j * block, block)
            y_ref[:, lanes] = mm(hidden_ref[rows, :], wdown_ref[:, lanes])
        for q in range(group):
            i = k * group + q
            near = rows_of(i)
            y = y_ref[pl.ds(q * padded, padded), :]
            gy_ref[flip(d, i, n)] = (y * scale_ref[near, 0:1]).astype(BF16)
            dot = jnp.sum(y * dy_ref[near, :].astype(F32), axis=-1, keepdims=True)
            dg_ref[i] = jnp.transpose(jnp.broadcast_to(dot, (padded, LANES)))[0:8, :]

            @pl.when(i > 0)
            def _():
                dg_copy(i).start()

        return carry

    take(0)
    for copy in weights[0:2]:
        copy.wait_recv()
    units(0, 1, 0)
    take(1)
    units(1, 2, 0)
    take(2)
    send_chunk(3)
    units(2, 3, 0)
    chip_load.wait()
    weights[3].wait_recv()
    weights[4].start()
    weights[2].wait_recv()
    weights[4].wait_recv()
    units(0, 3, 1)
    lax.fori_loop(2, 3, close, 0)
    lax.fori_loop(0, 2, close, 0)
    take(3)
    units(3, 4, 0)
    units(3, 4, 1)
    lax.fori_loop(3, 4, close, 0)
    stores[0].start()
    keeps = [
        pltpu.make_async_copy(dx_ref.at[rows_of(0)], dx_all_ref.at[c, d], load.at[0]),
        pltpu.make_async_copy(dg_ref.at[0], dg_all_ref.at[c, d], load.at[1]),
    ]
    for copy in keeps:
        copy.start()

    def forward(first, last):
        def step(i, carry):
            dx_copy(i).wait_recv()
            dg_copy(i).wait_recv()
            hand(0, i).start()
            hand(1, i).start()
            return carry

        lax.fori_loop(first, last, step, 0)

    def grad_in(s, kind, b):
        far = pl.ds(pl.multiple_of(s * share + b * block, block), block)
        return mm(xt_ref[...], (dgate_ref, dup_ref)[kind][:, far])

    def grad_down(s, b):
        far = pl.ds(pl.multiple_of(s * share + b * block, block), block)
        return mm_tn(hidden_ref[:, far], scaled_ref[...])

    def sum_copies(j):
        return [
            remote(win_ref.at[j], land_in_ref.at[j], sum_send.at[j], sum_recv.at[j], partner),
            remote(
                wdown_ref.at[pl.ds(j * share, share)],
                land_down_ref.at[j],
                sum_send.at[2 + j],
                sum_recv.at[2 + j],
                partner,
            ),
        ]

    for copy in weights:
        copy.wait_send()

    def down_sums(s, put):
        def unit(b, carry):
            put(pl.ds(pl.multiple_of(b * block, block), block), grad_down(s, b))
            return carry

        lax.fori_loop(0, per, unit, 0)

    def in_sums(s, put):
        def unit(b, carry):
            lanes = pl.ds(pl.multiple_of(b * block, block), block)
            for kind in range(2):
                put(kind, lanes, grad_in(s, kind, b))
            return carry

        lax.fori_loop(0, per, unit, 0)

    def leave_down(j, s):
        def put(rows, value):
            near = pl.multiple_of(rows.start + j * share, block)
            wdown_ref[pl.ds(near, block), :] = value.astype(BF16)

        down_sums(s, put)
        sum_copies(j)[1].start()

    def leave_in(j, s):
        def put(kind, lanes, value):
            win_ref[j, kind, :, lanes] = value.astype(BF16)

        in_sums(s, put)
        sum_copies(j)[0].start()

    leave_down(0, 3)
    leave_down(1, 1)
    sum_copies(0)[1].wait_recv()

    def chip_down(lanes, value):
        chip_down_ref[0, lanes, :] = (value + land_down_ref[0, lanes, :].astype(F32)).astype(BF16)

    down_sums(2, chip_down)
    far_copy = remote(chip_down_ref, far_down_ref, w_send.at[5], w_recv.at[5], across)
    far_copy.start()
    for copy in keeps:
        copy.wait()
    hand(0, 0).start()
    hand(1, 0).start()
    forward(1, 2 * group)
    leave_in(0, 3)
    leave_in(1, 1)
    sum_copies(0)[0].wait_recv()

    def chip_in(kind, lanes, value):
        chip_in_ref[0, kind, :, lanes] = (
            value + land_in_ref[0, kind, :, lanes].astype(F32)
        ).astype(BF16)

    in_sums(2, chip_in)
    stores[1].start()
    for copy in sum_copies(1):
        copy.wait_recv()

    def own_in(kind, lanes, value):
        own_in_ref[0, kind, :, lanes] = value + land_in_ref[1, kind, :, lanes].astype(F32)

    def own_down(lanes, value):
        own_down_ref[0, lanes, :] = value + land_down_ref[1, lanes, :].astype(F32)

    in_sums(0, own_in)
    stores[2].start()
    down_sums(0, own_down)
    stores[3].start()
    forward(2 * group, n)

    def clear(i, carry):
        for copy in (slot_copy(i), gate_copy(i), dx_copy(i), dg_copy(i)):
            copy.wait_send()
        return carry

    lax.fori_loop(1, n, clear, 0)

    def passed(i, carry):
        hand(0, i).wait()
        hand(1, i).wait()
        return carry

    lax.fori_loop(0, n, passed, 0)
    for j in range(2):
        for copy in sum_copies(j):
            copy.wait_send()
    far_copy.wait()
    for copy in stores:
        copy.wait()


def expert_kernel(
    sources,
    padded,
    x_ref,
    dy_ref,
    gate_ref,
    *refs,
):
    weights, outs = refs[:8], refs[8:19]
    in_refs, down_refs = weights[0:4], weights[4:8]
    gy_ref, dx_ref, dg_ref = outs[0:3]
    gin_refs, gdown_refs = outs[3:7], outs[7:11]
    xt_ref, scaled_ref, scale_ref, y_acc, dx_acc, win_ref, wdown_ref = refs[19:]
    step = pl.program_id(0)
    last = pl.num_programs(0) - 1

    @pl.when(step == 0)
    def _():
        xt_ref[...] = jnp.transpose(x_ref[...])
        for s in range(sources):
            rows = pl.ds(s * padded, padded)
            line = jnp.broadcast_to(gate_ref[s, 0:1, :], (LANES, padded))
            scale = jnp.transpose(line)
            scale_ref[rows, :] = scale
            scaled_ref[rows, :] = (dy_ref[rows, :].astype(F32) * scale[:, 0:1]).astype(BF16)
        y_acc[...] = jnp.zeros_like(y_acc)
        dx_acc[...] = jnp.zeros_like(dx_acc)

    per = pl.num_programs(0) // 4
    for i in range(4):

        @pl.when(lax.div(step, per) == i)
        def _():
            win_ref[...] = in_refs[i][0]
            wdown_ref[...] = down_refs[i][0]

    x = x_ref[...]
    gate = mm(x, win_ref[0])
    up = mm(x, win_ref[1])
    sigma = 1.0 / (1.0 + jnp.exp(-gate))
    active = gate * sigma
    hidden = (active * up).astype(BF16)
    y_acc[...] += mm(hidden, wdown_ref[...])
    scaled = scaled_ref[...]
    grad_hidden = mm_nt(scaled, wdown_ref[...])
    grad_gate = (grad_hidden * up * (sigma * (1.0 + gate * (1.0 - sigma)))).astype(BF16)
    grad_up = (grad_hidden * active).astype(BF16)
    dx_acc[...] += mm_nt(grad_gate, win_ref[0]) + mm_nt(grad_up, win_ref[1])
    xt = xt_ref[...]
    part_gate = mm(xt, grad_gate).astype(BF16)
    part_up = mm(xt, grad_up).astype(BF16)
    part_down = mm_tn(hidden, scaled).astype(BF16)
    for i in range(4):

        @pl.when(lax.div(step, per) == i)
        def _():
            gin_refs[i][0, 0] = part_gate
            gin_refs[i][0, 1] = part_up
            gdown_refs[i][0] = part_down

    @pl.when(step == last)
    def _():
        for s in range(sources):
            rows = pl.ds(s * padded, padded)
            y = y_acc[rows, :]
            gy_ref[s] = (y * scale_ref[rows, 0:1]).astype(BF16)
            dot = jnp.sum(y * dy_ref[rows, :].astype(F32), axis=-1, keepdims=True)
            dg_ref[s] = jnp.transpose(jnp.broadcast_to(dot, (padded, LANES)))[0:8, :]
            dx_ref[s] = dx_acc[rows, :].astype(BF16)


def rear_kernel(n, half, padded, gathered, part, *refs):
    crossing = 0 if gathered else 1
    chip_in_refs, refs = refs[:crossing], refs[crossing:]
    gy_src_ref, tokens_ref, cotangent_ref, o_all_ref = refs[:4]
    loaded, refs = refs[4:17], refs[17:]
    stat_ref, pos_ref, small_ref, extra_ref, dg_ref = refs[:5]
    result_ref, grad_x_ref, logit_ref, grads_ref, lines_ref, norm_out_ref = refs[5:11]
    far_in_refs, refs = refs[11 : 11 + crossing], refs[11 + crossing :]
    kept, refs = refs[:13], refs[13:]
    dx_ref, h_ref, wo_ref, ub_ref, q_ref, k_ref, v_ref = kept[:7]
    lse_ref, cos_ref, sin_ref, a_ref, spread_a_ref, spread_b_ref = kept[7:]
    x_ref, dy_ref, o_ref, gy_ref, dh_ref, dzb_ref, do_ref, low_ref, row_ref = refs[:9]
    dp_ref, dk_acc, dv_acc, wo_odd_ref, pack_ref, line_ref, y_in_ref, z_in_ref = refs[9:17]
    line_in_ref, cross_ref, cross_in_ref, cross_line_ref = refs[17:21]
    da_out_ref, da_in_ref, da_own_ref, norm_ref, norm_in_ref, half_ref = refs[21:27]
    norm_line_ref, norm_all_ref, norm_cross_ref, line_low_ref = refs[27:31]
    load, fetch_sem, gy_send, gy_recv, stay, pass_send, pass_recv = refs[31:38]
    grad_send, grad_recv, line_send, line_recv, pair_send, pair_recv = refs[38:44]
    out_send, out_recv, sum_send, sum_recv, norm_send, norm_recv = refs[44:]

    def fetch(i):
        src = loaded[i]
        if i == 11:
            src = src.at[:, :, pl.ds(0, 3 * LANES)]
        if i == 12:
            src = src.at[:, :, pl.ds(4 * LANES, 2 * LANES)]
        return pltpu.make_async_copy(src, kept[i], fetch_sem.at[i])

    rows_all, width = dy_ref.shape
    blocks = rows_all // BLK
    pairs = q_ref.shape[0]
    local = pairs * LANES
    columns = n + 4
    slots = n * padded
    d, t = lax.axis_index("dp"), lax.axis_index("tensor")
    m, c = lax.div(t, 2), lax.rem(t, 2)
    partner = (d, t + 1 - 2 * c)
    across = (d, lax.rem(t + 2, 4))
    rows_half = rows_all // 2
    own = pl.multiple_of(c * local, LANES)
    own_lanes = pl.ds(own, local)
    place = pl.ds(pl.multiple_of(c * rows_half, BLK), rows_half)
    loads = [
        pltpu.make_async_copy(src, dst, load.at[i])
        for i, (src, dst) in enumerate(
            [
                (cotangent_ref.at[m], dy_ref),
                (tokens_ref.at[m, place], x_ref),
                (o_all_ref.at[:, own_lanes], o_ref),
            ]
        )
    ]
    for i in range(2):
        fetch(i).start()
    for copy in loads:
        copy.start()
    for i in range(2, 13):
        fetch(i).start()
    greet(plane_peers(n, d, t) + [partner, across])

    sum_copies = [
        remote(src, land, sum_send.at[0], sum_recv.at[0], across)
        for src, land in zip(chip_in_refs, far_in_refs)
    ]
    for copy in sum_copies:
        copy.start()

    def give(j):
        s = lax.rem(d + j, n)
        return remote(gy_src_ref.at[s], gy_ref.at[c, d], gy_send.at[j], gy_recv.at[j], (s, t))

    def hand(j):
        block = gy_ref.at[c, lax.rem(d + n - j, n)]
        return remote(block, block, pass_send.at[j], pass_recv.at[j], partner)

    keep = pltpu.make_async_copy(gy_src_ref.at[d], gy_ref.at[c, d], stay.at[0])
    keep.start()

    def give_start(j, carry):
        give(j).start()
        return carry

    lax.fori_loop(1, n, give_start, 0)

    def collect():
        keep.wait()
        hand(0).start()

        def step(j, carry):
            give(j).wait_recv()
            hand(j).start()
            return carry

        lax.fori_loop(1, n, step, 0)

    def settle():
        def step(j, carry):
            hand(j).wait_recv()
            return carry

        lax.fori_loop(0, n, step, 0)

    row_ref[...] = jnp.zeros_like(row_ref)
    for copy in loads:
        copy.wait()
    for i in range(3):
        fetch(i).wait()

    gain_moe = extra_ref[columns + 5 : columns + 6, :]
    vec0 = extra_ref[columns + 6 : columns + 7, :]
    vec1 = extra_ref[columns + 7 : columns + 8, :]
    group = max(1, min(n, (1024 if slots <= 1024 else 512) // padded))
    span = group * padded

    def combine(wheres, ref, lines=None):
        total = jnp.zeros((BLK, width), F32)
        entries = [jnp.zeros((BLK, 1), F32) for _ in wheres]
        slot = lax.broadcasted_iota(jnp.int32, (BLK, span), 1)
        for side in range(2):
            for first in range(0, n, group):
                start = side * slots + first * padded
                hots = [slot == where - start for where in wheres]
                hot = jnp.where(hots[0] | hots[1], 1.0, 0.0).astype(BF16)
                block = ref[side, first : first + group].reshape(span, width)
                total = total + mm(hot, block)
                if lines is not None:
                    line = jnp.concatenate(
                        [lines[side, first + e, 0:1, :] for e in range(group)], axis=1
                    )
                    entries = [
                        entry + jnp.sum(jnp.where(one, line, 0.0), axis=-1, keepdims=True)
                        for entry, one in zip(entries, hots)
                    ]
        return total, entries

    def facts(rows):
        lane = lane_ids(BLK)
        stats = stat_ref[rows, :]
        values = [stats[:, j : j + 1] for j in range(7)]
        e0, e1 = stats[:, 7:8].astype(jnp.int32), stats[:, 8:9].astype(jnp.int32)
        wheres = []
        places = pos_ref[rows, :]
        for e in (e0, e1):
            place = pick(lane == e, places).astype(jnp.int32)
            side = (place >= half).astype(jnp.int32)
            where = side * (slots - half) + e * padded + place
            wheres.append(jnp.where(e < n, where, -1))
        g0, g1 = values[0:2]

        def named(number):
            return jnp.where(e0 == number, g0, 0.0) + jnp.where(e1 == number, g1, 0.0)

        copied, first, second = named(n + 1), named(n + 2), named(n + 3)
        on_u = copied + first * values[2] + second * values[4]
        return values, e0, e1, wheres, first, second, on_u

    def back(i, carry):
        rows = pl.ds(pl.multiple_of(i * BLK, BLK), BLK)
        values, e0, e1, wheres, first, second, on_u = facts(rows)
        g0, g1, a00, a01, a10, a11, r = values
        lane = lane_ids(BLK)
        grads, (f0, f1) = combine(wheres, dx_ref, dg_ref)
        h = h_ref[rows, :]
        normed = h * r
        u = normed * gain_moe
        dy = dy_ref[rows, :].astype(F32)
        s_u = jnp.sum(dy * u, axis=-1, keepdims=True)
        s_0 = jnp.sum(dy * vec0, axis=-1, keepdims=True)
        s_1 = jnp.sum(dy * vec1, axis=-1, keepdims=True)

        def other(e):
            value = jnp.where(e == n + 1, s_u, 0.0)
            value = jnp.where(e == n + 2, a00 * s_u + a01 * s_0, value)
            return jnp.where(e == n + 3, a10 * s_u + a11 * s_1, value)

        dg0, dg1 = f0 + other(e0), f1 + other(e1)
        mean = g0 * dg0 + g1 * dg1
        dl = jnp.where(lane == e0, g0 * (dg0 - mean), 0.0) + jnp.where(
            lane == e1, g1 * (dg1 - mean), 0.0
        )
        turned = jnp.transpose(dl)
        logit_ref[m, :, rows] = turned[0 : logit_ref.shape[1], :]
        d00, d01 = first * s_u, first * s_0
        d10, d11 = second * s_u, second * s_1
        m0 = a00 * d00 + a01 * d01
        m1 = a10 * d10 + a11 * d11
        low = dl
        for j, value in enumerate(
            [a00 * (d00 - m0), a01 * (d01 - m0), a10 * (d10 - m1), a11 * (d11 - m1)]
        ):
            low = jnp.where(lane == columns + j, value, low)
        low = low.astype(BF16)
        low_ref[rows, :] = low
        du = grads + mm_nt(low, small_ref[...]) + on_u * dy
        row_ref[0:1, :] += jnp.sum(du * normed, axis=0, keepdims=True)
        row_ref[1:2, :] += jnp.sum((first * a01) * dy, axis=0, keepdims=True)
        row_ref[2:3, :] += jnp.sum((second * a11) * dy, axis=0, keepdims=True)
        dn = du * gain_moe
        dh = dy + r * (dn - normed * jnp.mean(dn * normed, axis=-1, keepdims=True))

        @pl.when(lax.div(i, blocks // 2) == c)
        def _():
            near = pl.multiple_of(i * BLK - c * rows_half, BLK)
            dh_ref[pl.ds(near, BLK), :] = dh

        dzb = dh.astype(BF16)
        dzb_ref[rows, :] = dzb
        do_ref[rows, :] = mm(dzb, wo_ref[:, own_lanes]).astype(BF16)
        return carry

    lax.fori_loop(0, blocks, back, 0)
    logit_copy = remote(
        logit_ref.at[m], logit_ref.at[m], pair_send.at[0], pair_recv.at[0], across
    )
    logit_copy.start()

    fetch(3).wait()
    grad_wo = mm_tn(dzb_ref[...], o_ref[...])
    pack_ref[0, :, 3 * LANES : 4 * LANES] = grad_wo[:, 0:LANES].astype(BF16)
    pack_ref[1, :, 3 * LANES : 4 * LANES] = grad_wo[:, LANES : 2 * LANES].astype(BF16)
    wo_odd_ref[...] = grad_wo[:, 2 * LANES : 3 * LANES]
    lines = mm_tn(ub_ref[...], low_ref[...])
    lane_of = lax.broadcasted_iota(jnp.int32, (width, LANES), 1)
    turned = jnp.concatenate([row_ref[...], jnp.zeros((LANES - 8, width), F32)], axis=0)
    turned = jnp.transpose(turned)
    for j in range(3):
        lines = jnp.where(lane_of == columns + 5 + j, turned[:, j : j + 1], lines)
    line_ref[...] = lines

    def slab(owner):
        return pl.ds(pl.multiple_of(owner * part, part), part)

    ring = n // 2
    y_own = lax.rem(d, 2)
    beside = (d + 1 - 2 * y_own, t)
    z_own = lax.div(d, 2)
    wide_lanes = (pl.ds(0, 3 * LANES), pl.ds(3 * LANES, 3 * LANES))

    def y_copy(s, stage, z):
        lanes = wide_lanes[stage]
        return remote(
            pack_ref.at[s, slab(2 * z + 1 - y_own), lanes],
            y_in_ref.at[s, z, :, lanes],
            grad_send.at[stage, s, z],
            grad_recv.at[stage, s, z],
            beside,
        )

    def z_copy(s, stage, j):
        lanes = wide_lanes[stage]
        z = lax.rem(z_own + j, ring)
        return remote(
            pack_ref.at[s, slab(2 * z + y_own), lanes],
            z_in_ref.at[s, j, :, lanes],
            grad_send.at[2 + stage, s, j],
            grad_recv.at[2 + stage, s, j],
            (2 * z + y_own, t),
        )

    def y_start(s, stage):
        for z in range(ring):
            y_copy(s, stage, z).start()

    def z_start(s, stage):
        lanes = wide_lanes[stage]
        for z in range(ring):
            y_copy(s, stage, z).wait()
            rows = slab(2 * z + y_own)
            value = pack_ref[s, rows, lanes].astype(F32) + y_in_ref[s, z, :, lanes].astype(F32)
            pack_ref[s, rows, lanes] = value.astype(BF16)
        for j in range(1, ring):
            z_copy(s, stage, j).start()

    def line_copy(j):
        e = lax.rem(d + j, n)
        return remote(
            line_low_ref.at[slab(e), :],
            line_in_ref.at[d],
            line_send.at[j],
            line_recv.at[j],
            (e, t),
        )

    head = half_mask(BLK)

    def attend_back(p):
        dk_acc[...] = jnp.zeros_like(dk_acc)
        dv_acc[...] = jnp.zeros_like(dv_acc)
        dq = []
        for i in range(blocks):
            rows = pl.ds(i * BLK, BLK)
            seen = pl.ds(0, (i + 1) * BLK)
            lanes = pl.ds(pl.multiple_of(p * LANES, LANES), LANES)
            q, do = q_ref[p, rows, :], do_ref[rows, lanes]
            k, v = k_ref[p, seen, :], v_ref[p, seen, :]
            zero = jnp.zeros_like(q)
            parts = []
            dk, dv = dk_acc[seen, :], dv_acc[seen, :]
            for side in range(2):
                chosen = head if side == 0 else jnp.logical_not(head)
                qm, dom = jnp.where(chosen, q, zero), jnp.where(chosen, do, zero)
                prob = jnp.exp(mm_nt(k, qm) - lse_ref[2 * p + side, 0:1, rows])
                grad_prob = mm_nt(v, dom)
                total = jnp.sum(prob * grad_prob, axis=0, keepdims=True)
                grad_score = (prob * (grad_prob - total)).astype(BF16)
                dv = dv + mm(prob.astype(BF16), dom)
                dk = dk + mm(grad_score, qm)
                parts.append(mm_tn(grad_score, k))
            dk_acc[seen, :] = dk
            dv_acc[seen, :] = dv
            value = jnp.where(head, parts[0], parts[1]) * (HD**-0.5)
            dq.append(turn(value, cos_ref[rows, :], -sin_ref[rows, :]))
        return (
            jnp.concatenate(dq, axis=0),
            turn(dk_acc[...], cos_ref[...], -sin_ref[...]),
            dv_acc[...],
        )

    for i in range(4, 11):
        fetch(i).wait()
    dq, dk, dv = attend_back(2)
    wide = half_mask(rows_all)
    odd = [
        (jnp.where(wide, dq, swap_halves(dk)), jnp.where(wide, dv, 0.0)),
        (jnp.where(wide, swap_halves(dq), dk), jnp.where(wide, swap_halves(dv), 0.0)),
    ]
    tall = half_mask(width)
    for s in range(2):
        for j in range(2):
            dp_ref[s, :, (3 + j) * LANES : (4 + j) * LANES] = odd[s][j].astype(BF16)
    for s in range(2):
        pack_ref[s, :, 4 * LANES : 5 * LANES] = mm_tn(
            a_ref[...], dp_ref[s, :, 3 * LANES : 4 * LANES]
        ).astype(BF16)
        last = mm_tn(a_ref[...], dp_ref[s, :, 4 * LANES : 5 * LANES])
        side = wo_odd_ref[...]
        side = swap_halves(side) if s == 0 else side
        pack_ref[s, :, 5 * LANES : 6 * LANES] = jnp.where(tall, last, side).astype(BF16)
    if not gathered:
        y_start(0, 1)
        y_start(1, 1)

    def shard_step(i, carry):
        s = lax.rem(m + 1 + i, 2)
        for j, value in enumerate(attend_back(s)):
            dp_ref[s, :, j * LANES : (j + 1) * LANES] = value.astype(BF16)
        for j in range(3):
            lanes = pl.ds(j * LANES, LANES)
            pack_ref[s, :, lanes] = mm_tn(a_ref[...], dp_ref[s, :, lanes]).astype(BF16)
        if not gathered:
            y_start(s, 0)
        return carry

    lax.fori_loop(0, 2, shard_step, 0)
    collect()
    if not gathered:
        z_start(0, 1)
        z_start(1, 1)

        def send_line(j, carry):
            line_copy(j).start()
            return carry

        line_low_ref[...] = line_ref[...].astype(BF16)
        lax.fori_loop(1, n, send_line, 0)
        line_in_ref[d] = line_low_ref[slab(d), :]

    def publish(kind, out_ref):
        block = out_ref.at[m, place]
        copies = [
            remote(half_ref.at[kind], block, out_send.at[kind, 0], out_recv.at[kind, 0], across),
            remote(half_ref.at[kind], block, out_send.at[kind, 1], out_recv.at[kind, 1], partner),
            pltpu.make_async_copy(half_ref.at[kind], block, stay.at[1 + kind]),
        ]
        for copy in copies:
            copy.start()
        block = out_ref.at[1 - m, place]
        relay = remote(block, block, out_send.at[kind, 2], out_recv.at[kind, 2], partner)
        return copies, relay

    settle()

    def results(i, carry):
        rows = pl.ds(pl.multiple_of(i * BLK, BLK), BLK)
        far = pl.ds(pl.multiple_of(c * rows_half + i * BLK, BLK), BLK)
        values, e0, e1, wheres, first, second, on_u = facts(far)
        sums, _ = combine(wheres, gy_ref)
        h = h_ref[far, :]
        u = h * values[6] * gain_moe
        result = h + (sums + on_u * u + (first * values[3]) * vec0 + (second * values[5]) * vec1)
        half_ref[1, rows, :] = result.astype(BF16)
        return carry

    lax.fori_loop(0, rows_half // BLK, results, 0)
    result_copies, result_relay = publish(1, result_ref)

    def da_rows(start):
        rows = pl.ds(pl.multiple_of(start, BLK), BLK)
        total = jnp.zeros((BLK, width), F32)
        for s in range(2):
            total = total + mm_nt(dp_ref[s, rows, 0 : 3 * LANES], spread_a_ref[s])
            total = total + mm_nt(dp_ref[s, rows, 3 * LANES : 5 * LANES], spread_b_ref[s])
        return total

    fetch(11).wait()
    fetch(12).wait()

    def da_other(i, carry):
        rows = pl.ds(pl.multiple_of(i * BLK, BLK), BLK)
        da_out_ref[rows, :] = da_rows((1 - c) * rows_half + i * BLK).astype(BF16)
        return carry

    lax.fori_loop(0, rows_half // BLK, da_other, 0)
    da_copy = remote(da_out_ref, da_in_ref, pair_send.at[1], pair_recv.at[1], partner)
    da_copy.start()

    def da_own(i, carry):
        rows = pl.ds(pl.multiple_of(i * BLK, BLK), BLK)
        da_own_ref[rows, :] = da_rows(c * rows_half + i * BLK)
        return carry

    lax.fori_loop(0, rows_half // BLK, da_own, 0)
    if not gathered:
        z_start(1 - m, 0)
    da_copy.wait()
    gain_attn = extra_ref[columns + 4 : columns + 5, :]
    norm_ref[...] = jnp.zeros_like(norm_ref)

    def finish(i, carry):
        rows = pl.ds(pl.multiple_of(i * BLK, BLK), BLK)
        x = x_ref[rows, :].astype(F32)
        r = lax.rsqrt(jnp.mean(x * x, axis=-1, keepdims=True) + EPSILON)
        normed = x * r
        da = da_own_ref[rows, :] + da_in_ref[rows, :].astype(F32)
        norm_ref[0:1, :] += jnp.sum(da * normed, axis=0, keepdims=True)
        dn = da * gain_attn
        grad = dh_ref[rows, :] + r * (dn - normed * jnp.mean(dn * normed, axis=-1, keepdims=True))
        half_ref[0, rows, :] = grad.astype(BF16)
        return carry

    lax.fori_loop(0, rows_half // BLK, finish, 0)
    norm_copy = remote(norm_ref, norm_in_ref, pair_send.at[2], pair_recv.at[2], partner)
    norm_copy.start()

    grad_x_copies, grad_x_relay = publish(0, grad_x_ref)
    if not gathered:
        z_start(m, 0)

    norm_copy.wait()
    norm = norm_ref[...] + norm_in_ref[...]
    if gathered:
        turned = jnp.concatenate([norm, jnp.zeros((LANES - 8, width), F32)], axis=0)
        turned = jnp.transpose(turned)
        line_ref[...] = jnp.where(lane_of == columns + 4, turned[:, 0:1], line_ref[...])
        norm_out_ref[...] = jnp.zeros_like(norm_out_ref)
        packs = [
            pltpu.make_async_copy(pack_ref, grads_ref, load.at[0]),
            pltpu.make_async_copy(line_ref, lines_ref, load.at[1]),
        ]
        for copy in packs:
            copy.start()
        for copy in packs:
            copy.wait()
    else:
        norm_line_ref[...] = jnp.zeros_like(norm_line_ref)
        for j in range(width // LANES):
            norm_line_ref[j : j + 1, :] = norm[0:1, j * LANES : (j + 1) * LANES]

        def norm_give(j):
            e = lax.rem(d + j, n)
            return remote(
                norm_line_ref, norm_all_ref.at[d], norm_send.at[j], norm_recv.at[j], (e, t)
            )

        def norm_start(j, carry):
            norm_give(j).start()
            return carry

        lax.fori_loop(1, n, norm_start, 0)
        norm_all_ref[d] = norm_line_ref[...]

        def norm_wait(j, carry):
            norm_give(j).wait()
            return carry

        lax.fori_loop(1, n, norm_wait, 0)
        value = norm_all_ref[0]
        for e in range(1, n):
            value = value + norm_all_ref[e]
        norm_cross_ref[0] = value
        norm_cross_copy = remote(
            norm_cross_ref.at[0], norm_cross_ref.at[1], pair_send.at[5], pair_recv.at[5], across
        )
        norm_cross_copy.start()
        def arrive_lines(j, carry):
            line_copy(j).wait()
            return carry

        lax.fori_loop(1, n, arrive_lines, 0)
        value = line_in_ref[0].astype(F32)
        for e in range(1, n):
            value = value + line_in_ref[e].astype(F32)
        cross_line_ref[0] = value
        cross_line_copy = remote(
            cross_line_ref.at[0], cross_line_ref.at[1], pair_send.at[4], pair_recv.at[4], across
        )
        cross_line_copy.start()
        for s, stage in ((0, 1), (1, 1), (1 - m, 0)):
            for j in range(1, ring):
                z_copy(s, stage, j).wait()

        def total(s):
            value = pack_ref[s, slab(d), :].astype(F32)
            for j in range(1, ring):
                value = value + z_in_ref[s, j].astype(F32)
            return value

        cross_ref[...] = total(1 - m).astype(BF16)
        cross_copy = remote(cross_ref, cross_in_ref, pair_send.at[3], pair_recv.at[3], across)
        cross_copy.start()
        for j in range(1, ring):
            z_copy(m, 0, j).wait()
        grads_ref[...] = total(m)
        result_copies[0].wait_recv()
        result_relay.start()

        cross_copy.wait()
        grads_ref[...] += cross_in_ref[...].astype(F32)
        cross_line_copy.wait()
        lines_ref[...] = cross_line_ref[0] + cross_line_ref[1]
        norm_cross_copy.wait()
        norm_out_ref[...] = norm_cross_ref[0] + norm_cross_ref[1]

    grad_x_copies[0].wait_recv()
    grad_x_relay.start()
    if gathered:
        result_copies[0].wait_recv()
        result_relay.start()
    for copies, relay in ((grad_x_copies, grad_x_relay), (result_copies, result_relay)):
        copies[0].wait_send()
        copies[1].wait()
        copies[2].wait()
        relay.wait()
    logit_copy.wait()

    for copy in sum_copies:
        copy.wait()

    def clear(j, carry):
        give(j).wait_send()
        return carry

    lax.fori_loop(1, n, clear, 0)

    def passed(j, carry):
        hand(j).wait_send()
        return carry

    lax.fori_loop(0, n, passed, 0)


def last_kernel(
    part,
    columns,
    results_ref,
    grad_x_ref,
    own_in_ref,
    far_in_ref,
    own_down_ref,
    far_down_ref,
    logit_ref,
    grads_ref,
    lines_ref,
    norm_ref,
    results_out,
    grad_x_out,
    in_out,
    down_out,
    logit_out,
    attn_out,
    moe_out,
    heads_out,
    out_out,
    router_out,
    const_out,
    vec_out,
):
    results_out[...] = results_ref[...]
    grad_x_out[...] = grad_x_ref[...]
    in_out[...] = own_in_ref[...] + far_in_ref[...].astype(F32)
    down_out[...] = own_down_ref[...] + far_down_ref[...].astype(F32)

    @pl.when(pl.program_id(0) == 0)
    def _():
        for m in range(2):
            logit_out[:, m, :] = logit_ref[m, 0:columns, :]
        firsts = [grads_ref[:, j * LANES : (j + 1) * LANES] for j in range(4)]
        odds = []
        for j in range(2):
            both = grads_ref[:, (4 + j) * LANES : (5 + j) * LANES]
            odds.extend([both, swap_halves(both)])
        for j in range(3):
            heads_out[j, :, 0:LANES] = firsts[j]
            heads_out[j, :, LANES : LANES + HD] = odds[j][:, 0:HD]
        spare = jnp.zeros((LANES - part, 2 * LANES), F32)
        rows = jnp.concatenate([firsts[3], odds[3]], axis=1)
        turned = jnp.transpose(jnp.concatenate([rows, spare], axis=0))
        out_out[...] = turned[0 : LANES + HD, 0:part]
        lines = jnp.concatenate([lines_ref[...], spare[:, 0:LANES]], axis=0)
        lines = jnp.transpose(lines)[:, 0:part]
        router_out[...] = lines[0:columns]
        const_out[...] = lines[columns : columns + 4]
        norm = jnp.concatenate([norm_ref[...], jnp.zeros((LANES - 8, LANES), F32)], axis=0)
        norm = jnp.transpose(norm)
        place = lax.broadcasted_iota(jnp.int32, (LANES, part), 0)
        wanted = lax.broadcasted_iota(jnp.int32, (LANES, part), 1) + lax.axis_index("dp") * part
        total = jnp.zeros((1, part), F32)
        for j in range(results_ref.shape[2] // LANES):
            chosen = jnp.where(place + j * LANES == wanted, norm[:, j : j + 1], 0.0)
            total = total + jnp.sum(chosen, axis=0, keepdims=True)
        attn_out[...] = total
        moe_out[...] = lines[columns + 5 : columns + 6]
        vec_out[...] = lines[columns + 6 : columns + 8]


def across_chips(value):
    return lax.ppermute(value, "tensor", [(0, 2), (2, 0), (1, 3), (3, 1)])


def across_cores(value):
    return lax.ppermute(value, "tensor", [(0, 1), (1, 0), (2, 3), (3, 2)])


def body(
    tokens,
    cotangent,
    prev_logits,
    routes,
    norm_attn,
    norm_moe,
    w_qkv,
    w_out,
    w_router,
    w_const,
    const_vec,
    w_in,
    w_down,
):
    rows, width = tokens.shape[1:]
    n = lax.axis_size("dp")
    experts = n
    columns = prev_logits.shape[2]
    capacity = 4 * max(1, 3 * rows // (4 * (experts + 4)))
    half = capacity // 2
    padded = -(-half // 16) * 16
    share = w_qkv.shape[2]
    local = 2 * share
    part = w_qkv.shape[1]
    t = lax.axis_index("tensor")
    m, c = t // 2, t % 2

    cosine, sine = (jnp.asarray(v) for v in rope_constants())
    pairs = local // LANES

    tinies = [w_router.T, w_const.T, norm_attn[None], norm_moe[None], const_vec]
    gathered = part % 16 != 0
    if gathered:
        wo_rows = w_out.T
        tiny = jnp.concatenate(
            tinies + [jnp.zeros((LANES - columns - 8, part), BF16)], axis=0
        )
        packed = jnp.concatenate(
            [w_qkv[i, :, :LANES] for i in range(3)]
            + [wo_rows[:, :LANES]]
            + [w_qkv[i, :, LANES:] for i in range(3)]
            + [wo_rows[:, LANES:], tiny.T],
            axis=1,
        )
    if gathered:
        packed = lax.all_gather(packed, "dp", axis=0, tiled=True)
        other = across_chips(packed)
        tinies = [jnp.where(m == 0, jnp.stack([packed, other]), jnp.stack([other, packed]))]
    late = [
        struct((n, padded, width), BF16),
        struct((n, 8, padded), F32),
        struct((LANES, width), F32),
    ]
    early = [
        struct((rows, width), BF16),
        struct((pairs, rows, LANES), BF16),
        struct((pairs, rows, LANES), BF16),
        struct((pairs, rows, LANES), BF16),
        struct((rows, width), BF16),
        struct((8, 8, rows), F32),
        struct((rows, LANES), F32),
        struct((width, width), BF16),
        struct((width, LANES), BF16),
        struct((2, width, 7 * LANES), BF16),
        struct((rows, width), F32),
        struct((rows, width), BF16),
        struct((rows, LANES), F32),
    ]
    landing = [struct((n, padded, width), BF16), struct(w_in.shape, BF16)]
    dma = pltpu.SemaphoreType.DMA
    outs = pl.pallas_call(
        functools.partial(front_kernel, n, half, padded, gathered, len(early)),
        out_shape=late + early + landing,
        in_specs=[aspec()] * 3 + [vspec()] * 5 + [aspec()] + [vspec()] * len(tinies),
        out_specs=[vspec()] * len(late) + [aspec()] * (len(early) + len(landing)),
        scratch_shapes=[pltpu.VMEM(o.shape, o.dtype) for o in early]
        + [
            pltpu.VMEM((rows, width), BF16),
            pltpu.VMEM((rows, width), BF16),
            pltpu.VMEM((2, rows), jnp.int32),
            pltpu.VMEM((LANES, rows), F32),
            pltpu.VMEM((LANES, rows), F32),
            pltpu.VMEM((n, padded, width), BF16),
            dma((3,)),
            dma((8, n // 2)),
            dma((8, n // 2)),
            dma((n,)),
            dma((n,)),
            dma((1,)),
            dma((pairs + 1,)),
            dma((pairs + 1,)),
            dma((1,)),
            dma((1,)),
            dma((len(early),)),
        ],
        compiler_params=pltpu.CompilerParams(
            collective_id=0, has_side_effects=True, vmem_limit_bytes=VMEM_LIMIT
        ),
        cost_estimate=pl.CostEstimate(
            flops=60_000_000_000, bytes_accessed=60_000_000, transcendentals=0
        ),
    )(
        tokens,
        cotangent,
        jnp.swapaxes(routes, 1, 2),
        jnp.transpose(prev_logits, (2, 0, 1)),
        w_qkv,
        w_out,
        cosine,
        sine,
        w_in,
        *tinies,
    )
    slots, gate_slots, extra, a, q, k, v, o_all, lse, pos = outs[:10]
    wo_all, small_all, spread, h, ub, stats, dy_arrived, in_x = outs[10:]

    hidden_width = w_in.shape[3]
    slots_all = experts * padded
    if gathered:
        in_x, down_x = across_chips(w_in), across_chips(w_down)
        in_c, down_c = across_cores(w_in), across_cores(w_down)
        in_d, down_d = across_cores(in_x), across_cores(down_x)
        chunk = min(256 if slots_all <= 1024 else 128, hidden_width)
        per = hidden_width // chunk

        def in_map(i):
            return lambda f: (0, 0, 0, jnp.clip(f - per * i, 0, per - 1))

        def down_map(i):
            return lambda f: (0, jnp.clip(f - per * i, 0, per - 1), 0)

        in_blocks = [pl.BlockSpec((1, 2, width, chunk), in_map(i)) for i in range(4)]
        down_blocks = [pl.BlockSpec((1, chunk, width), down_map(i)) for i in range(4)]
        expert_outs = (
            [
                struct((n, padded, width), BF16),
                struct((n, padded, width), BF16),
                struct((n, 8, padded), F32),
            ]
            + [struct(w_in.shape, BF16)] * 4
            + [struct(w_down.shape, BF16)] * 4
        )

        def whole(shape):
            return pl.BlockSpec(
                shape, lambda f: (0,) * len(shape), pipeline_mode=pl.Buffered(1)
            )

        parts = pl.pallas_call(
            functools.partial(expert_kernel, n, padded),
            grid=(4 * per,),
            out_shape=expert_outs,
            in_specs=[
                whole((slots_all, width)),
                whole((slots_all, width)),
                whole((n, 8, padded)),
            ]
            + in_blocks
            + down_blocks,
            out_specs=[
                whole((n, padded, width)),
                whole((n, padded, width)),
                whole((n, 8, padded)),
            ]
            + in_blocks
            + down_blocks,
            scratch_shapes=[
                pltpu.VMEM((width, slots_all), BF16),
                pltpu.VMEM((slots_all, width), BF16),
                pltpu.VMEM((slots_all, LANES), F32),
                pltpu.VMEM((slots_all, width), F32),
                pltpu.VMEM((slots_all, width), F32),
                pltpu.VMEM((2, width, chunk), BF16),
                pltpu.VMEM((chunk, width), BF16),
            ],
            compiler_params=pltpu.CompilerParams(vmem_limit_bytes=VMEM_LIMIT),
            cost_estimate=pl.CostEstimate(
                flops=18 * slots_all * width * 4 * hidden_width,
                bytes_accessed=30_000_000,
                transcendentals=0,
            ),
        )(
            lax.all_to_all(slots, "dp", split_axis=0, concat_axis=0, tiled=True).reshape(
                slots_all, width
            ),
            dy_arrived.reshape(slots_all, width),
            lax.all_to_all(gate_slots, "dp", split_axis=0, concat_axis=0, tiled=True),
            w_in,
            in_c,
            in_x,
            in_d,
            w_down,
            down_c,
            down_x,
            down_d,
        )
        gy, dx, dg = parts[0:3]
        gin, gdown = parts[3:7], parts[7:11]

        def everywhere(value):
            value = lax.all_to_all(value, "dp", split_axis=0, concat_axis=0, tiled=True)
            other = across_cores(value)
            return jnp.where(c == 0, jnp.stack([value, other]), jnp.stack([other, value]))

        dx_all, dg_all = everywhere(dx), everywhere(dg)

        def total(own, core, chip, diagonal):
            chip = (chip.astype(F32) + across_cores(diagonal).astype(F32)).astype(BF16)
            own = own.astype(F32) + across_cores(core).astype(F32)
            return own + across_chips(chip).astype(F32)

        grad_in, grad_down = total(*gin), total(*gdown)
        chip_in = []
    else:
        gy, own_in, own_down, chip_in, far_down, dx_all, dg_all = pl.pallas_call(
            functools.partial(expert_exchange_kernel, n, padded),
            out_shape=[
                struct((n, padded, width), BF16),
                struct(w_in.shape, F32),
                struct(w_down.shape, F32),
                struct(w_in.shape, BF16),
                struct(w_down.shape, BF16),
                struct((2, n, padded, width), BF16),
                struct((2, n, 8, padded), F32),
            ],
            in_specs=[aspec()] * 6,
            out_specs=[aspec()] * 7,
            scratch_shapes=[
                pltpu.VMEM((n, padded, width), BF16),
                pltpu.VMEM(w_in.shape, F32),
                pltpu.VMEM(w_down.shape, F32),
                pltpu.VMEM(w_in.shape, BF16),
                pltpu.VMEM((slots_all, width), BF16),
                pltpu.VMEM((width, slots_all), BF16),
                pltpu.VMEM((slots_all, width), BF16),
                pltpu.VMEM((slots_all, width), BF16),
                pltpu.VMEM((slots_all, LANES), F32),
                pltpu.VMEM((n, 8, padded), F32),
                pltpu.VMEM((4, 2, width, hidden_width), BF16),
                pltpu.VMEM((4 * hidden_width, width), BF16),
                pltpu.VMEM((slots_all, 4 * hidden_width), BF16),
                pltpu.VMEM((slots_all, 4 * hidden_width), BF16),
                pltpu.VMEM((slots_all, 4 * hidden_width), BF16),
                pltpu.VMEM((slots_all // 4, width), F32),
                pltpu.VMEM((slots_all, width), BF16),
                pltpu.VMEM((n, 8, padded), F32),
                pltpu.VMEM((2,) + w_in.shape[1:], BF16),
                pltpu.VMEM((2,) + w_down.shape[1:], BF16),
                pltpu.VMEM(w_down.shape, BF16),
                dma((10 + n,)),
                dma((n,)),
                dma((n,)),
                dma((n,)),
                dma((n,)),
                dma((n,)),
                dma((n,)),
                dma((n,)),
                dma((n,)),
                dma((2, n)),
                dma((2, n)),
                dma((4,)),
                dma((4,)),
                dma((6,)),
                dma((6,)),
                dma((4,)),
            ],
            compiler_params=pltpu.CompilerParams(
                collective_id=2, has_side_effects=True, vmem_limit_bytes=VMEM_LIMIT
            ),
            cost_estimate=pl.CostEstimate(
                flops=60_000_000_000, bytes_accessed=40_000_000, transcendentals=0
            ),
        )(
            slots,
            gate_slots,
            dy_arrived,
            w_in,
            in_x,
            w_down,
        )
        chip_in = [chip_in]

    groups = 6 * LANES
    logit_rows = -(-columns // 8) * 8
    rear_outs = [
        struct((2, logit_rows, rows), F32),
        struct((2, width, groups), BF16) if gathered else struct((part, groups), F32),
        struct((width if gathered else part, LANES), F32),
        struct((8, LANES), F32),
    ]
    half_rows = rows // 2
    spread_n = 1 if gathered else n // 2
    line_n = 1 if gathered else n
    kept = [
        struct((2, n, padded, width), BF16),
        struct((rows, width), F32),
        struct((width, width), BF16),
        struct((rows, width), BF16),
        struct((pairs, rows, LANES), BF16),
        struct((pairs, rows, LANES), BF16),
        struct((pairs, rows, LANES), BF16),
        struct((8, 8, rows), F32),
        struct((rows, LANES), F32),
        struct((rows, LANES), F32),
        struct((rows, width), BF16),
        struct((2, width, 3 * LANES), BF16),
        struct((2, width, 2 * LANES), BF16),
    ]
    results, input_grads, logits, grads, lines, norm_line, *far_in = pl.pallas_call(
        functools.partial(rear_kernel, n, half, padded, gathered, part),
        out_shape=[struct((2, rows, width), BF16)] * 2
        + rear_outs
        + [struct(w_in.shape, BF16)] * len(chip_in),
        in_specs=[aspec()] * (len(chip_in) + 4 + len(kept)) + [vspec()] * 5,
        out_specs=[aspec()] * 2
        + [vspec()]
        + [aspec() if gathered else vspec()] * 2
        + [vspec()]
        + [aspec()] * len(chip_in),
        scratch_shapes=[pltpu.VMEM(o.shape, o.dtype) for o in kept]
        + [
            pltpu.VMEM((half_rows, width), BF16),
            pltpu.VMEM((rows, width), BF16),
            pltpu.VMEM((rows, local), BF16),
            pltpu.VMEM((2, n, padded, width), BF16),
            pltpu.VMEM((half_rows, width), F32),
            pltpu.VMEM((rows, width), BF16),
            pltpu.VMEM((rows, local), BF16),
            pltpu.VMEM((rows, LANES), BF16),
            pltpu.VMEM((8, width), F32),
            pltpu.VMEM((2, rows, 5 * LANES), BF16),
            pltpu.VMEM((rows, LANES), F32),
            pltpu.VMEM((rows, LANES), F32),
            pltpu.VMEM((width, LANES), F32),
            pltpu.VMEM((2, width, groups), BF16),
            pltpu.VMEM((width, LANES), F32),
            pltpu.VMEM((2, spread_n, part, groups), BF16),
            pltpu.VMEM((2, spread_n, part, groups), BF16),
            pltpu.VMEM((line_n, part, LANES), BF16),
            pltpu.VMEM((part, groups), BF16),
            pltpu.VMEM((part, groups), BF16),
            pltpu.VMEM((2, part, LANES), F32),
            pltpu.VMEM((half_rows, width), BF16),
            pltpu.VMEM((half_rows, width), BF16),
            pltpu.VMEM((half_rows, width), F32),
            pltpu.VMEM((8, width), F32),
            pltpu.VMEM((8, width), F32),
            pltpu.VMEM((2, half_rows, width), BF16),
            pltpu.VMEM((8, LANES), F32),
            pltpu.VMEM((line_n, 8, LANES), F32),
            pltpu.VMEM((2, 8, LANES), F32),
            pltpu.VMEM((width, LANES), BF16),
            dma((3,)),
            dma((len(kept),)),
            dma((n,)),
            dma((n,)),
            dma((3,)),
            dma((n,)),
            dma((n,)),
            dma((4, 2, n // 2)),
            dma((4, 2, n // 2)),
            dma((n,)),
            dma((n,)),
            dma((6,)),
            dma((6,)),
            dma((2, 3)),
            dma((2, 3)),
            dma((1,)),
            dma((1,)),
            dma((n,)),
            dma((n,)),
        ],
        compiler_params=pltpu.CompilerParams(
            collective_id=1, has_side_effects=True, vmem_limit_bytes=VMEM_LIMIT
        ),
        cost_estimate=pl.CostEstimate(
            flops=100_000_000_000, bytes_accessed=60_000_000, transcendentals=0
        ),
    )(
        *chip_in,
        gy,
        tokens,
        cotangent,
        o_all,
        dx_all,
        h,
        wo_all,
        ub,
        q,
        k,
        v,
        lse,
        cosine,
        sine,
        a,
        spread,
        spread,
        stats,
        pos,
        small_all,
        extra,
        dg_all,
    )
    if not gathered:
        steps = 4

        def split(value, axis):
            block = list(value.shape)
            block[axis] //= steps

            def index(i):
                where = [0] * len(block)
                where[axis] = i
                return tuple(where)

            return pl.BlockSpec(tuple(block), index)

        def full(value):
            return pl.BlockSpec(value.shape, lambda i: (0,) * len(value.shape))

        large = [
            (results, 1),
            (input_grads, 1),
            (own_in, 2),
            (far_in[0], 2),
            (own_down, 1),
            (far_down, 1),
        ]
        tinies = [
            struct((columns, 2, rows), F32),
            struct((1, part), F32),
            struct((1, part), F32),
            struct((3, part, share), F32),
            struct((share, part), F32),
            struct((columns, part), F32),
            struct((4, part), F32),
            struct((2, part), F32),
        ]
        final = [large[0], large[1], large[2], large[4]]
        done = pl.pallas_call(
            functools.partial(last_kernel, part, columns),
            grid=(steps,),
            out_shape=[struct(v.shape, v.dtype) for v, _ in final] + tinies,
            in_specs=[split(v, axis) for v, axis in large]
            + [full(v) for v in (logits, grads, lines, norm_line)],
            out_specs=[split(v, axis) for v, axis in final] + [full(v) for v in tinies],
            compiler_params=pltpu.CompilerParams(vmem_limit_bytes=VMEM_LIMIT),
        )(*(v for v, _ in large), logits, grads, lines, norm_line)
        results, input_grads, grad_in, grad_down, logits = done[:5]
        gain_attn, gain_moe, heads, out, router, const, vec = done[5:]
        return (
            results,
            input_grads,
            jnp.transpose(logits, (1, 2, 0)),
            gain_attn[0],
            gain_moe[0],
            heads,
            out,
            router.T,
            const.T,
            vec,
            grad_in,
            grad_down,
        )
    grads = lax.psum_scatter(grads.astype(F32), "dp", scatter_dimension=1, tiled=True)
    lines = lax.psum_scatter(lines, "dp", scatter_dimension=0, tiled=True)
    other = lax.dynamic_index_in_dim(grads, 1 - m, 0, keepdims=False)
    grads = lax.dynamic_index_in_dim(grads, m, 0, keepdims=False) + across_chips(other)
    lines = lines + across_chips(lines)

    def heads(j):
        start = (4 + (j % 4) // 2) * LANES + (j % 2) * HD
        return jnp.concatenate(
            [grads[:, j * LANES : (j + 1) * LANES], grads[:, start : start + HD]], axis=1
        )

    return (
        results,
        input_grads,
        jnp.swapaxes(logits[:, :columns], 1, 2),
        lines[:, columns + 4],
        lines[:, columns + 5],
        jnp.stack([heads(i) for i in range(3)]),
        heads(3).T,
        lines[:, :columns],
        lines[:, columns : columns + 4],
        lines[:, columns + 6 : columns + 8].T,
        grad_in,
        grad_down,
    )


def solution(mesh):
    in_specs = (
        P(None, "dp", None),
        P(None, "dp", None),
        P(None, "dp", None),
        P(None, "dp", None),
        P("dp"),
        P("dp"),
        P(None, "dp", "tensor"),
        P("tensor", "dp"),
        P("dp", None),
        P("dp", None),
        P(None, "dp"),
        P("dp", None, None, "tensor"),
        P("dp", "tensor", None),
    )
    out_specs = (
        P(None, "dp", None),
        P(None, "dp", None),
        P(None, "dp", None),
        P("dp"),
        P("dp"),
        P(None, "dp", "tensor"),
        P("tensor", "dp"),
        P("dp", None),
        P("dp", None),
        P(None, "dp"),
        P("dp", None, None, "tensor"),
        P("dp", "tensor", None),
    )
    return jax.shard_map(body, mesh=mesh, in_specs=in_specs, out_specs=out_specs, check_vma=False)
```

```python
import functools

import jax
import jax.numpy as jnp
import numpy as np
from jax import lax
from jax.experimental import pallas as pl
from jax.experimental.pallas import tpu as pltpu
from jax.sharding import PartitionSpec as P

HD = 64
LEN = 1024
BLK = 256
EPSILON = 1e-06
LANES = 128
F32 = jnp.float32
BF16 = jnp.bfloat16
MESH = pl.DeviceIdType.MESH
VMEM_LIMIT = 60 * 1024 * 1024


def mm(a, b):
    return lax.dot_general(a, b, (((1,), (0,)), ((), ())), preferred_element_type=F32)


def mm_nt(a, b):
    return lax.dot_general(a, b, (((1,), (1,)), ((), ())), preferred_element_type=F32)


def mm_tn(a, b):
    return lax.dot_general(a, b, (((0,), (0,)), ((), ())), preferred_element_type=F32)


def vspec():
    return pl.BlockSpec(memory_space=pltpu.VMEM)


def aspec():
    return pl.BlockSpec(memory_space=pl.ANY)


def struct(shape, dtype):
    return jax.ShapeDtypeStruct(shape, dtype)


def greet(peers):
    barrier = pltpu.get_barrier_semaphore()
    for peer in peers:
        pl.semaphore_signal(barrier, inc=1, device_id=peer, device_id_type=MESH)
    pl.semaphore_wait(barrier, len(peers))


def remote(src, dst, send, recv, peer):
    return pltpu.make_async_remote_copy(
        src_ref=src,
        dst_ref=dst,
        send_sem=send,
        recv_sem=recv,
        device_id=peer,
        device_id_type=MESH,
    )


def plane_peers(n, d, t):
    return [(lax.rem(d + j, n), t) for j in range(1, n)]


def slot_hot(half, padded, base, places):
    rows = places.shape[1]
    slot = lax.broadcasted_iota(jnp.int32, (padded, rows), 0)
    wanted = jnp.where(slot < half, slot + base, -2).astype(F32)
    return (wanted == places).astype(F32).astype(BF16)


def rope_constants():
    half = HD // 2
    frequency = 10000.0 ** (-2.0 * np.arange(half) / HD)
    angle = np.arange(LEN)[:, None] * frequency[None, :]
    cosine, sine = np.cos(angle), np.sin(angle)
    cosine = np.concatenate([cosine, cosine, cosine, cosine], axis=1)
    sine = np.concatenate([-sine, sine, -sine, sine], axis=1)
    return cosine.astype(np.float32), sine.astype(np.float32)


def turn(field, cosine, sine):
    lane = lax.broadcasted_iota(jnp.int32, field.shape, 1)
    other = jnp.where(
        lax.rem(lane, HD) < HD // 2,
        pltpu.roll(field, LANES - HD // 2, 1),
        pltpu.roll(field, HD // 2, 1),
    )
    return field * cosine + other * sine


def pick(hot, values):
    return jnp.sum(jnp.where(hot, values, 0.0), axis=-1, keepdims=True)


def lane_ids(rows):
    return lax.broadcasted_iota(jnp.int32, (rows, LANES), 1)


def soft_pair(first, second):
    high = jnp.maximum(first, second)
    e0, e1 = jnp.exp(first - high), jnp.exp(second - high)
    return e0 / (e0 + e1), e1 / (e0 + e1)


def half_mask(rows):
    return lax.broadcasted_iota(jnp.int32, (rows, LANES), 1) < HD


def swap_halves(value):
    return pltpu.roll(value, HD, 1)


def front_kernel(
    n,
    half,
    padded,
    gathered,
    early,
    tokens_ref,
    cotangent_ref,
    routes_all_ref,
    prev_all_ref,
    heads_ref,
    out_ref,
    cos_ref,
    sin_ref,
    win_ref,
    *refs,
):
    tiny_refs, refs = refs[: 1 if gathered else 5], refs[1 if gathered else 5 :]
    slot_ref, gate_ref, extra_ref = refs[:3]
    stored = refs[3 : 3 + early]
    dy_arrived_ref, in_x_ref = refs[3 + early : 5 + early]
    refs = refs[5 + early :]
    kept, refs = refs[:early], refs[early:]
    a_ref, q_ref, k_ref, v_ref, o_ref, lse_ref, pos_ref, wo_ref, small_ref, spread_ref = kept[:10]
    h_ref, ub_ref, stat_ref = kept[10:]
    x_ref, dy_ref, routes_ref, place_ref, gates_ref, dy_slot_ref = refs[:6]
    refs = refs[6:]
    load, pack_send, pack_recv, dy_send, dy_recv, stay = refs[:6]
    core_send, core_recv, w_send, w_recv, store_sem = refs[6:]

    def store(*which):
        for i in which:
            pltpu.make_async_copy(kept[i], stored[i], store_sem.at[i]).start()

    rows_all, width = x_ref.shape
    blocks = rows_all // BLK
    pairs = q_ref.shape[0]
    local = pairs * LANES
    columns = prev_all_ref.shape[0]
    d, t = lax.axis_index("dp"), lax.axis_index("tensor")
    m, c = lax.div(t, 2), lax.rem(t, 2)
    partner = (d, t + 1 - 2 * c)
    across = (d, lax.rem(t + 2, 4))
    loads = [
        pltpu.make_async_copy(src.at[m], dst, load.at[i])
        for i, (src, dst) in enumerate(
            [
                (routes_all_ref, routes_ref),
                (cotangent_ref, dy_ref),
                (tokens_ref, x_ref),
            ]
        )
    ]
    for copy in loads:
        copy.start()
    greet(plane_peers(n, d, t) + [partner, across])
    part = heads_ref.shape[1]

    def pack():
        side = lax.broadcasted_iota(jnp.int32, (part, part), 0)
        eye = jnp.where(side == lax.broadcasted_iota(jnp.int32, (part, part), 1), 1.0, 0.0)
        eye = eye.astype(BF16)
        wo = mm_nt(eye, out_ref[...])
        tiny = [ref[...].astype(F32) for ref in tiny_refs]
        tiny.append(jnp.zeros((LANES - columns - 8, part), F32))
        tiny = mm_nt(eye, jnp.concatenate(tiny, axis=0).astype(BF16))
        wide = [heads_ref[i].astype(F32) for i in range(3)] + [wo]
        firsts = [value[:, :LANES] for value in wide]
        odds = [
            jnp.concatenate([wide[i][:, LANES:], wide[i + 1][:, LANES:]], axis=1) for i in (0, 2)
        ]
        return jnp.concatenate(firsts + odds + [tiny], axis=1).astype(BF16)

    beside = (d + 1 - 2 * lax.rem(d, 2), t)
    lanes_a = pl.ds(0, 3 * LANES)
    lanes_b = pl.ds(3 * LANES, 4 * LANES)

    def behind(j):
        return lax.rem(d + n - 2 * j, n)

    def shard(chip, owner, lanes):
        return spread_ref.at[chip, pl.ds(pl.multiple_of(owner * part, part), part), lanes]

    def pass_on(chip, owner, lanes, row, j, peer):
        block = shard(chip, owner, lanes)
        return remote(block, block, pack_send.at[row, j], pack_recv.at[row, j], peer)

    def ahead(j):
        return (lax.rem(d + 2 * j, n), t)

    ring = n // 2
    if gathered:
        spread_ref[...] = tiny_refs[0][...]
    else:
        spread_ref[m, pl.ds(pl.multiple_of(d * part, part), part), :] = pack()
        a_x = pass_on(m, d, lanes_a, 4, 0, across)
        sends = [a_x]
        for j in range(1, ring):
            sends.append(pass_on(m, d, lanes_a, 0, j, ahead(j)))
            sends.append(pass_on(m, d, lanes_b, 4, j, ahead(j)))
        sends.append(pass_on(m, d, lanes_a, 2, 0, beside))
        sends.append(pass_on(m, d, lanes_b, 5, 0, beside))
        sends.append(pass_on(m, d, lanes_b, 6, 0, across))
        for copy in sends:
            copy.start()

    def relay_gather(after_z, after_x):
        if gathered:
            after_z()
            after_x()
            return
        a_x.wait_recv()
        more = [pass_on(1 - m, d, lanes_a, 1, j, ahead(j)) for j in range(1, ring)]
        more.append(pass_on(1 - m, d, lanes_a, 3, 0, beside))
        for copy in more:
            copy.start()
        sends.extend(more)
        for j in range(1, ring):
            pass_on(m, d, lanes_b, 4, j, ahead(j)).wait_recv()
            more = [
                pass_on(m, behind(j), lanes_b, 5, j, beside),
                pass_on(m, behind(j), lanes_b, 6, j, across),
            ]
            pass_on(m, d, lanes_a, 0, j, ahead(j)).wait_recv()
            more.append(pass_on(m, behind(j), lanes_a, 2, j, beside))
            for copy in more:
                copy.start()
            sends.extend(more)
        for j in range(1, ring):
            pass_on(1 - m, d, lanes_a, 1, j, ahead(j)).wait_recv()
            copy = pass_on(1 - m, behind(j), lanes_a, 3, j, beside)
            copy.start()
            sends.append(copy)
        after_z()
        for j in range(ring):
            pass_on(m, d, lanes_b, 5, j, beside).wait_recv()
            owner = lax.rem(beside[0] + n - 2 * j, n)
            copy = pass_on(m, owner, lanes_b, 7, j, across)
            copy.start()
            sends.append(copy)
        after_x()
        for j in range(ring):
            pass_on(m, d, lanes_a, 2, j, beside).wait_recv()
            pass_on(m, d, lanes_a, 3, j, beside).wait_recv()
            pass_on(m, d, lanes_b, 6, j, across).wait_recv()
            pass_on(m, d, lanes_b, 7, j, across).wait_recv()

    loads[0].wait()
    named = routes_ref[...].astype(F32)
    ids = lax.broadcasted_iota(jnp.int32, (LANES, rows_all), 0).astype(F32)
    hit = ((ids == named[0:1, :]) | (ids == named[1:2, :])) & (ids < float(n))
    before = lax.broadcasted_iota(jnp.int32, (rows_all, rows_all), 0) < lax.broadcasted_iota(
        jnp.int32, (rows_all, rows_all), 1
    )
    count = mm(hit.astype(F32).astype(BF16), before.astype(F32).astype(BF16))
    places = jnp.where(hit, count, -1.0)
    place_ref[...] = places
    pos_ref[...] = jnp.transpose(places)
    store(6)
    base = c * half

    def dy_copy(j):
        e = lax.rem(d + j, n)
        return remote(
            dy_slot_ref.at[e], dy_arrived_ref.at[d], dy_send.at[j], dy_recv.at[j], (e, t)
        )

    stays = [pltpu.make_async_copy(dy_slot_ref.at[d], dy_arrived_ref.at[d], stay.at[0])]
    loads[1].wait()

    def two_hot(i):
        return jnp.concatenate(
            [
                slot_hot(half, padded, base, place_ref[pl.ds(2 * i + side, 1), :])
                for side in range(2)
            ],
            axis=0,
        )

    def dy_step(i, carry):
        rows = mm(two_hot(i), dy_ref[...]).astype(BF16)
        for side in range(2):
            dy_slot_ref[2 * i + side] = rows[side * padded : (side + 1) * padded]
        return carry

    lax.fori_loop(0, n // 2, dy_step, 0)
    weight_copies = []
    if not gathered:
        weight_copies.append(remote(win_ref, in_x_ref, w_send.at[0], w_recv.at[0], across))

    def dy_start(j, carry):
        dy_copy(j).start()
        return carry

    relay_gather(
        lambda: lax.fori_loop(1, n, dy_start, 0), lambda: [c.start() for c in weight_copies]
    )
    stays[0].start()
    store(9)

    table = spread_ref[0, :, 6 * LANES : 7 * LANES]
    extra_ref[...] = jnp.transpose(table.astype(F32))
    keep = lax.broadcasted_iota(jnp.int32, (width, LANES), 1) < columns + 4
    small_ref[...] = jnp.where(keep, table, jnp.zeros_like(table))
    mask = half_mask(width)
    own = pl.multiple_of(c * local, LANES)
    wo_ref[:, pl.ds(own, LANES)] = spread_ref[0, :, 3 * LANES : 4 * LANES]
    wo_ref[:, pl.ds(own + LANES, LANES)] = spread_ref[1, :, 3 * LANES : 4 * LANES]
    wo_ref[:, pl.ds(own + 2 * LANES, LANES)] = jnp.where(
        mask,
        swap_halves(spread_ref[0, :, 5 * LANES : 6 * LANES].astype(F32)),
        spread_ref[1, :, 5 * LANES : 6 * LANES].astype(F32),
    ).astype(BF16)
    own_lanes = pl.ds(own, local)
    wo_copy = remote(
        wo_ref.at[:, own_lanes],
        wo_ref.at[:, own_lanes],
        core_send.at[pairs],
        core_recv.at[pairs],
        partner,
    )
    wo_copy.start()
    store(8)

    loads[2].wait()
    gain = extra_ref[columns + 4 : columns + 5, :]
    head = half_mask(BLK)

    def project(i, carry):
        rows = pl.ds(pl.multiple_of(i * BLK, BLK), BLK)
        x = x_ref[rows, :].astype(F32)
        r = lax.rsqrt(jnp.mean(x * x, axis=-1, keepdims=True) + EPSILON)
        a = (x * r * gain).astype(BF16)
        a_ref[rows, :] = a
        cosine, sine = cos_ref[rows, :], sin_ref[rows, :]

        def put(pair, q, k, v):
            q_ref[pair, rows, :] = turn(q, cosine, sine).astype(BF16) * BF16(HD**-0.5)
            k_ref[pair, rows, :] = turn(k, cosine, sine).astype(BF16)
            v_ref[pair, rows, :] = v.astype(BF16)

        odd = []
        for s in range(2):
            both = mm(a, spread_ref[s, :, 0 : 3 * LANES])
            put(s, *(both[:, j * LANES : (j + 1) * LANES] for j in range(3)))
            both = mm(a, spread_ref[s, :, 4 * LANES : 6 * LANES])
            odd.append((both[:, :LANES], both[:, LANES:]))
        put(
            2,
            jnp.where(head, odd[0][0], swap_halves(odd[1][0])),
            jnp.where(head, swap_halves(odd[0][0]), odd[1][0]),
            jnp.where(head, odd[0][1], swap_halves(odd[1][1])),
        )
        return carry

    lax.fori_loop(0, blocks, project, 0)
    store(0, 1, 2, 3)

    def o_copy(p):
        lanes = pl.ds(pl.multiple_of(own + p * LANES, LANES), LANES)
        return remote(
            o_ref.at[:, lanes], o_ref.at[:, lanes], core_send.at[p], core_recv.at[p], partner
        )

    def attend(p, carry):
        lanes = pl.ds(pl.multiple_of(own + p * LANES, LANES), LANES)
        for i in range(blocks):
            rows = pl.ds(i * BLK, BLK)
            seen = pl.ds(0, (i + 1) * BLK)
            q, k, v = q_ref[p, rows, :], k_ref[p, seen, :], v_ref[p, seen, :]
            halves = []
            for side in range(2):
                chosen = head if side == 0 else jnp.logical_not(head)
                s = mm_nt(jnp.where(chosen, q, jnp.zeros_like(q)), k)
                high = jnp.max(s, axis=-1, keepdims=True)
                e = jnp.exp(s - high)
                total = jnp.sum(e, axis=-1, keepdims=True)
                halves.append(mm(e.astype(BF16), v) * (1.0 / total))
                log_total = jnp.broadcast_to(high + jnp.log(total), (BLK, LANES))
                lse_ref[2 * p + side, :, rows] = jnp.transpose(log_total)[0:8, :]
            o_ref[rows, lanes] = jnp.where(head, halves[0], halves[1]).astype(BF16)
        o_copy(p).start()
        return carry

    lax.fori_loop(0, pairs, attend, 0)
    wo_copy.wait()
    for p in range(pairs):
        o_copy(p).wait()
    store(4, 5, 7)
    prev_lines = jnp.where(m == 0, prev_all_ref[:, 0, :], prev_all_ref[:, 1, :])
    spare = jnp.zeros((LANES - columns - 2, rows_all), F32)
    facts = jnp.concatenate([prev_lines, routes_ref[...].astype(F32), spare], axis=0)
    gates_ref[...] = facts

    gain_moe = extra_ref[columns + 5 : columns + 6, :]

    def middle(i, carry):
        rows = pl.ds(pl.multiple_of(i * BLK, BLK), BLK)
        z = mm_nt(o_ref[rows, :], wo_ref[...])
        h = x_ref[rows, :].astype(F32) + z
        r = lax.rsqrt(jnp.mean(h * h, axis=-1, keepdims=True) + EPSILON)
        ub = (h * r * gain_moe).astype(BF16)
        h_ref[rows, :] = h
        ub_ref[rows, :] = ub
        scores = mm(ub, small_ref[...])
        lane = lane_ids(BLK)
        facts = jnp.transpose(gates_ref[:, rows])
        e0 = facts[:, columns : columns + 1]
        e1 = facts[:, columns + 1 : columns + 2]
        hot0, hot1 = lane.astype(F32) == e0, lane.astype(F32) == e1
        logits = scores + facts
        g0, g1 = soft_pair(pick(hot0, logits), pick(hot1, logits))
        mix = [pick(lane == columns + j, scores) for j in range(4)]
        a00, a01 = soft_pair(mix[0], mix[1])
        a10, a11 = soft_pair(mix[2], mix[3])
        table = jnp.zeros((BLK, LANES), F32)
        for j, value in enumerate([g0, g1, a00, a01, a10, a11, r, e0, e1]):
            table = jnp.where(lane == j, value, table)
        stat_ref[rows, :] = table
        gates = jnp.where(hot0, g0, 0.0) + jnp.where(hot1, g1, 0.0)
        gates_ref[:, rows] = jnp.transpose(gates)
        return carry

    lax.fori_loop(0, blocks, middle, 0)
    store(10, 11, 12)
    piece = lax.broadcasted_iota(jnp.int32, (8, rows_all), 0)

    def slot_step(i, carry):
        hot = two_hot(i)
        rows = mm(hot, ub_ref[...]).astype(BF16)
        for side in range(2):
            e = 2 * i + side
            slot_ref[e] = rows[side * padded : (side + 1) * padded]
            gate = gates_ref[pl.ds(e, 1), :]
            high = gate.astype(BF16).astype(F32)
            mid = (gate - high).astype(BF16).astype(F32)
            low = gate - high - mid
            lines = jnp.where(piece == 0, high, jnp.where(piece == 1, mid, low))
            lines = jnp.where(piece < 3, lines, 0.0).astype(BF16)
            gate = mm_nt(lines, hot[side * padded : (side + 1) * padded])
            gate = jnp.sum(gate, axis=0, keepdims=True)
            gate_ref[e] = jnp.broadcast_to(gate, (8, padded))
        return carry

    lax.fori_loop(0, n // 2, slot_step, 0)
    def finish(j, carry):
        dy_copy(j).wait()
        return carry

    lax.fori_loop(1, n, finish, 0)
    for copy in stays:
        copy.wait()
    for copy in [] if gathered else sends:
        copy.wait_send()
    for copy in weight_copies:
        copy.wait()
    for i in range(early):
        pltpu.make_async_copy(kept[i], stored[i], store_sem.at[i]).wait()


def flip(value, index, size):
    bit = 1
    while bit < size:
        chosen = lax.rem(lax.div(index, bit), 2)
        value = value + chosen * (bit - 2 * bit * lax.rem(lax.div(value, bit), 2))
        bit *= 2
    return value


def expert_exchange_kernel(
    n,
    padded,
    slot_src_ref,
    gate_src_ref,
    dy_src_ref,
    in_own_ref,
    in_chip_ref,
    down_own_ref,
    gy_out_ref,
    own_in_out_ref,
    own_down_out_ref,
    chip_in_out_ref,
    far_down_ref,
    dx_all_ref,
    dg_all_ref,
    gy_ref,
    own_in_ref,
    own_down_ref,
    chip_in_ref,
    x_ref,
    xt_ref,
    dy_ref,
    scaled_ref,
    scale_ref,
    gate_ref,
    win_ref,
    wdown_ref,
    hidden_ref,
    dgate_ref,
    dup_ref,
    y_ref,
    dx_ref,
    dg_ref,
    land_in_ref,
    land_down_ref,
    chip_down_ref,
    load,
    slot_send,
    slot_recv,
    gate_send,
    gate_recv,
    dx_send,
    dx_recv,
    dg_send,
    dg_recv,
    pass_send,
    pass_recv,
    sum_send,
    sum_recv,
    w_send,
    w_recv,
    store_sem,
):
    width = x_ref.shape[1]
    share = win_ref.shape[3]
    chunks = 4
    group = n // chunks
    span = group * padded
    block = 256
    d, t = lax.axis_index("dp"), lax.axis_index("tensor")
    c = lax.rem(t, 2)
    partner = (d, t + 1 - 2 * c)
    across = (d, lax.rem(t + 2, 4))
    stores = [
        pltpu.make_async_copy(src, dst, store_sem.at[i])
        for i, (src, dst) in enumerate(
            [
                (gy_ref, gy_out_ref),
                (chip_in_ref, chip_in_out_ref),
                (own_in_ref, own_in_out_ref),
                (own_down_ref, own_down_out_ref),
            ]
        )
    ]
    greet(plane_peers(n, d, t) + [partner, across])

    def rows_of(i):
        return pl.ds(pl.multiple_of(i * padded, padded), padded)

    def slot_copy(i):
        e = flip(d, i, n)
        return remote(
            slot_src_ref.at[e], x_ref.at[rows_of(i)], slot_send.at[i], slot_recv.at[i], (e, t)
        )

    def gate_copy(i):
        e = flip(d, i, n)
        return remote(
            gate_src_ref.at[e], gate_ref.at[i], gate_send.at[i], gate_recv.at[i], (e, t)
        )

    def dx_copy(i):
        e = flip(d, i, n)
        return remote(
            dx_ref.at[rows_of(i)], dx_all_ref.at[c, d], dx_send.at[i], dx_recv.at[i], (e, t)
        )

    def dg_copy(i):
        e = flip(d, i, n)
        return remote(dg_ref.at[i], dg_all_ref.at[c, d], dg_send.at[i], dg_recv.at[i], (e, t))

    def hand(kind, i):
        ref = (dx_all_ref, dg_all_ref)[kind]
        block_ref = ref.at[c, flip(d, i, n)]
        return remote(
            block_ref, block_ref, pass_send.at[kind, i], pass_recv.at[kind, i], partner
        )

    def down_rows(s):
        return pl.ds(s * share, share)

    def send_chunk(k):
        for q in range(group):
            if k + q > 0:
                slot_copy(k * group + q).start()
                gate_copy(k * group + q).start()

    send_chunk(2)
    send_chunk(1)
    if group > 1:
        send_chunk(0)
    stays = [
        pltpu.make_async_copy(slot_src_ref.at[d], x_ref.at[rows_of(0)], load.at[0]),
        pltpu.make_async_copy(gate_src_ref.at[d], gate_ref.at[0], load.at[1]),
    ]
    own_loads = [
        pltpu.make_async_copy(in_own_ref.at[0], win_ref.at[0], load.at[2]),
        pltpu.make_async_copy(down_own_ref.at[0], wdown_ref.at[down_rows(0)], load.at[3]),
    ]
    chip_load = pltpu.make_async_copy(in_chip_ref.at[0], win_ref.at[2], load.at[4])
    weights = [
        remote(in_own_ref.at[0], win_ref.at[1], w_send.at[0], w_recv.at[0], partner),
        remote(
            down_own_ref.at[0], wdown_ref.at[down_rows(1)], w_send.at[1], w_recv.at[1], partner
        ),
        remote(in_chip_ref.at[0], win_ref.at[3], w_send.at[2], w_recv.at[2], partner),
        remote(
            down_own_ref.at[0], wdown_ref.at[down_rows(2)], w_send.at[3], w_recv.at[3], across
        ),
        remote(
            wdown_ref.at[down_rows(2)],
            wdown_ref.at[down_rows(3)],
            w_send.at[4],
            w_recv.at[4],
            partner,
        ),
    ]

    def dy_load(i):
        return pltpu.make_async_copy(
            dy_src_ref.at[flip(d, i, n)], dy_ref.at[rows_of(i)], load.at[10 + i]
        )

    for copy in [weights[3]] + stays + own_loads:
        copy.start()
    for i in range(n):
        dy_load(i).start()
    chip_load.start()
    for copy in weights[0:3]:
        copy.start()
    for copy in stays + own_loads:
        copy.wait()

    def take(k):
        rows = pl.ds(k * span, span)
        for q in range(group):
            i = k * group + q
            if i > 0:
                slot_copy(i).wait_recv()
                gate_copy(i).wait_recv()
            dy_load(i).wait()
            near = rows_of(i)
            line = jnp.broadcast_to(gate_ref[i, 0:1, :], (LANES, padded))
            scale = jnp.transpose(line)
            scale_ref[near, :] = scale
            scaled_ref[near, :] = (dy_ref[near, :].astype(F32) * scale[:, 0:1]).astype(BF16)
        xt_ref[:, rows] = jnp.transpose(x_ref[rows, :])

    per = share // block

    def units(first, last, chosen):
        def unit(u, carry):
            k = first + lax.div(u, 2 * per)
            b = lax.rem(u, 2 * per)
            s = chosen * 2 + lax.div(b, per)
            rows = pl.ds(pl.multiple_of(k * span, span), span)
            lanes = pl.ds(pl.multiple_of(lax.rem(b, per) * block, block), block)
            far = pl.ds(pl.multiple_of((chosen * 2 * per + b) * block, block), block)
            x = x_ref[rows, :]
            gate = mm(x, win_ref[s, 0, :, lanes])
            up = mm(x, win_ref[s, 1, :, lanes])
            grad = mm_nt(scaled_ref[rows, :], wdown_ref[far, :])
            sigma = 0.5 * jnp.tanh(0.5 * gate) + 0.5
            active = gate * sigma
            hidden_ref[rows, far] = (active * up).astype(BF16)
            dgate_ref[rows, far] = (grad * up * (sigma * (1.0 + gate * (1.0 - sigma)))).astype(
                BF16
            )
            dup_ref[rows, far] = (grad * active).astype(BF16)
            return carry

        lax.fori_loop(0, (last - first) * 2 * per, unit, 0)

    def close(k, carry):
        rows = pl.ds(pl.multiple_of(k * span, span), span)
        for j in range(width // block):
            lanes = pl.ds(j * block, block)
            total = jnp.zeros((span, block), F32)
            for s in range(4):
                far = pl.ds(s * share, share)
                total = total + mm_nt(dgate_ref[rows, far], win_ref[s, 0, lanes, :])
                total = total + mm_nt(dup_ref[rows, far], win_ref[s, 1, lanes, :])
            dx_ref[rows, lanes] = total.astype(BF16)
        for q in range(group):
            i = k * group + q

            @pl.when(i > 0)
            def _():
                dx_copy(i).start()

        for j in range(width // block):
            lanes = pl.ds(j * block, block)
            y_ref[:, lanes] = mm(hidden_ref[rows, :], wdown_ref[:, lanes])
        for q in range(group):
            i = k * group + q
            near = rows_of(i)
            y = y_ref[pl.ds(q * padded, padded), :]
            gy_ref[flip(d, i, n)] = (y * scale_ref[near, 0:1]).astype(BF16)
            dot = jnp.sum(y * dy_ref[near, :].astype(F32), axis=-1, keepdims=True)
            dg_ref[i] = jnp.transpose(jnp.broadcast_to(dot, (padded, LANES)))[0:8, :]

            @pl.when(i > 0)
            def _():
                dg_copy(i).start()

        return carry

    take(0)
    for copy in weights[0:2]:
        copy.wait_recv()
    units(0, 1, 0)
    take(1)
    units(1, 2, 0)
    take(2)
    send_chunk(3)
    units(2, 3, 0)
    chip_load.wait()
    weights[3].wait_recv()
    weights[4].start()
    weights[2].wait_recv()
    weights[4].wait_recv()
    units(0, 3, 1)
    lax.fori_loop(2, 3, close, 0)
    lax.fori_loop(0, 2, close, 0)
    take(3)
    units(3, 4, 0)
    units(3, 4, 1)
    lax.fori_loop(3, 4, close, 0)
    stores[0].start()
    keeps = [
        pltpu.make_async_copy(dx_ref.at[rows_of(0)], dx_all_ref.at[c, d], load.at[0]),
        pltpu.make_async_copy(dg_ref.at[0], dg_all_ref.at[c, d], load.at[1]),
    ]
    for copy in keeps:
        copy.start()

    def forward(first, last):
        def step(i, carry):
            dx_copy(i).wait_recv()
            dg_copy(i).wait_recv()
            hand(0, i).start()
            hand(1, i).start()
            return carry

        lax.fori_loop(first, last, step, 0)

    def grad_in(s, kind, b):
        far = pl.ds(pl.multiple_of(s * share + b * block, block), block)
        return mm(xt_ref[...], (dgate_ref, dup_ref)[kind][:, far])

    def grad_down(s, b):
        far = pl.ds(pl.multiple_of(s * share + b * block, block), block)
        return mm_tn(hidden_ref[:, far], scaled_ref[...])

    def sum_copies(j):
        return [
            remote(win_ref.at[j], land_in_ref.at[j], sum_send.at[j], sum_recv.at[j], partner),
            remote(
                wdown_ref.at[pl.ds(j * share, share)],
                land_down_ref.at[j],
                sum_send.at[2 + j],
                sum_recv.at[2 + j],
                partner,
            ),
        ]

    for copy in weights:
        copy.wait_send()

    def down_sums(s, put):
        def unit(b, carry):
            put(pl.ds(pl.multiple_of(b * block, block), block), grad_down(s, b))
            return carry

        lax.fori_loop(0, per, unit, 0)

    def in_sums(s, put):
        def unit(b, carry):
            lanes = pl.ds(pl.multiple_of(b * block, block), block)
            for kind in range(2):
                put(kind, lanes, grad_in(s, kind, b))
            return carry

        lax.fori_loop(0, per, unit, 0)

    def leave_down(j, s):
        def put(rows, value):
            near = pl.multiple_of(rows.start + j * share, block)
            wdown_ref[pl.ds(near, block), :] = value.astype(BF16)

        down_sums(s, put)
        sum_copies(j)[1].start()

    def leave_in(j, s):
        def put(kind, lanes, value):
            win_ref[j, kind, :, lanes] = value.astype(BF16)

        in_sums(s, put)
        sum_copies(j)[0].start()

    leave_down(0, 3)
    leave_down(1, 1)
    sum_copies(0)[1].wait_recv()

    def chip_down(lanes, value):
        chip_down_ref[0, lanes, :] = (value + land_down_ref[0, lanes, :].astype(F32)).astype(BF16)

    down_sums(2, chip_down)
    far_copy = remote(chip_down_ref, far_down_ref, w_send.at[5], w_recv.at[5], across)
    far_copy.start()
    for copy in keeps:
        copy.wait()
    hand(0, 0).start()
    hand(1, 0).start()
    forward(1, 2 * group)
    leave_in(0, 3)
    leave_in(1, 1)
    sum_copies(0)[0].wait_recv()

    def chip_in(kind, lanes, value):
        chip_in_ref[0, kind, :, lanes] = (
            value + land_in_ref[0, kind, :, lanes].astype(F32)
        ).astype(BF16)

    in_sums(2, chip_in)
    stores[1].start()
    for copy in sum_copies(1):
        copy.wait_recv()

    def own_in(kind, lanes, value):
        own_in_ref[0, kind, :, lanes] = value + land_in_ref[1, kind, :, lanes].astype(F32)

    def own_down(lanes, value):
        own_down_ref[0, lanes, :] = value + land_down_ref[1, lanes, :].astype(F32)

    in_sums(0, own_in)
    stores[2].start()
    down_sums(0, own_down)
    stores[3].start()
    forward(2 * group, n)

    def clear(i, carry):
        for copy in (slot_copy(i), gate_copy(i), dx_copy(i), dg_copy(i)):
            copy.wait_send()
        return carry

    lax.fori_loop(1, n, clear, 0)

    def passed(i, carry):
        hand(0, i).wait()
        hand(1, i).wait()
        return carry

    lax.fori_loop(0, n, passed, 0)
    for j in range(2):
        for copy in sum_copies(j):
            copy.wait_send()
    far_copy.wait()
    for copy in stores:
        copy.wait()


def expert_kernel(
    sources,
    padded,
    x_ref,
    dy_ref,
    gate_ref,
    *refs,
):
    weights, outs = refs[:8], refs[8:19]
    in_refs, down_refs = weights[0:4], weights[4:8]
    gy_ref, dx_ref, dg_ref = outs[0:3]
    gin_refs, gdown_refs = outs[3:7], outs[7:11]
    xt_ref, scaled_ref, scale_ref, y_acc, dx_acc, win_ref, wdown_ref = refs[19:]
    step = pl.program_id(0)
    last = pl.num_programs(0) - 1

    @pl.when(step == 0)
    def _():
        xt_ref[...] = jnp.transpose(x_ref[...])
        for s in range(sources):
            rows = pl.ds(s * padded, padded)
            line = jnp.broadcast_to(gate_ref[s, 0:1, :], (LANES, padded))
            scale = jnp.transpose(line)
            scale_ref[rows, :] = scale
            scaled_ref[rows, :] = (dy_ref[rows, :].astype(F32) * scale[:, 0:1]).astype(BF16)
        y_acc[...] = jnp.zeros_like(y_acc)
        dx_acc[...] = jnp.zeros_like(dx_acc)

    per = pl.num_programs(0) // 4
    for i in range(4):

        @pl.when(lax.div(step, per) == i)
        def _():
            win_ref[...] = in_refs[i][0]
            wdown_ref[...] = down_refs[i][0]

    x = x_ref[...]
    gate = mm(x, win_ref[0])
    up = mm(x, win_ref[1])
    sigma = 1.0 / (1.0 + jnp.exp(-gate))
    active = gate * sigma
    hidden = (active * up).astype(BF16)
    y_acc[...] += mm(hidden, wdown_ref[...])
    scaled = scaled_ref[...]
    grad_hidden = mm_nt(scaled, wdown_ref[...])
    grad_gate = (grad_hidden * up * (sigma * (1.0 + gate * (1.0 - sigma)))).astype(BF16)
    grad_up = (grad_hidden * active).astype(BF16)
    dx_acc[...] += mm_nt(grad_gate, win_ref[0]) + mm_nt(grad_up, win_ref[1])
    xt = xt_ref[...]
    part_gate = mm(xt, grad_gate).astype(BF16)
    part_up = mm(xt, grad_up).astype(BF16)
    part_down = mm_tn(hidden, scaled).astype(BF16)
    for i in range(4):

        @pl.when(lax.div(step, per) == i)
        def _():
            gin_refs[i][0, 0] = part_gate
            gin_refs[i][0, 1] = part_up
            gdown_refs[i][0] = part_down

    @pl.when(step == last)
    def _():
        for s in range(sources):
            rows = pl.ds(s * padded, padded)
            y = y_acc[rows, :]
            gy_ref[s] = (y * scale_ref[rows, 0:1]).astype(BF16)
            dot = jnp.sum(y * dy_ref[rows, :].astype(F32), axis=-1, keepdims=True)
            dg_ref[s] = jnp.transpose(jnp.broadcast_to(dot, (padded, LANES)))[0:8, :]
            dx_ref[s] = dx_acc[rows, :].astype(BF16)


def rear_kernel(n, half, padded, gathered, part, *refs):
    crossing = 0 if gathered else 1
    chip_in_refs, refs = refs[:crossing], refs[crossing:]
    gy_src_ref, tokens_ref, cotangent_ref, o_all_ref = refs[:4]
    loaded, refs = refs[4:17], refs[17:]
    stat_ref, pos_ref, small_ref, extra_ref, dg_ref = refs[:5]
    result_ref, grad_x_ref, logit_ref, grads_ref, lines_ref, norm_out_ref = refs[5:11]
    far_in_refs, refs = refs[11 : 11 + crossing], refs[11 + crossing :]
    kept, refs = refs[:13], refs[13:]
    dx_ref, h_ref, wo_ref, ub_ref, q_ref, k_ref, v_ref = kept[:7]
    lse_ref, cos_ref, sin_ref, a_ref, spread_a_ref, spread_b_ref = kept[7:]
    x_ref, dy_ref, o_ref, gy_ref, dh_ref, dzb_ref, do_ref, low_ref, row_ref = refs[:9]
    dp_ref, dk_acc, dv_acc, wo_odd_ref, pack_ref, line_ref, y_in_ref, z_in_ref = refs[9:17]
    line_in_ref, cross_ref, cross_in_ref, cross_line_ref = refs[17:21]
    da_out_ref, da_in_ref, da_own_ref, norm_ref, norm_in_ref, half_ref = refs[21:27]
    norm_line_ref, norm_all_ref, norm_cross_ref, line_low_ref = refs[27:31]
    load, fetch_sem, gy_send, gy_recv, stay, pass_send, pass_recv = refs[31:38]
    grad_send, grad_recv, line_send, line_recv, pair_send, pair_recv = refs[38:44]
    out_send, out_recv, sum_send, sum_recv, norm_send, norm_recv = refs[44:]

    def fetch(i):
        src = loaded[i]
        if i == 11:
            src = src.at[:, :, pl.ds(0, 3 * LANES)]
        if i == 12:
            src = src.at[:, :, pl.ds(4 * LANES, 2 * LANES)]
        return pltpu.make_async_copy(src, kept[i], fetch_sem.at[i])

    rows_all, width = dy_ref.shape
    blocks = rows_all // BLK
    pairs = q_ref.shape[0]
    local = pairs * LANES
    columns = n + 4
    slots = n * padded
    d, t = lax.axis_index("dp"), lax.axis_index("tensor")
    m, c = lax.div(t, 2), lax.rem(t, 2)
    partner = (d, t + 1 - 2 * c)
    across = (d, lax.rem(t + 2, 4))
    rows_half = rows_all // 2
    own = pl.multiple_of(c * local, LANES)
    own_lanes = pl.ds(own, local)
    place = pl.ds(pl.multiple_of(c * rows_half, BLK), rows_half)
    loads = [
        pltpu.make_async_copy(src, dst, load.at[i])
        for i, (src, dst) in enumerate(
            [
                (cotangent_ref.at[m], dy_ref),
                (tokens_ref.at[m, place], x_ref),
                (o_all_ref.at[:, own_lanes], o_ref),
            ]
        )
    ]
    for i in range(2):
        fetch(i).start()
    for copy in loads:
        copy.start()
    for i in range(2, 13):
        fetch(i).start()
    greet(plane_peers(n, d, t) + [partner, across])

    sum_copies = [
        remote(src, land, sum_send.at[0], sum_recv.at[0], across)
        for src, land in zip(chip_in_refs, far_in_refs)
    ]
    for copy in sum_copies:
        copy.start()

    def give(j):
        s = lax.rem(d + j, n)
        return remote(gy_src_ref.at[s], gy_ref.at[c, d], gy_send.at[j], gy_recv.at[j], (s, t))

    def hand(j):
        block = gy_ref.at[c, lax.rem(d + n - j, n)]
        return remote(block, block, pass_send.at[j], pass_recv.at[j], partner)

    keep = pltpu.make_async_copy(gy_src_ref.at[d], gy_ref.at[c, d], stay.at[0])
    keep.start()

    def give_start(j, carry):
        give(j).start()
        return carry

    lax.fori_loop(1, n, give_start, 0)

    def collect():
        keep.wait()
        hand(0).start()

        def step(j, carry):
            give(j).wait_recv()
            hand(j).start()
            return carry

        lax.fori_loop(1, n, step, 0)

    def settle():
        def step(j, carry):
            hand(j).wait_recv()
            return carry

        lax.fori_loop(0, n, step, 0)

    row_ref[...] = jnp.zeros_like(row_ref)
    for copy in loads:
        copy.wait()
    for i in range(3):
        fetch(i).wait()

    gain_moe = extra_ref[columns + 5 : columns + 6, :]
    vec0 = extra_ref[columns + 6 : columns + 7, :]
    vec1 = extra_ref[columns + 7 : columns + 8, :]
    group = max(1, min(n, (1024 if slots <= 1024 else 512) // padded))
    span = group * padded

    def combine(wheres, ref, lines=None):
        total = jnp.zeros((BLK, width), F32)
        entries = [jnp.zeros((BLK, 1), F32) for _ in wheres]
        slot = lax.broadcasted_iota(jnp.int32, (BLK, span), 1)
        for side in range(2):
            for first in range(0, n, group):
                start = side * slots + first * padded
                hots = [slot == where - start for where in wheres]
                hot = jnp.where(hots[0] | hots[1], 1.0, 0.0).astype(BF16)
                block = ref[side, first : first + group].reshape(span, width)
                total = total + mm(hot, block)
                if lines is not None:
                    line = jnp.concatenate(
                        [lines[side, first + e, 0:1, :] for e in range(group)], axis=1
                    )
                    entries = [
                        entry + jnp.sum(jnp.where(one, line, 0.0), axis=-1, keepdims=True)
                        for entry, one in zip(entries, hots)
                    ]
        return total, entries

    def facts(rows):
        lane = lane_ids(BLK)
        stats = stat_ref[rows, :]
        values = [stats[:, j : j + 1] for j in range(7)]
        e0, e1 = stats[:, 7:8].astype(jnp.int32), stats[:, 8:9].astype(jnp.int32)
        wheres = []
        places = pos_ref[rows, :]
        for e in (e0, e1):
            place = pick(lane == e, places).astype(jnp.int32)
            side = (place >= half).astype(jnp.int32)
            where = side * (slots - half) + e * padded + place
            wheres.append(jnp.where(e < n, where, -1))
        g0, g1 = values[0:2]

        def named(number):
            return jnp.where(e0 == number, g0, 0.0) + jnp.where(e1 == number, g1, 0.0)

        copied, first, second = named(n + 1), named(n + 2), named(n + 3)
        on_u = copied + first * values[2] + second * values[4]
        return values, e0, e1, wheres, first, second, on_u

    def back(i, carry):
        rows = pl.ds(pl.multiple_of(i * BLK, BLK), BLK)
        values, e0, e1, wheres, first, second, on_u = facts(rows)
        g0, g1, a00, a01, a10, a11, r = values
        lane = lane_ids(BLK)
        grads, (f0, f1) = combine(wheres, dx_ref, dg_ref)
        h = h_ref[rows, :]
        normed = h * r
        u = normed * gain_moe
        dy = dy_ref[rows, :].astype(F32)
        s_u = jnp.sum(dy * u, axis=-1, keepdims=True)
        s_0 = jnp.sum(dy * vec0, axis=-1, keepdims=True)
        s_1 = jnp.sum(dy * vec1, axis=-1, keepdims=True)

        def other(e):
            value = jnp.where(e == n + 1, s_u, 0.0)
            value = jnp.where(e == n + 2, a00 * s_u + a01 * s_0, value)
            return jnp.where(e == n + 3, a10 * s_u + a11 * s_1, value)

        dg0, dg1 = f0 + other(e0), f1 + other(e1)
        mean = g0 * dg0 + g1 * dg1
        dl = jnp.where(lane == e0, g0 * (dg0 - mean), 0.0) + jnp.where(
            lane == e1, g1 * (dg1 - mean), 0.0
        )
        turned = jnp.transpose(dl)
        logit_ref[m, :, rows] = turned[0 : logit_ref.shape[1], :]
        d00, d01 = first * s_u, first * s_0
        d10, d11 = second * s_u, second * s_1
        m0 = a00 * d00 + a01 * d01
        m1 = a10 * d10 + a11 * d11
        low = dl
        for j, value in enumerate(
            [a00 * (d00 - m0), a01 * (d01 - m0), a10 * (d10 - m1), a11 * (d11 - m1)]
        ):
            low = jnp.where(lane == columns + j, value, low)
        low = low.astype(BF16)
        low_ref[rows, :] = low
        du = grads + mm_nt(low, small_ref[...]) + on_u * dy
        row_ref[0:1, :] += jnp.sum(du * normed, axis=0, keepdims=True)
        row_ref[1:2, :] += jnp.sum((first * a01) * dy, axis=0, keepdims=True)
        row_ref[2:3, :] += jnp.sum((second * a11) * dy, axis=0, keepdims=True)
        dn = du * gain_moe
        dh = dy + r * (dn - normed * jnp.mean(dn * normed, axis=-1, keepdims=True))

        @pl.when(lax.div(i, blocks // 2) == c)
        def _():
            near = pl.multiple_of(i * BLK - c * rows_half, BLK)
            dh_ref[pl.ds(near, BLK), :] = dh

        dzb = dh.astype(BF16)
        dzb_ref[rows, :] = dzb
        do_ref[rows, :] = mm(dzb, wo_ref[:, own_lanes]).astype(BF16)
        return carry

    lax.fori_loop(0, blocks, back, 0)
    logit_copy = remote(
        logit_ref.at[m], logit_ref.at[m], pair_send.at[0], pair_recv.at[0], across
    )
    logit_copy.start()

    fetch(3).wait()
    grad_wo = mm_tn(dzb_ref[...], o_ref[...])
    pack_ref[0, :, 3 * LANES : 4 * LANES] = grad_wo[:, 0:LANES].astype(BF16)
    pack_ref[1, :, 3 * LANES : 4 * LANES] = grad_wo[:, LANES : 2 * LANES].astype(BF16)
    wo_odd_ref[...] = grad_wo[:, 2 * LANES : 3 * LANES]
    lines = mm_tn(ub_ref[...], low_ref[...])
    lane_of = lax.broadcasted_iota(jnp.int32, (width, LANES), 1)
    turned = jnp.concatenate([row_ref[...], jnp.zeros((LANES - 8, width), F32)], axis=0)
    turned = jnp.transpose(turned)
    for j in range(3):
        lines = jnp.where(lane_of == columns + 5 + j, turned[:, j : j + 1], lines)
    line_ref[...] = lines

    def slab(owner):
        return pl.ds(pl.multiple_of(owner * part, part), part)

    ring = n // 2
    y_own = lax.rem(d, 2)
    beside = (d + 1 - 2 * y_own, t)
    z_own = lax.div(d, 2)
    wide_lanes = (pl.ds(0, 3 * LANES), pl.ds(3 * LANES, 3 * LANES))

    def y_copy(s, stage, z):
        lanes = wide_lanes[stage]
        return remote(
            pack_ref.at[s, slab(2 * z + 1 - y_own), lanes],
            y_in_ref.at[s, z, :, lanes],
            grad_send.at[stage, s, z],
            grad_recv.at[stage, s, z],
            beside,
        )

    def z_copy(s, stage, j):
        lanes = wide_lanes[stage]
        z = lax.rem(z_own + j, ring)
        return remote(
            pack_ref.at[s, slab(2 * z + y_own), lanes],
            z_in_ref.at[s, j, :, lanes],
            grad_send.at[2 + stage, s, j],
            grad_recv.at[2 + stage, s, j],
            (2 * z + y_own, t),
        )

    def y_start(s, stage):
        for z in range(ring):
            y_copy(s, stage, z).start()

    def z_start(s, stage):
        lanes = wide_lanes[stage]
        for z in range(ring):
            y_copy(s, stage, z).wait()
            rows = slab(2 * z + y_own)
            value = pack_ref[s, rows, lanes].astype(F32) + y_in_ref[s, z, :, lanes].astype(F32)
            pack_ref[s, rows, lanes] = value.astype(BF16)
        for j in range(1, ring):
            z_copy(s, stage, j).start()

    def line_copy(j):
        e = lax.rem(d + j, n)
        return remote(
            line_low_ref.at[slab(e), :],
            line_in_ref.at[d],
            line_send.at[j],
            line_recv.at[j],
            (e, t),
        )

    head = half_mask(BLK)

    def attend_back(p):
        dk_acc[...] = jnp.zeros_like(dk_acc)
        dv_acc[...] = jnp.zeros_like(dv_acc)
        dq = []
        for i in range(blocks):
            rows = pl.ds(i * BLK, BLK)
            seen = pl.ds(0, (i + 1) * BLK)
            lanes = pl.ds(pl.multiple_of(p * LANES, LANES), LANES)
            q, do = q_ref[p, rows, :], do_ref[rows, lanes]
            k, v = k_ref[p, seen, :], v_ref[p, seen, :]
            zero = jnp.zeros_like(q)
            parts = []
            dk, dv = dk_acc[seen, :], dv_acc[seen, :]
            for side in range(2):
                chosen = head if side == 0 else jnp.logical_not(head)
                qm, dom = jnp.where(chosen, q, zero), jnp.where(chosen, do, zero)
                prob = jnp.exp(mm_nt(k, qm) - lse_ref[2 * p + side, 0:1, rows])
                grad_prob = mm_nt(v, dom)
                total = jnp.sum(prob * grad_prob, axis=0, keepdims=True)
                grad_score = (prob * (grad_prob - total)).astype(BF16)
                dv = dv + mm(prob.astype(BF16), dom)
                dk = dk + mm(grad_score, qm)
                parts.append(mm_tn(grad_score, k))
            dk_acc[seen, :] = dk
            dv_acc[seen, :] = dv
            value = jnp.where(head, parts[0], parts[1]) * (HD**-0.5)
            dq.append(turn(value, cos_ref[rows, :], -sin_ref[rows, :]))
        return (
            jnp.concatenate(dq, axis=0),
            turn(dk_acc[...], cos_ref[...], -sin_ref[...]),
            dv_acc[...],
        )

    for i in range(4, 11):
        fetch(i).wait()
    dq, dk, dv = attend_back(2)
    wide = half_mask(rows_all)
    odd = [
        (jnp.where(wide, dq, swap_halves(dk)), jnp.where(wide, dv, 0.0)),
        (jnp.where(wide, swap_halves(dq), dk), jnp.where(wide, swap_halves(dv), 0.0)),
    ]
    tall = half_mask(width)
    for s in range(2):
        for j in range(2):
            dp_ref[s, :, (3 + j) * LANES : (4 + j) * LANES] = odd[s][j].astype(BF16)
    for s in range(2):
        pack_ref[s, :, 4 * LANES : 5 * LANES] = mm_tn(
            a_ref[...], dp_ref[s, :, 3 * LANES : 4 * LANES]
        ).astype(BF16)
        last = mm_tn(a_ref[...], dp_ref[s, :, 4 * LANES : 5 * LANES])
        side = wo_odd_ref[...]
        side = swap_halves(side) if s == 0 else side
        pack_ref[s, :, 5 * LANES : 6 * LANES] = jnp.where(tall, last, side).astype(BF16)
    if not gathered:
        y_start(0, 1)
        y_start(1, 1)

    def shard_step(i, carry):
        s = lax.rem(m + 1 + i, 2)
        for j, value in enumerate(attend_back(s)):
            dp_ref[s, :, j * LANES : (j + 1) * LANES] = value.astype(BF16)
        for j in range(3):
            lanes = pl.ds(j * LANES, LANES)
            pack_ref[s, :, lanes] = mm_tn(a_ref[...], dp_ref[s, :, lanes]).astype(BF16)
        if not gathered:
            y_start(s, 0)
        return carry

    lax.fori_loop(0, 2, shard_step, 0)
    collect()
    if not gathered:
        z_start(0, 1)
        z_start(1, 1)

        def send_line(j, carry):
            line_copy(j).start()
            return carry

        line_low_ref[...] = line_ref[...].astype(BF16)
        lax.fori_loop(1, n, send_line, 0)
        line_in_ref[d] = line_low_ref[slab(d), :]

    def publish(kind, out_ref):
        block = out_ref.at[m, place]
        copies = [
            remote(half_ref.at[kind], block, out_send.at[kind, 0], out_recv.at[kind, 0], across),
            remote(half_ref.at[kind], block, out_send.at[kind, 1], out_recv.at[kind, 1], partner),
            pltpu.make_async_copy(half_ref.at[kind], block, stay.at[1 + kind]),
        ]
        for copy in copies:
            copy.start()
        block = out_ref.at[1 - m, place]
        relay = remote(block, block, out_send.at[kind, 2], out_recv.at[kind, 2], partner)
        return copies, relay

    settle()

    def results(i, carry):
        rows = pl.ds(pl.multiple_of(i * BLK, BLK), BLK)
        far = pl.ds(pl.multiple_of(c * rows_half + i * BLK, BLK), BLK)
        values, e0, e1, wheres, first, second, on_u = facts(far)
        sums, _ = combine(wheres, gy_ref)
        h = h_ref[far, :]
        u = h * values[6] * gain_moe
        result = h + (sums + on_u * u + (first * values[3]) * vec0 + (second * values[5]) * vec1)
        half_ref[1, rows, :] = result.astype(BF16)
        return carry

    lax.fori_loop(0, rows_half // BLK, results, 0)
    result_copies, result_relay = publish(1, result_ref)

    def da_rows(start):
        rows = pl.ds(pl.multiple_of(start, BLK), BLK)
        total = jnp.zeros((BLK, width), F32)
        for s in range(2):
            total = total + mm_nt(dp_ref[s, rows, 0 : 3 * LANES], spread_a_ref[s])
            total = total + mm_nt(dp_ref[s, rows, 3 * LANES : 5 * LANES], spread_b_ref[s])
        return total

    fetch(11).wait()
    fetch(12).wait()

    def da_other(i, carry):
        rows = pl.ds(pl.multiple_of(i * BLK, BLK), BLK)
        da_out_ref[rows, :] = da_rows((1 - c) * rows_half + i * BLK).astype(BF16)
        return carry

    lax.fori_loop(0, rows_half // BLK, da_other, 0)
    da_copy = remote(da_out_ref, da_in_ref, pair_send.at[1], pair_recv.at[1], partner)
    da_copy.start()

    def da_own(i, carry):
        rows = pl.ds(pl.multiple_of(i * BLK, BLK), BLK)
        da_own_ref[rows, :] = da_rows(c * rows_half + i * BLK)
        return carry

    lax.fori_loop(0, rows_half // BLK, da_own, 0)
    da_copy.wait()
    gain_attn = extra_ref[columns + 4 : columns + 5, :]
    norm_ref[...] = jnp.zeros_like(norm_ref)

    def finish(i, carry):
        rows = pl.ds(pl.multiple_of(i * BLK, BLK), BLK)
        x = x_ref[rows, :].astype(F32)
        r = lax.rsqrt(jnp.mean(x * x, axis=-1, keepdims=True) + EPSILON)
        normed = x * r
        da = da_own_ref[rows, :] + da_in_ref[rows, :].astype(F32)
        norm_ref[0:1, :] += jnp.sum(da * normed, axis=0, keepdims=True)
        dn = da * gain_attn
        grad = dh_ref[rows, :] + r * (dn - normed * jnp.mean(dn * normed, axis=-1, keepdims=True))
        half_ref[0, rows, :] = grad.astype(BF16)
        return carry

    lax.fori_loop(0, rows_half // BLK, finish, 0)
    norm_copy = remote(norm_ref, norm_in_ref, pair_send.at[2], pair_recv.at[2], partner)
    norm_copy.start()

    grad_x_copies, grad_x_relay = publish(0, grad_x_ref)
    if not gathered:
        z_start(1 - m, 0)
        z_start(m, 0)

    norm_copy.wait()
    norm = norm_ref[...] + norm_in_ref[...]
    if gathered:
        turned = jnp.concatenate([norm, jnp.zeros((LANES - 8, width), F32)], axis=0)
        turned = jnp.transpose(turned)
        line_ref[...] = jnp.where(lane_of == columns + 4, turned[:, 0:1], line_ref[...])
        norm_out_ref[...] = jnp.zeros_like(norm_out_ref)
        packs = [
            pltpu.make_async_copy(pack_ref, grads_ref, load.at[0]),
            pltpu.make_async_copy(line_ref, lines_ref, load.at[1]),
        ]
        for copy in packs:
            copy.start()
        for copy in packs:
            copy.wait()
    else:
        norm_line_ref[...] = jnp.zeros_like(norm_line_ref)
        for j in range(width // LANES):
            norm_line_ref[j : j + 1, :] = norm[0:1, j * LANES : (j + 1) * LANES]

        def norm_give(j):
            e = lax.rem(d + j, n)
            return remote(
                norm_line_ref, norm_all_ref.at[d], norm_send.at[j], norm_recv.at[j], (e, t)
            )

        def norm_start(j, carry):
            norm_give(j).start()
            return carry

        lax.fori_loop(1, n, norm_start, 0)
        norm_all_ref[d] = norm_line_ref[...]

        def norm_wait(j, carry):
            norm_give(j).wait()
            return carry

        lax.fori_loop(1, n, norm_wait, 0)
        value = norm_all_ref[0]
        for e in range(1, n):
            value = value + norm_all_ref[e]
        norm_cross_ref[0] = value
        norm_cross_copy = remote(
            norm_cross_ref.at[0], norm_cross_ref.at[1], pair_send.at[5], pair_recv.at[5], across
        )
        norm_cross_copy.start()
        def arrive_lines(j, carry):
            line_copy(j).wait()
            return carry

        lax.fori_loop(1, n, arrive_lines, 0)
        value = line_in_ref[0].astype(F32)
        for e in range(1, n):
            value = value + line_in_ref[e].astype(F32)
        cross_line_ref[0] = value
        cross_line_copy = remote(
            cross_line_ref.at[0], cross_line_ref.at[1], pair_send.at[4], pair_recv.at[4], across
        )
        cross_line_copy.start()
        for s, stage in ((0, 1), (1, 1), (1 - m, 0)):
            for j in range(1, ring):
                z_copy(s, stage, j).wait()

        def total(s):
            value = pack_ref[s, slab(d), :].astype(F32)
            for j in range(1, ring):
                value = value + z_in_ref[s, j].astype(F32)
            return value

        cross_ref[...] = total(1 - m).astype(BF16)
        cross_copy = remote(cross_ref, cross_in_ref, pair_send.at[3], pair_recv.at[3], across)
        cross_copy.start()
        for j in range(1, ring):
            z_copy(m, 0, j).wait()
        grads_ref[...] = total(m)
        result_copies[0].wait_recv()
        result_relay.start()

        cross_copy.wait()
        grads_ref[...] += cross_in_ref[...].astype(F32)
        cross_line_copy.wait()
        lines_ref[...] = cross_line_ref[0] + cross_line_ref[1]
        norm_cross_copy.wait()
        norm_out_ref[...] = norm_cross_ref[0] + norm_cross_ref[1]

    grad_x_copies[0].wait_recv()
    grad_x_relay.start()
    if gathered:
        result_copies[0].wait_recv()
        result_relay.start()
    for copies, relay in ((grad_x_copies, grad_x_relay), (result_copies, result_relay)):
        copies[0].wait_send()
        copies[1].wait()
        copies[2].wait()
        relay.wait()
    logit_copy.wait()

    for copy in sum_copies:
        copy.wait()

    def clear(j, carry):
        give(j).wait_send()
        return carry

    lax.fori_loop(1, n, clear, 0)

    def passed(j, carry):
        hand(j).wait_send()
        return carry

    lax.fori_loop(0, n, passed, 0)


def last_kernel(
    part,
    columns,
    results_ref,
    grad_x_ref,
    own_in_ref,
    far_in_ref,
    own_down_ref,
    far_down_ref,
    logit_ref,
    grads_ref,
    lines_ref,
    norm_ref,
    results_out,
    grad_x_out,
    in_out,
    down_out,
    logit_out,
    attn_out,
    moe_out,
    heads_out,
    out_out,
    router_out,
    const_out,
    vec_out,
):
    results_out[...] = results_ref[...]
    grad_x_out[...] = grad_x_ref[...]
    in_out[...] = own_in_ref[...] + far_in_ref[...].astype(F32)
    down_out[...] = own_down_ref[...] + far_down_ref[...].astype(F32)

    @pl.when(pl.program_id(0) == 0)
    def _():
        for m in range(2):
            logit_out[:, m, :] = logit_ref[m, 0:columns, :]
        firsts = [grads_ref[:, j * LANES : (j + 1) * LANES] for j in range(4)]
        odds = []
        for j in range(2):
            both = grads_ref[:, (4 + j) * LANES : (5 + j) * LANES]
            odds.extend([both, swap_halves(both)])
        for j in range(3):
            heads_out[j, :, 0:LANES] = firsts[j]
            heads_out[j, :, LANES : LANES + HD] = odds[j][:, 0:HD]
        spare = jnp.zeros((LANES - part, 2 * LANES), F32)
        rows = jnp.concatenate([firsts[3], odds[3]], axis=1)
        turned = jnp.transpose(jnp.concatenate([rows, spare], axis=0))
        out_out[...] = turned[0 : LANES + HD, 0:part]
        lines = jnp.concatenate([lines_ref[...], spare[:, 0:LANES]], axis=0)
        lines = jnp.transpose(lines)[:, 0:part]
        router_out[...] = lines[0:columns]
        const_out[...] = lines[columns : columns + 4]
        norm = jnp.concatenate([norm_ref[...], jnp.zeros((LANES - 8, LANES), F32)], axis=0)
        norm = jnp.transpose(norm)
        place = lax.broadcasted_iota(jnp.int32, (LANES, part), 0)
        wanted = lax.broadcasted_iota(jnp.int32, (LANES, part), 1) + lax.axis_index("dp") * part
        total = jnp.zeros((1, part), F32)
        for j in range(results_ref.shape[2] // LANES):
            chosen = jnp.where(place + j * LANES == wanted, norm[:, j : j + 1], 0.0)
            total = total + jnp.sum(chosen, axis=0, keepdims=True)
        attn_out[...] = total
        moe_out[...] = lines[columns + 5 : columns + 6]
        vec_out[...] = lines[columns + 6 : columns + 8]


def across_chips(value):
    return lax.ppermute(value, "tensor", [(0, 2), (2, 0), (1, 3), (3, 1)])


def across_cores(value):
    return lax.ppermute(value, "tensor", [(0, 1), (1, 0), (2, 3), (3, 2)])


def body(
    tokens,
    cotangent,
    prev_logits,
    routes,
    norm_attn,
    norm_moe,
    w_qkv,
    w_out,
    w_router,
    w_const,
    const_vec,
    w_in,
    w_down,
):
    rows, width = tokens.shape[1:]
    n = lax.axis_size("dp")
    experts = n
    columns = prev_logits.shape[2]
    capacity = 4 * max(1, 3 * rows // (4 * (experts + 4)))
    half = capacity // 2
    padded = -(-half // 16) * 16
    share = w_qkv.shape[2]
    local = 2 * share
    part = w_qkv.shape[1]
    t = lax.axis_index("tensor")
    m, c = t // 2, t % 2

    cosine, sine = (jnp.asarray(v) for v in rope_constants())
    pairs = local // LANES

    tinies = [w_router.T, w_const.T, norm_attn[None], norm_moe[None], const_vec]
    gathered = part % 16 != 0
    if gathered:
        wo_rows = w_out.T
        tiny = jnp.concatenate(
            tinies + [jnp.zeros((LANES - columns - 8, part), BF16)], axis=0
        )
        packed = jnp.concatenate(
            [w_qkv[i, :, :LANES] for i in range(3)]
            + [wo_rows[:, :LANES]]
            + [w_qkv[i, :, LANES:] for i in range(3)]
            + [wo_rows[:, LANES:], tiny.T],
            axis=1,
        )
    if gathered:
        packed = lax.all_gather(packed, "dp", axis=0, tiled=True)
        other = across_chips(packed)
        tinies = [jnp.where(m == 0, jnp.stack([packed, other]), jnp.stack([other, packed]))]
    late = [
        struct((n, padded, width), BF16),
        struct((n, 8, padded), F32),
        struct((LANES, width), F32),
    ]
    early = [
        struct((rows, width), BF16),
        struct((pairs, rows, LANES), BF16),
        struct((pairs, rows, LANES), BF16),
        struct((pairs, rows, LANES), BF16),
        struct((rows, width), BF16),
        struct((8, 8, rows), F32),
        struct((rows, LANES), F32),
        struct((width, width), BF16),
        struct((width, LANES), BF16),
        struct((2, width, 7 * LANES), BF16),
        struct((rows, width), F32),
        struct((rows, width), BF16),
        struct((rows, LANES), F32),
    ]
    landing = [struct((n, padded, width), BF16), struct(w_in.shape, BF16)]
    dma = pltpu.SemaphoreType.DMA
    outs = pl.pallas_call(
        functools.partial(front_kernel, n, half, padded, gathered, len(early)),
        out_shape=late + early + landing,
        in_specs=[aspec()] * 3 + [vspec()] * 5 + [aspec()] + [vspec()] * len(tinies),
        out_specs=[vspec()] * len(late) + [aspec()] * (len(early) + len(landing)),
        scratch_shapes=[pltpu.VMEM(o.shape, o.dtype) for o in early]
        + [
            pltpu.VMEM((rows, width), BF16),
            pltpu.VMEM((rows, width), BF16),
            pltpu.VMEM((2, rows), jnp.int32),
            pltpu.VMEM((LANES, rows), F32),
            pltpu.VMEM((LANES, rows), F32),
            pltpu.VMEM((n, padded, width), BF16),
            dma((3,)),
            dma((8, n // 2)),
            dma((8, n // 2)),
            dma((n,)),
            dma((n,)),
            dma((1,)),
            dma((pairs + 1,)),
            dma((pairs + 1,)),
            dma((1,)),
            dma((1,)),
            dma((len(early),)),
        ],
        compiler_params=pltpu.CompilerParams(
            collective_id=0, has_side_effects=True, vmem_limit_bytes=VMEM_LIMIT
        ),
        cost_estimate=pl.CostEstimate(
            flops=60_000_000_000, bytes_accessed=60_000_000, transcendentals=0
        ),
    )(
        tokens,
        cotangent,
        jnp.swapaxes(routes, 1, 2),
        jnp.transpose(prev_logits, (2, 0, 1)),
        w_qkv,
        w_out,
        cosine,
        sine,
        w_in,
        *tinies,
    )
    slots, gate_slots, extra, a, q, k, v, o_all, lse, pos = outs[:10]
    wo_all, small_all, spread, h, ub, stats, dy_arrived, in_x = outs[10:]

    hidden_width = w_in.shape[3]
    slots_all = experts * padded
    if gathered:
        in_x, down_x = across_chips(w_in), across_chips(w_down)
        in_c, down_c = across_cores(w_in), across_cores(w_down)
        in_d, down_d = across_cores(in_x), across_cores(down_x)
        chunk = min(256 if slots_all <= 1024 else 128, hidden_width)
        per = hidden_width // chunk

        def in_map(i):
            return lambda f: (0, 0, 0, jnp.clip(f - per * i, 0, per - 1))

        def down_map(i):
            return lambda f: (0, jnp.clip(f - per * i, 0, per - 1), 0)

        in_blocks = [pl.BlockSpec((1, 2, width, chunk), in_map(i)) for i in range(4)]
        down_blocks = [pl.BlockSpec((1, chunk, width), down_map(i)) for i in range(4)]
        expert_outs = (
            [
                struct((n, padded, width), BF16),
                struct((n, padded, width), BF16),
                struct((n, 8, padded), F32),
            ]
            + [struct(w_in.shape, BF16)] * 4
            + [struct(w_down.shape, BF16)] * 4
        )

        def whole(shape):
            return pl.BlockSpec(
                shape, lambda f: (0,) * len(shape), pipeline_mode=pl.Buffered(1)
            )

        parts = pl.pallas_call(
            functools.partial(expert_kernel, n, padded),
            grid=(4 * per,),
            out_shape=expert_outs,
            in_specs=[
                whole((slots_all, width)),
                whole((slots_all, width)),
                whole((n, 8, padded)),
            ]
            + in_blocks
            + down_blocks,
            out_specs=[
                whole((n, padded, width)),
                whole((n, padded, width)),
                whole((n, 8, padded)),
            ]
            + in_blocks
            + down_blocks,
            scratch_shapes=[
                pltpu.VMEM((width, slots_all), BF16),
                pltpu.VMEM((slots_all, width), BF16),
                pltpu.VMEM((slots_all, LANES), F32),
                pltpu.VMEM((slots_all, width), F32),
                pltpu.VMEM((slots_all, width), F32),
                pltpu.VMEM((2, width, chunk), BF16),
                pltpu.VMEM((chunk, width), BF16),
            ],
            compiler_params=pltpu.CompilerParams(vmem_limit_bytes=VMEM_LIMIT),
            cost_estimate=pl.CostEstimate(
                flops=18 * slots_all * width * 4 * hidden_width,
                bytes_accessed=30_000_000,
                transcendentals=0,
            ),
        )(
            lax.all_to_all(slots, "dp", split_axis=0, concat_axis=0, tiled=True).reshape(
                slots_all, width
            ),
            dy_arrived.reshape(slots_all, width),
            lax.all_to_all(gate_slots, "dp", split_axis=0, concat_axis=0, tiled=True),
            w_in,
            in_c,
            in_x,
            in_d,
            w_down,
            down_c,
            down_x,
            down_d,
        )
        gy, dx, dg = parts[0:3]
        gin, gdown = parts[3:7], parts[7:11]

        def everywhere(value):
            value = lax.all_to_all(value, "dp", split_axis=0, concat_axis=0, tiled=True)
            other = across_cores(value)
            return jnp.where(c == 0, jnp.stack([value, other]), jnp.stack([other, value]))

        dx_all, dg_all = everywhere(dx), everywhere(dg)

        def total(own, core, chip, diagonal):
            chip = (chip.astype(F32) + across_cores(diagonal).astype(F32)).astype(BF16)
            own = own.astype(F32) + across_cores(core).astype(F32)
            return own + across_chips(chip).astype(F32)

        grad_in, grad_down = total(*gin), total(*gdown)
        chip_in = []
    else:
        gy, own_in, own_down, chip_in, far_down, dx_all, dg_all = pl.pallas_call(
            functools.partial(expert_exchange_kernel, n, padded),
            out_shape=[
                struct((n, padded, width), BF16),
                struct(w_in.shape, F32),
                struct(w_down.shape, F32),
                struct(w_in.shape, BF16),
                struct(w_down.shape, BF16),
                struct((2, n, padded, width), BF16),
                struct((2, n, 8, padded), F32),
            ],
            in_specs=[aspec()] * 6,
            out_specs=[aspec()] * 7,
            scratch_shapes=[
                pltpu.VMEM((n, padded, width), BF16),
                pltpu.VMEM(w_in.shape, F32),
                pltpu.VMEM(w_down.shape, F32),
                pltpu.VMEM(w_in.shape, BF16),
                pltpu.VMEM((slots_all, width), BF16),
                pltpu.VMEM((width, slots_all), BF16),
                pltpu.VMEM((slots_all, width), BF16),
                pltpu.VMEM((slots_all, width), BF16),
                pltpu.VMEM((slots_all, LANES), F32),
                pltpu.VMEM((n, 8, padded), F32),
                pltpu.VMEM((4, 2, width, hidden_width), BF16),
                pltpu.VMEM((4 * hidden_width, width), BF16),
                pltpu.VMEM((slots_all, 4 * hidden_width), BF16),
                pltpu.VMEM((slots_all, 4 * hidden_width), BF16),
                pltpu.VMEM((slots_all, 4 * hidden_width), BF16),
                pltpu.VMEM((slots_all // 4, width), F32),
                pltpu.VMEM((slots_all, width), BF16),
                pltpu.VMEM((n, 8, padded), F32),
                pltpu.VMEM((2,) + w_in.shape[1:], BF16),
                pltpu.VMEM((2,) + w_down.shape[1:], BF16),
                pltpu.VMEM(w_down.shape, BF16),
                dma((10 + n,)),
                dma((n,)),
                dma((n,)),
                dma((n,)),
                dma((n,)),
                dma((n,)),
                dma((n,)),
                dma((n,)),
                dma((n,)),
                dma((2, n)),
                dma((2, n)),
                dma((4,)),
                dma((4,)),
                dma((6,)),
                dma((6,)),
                dma((4,)),
            ],
            compiler_params=pltpu.CompilerParams(
                collective_id=2, has_side_effects=True, vmem_limit_bytes=VMEM_LIMIT
            ),
            cost_estimate=pl.CostEstimate(
                flops=60_000_000_000, bytes_accessed=40_000_000, transcendentals=0
            ),
        )(
            slots,
            gate_slots,
            dy_arrived,
            w_in,
            in_x,
            w_down,
        )
        chip_in = [chip_in]

    groups = 6 * LANES
    logit_rows = -(-columns // 8) * 8
    rear_outs = [
        struct((2, logit_rows, rows), F32),
        struct((2, width, groups), BF16) if gathered else struct((part, groups), F32),
        struct((width if gathered else part, LANES), F32),
        struct((8, LANES), F32),
    ]
    half_rows = rows // 2
    spread_n = 1 if gathered else n // 2
    line_n = 1 if gathered else n
    kept = [
        struct((2, n, padded, width), BF16),
        struct((rows, width), F32),
        struct((width, width), BF16),
        struct((rows, width), BF16),
        struct((pairs, rows, LANES), BF16),
        struct((pairs, rows, LANES), BF16),
        struct((pairs, rows, LANES), BF16),
        struct((8, 8, rows), F32),
        struct((rows, LANES), F32),
        struct((rows, LANES), F32),
        struct((rows, width), BF16),
        struct((2, width, 3 * LANES), BF16),
        struct((2, width, 2 * LANES), BF16),
    ]
    results, input_grads, logits, grads, lines, norm_line, *far_in = pl.pallas_call(
        functools.partial(rear_kernel, n, half, padded, gathered, part),
        out_shape=[struct((2, rows, width), BF16)] * 2
        + rear_outs
        + [struct(w_in.shape, BF16)] * len(chip_in),
        in_specs=[aspec()] * (len(chip_in) + 4 + len(kept)) + [vspec()] * 5,
        out_specs=[aspec()] * 2
        + [vspec()]
        + [aspec() if gathered else vspec()] * 2
        + [vspec()]
        + [aspec()] * len(chip_in),
        scratch_shapes=[pltpu.VMEM(o.shape, o.dtype) for o in kept]
        + [
            pltpu.VMEM((half_rows, width), BF16),
            pltpu.VMEM((rows, width), BF16),
            pltpu.VMEM((rows, local), BF16),
            pltpu.VMEM((2, n, padded, width), BF16),
            pltpu.VMEM((half_rows, width), F32),
            pltpu.VMEM((rows, width), BF16),
            pltpu.VMEM((rows, local), BF16),
            pltpu.VMEM((rows, LANES), BF16),
            pltpu.VMEM((8, width), F32),
            pltpu.VMEM((2, rows, 5 * LANES), BF16),
            pltpu.VMEM((rows, LANES), F32),
            pltpu.VMEM((rows, LANES), F32),
            pltpu.VMEM((width, LANES), F32),
            pltpu.VMEM((2, width, groups), BF16),
            pltpu.VMEM((width, LANES), F32),
            pltpu.VMEM((2, spread_n, part, groups), BF16),
            pltpu.VMEM((2, spread_n, part, groups), BF16),
            pltpu.VMEM((line_n, part, LANES), BF16),
            pltpu.VMEM((part, groups), BF16),
            pltpu.VMEM((part, groups), BF16),
            pltpu.VMEM((2, part, LANES), F32),
            pltpu.VMEM((half_rows, width), BF16),
            pltpu.VMEM((half_rows, width), BF16),
            pltpu.VMEM((half_rows, width), F32),
            pltpu.VMEM((8, width), F32),
            pltpu.VMEM((8, width), F32),
            pltpu.VMEM((2, half_rows, width), BF16),
            pltpu.VMEM((8, LANES), F32),
            pltpu.VMEM((line_n, 8, LANES), F32),
            pltpu.VMEM((2, 8, LANES), F32),
            pltpu.VMEM((width, LANES), BF16),
            dma((3,)),
            dma((len(kept),)),
            dma((n,)),
            dma((n,)),
            dma((3,)),
            dma((n,)),
            dma((n,)),
            dma((4, 2, n // 2)),
            dma((4, 2, n // 2)),
            dma((n,)),
            dma((n,)),
            dma((6,)),
            dma((6,)),
            dma((2, 3)),
            dma((2, 3)),
            dma((1,)),
            dma((1,)),
            dma((n,)),
            dma((n,)),
        ],
        compiler_params=pltpu.CompilerParams(
            collective_id=1, has_side_effects=True, vmem_limit_bytes=VMEM_LIMIT
        ),
        cost_estimate=pl.CostEstimate(
            flops=100_000_000_000, bytes_accessed=60_000_000, transcendentals=0
        ),
    )(
        *chip_in,
        gy,
        tokens,
        cotangent,
        o_all,
        dx_all,
        h,
        wo_all,
        ub,
        q,
        k,
        v,
        lse,
        cosine,
        sine,
        a,
        spread,
        spread,
        stats,
        pos,
        small_all,
        extra,
        dg_all,
    )
    if not gathered:
        steps = 4

        def split(value, axis):
            block = list(value.shape)
            block[axis] //= steps

            def index(i):
                where = [0] * len(block)
                where[axis] = i
                return tuple(where)

            return pl.BlockSpec(tuple(block), index)

        def full(value):
            return pl.BlockSpec(value.shape, lambda i: (0,) * len(value.shape))

        large = [
            (results, 1),
            (input_grads, 1),
            (own_in, 2),
            (far_in[0], 2),
            (own_down, 1),
            (far_down, 1),
        ]
        tinies = [
            struct((columns, 2, rows), F32),
            struct((1, part), F32),
            struct((1, part), F32),
            struct((3, part, share), F32),
            struct((share, part), F32),
            struct((columns, part), F32),
            struct((4, part), F32),
            struct((2, part), F32),
        ]
        final = [large[0], large[1], large[2], large[4]]
        done = pl.pallas_call(
            functools.partial(last_kernel, part, columns),
            grid=(steps,),
            out_shape=[struct(v.shape, v.dtype) for v, _ in final] + tinies,
            in_specs=[split(v, axis) for v, axis in large]
            + [full(v) for v in (logits, grads, lines, norm_line)],
            out_specs=[split(v, axis) for v, axis in final] + [full(v) for v in tinies],
            compiler_params=pltpu.CompilerParams(vmem_limit_bytes=VMEM_LIMIT),
        )(*(v for v, _ in large), logits, grads, lines, norm_line)
        results, input_grads, grad_in, grad_down, logits = done[:5]
        gain_attn, gain_moe, heads, out, router, const, vec = done[5:]
        return (
            results,
            input_grads,
            jnp.transpose(logits, (1, 2, 0)),
            gain_attn[0],
            gain_moe[0],
            heads,
            out,
            router.T,
            const.T,
            vec,
            grad_in,
            grad_down,
        )
    grads = lax.psum_scatter(grads.astype(F32), "dp", scatter_dimension=1, tiled=True)
    lines = lax.psum_scatter(lines, "dp", scatter_dimension=0, tiled=True)
    other = lax.dynamic_index_in_dim(grads, 1 - m, 0, keepdims=False)
    grads = lax.dynamic_index_in_dim(grads, m, 0, keepdims=False) + across_chips(other)
    lines = lines + across_chips(lines)

    def heads(j):
        start = (4 + (j % 4) // 2) * LANES + (j % 2) * HD
        return jnp.concatenate(
            [grads[:, j * LANES : (j + 1) * LANES], grads[:, start : start + HD]], axis=1
        )

    return (
        results,
        input_grads,
        jnp.swapaxes(logits[:, :columns], 1, 2),
        lines[:, columns + 4],
        lines[:, columns + 5],
        jnp.stack([heads(i) for i in range(3)]),
        heads(3).T,
        lines[:, :columns],
        lines[:, columns : columns + 4],
        lines[:, columns + 6 : columns + 8].T,
        grad_in,
        grad_down,
    )


def solution(mesh):
    in_specs = (
        P(None, "dp", None),
        P(None, "dp", None),
        P(None, "dp", None),
        P(None, "dp", None),
        P("dp"),
        P("dp"),
        P(None, "dp", "tensor"),
        P("tensor", "dp"),
        P("dp", None),
        P("dp", None),
        P(None, "dp"),
        P("dp", None, None, "tensor"),
        P("dp", "tensor", None),
    )
    out_specs = (
        P(None, "dp", None),
        P(None, "dp", None),
        P(None, "dp", None),
        P("dp"),
        P("dp"),
        P(None, "dp", "tensor"),
        P("tensor", "dp"),
        P("dp", None),
        P("dp", None),
        P(None, "dp"),
        P("dp", None, None, "tensor"),
        P("dp", "tensor", None),
    )
    return jax.shard_map(body, mesh=mesh, in_specs=in_specs, out_specs=out_specs, check_vma=False)
```
